32 devices in a mesh: grp: 4 (over z), frac: 8 (over y, x, core).
Axes of the slice: x: 2, y: 2, z: 4, core: 2. Of those that a mesh axis runs over, the one named last changes fastest.
Arguments:
- matrix_state: float32 [2, 512, 2048], P(None, 'grp', 'frac'), may hold values from 0 to 1
- matrix_perm: float32 [512, 2048], P('grp', 'frac'), may hold values from 0.1 to 10
- frac_state: float32 [2, 4, 65536], P(None, 'grp', 'frac'), may hold values from 0 to 1
- frac_aperture: float32 [4, 65536], P('grp', 'frac'), may hold values from 0.5 to 4
- link_cell: int32 [4, 8, 8, 256], P('grp', 'frac'), may hold values from 0 to 32767
- link_seg: int32 [4, 8, 8, 256], P('grp', 'frac'), may hold values from 0 to 8191
- link_trans: float32 [4, 8, 8, 256], P('grp', 'frac'), may hold values from 0.1 to 2
- link_count: int32 [4, 8, 8], P('grp', 'frac'), may hold values from 32 to 256, as said below
- link_upwind: int32 [3, 4, 8, 8, 256], P(None, 'grp', 'frac'), may hold values from 0 to 1
Outputs:
- matrix_out: float32 [2, 512, 2048], P(None, 'grp', 'frac')
- frac_out: float32 [2, 4, 65536], P(None, 'grp', 'frac')
The draws below stay inside these ranges and needn't reach their ends.
Inputs may be any that keep to these rules, and one draw needn't show every extreme that they name: `link_count`: in each source device's list at least one owner block holds exactly 256 live slots; slots at or beyond a block's count are padding. `link_cell`: A live slot's cell index lies within the source device's 128 x 256 block. `link_seg`: A slot's segment index counts within the owner's 8192 segments. `link_upwind`: 1 takes the upwind saturation from the matrix cell, 0 from the fracture segment.
All inputs are finite; a program needn't handle non-finite values.
Results may differ from the reference program's by a relative error of at most 0.00002.
Values sent between devices are 32-bit elements; how exact they have to be, the bound alone decides.
No kernel may reach another device: no remote copies, remote signals or barrier semaphores. Data moves between devices by JAX's collectives and lax.ppermute only.
A program may use at most 128 MiB of HBM per device.

```python
import math
import jax
import jax.numpy as jnp

CR = 128
CC = 256
SEG_DEV = 8192
CAP = 256
ITERS = 3
SWEEPS = 4
GROUPS = 4
MEMBERS = 8
NR = 512
NC = 2048
SEG = 65536


def draw_link_count(key, part):
    first_key, second_key = jax.random.split(jax.random.fold_in(key, 17))
    lowest = max(1, CAP // 8)
    base_counts = jax.random.randint(first_key, (GROUPS, MEMBERS, MEMBERS), lowest, CAP + 1)
    full_owner = jax.random.randint(second_key, (GROUPS, MEMBERS, 1), 0, MEMBERS)
    owner_ids = jnp.arange(MEMBERS, dtype=jnp.int32)[None, None, :]
    return jnp.where(owner_ids == full_owner, CAP, base_counts).astype(jnp.int32)


def with_ends(array, rng, smallest, largest):
    longest = array.shape.index(max(array.shape))
    spots = []
    for shift in (0, 1):
        where = [jax.random.randint(jax.random.fold_in(rng, axis), (), 0, length) for axis, length in enumerate(array.shape)]
        where[longest] = (where[longest] + shift) % array.shape[longest]
        spots.append(tuple(where))
    return array.at[spots[0]].set(smallest).at[spots[1]].set(largest)


def steps_of(key, shape, cuts, low, largest):
    gain, own = 1.0, jax.random.fold_in(key, 6)
    for axis_at, parts in cuts:
        heights = jnp.exp(jax.random.uniform(jax.random.fold_in(own, axis_at), (parts,), jnp.float32, low / len(cuts), largest / len(cuts)))
        gain = gain * jnp.repeat(heights, shape[axis_at] // parts).reshape([-1 if axis == axis_at else 1 for axis in range(len(shape))])
    return gain


def setup_inputs(seed: int = 0) -> dict:
    splits = jax.random.split(jax.random.key(seed), 10)
    return {
        "matrix_state": jnp.clip(1.0 * jax.random.uniform(splits[0], (2, NR, NC), jnp.float32) ** steps_of(splits[0], (2, NR, NC), ((1, 4), (2, 8)), -0.2, 0.2), 0.0, 1.0),
        "matrix_perm": jnp.clip(jnp.exp(math.log(10.0) - 4.6051702 * jax.random.uniform(splits[1], (NR, NC), jnp.float32) ** steps_of(splits[1], (NR, NC), ((0, 4), (1, 8)), -0.2, 0.2)), 0.1, 10.0),
        "frac_state": jnp.clip(1.0 * jax.random.uniform(splits[2], (2, GROUPS, SEG), jnp.float32) ** steps_of(splits[2], (2, GROUPS, SEG), ((1, 4), (2, 8)), -0.2, 0.2), 0.0, 1.0),
        "frac_aperture": jnp.clip(jnp.exp(math.log(4.0) - 2.0794415 * jax.random.uniform(splits[3], (GROUPS, SEG), jnp.float32) ** steps_of(splits[3], (GROUPS, SEG), ((0, 4), (1, 8)), -0.2, 0.2)), 0.5, 4.0),
        "link_cell": with_ends(jax.random.randint(splits[4], (GROUPS, MEMBERS, MEMBERS, CAP), 0, CR * CC), jax.random.fold_in(splits[4], 1), 0, (CR * CC) - 1).astype(jnp.int32),
        "link_seg": with_ends(jax.random.randint(splits[5], (GROUPS, MEMBERS, MEMBERS, CAP), 0, SEG_DEV), jax.random.fold_in(splits[5], 1), 0, SEG_DEV - 1).astype(jnp.int32),
        "link_trans": jnp.clip(jnp.exp(math.log(2.0) - 2.9957323 * jax.random.uniform(splits[6], (GROUPS, MEMBERS, MEMBERS, CAP), jnp.float32) ** steps_of(splits[6], (GROUPS, MEMBERS, MEMBERS, CAP), ((0, 4), (1, 8)), -0.2, 0.2)), 0.1, 2.0),
        "link_count": draw_link_count(jax.random.fold_in(splits[9], 71), 0),
        "link_upwind": with_ends(jax.random.randint(splits[8], (ITERS, GROUPS, MEMBERS, MEMBERS, CAP), 0, 2), jax.random.fold_in(splits[8], 1), 0, 1).astype(jnp.int32),
    }


LOW_BOUND = 0.02
HIGH_BOUND = 1.98
TAU_STEP = 0.5
MOBILITY_FLOOR = 0.2


def apply_matrix(values, diagonal):
    padded = jnp.pad(values, 1)
    beside = padded[2:, 1:-1] + padded[:-2, 1:-1] + padded[1:-1, 2:] + padded[1:-1, :-2]
    return diagonal * values - beside


def chebyshev(start_field, right_side, diagonal):
    centre = 0.5 * (HIGH_BOUND + LOW_BOUND)
    half_width = 0.5 * (HIGH_BOUND - LOW_BOUND)
    scale_ratio = centre / half_width
    ratio_now = 1.0 / scale_ratio
    inverse = 1.0 / diagonal
    residual = inverse * (right_side - apply_matrix(start_field, diagonal))
    update = residual / centre
    iterate = start_field
    for sweep_index in range(SWEEPS):
        iterate = iterate + update
        if sweep_index + 1 < SWEEPS:
            residual = inverse * (right_side - apply_matrix(iterate, diagonal))
            ratio_next = 1.0 / (2.0 * scale_ratio - ratio_now)
            update = ratio_next * ratio_now * update + (2.0 * ratio_next / half_width) * residual
            ratio_now = ratio_next
    return iterate


def reference(matrix_state, matrix_perm, frac_state, frac_aperture, link_cell, link_seg, link_trans, link_count, link_upwind):
    shape_all = link_cell.shape
    group_ids = jnp.broadcast_to(jnp.arange(GROUPS, dtype=jnp.int32)[:, None, None, None], shape_all)
    source_ids = jnp.arange(MEMBERS, dtype=jnp.int32)[None, :, None, None]
    owner_ids = jnp.arange(MEMBERS, dtype=jnp.int32)[None, None, :, None]
    slot_ids = jnp.arange(CAP, dtype=jnp.int32)[None, None, None, :]
    live_slots = (slot_ids < link_count[..., None]).astype(jnp.int32)
    row_index = group_ids * CR + link_cell // CC
    column_index = jnp.broadcast_to(source_ids * CC + link_cell % CC, shape_all)
    segment_index = jnp.broadcast_to(owner_ids * SEG_DEV + link_seg, shape_all)
    pressure = matrix_state[0]
    saturation = matrix_state[1]
    frac_pressure = frac_state[0]
    frac_saturation = frac_state[1]
    for outer in range(ITERS):
        cell_pressure = pressure[row_index, column_index]
        cell_saturation = saturation[row_index, column_index]
        seg_pressure = frac_pressure[group_ids, segment_index]
        seg_saturation = frac_saturation[group_ids, segment_index]
        upwind_sat = jnp.where(link_upwind[outer] == 1, cell_saturation, seg_saturation)
        weight = jnp.where(live_slots == 1, link_trans * (MOBILITY_FLOOR + upwind_sat * upwind_sat), jnp.float32(0.0))
        water_flux = weight * (cell_pressure - seg_pressure) * upwind_sat
        empty_cells = jnp.zeros((NR, NC), jnp.float32)
        couple = empty_cells.at[row_index, column_index].add(weight)
        source_term = empty_cells.at[row_index, column_index].add(weight * seg_pressure)
        water_lost = empty_cells.at[row_index, column_index].add(water_flux)
        empty_segs = jnp.zeros((GROUPS, SEG), jnp.float32)
        inflow = empty_segs.at[group_ids, segment_index].add(weight * cell_pressure)
        weight_total = empty_segs.at[group_ids, segment_index].add(weight)
        gained = empty_segs.at[group_ids, segment_index].add(water_flux)
        diagonal = 4.0 + matrix_perm + couple
        new_pressure = chebyshev(pressure, matrix_perm * pressure + source_term, diagonal)
        new_saturation = saturation - TAU_STEP * water_lost / (matrix_perm + couple)
        left_values = jnp.pad(frac_pressure, ((0, 0), (1, 0)))[:, :-1]
        right_values = jnp.pad(frac_pressure, ((0, 0), (0, 1)))[:, 1:]
        new_frac_pressure = (frac_aperture * frac_pressure + inflow + left_values + right_values) / (frac_aperture + weight_total + 2.0)
        new_frac_saturation = frac_saturation + TAU_STEP * gained / (frac_aperture + weight_total)
        pressure = new_pressure
        saturation = new_saturation
        frac_pressure = new_frac_pressure
        frac_saturation = new_frac_saturation
    return jnp.stack([pressure, saturation]), jnp.stack([frac_pressure, frac_saturation])
```

```python
import functools

import jax
import jax.numpy as jnp
from jax import lax
from jax.experimental import pallas as pl
from jax.experimental.pallas import tpu as pltpu
from jax.sharding import PartitionSpec as P

ITERS = 3
SWEEPS = 4

LOW_BOUND = 0.02
HIGH_BOUND = 1.98
TAU_STEP = 0.5
MOBILITY_FLOOR = 0.2

F32 = jnp.float32
BF16 = jnp.bfloat16
LANES = 128
SUB = 8
DEPTH = SWEEPS - 1


def iota(shape, dim):
    return lax.broadcasted_iota(jnp.int32, shape, dim)


def parts_of(x):
    high = x.astype(BF16).astype(F32)
    rest = x - high
    mid = rest.astype(BF16).astype(F32)
    low = rest - mid
    return high, mid, low


def table_of(fields):
    split = [parts_of(f) for f in fields]
    return jnp.concatenate([s[p] for p in range(3) for s in split], axis=0).astype(BF16)


def one_hot(index_row, count):
    hit = iota((count, index_row.shape[1]), 0) == index_row
    return jnp.where(hit, 1.0, 0.0).astype(BF16)


def pick(table, fields, rows, row_index, hot):
    wide = jnp.dot(table, hot, preferred_element_type=F32)
    hit = iota((rows, row_index.shape[1]), 0) == row_index
    found = []
    for f in range(fields):
        total = sum(wide[(p * fields + f) * rows : (p * fields + f + 1) * rows] for p in range(3))
        found.append(jnp.sum(jnp.where(hit, total, 0.0), axis=0, keepdims=True))
    return found


def spread(left_ref, block, width, rows, row_index, values):
    hit = iota((rows, row_index.shape[1]), 0) == row_index
    at = slice(block * width, (block + 1) * width)
    for f, value in enumerate(values):
        for p, part in enumerate(parts_of(value)):
            row = (p * len(values) + f) * rows
            left_ref[row : row + rows, at] = jnp.where(hit, part, 0.0).astype(BF16)


def gathered_sum(left_ref, hot_ref, fields, rows):
    wide = lax.dot_general(
        left_ref[...], hot_ref[...], (((1,), (1,)), ((), ())), preferred_element_type=F32
    )
    return [
        sum(wide[(p * fields + f) * rows : (p * fields + f + 1) * rows] for p in range(3))
        for f in range(fields)
    ]


def flow(trans, upwind, cell_p, cell_s, seg_p, seg_s):
    u = jnp.where(upwind > 0.5, cell_s, seg_s)
    weight = trans * (MOBILITY_FLOOR + u * u)
    water = weight * (cell_p - seg_p) * u
    return weight, water


def cell_parts(cell_row, columns):
    return cell_row // columns, cell_row % columns


def ends_of(frac):
    rows = frac.shape[0]
    return jnp.concatenate([frac[0:1], frac[rows - 1 : rows]], axis=1)


def frac_step(frac, sat, aperture, before, after, inflow, total, gained):
    rows, lanes = frac.shape
    row, lane = iota((rows, lanes), 0), iota((rows, lanes), 1)
    back = pltpu.roll(frac, 1, 1)
    left = jnp.where(lane == 0, pltpu.roll(back, 1, 0), back)
    left = jnp.where((lane == 0) & (row == 0), before, left)
    ahead = pltpu.roll(frac, lanes - 1, 1)
    right = jnp.where(lane == lanes - 1, pltpu.roll(ahead, rows - 1, 0), ahead)
    right = jnp.where((lane == lanes - 1) & (row == rows - 1), after, right)
    new_frac = (aperture * frac + inflow + left + right) / (aperture + total + 2.0)
    new_sat = sat + TAU_STEP * gained / (aperture + total)
    return new_frac, new_sat


def chain_ends(ends_ref, row, members):
    me = lax.axis_index("frac")
    lanes = ends_ref.shape[2]
    prior = ends_ref[jnp.maximum(me - 1, 0), row : row + 1, :]
    later = ends_ref[jnp.minimum(me + 1, members - 1), row : row + 1, :]
    before = jnp.where(me > 0, prior[:, lanes - 1 :], 0.0)
    after = jnp.where(me < members - 1, later[:, 0:1], 0.0)
    return before, after


def partial_residual(pressure, couple, source, inverse):
    rows, columns = pressure.shape
    row, col = iota((rows, columns), 0), iota((rows, columns), 1)
    beside = jnp.where(row == 0, 0.0, pltpu.roll(pressure, 1, 0))
    beside += jnp.where(row == rows - 1, 0.0, pltpu.roll(pressure, rows - 1, 0))
    beside += jnp.where(col == 0, 0.0, pltpu.roll(pressure, 1, 1))
    beside += jnp.where(col == columns - 1, 0.0, pltpu.roll(pressure, columns - 1, 1))
    return inverse * (source - (4.0 + couple) * pressure + beside)


def pack_low(q, inv, p, at, axis):
    return jnp.where(
        at < DEPTH, q, jnp.where(at < 2 * DEPTH, pltpu.roll(inv, DEPTH, axis), pltpu.roll(p, 2 * DEPTH, axis))
    )


def pack_high(q, inv, p, at, axis):
    size = q.shape[axis]
    return jnp.where(
        at >= size - DEPTH,
        q,
        jnp.where(
            at >= size - 2 * DEPTH,
            pltpu.roll(inv, size - DEPTH, axis),
            pltpu.roll(p, size - 2 * DEPTH, axis),
        ),
    )


def send_halo(out_ref, q, inv, p, groups, members):
    rows, columns = q.shape
    g, f = lax.axis_index("grp"), lax.axis_index("frac")
    here = g * members + f
    sub = iota((SUB, columns), 0)
    top = pack_low(q[:SUB], inv[:SUB], p[:SUB], sub, 0)
    bottom = pack_high(q[rows - SUB :], inv[rows - SUB :], p[rows - SUB :], sub, 0)
    lane = iota((rows, LANES), 1)
    low = pack_low(q[:, :LANES], inv[:, :LANES], p[:, :LANES], lane, 1)
    high = pack_high(q[:, columns - LANES :], inv[:, columns - LANES :], p[:, columns - LANES :], lane, 1)
    turned = jnp.transpose(jnp.where(lane < LANES // 2, low, high))
    left, right = turned[:SUB], turned[LANES - SUB :]
    p_top, p_bottom = p[:SUB], p[rows - SUB :]

    for step, strip, p_strip in ((-1, top, p_top), (1, bottom, p_bottom)):
        inside = (g + step >= 0) & (g + step < groups)
        base = here + step * members

        @pl.when(inside)
        def _():
            out_ref[base] = strip

        @pl.when(inside & (f > 0))
        def _():
            out_ref[base - 1, :, 0:LANES] = strip[:, :LANES]
            out_ref[base - 1, :, LANES : 2 * LANES] = p_strip[:, :LANES]

        @pl.when(inside & (f < members - 1))
        def _():
            out_ref[base + 1, :, 0:LANES] = strip[:, columns - LANES :]
            out_ref[base + 1, :, LANES : 2 * LANES] = p_strip[:, columns - LANES :]

    @pl.when(f > 0)
    def _():
        out_ref[here - 1, :, 0:LANES] = left

    @pl.when(f < members - 1)
    def _():
        out_ref[here + 1, :, 0:LANES] = right


def chebyshev(in_ref, q, inv, p, q_ext, inv_ext, p_ext, groups, members):
    rows, columns = q.shape
    g, f = lax.axis_index("grp"), lax.axis_index("frac")
    here = g * members + f
    last = groups * members - 1

    def block(dg, df):
        ok = (g + dg >= 0) & (g + dg < groups) & (f + df >= 0) & (f + df < members)
        at = jnp.clip(here + dg * members + df, 0, last)
        return jnp.where(ok, in_ref[at], 0.0)

    sub = iota((SUB, columns), 0)
    below, above = block(1, 0), block(-1, 0)

    def both(low, high, at, count, size):
        return jnp.where(at < count, low, jnp.where(at >= size - count, high, 0.0))

    q_ext[0:rows, 0:columns] = q
    inv_ext[0:rows, 0:columns] = inv
    p_ext[0:rows, 0:columns] = p
    q_ext[rows : rows + SUB, 0:columns] = both(below, above, sub, DEPTH, SUB)
    inv_ext[rows : rows + SUB, 0:columns] = both(
        pltpu.roll(below, SUB - DEPTH, 0), pltpu.roll(above, DEPTH, 0), sub, DEPTH, SUB
    )
    p_ext[rows : rows + SUB, 0:columns] = both(
        pltpu.roll(below, SUB - 2 * DEPTH, 0), pltpu.roll(above, 2 * DEPTH, 0), sub, 2, SUB
    )
    right, left = block(0, 1)[:, :LANES], block(0, -1)[:, :LANES]
    turned = jnp.transpose(
        jnp.concatenate([right, jnp.zeros((LANES - 2 * SUB, rows), F32), left], axis=0)
    )
    lane = iota((rows, LANES), 1)
    side = slice(columns, columns + LANES)
    q_ext[0:rows, side] = both(turned, turned, lane, DEPTH, LANES)
    inv_ext[0:rows, side] = both(
        pltpu.roll(turned, LANES - DEPTH, 1), pltpu.roll(turned, DEPTH, 1), lane, DEPTH, LANES
    )
    p_ext[0:rows, side] = both(
        pltpu.roll(turned, LANES - 2 * DEPTH, 1), pltpu.roll(turned, 2 * DEPTH, 1), lane, 2, LANES
    )
    sub = iota((SUB, LANES), 0)
    lane = iota((SUB, LANES), 1)
    low_right, low_left = block(1, 1), block(1, -1)
    high_right, high_left = block(-1, 1), block(-1, -1)
    low = both(low_right, low_left, iota((SUB, 2 * LANES), 1) % LANES, DEPTH, LANES)
    high = both(high_right, high_left, iota((SUB, 2 * LANES), 1) % LANES, DEPTH, LANES)
    corner = slice(rows, rows + SUB)
    q_ext[corner, side] = both(low[:, :LANES], high[:, :LANES], sub, DEPTH, SUB)
    inv_ext[corner, side] = both(
        pltpu.roll(low[:, :LANES], SUB - DEPTH, 0), pltpu.roll(high[:, :LANES], DEPTH, 0), sub, DEPTH, SUB
    )
    p_ext[corner, side] = both(low[:, LANES:], high[:, LANES:], sub, DEPTH, SUB)

    shape = (rows + SUB, columns + LANES)
    row, col = iota(shape, 0), iota(shape, 1)
    field = p_ext[...]
    missing = jnp.where((row == 0) | (row == rows), pltpu.roll(field, 1, 0), 0.0)
    missing += jnp.where((row == rows - 1) | (row == rows + SUB - 1), pltpu.roll(field, shape[0] - 1, 0), 0.0)
    missing += jnp.where((col == 0) | (col == columns), pltpu.roll(field, 1, 1), 0.0)
    missing += jnp.where(
        (col == columns - 1) | (col == columns + LANES - 1), pltpu.roll(field, shape[1] - 1, 1), 0.0
    )
    inverse = inv_ext[...]
    start = q_ext[...] + inverse * missing

    centre = 0.5 * (HIGH_BOUND + LOW_BOUND)
    half_width = 0.5 * (HIGH_BOUND - LOW_BOUND)
    scale_ratio = centre / half_width
    ratio_now = 1.0 / scale_ratio
    update = start / centre if centre != 1.0 else start
    change = update
    for _ in range(SWEEPS - 1):
        beside = (
            pltpu.roll(change, 1, 0)
            + pltpu.roll(change, shape[0] - 1, 0)
            + pltpu.roll(change, 1, 1)
            + pltpu.roll(change, shape[1] - 1, 1)
        )
        residual = start - change + inverse * beside
        ratio_next = 1.0 / (2.0 * scale_ratio - ratio_now)
        update = ratio_next * ratio_now * update + (2.0 * ratio_next / half_width) * residual
        ratio_now = ratio_next
        change = change + update
    return p + change[0:rows, 0:columns]


ROW_SEG = 0
ROW_TRANS = 1
ROW_UP = 2
ROW_P = ROW_UP + ITERS
ROW_S = ROW_P + 1
ROW_ENDS = ROW_S + 1


def first_kernel(members, cell_ref, seg_ref, trans_ref, count_ref, up_ref, state_ref, frac_ref, out_ref):
    _, rows, columns = state_ref.shape
    width = cell_ref.shape[1]
    table = table_of([state_ref[0], state_ref[1]])
    ends = ends_of(frac_ref[0])
    for o in range(members):
        one = slice(o, o + 1)
        row, col = cell_parts(cell_ref[one, :], columns)
        cell_p, cell_s = pick(table, 2, rows, row, one_hot(col, columns))
        live = iota((1, width), 1) < count_ref[0, o]
        out_ref[o, ROW_SEG : ROW_SEG + 1, :] = seg_ref[one, :].astype(F32)
        out_ref[o, ROW_TRANS : ROW_TRANS + 1, :] = jnp.where(live, trans_ref[one, :], 0.0)
        for t in range(ITERS):
            out_ref[o, ROW_UP + t : ROW_UP + t + 1, :] = up_ref[t, one, :].astype(F32)
        out_ref[o, ROW_P : ROW_P + 1, :] = cell_p
        out_ref[o, ROW_S : ROW_S + 1, :] = cell_s
        out_ref[o, ROW_ENDS : ROW_ENDS + 1, :] = ends


def seg_parts(slot_ref, s):
    seg = slot_ref[s, ROW_SEG : ROW_SEG + 1, :].astype(jnp.int32)
    return seg // LANES, seg % LANES


def seg_hots(slot_ref, hot_ref, members, width):
    for s in range(members):
        hot_ref[:, s * width : (s + 1) * width] = one_hot(seg_parts(slot_ref, s)[1], LANES)


def seg_gather(slot_ref, hot_ref, fields, s, width, table):
    return pick(table, 2, fields, seg_parts(slot_ref, s)[0], hot_ref[:, s * width : (s + 1) * width])


def owner_start_kernel(members, slot_ref, frac_ref, aperture_ref, out_ref, new_ref, hot_ref, left_ref):
    width = slot_ref.shape[2]
    rows = frac_ref.shape[1]
    frac, sat = frac_ref[0], frac_ref[1]
    seg_hots(slot_ref, hot_ref, members, width)
    table = table_of([frac, sat])
    for s in range(members):
        seg_p, seg_s = seg_gather(slot_ref, hot_ref, rows, s, width, table)
        out_ref[s, 0:1, :] = seg_p
        out_ref[s, 1:2, :] = seg_s
        slot = slot_ref[s]
        cell_p = slot[ROW_P : ROW_P + 1]
        weight, water = flow(
            slot[ROW_TRANS : ROW_TRANS + 1],
            slot[ROW_UP : ROW_UP + 1],
            cell_p,
            slot[ROW_S : ROW_S + 1],
            seg_p,
            seg_s,
        )
        spread(left_ref, s, width, rows, seg_parts(slot_ref, s)[0], [weight * cell_p, weight, water])
    inflow, total, gained = gathered_sum(left_ref, hot_ref, 3, rows)
    before, after = chain_ends(slot_ref, ROW_ENDS, members)
    new_frac, new_sat = frac_step(frac, sat, aperture_ref[...], before, after, inflow, total, gained)
    new_ref[0] = new_frac
    new_ref[1] = new_sat
    table = table_of([new_frac, new_sat])
    ends = ends_of(new_frac)
    for s in range(members):
        seg_p, seg_s = seg_gather(slot_ref, hot_ref, rows, s, width, table)
        out_ref[s, 2:3, :] = seg_p
        out_ref[s, 3:4, :] = seg_s
        out_ref[s, 4:5, :] = ends


def cell_update(
    members, t, cell_ref, sent_ref, cell_rows, seg_rows, pressure, saturation, perm, hot_ref, left_ref
):
    rows, columns = pressure.shape
    width = cell_ref.shape[1]
    for o in range(members):
        row, col = cell_parts(cell_ref[o : o + 1, :], columns)
        hot_ref[:, o * width : (o + 1) * width] = one_hot(col, columns)
        seg_p, seg_s = seg_rows(o)
        cell_p, cell_s = cell_rows(o)
        weight, water = flow(
            sent_ref[o, ROW_TRANS : ROW_TRANS + 1, :],
            sent_ref[o, ROW_UP + t : ROW_UP + t + 1, :],
            cell_p,
            cell_s,
            seg_p,
            seg_s,
        )
        spread(left_ref, o, width, rows, row, [weight, weight * seg_p, water])
    couple, source, lost = gathered_sum(left_ref, hot_ref, 3, rows)
    inverse = 1.0 / (4.0 + perm + couple)
    new_saturation = saturation - TAU_STEP * lost / (perm + couple)
    return new_saturation, partial_residual(pressure, couple, source, inverse), inverse


def source_start_kernel(
    groups, members, cell_ref, sent_ref, seg_ref, state_ref, perm_ref, out_ref, keep_ref, hot_ref, left_ref
):
    pressure = state_ref[0]
    new_saturation, q, inv = cell_update(
        members,
        0,
        cell_ref,
        sent_ref,
        lambda o: (sent_ref[o, ROW_P : ROW_P + 1, :], sent_ref[o, ROW_S : ROW_S + 1, :]),
        lambda o: (seg_ref[o, 0:1, :], seg_ref[o, 1:2, :]),
        pressure,
        state_ref[1],
        perm_ref[...],
        hot_ref,
        left_ref,
    )
    keep_ref[0] = pressure
    keep_ref[1] = new_saturation
    keep_ref[2] = q
    keep_ref[3] = inv
    send_halo(out_ref, q, inv, pressure, groups, members)


def cell_gather(members, cell_ref, fields, put):
    rows, columns = fields[0].shape
    table = table_of(fields)
    for o in range(members):
        row, col = cell_parts(cell_ref[o : o + 1, :], columns)
        put(o, *pick(table, len(fields), rows, row, one_hot(col, columns)))


def middle_kernel(
    groups, members, halo_ref, cell_ref, sent_ref, seg_ref, kept_ref, perm_ref, out_ref, keep_ref,
    slots_ref, hot_ref, left_ref, q_ext, inv_ext, p_ext,
):
    pressure = chebyshev(
        halo_ref, kept_ref[2], kept_ref[3], kept_ref[0], q_ext, inv_ext, p_ext, groups, members
    )
    saturation = kept_ref[1]
    g = lax.axis_index("grp")

    def put(o, cell_p, cell_s):
        slots_ref[o, 0:1, :] = cell_p
        slots_ref[o, 1:2, :] = cell_s
        for half in range(2):
            at = slice(half * LANES, (half + 1) * LANES)
            out_ref[g * members + o, half : half + 1, LANES : 2 * LANES] = cell_p[:, at]
            out_ref[g * members + o, 2 + half : 3 + half, LANES : 2 * LANES] = cell_s[:, at]

    cell_gather(members, cell_ref, [pressure, saturation], put)
    new_saturation, q, inv = cell_update(
        members,
        1,
        cell_ref,
        sent_ref,
        lambda o: (slots_ref[o, 0:1, :], slots_ref[o, 1:2, :]),
        lambda o: (seg_ref[o, 2:3, :], seg_ref[o, 3:4, :]),
        pressure,
        saturation,
        perm_ref[...],
        hot_ref,
        left_ref,
    )
    keep_ref[0] = pressure
    keep_ref[1] = new_saturation
    keep_ref[2] = q
    keep_ref[3] = inv
    send_halo(out_ref, q, inv, pressure, groups, members)


def owner_update(members, t, slot_ref, cell_rows, seg_rows, frac, sat, aperture, ends, hot_ref, left_ref):
    width = slot_ref.shape[2]
    rows = frac.shape[0]
    seg_hots(slot_ref, hot_ref, members, width)
    for s in range(members):
        cell_p, cell_s = cell_rows(s)
        weight, water = flow(
            slot_ref[s, ROW_TRANS : ROW_TRANS + 1, :],
            slot_ref[s, ROW_UP + t : ROW_UP + t + 1, :],
            cell_p,
            cell_s,
            *seg_rows(s),
        )
        spread(left_ref, s, width, rows, seg_parts(slot_ref, s)[0], [weight * cell_p, weight, water])
    inflow, total, gained = gathered_sum(left_ref, hot_ref, 3, rows)
    return frac_step(frac, sat, aperture, *ends, inflow, total, gained)


def exchange_kernel(
    groups, members, halo_ref, cell_ref, slot_ref, ends_ref, own_ref, frac_ref, aperture_ref, kept_ref,
    out_ref, new_ref, pressure_ref, hot_ref, left_ref, q_ext, inv_ext, p_ext,
):
    width = slot_ref.shape[2]
    rows = frac_ref.shape[1]
    g = lax.axis_index("grp")

    def cell_rows(s):
        block = halo_ref[g * members + s]
        half = block[:, LANES : 2 * LANES]
        return (
            jnp.concatenate([half[0:1], half[1:2]], axis=1),
            jnp.concatenate([half[2:3], half[3:4]], axis=1),
        )

    new_frac, new_sat = owner_update(
        members,
        1,
        slot_ref,
        cell_rows,
        lambda s: (own_ref[s, 2:3, :], own_ref[s, 3:4, :]),
        frac_ref[0],
        frac_ref[1],
        aperture_ref[...],
        chain_ends(ends_ref, 4, members),
        hot_ref,
        left_ref,
    )
    new_ref[0] = new_frac
    new_ref[1] = new_sat
    table = table_of([new_frac, new_sat])
    ends = ends_of(new_frac)
    for s in range(members):
        seg_p, seg_s = seg_gather(slot_ref, hot_ref, rows, s, width, table)
        out_ref[s, 2:3, :] = seg_p
        out_ref[s, 3:4, :] = seg_s
        out_ref[s, 4:5, :] = ends

    pressure = chebyshev(
        halo_ref, kept_ref[2], kept_ref[3], kept_ref[0], q_ext, inv_ext, p_ext, groups, members
    )
    pressure_ref[...] = pressure

    def put(o, cell_p, cell_s):
        out_ref[o, 0:1, :] = cell_p
        out_ref[o, 1:2, :] = cell_s

    cell_gather(members, cell_ref, [pressure, kept_ref[1]], put)


def source_last_kernel(
    groups, members, cell_ref, sent_ref, own_ref, seg_ref, pressure_ref, kept_ref, perm_ref, out_ref, keep_ref,
    hot_ref, left_ref,
):
    pressure = pressure_ref[...]
    new_saturation, q, inv = cell_update(
        members,
        2,
        cell_ref,
        sent_ref,
        lambda o: (own_ref[o, 0:1, :], own_ref[o, 1:2, :]),
        lambda o: (seg_ref[o, 2:3, :], seg_ref[o, 3:4, :]),
        pressure,
        kept_ref[1],
        perm_ref[...],
        hot_ref,
        left_ref,
    )
    keep_ref[0] = new_saturation
    keep_ref[1] = q
    keep_ref[2] = inv
    send_halo(out_ref, q, inv, pressure, groups, members)


def owner_last_kernel(members, slot_ref, own_ref, seg_ref, frac_ref, aperture_ref, out_ref, hot_ref, left_ref):
    new_frac, new_sat = owner_update(
        members,
        2,
        slot_ref,
        lambda s: (seg_ref[s, 0:1, :], seg_ref[s, 1:2, :]),
        lambda s: (own_ref[s, 2:3, :], own_ref[s, 3:4, :]),
        frac_ref[0],
        frac_ref[1],
        aperture_ref[...],
        chain_ends(seg_ref, 4, members),
        hot_ref,
        left_ref,
    )
    out_ref[0] = new_frac
    out_ref[1] = new_sat


def final_kernel(groups, members, halo_ref, pressure_ref, kept_ref, out_ref, q_ext, inv_ext, p_ext):
    out_ref[0] = chebyshev(
        halo_ref, kept_ref[1], kept_ref[2], pressure_ref[...], q_ext, inv_ext, p_ext, groups, members
    )
    out_ref[1] = kept_ref[0]


VMEM = pl.BlockSpec(memory_space=pltpu.VMEM)
SMEM = pl.BlockSpec(memory_space=pltpu.SMEM)


def call(kernel, statics, outs, scratch, *args, smem=()):
    outs = [jax.ShapeDtypeStruct(s, F32) for s in outs]
    return pl.pallas_call(
        functools.partial(kernel, *statics),
        out_shape=outs,
        in_specs=[SMEM if i in smem else VMEM for i in range(len(args))],
        out_specs=[VMEM] * len(outs),
        scratch_shapes=[pltpu.VMEM(s, t) for s, t in scratch],
        compiler_params=pltpu.CompilerParams(vmem_limit_bytes=32 * 1024 * 1024),
        name=kernel.__name__,
    )(*args)


def on_device(
    matrix_state,
    matrix_perm,
    frac_state,
    frac_aperture,
    link_cell,
    link_seg,
    link_trans,
    link_count,
    link_upwind,
):
    groups, members = lax.axis_size("grp"), lax.axis_size("frac")
    both = (groups, members)
    devices = groups * members
    cells = link_cell[0, 0]
    width = cells.shape[1]
    _, rows, columns = matrix_state.shape
    seg_dev = frac_state.shape[2]
    seg_rows = seg_dev // LANES
    frac = frac_state.reshape(2, seg_rows, LANES)
    aperture = frac_aperture.reshape(seg_rows, LANES)

    slots = (members, SUB, width)
    halo = (devices, SUB, columns)
    hot_cell = ((columns, members * width), BF16)
    left_cell = ((9 * rows, members * width), BF16)
    hot_seg = ((LANES, members * width), BF16)
    left_seg = ((9 * seg_rows, members * width), BF16)
    ext = [((rows + SUB, columns + LANES), F32)] * 3

    def to_group(x):
        return lax.all_to_all(x, "frac", split_axis=0, concat_axis=0, tiled=True)

    def to_all(x):
        return lax.all_to_all(x, ("grp", "frac"), split_axis=0, concat_axis=0, tiled=True)

    (sent,) = call(
        first_kernel, (members,), [slots], [],
        cells, link_seg[0, 0], link_trans[0, 0], link_count[0], link_upwind[:, 0, 0], matrix_state, frac,
        smem=(3,),
    )
    slot = to_group(sent)
    own, frac1 = call(
        owner_start_kernel, (members,), [slots, frac.shape], [hot_seg, left_seg], slot, frac, aperture
    )
    segs = to_group(own)
    edge, kept = call(
        source_start_kernel, both, [halo, (4, rows, columns)], [hot_cell, left_cell],
        cells, sent, segs, matrix_state, matrix_perm,
    )
    around = to_all(edge)
    edge, kept = call(
        middle_kernel, both, [halo, (4, rows, columns)], [(slots, F32), hot_cell, left_cell] + ext,
        around, cells, sent, segs, kept, matrix_perm,
    )
    around = to_all(edge)
    own, frac2, pressure = call(
        exchange_kernel, both, [slots, frac.shape, (rows, columns)], [hot_seg, left_seg] + ext,
        around, cells, slot, segs, own, frac1, aperture, kept,
    )
    segs = to_group(own)
    edge, kept = call(
        source_last_kernel, both, [halo, (3, rows, columns)], [hot_cell, left_cell],
        cells, sent, own, segs, pressure, kept, matrix_perm,
    )
    around = to_all(edge)
    (frac3,) = call(
        owner_last_kernel, (members,), [frac.shape], [hot_seg, left_seg], slot, own, segs, frac2, aperture
    )
    (matrix_out,) = call(final_kernel, both, [matrix_state.shape], ext, around, pressure, kept)
    return matrix_out, frac3.reshape(frac_state.shape)


def solution(mesh):
    return jax.shard_map(
        on_device,
        mesh=mesh,
        in_specs=(
            P(None, "grp", "frac"),
            P("grp", "frac"),
            P(None, "grp", "frac"),
            P("grp", "frac"),
            P("grp", "frac", None, None),
            P("grp", "frac", None, None),
            P("grp", "frac", None, None),
            P("grp", "frac", None),
            P(None, "grp", "frac", None, None),
        ),
        out_specs=(P(None, "grp", "frac"), P(None, "grp", "frac")),
        check_vma=False,
    )
```

```python
import functools

import jax
import jax.numpy as jnp
from jax import lax
from jax.experimental import pallas as pl
from jax.experimental.pallas import tpu as pltpu
from jax.sharding import PartitionSpec as P

ITERS = 3
SWEEPS = 4

LOW_BOUND = 0.02
HIGH_BOUND = 1.98
TAU_STEP = 0.5
MOBILITY_FLOOR = 0.2

F32 = jnp.float32
BF16 = jnp.bfloat16
LANES = 128
SUB = 8
DEPTH = SWEEPS - 1


def iota(shape, dim):
    return lax.broadcasted_iota(jnp.int32, shape, dim)


def parts_of(x):
    high = x.astype(BF16).astype(F32)
    return high, x - high


PARTS = 2


def table_of(fields):
    split = [parts_of(f) for f in fields]
    return jnp.concatenate([s[p] for p in range(PARTS) for s in split], axis=0).astype(BF16)


def one_hot(index_row, count):
    hit = iota((count, index_row.shape[1]), 0) == index_row
    return jnp.where(hit, 1.0, 0.0).astype(BF16)


def pick(table, fields, rows, row_index, hot):
    wide = jnp.dot(table, hot, preferred_element_type=F32)
    hit = iota((rows, row_index.shape[1]), 0) == row_index
    found = []
    for f in range(fields):
        total = sum(wide[(p * fields + f) * rows : (p * fields + f + 1) * rows] for p in range(PARTS))
        found.append(jnp.sum(jnp.where(hit, total, 0.0), axis=0, keepdims=True))
    return found


def spread(left_ref, row_hot_ref, block, values):
    rows = row_hot_ref.shape[0]
    width = values[0].shape[1]
    at = slice(block * width, (block + 1) * width)
    hot = row_hot_ref[:, at]
    for f, value in enumerate(values):
        for p, part in enumerate(parts_of(value)):
            row = (p * len(values) + f) * rows
            left_ref[row : row + rows, at] = hot * part.astype(BF16)


def gathered_sum(left_ref, hot_ref, fields, rows):
    wide = lax.dot_general(
        left_ref[...], hot_ref[...], (((1,), (1,)), ((), ())), preferred_element_type=F32
    )
    return [
        sum(wide[(p * fields + f) * rows : (p * fields + f + 1) * rows] for p in range(PARTS))
        for f in range(fields)
    ]


def flow(trans, upwind, cell_p, cell_s, seg_p, seg_s):
    u = jnp.where(upwind > 0.5, cell_s, seg_s)
    weight = trans * (MOBILITY_FLOOR + u * u)
    water = weight * (cell_p - seg_p) * u
    return weight, water


def cell_parts(cell_row, columns):
    return cell_row // columns, cell_row % columns


def ends_of(frac):
    rows = frac.shape[0]
    return jnp.concatenate([frac[0:1], frac[rows - 1 : rows]], axis=1)


def frac_step(frac, sat, aperture, before, after, inflow, total, gained):
    rows, lanes = frac.shape
    row, lane = iota((rows, lanes), 0), iota((rows, lanes), 1)
    back = pltpu.roll(frac, 1, 1)
    left = jnp.where(lane == 0, pltpu.roll(back, 1, 0), back)
    left = jnp.where((lane == 0) & (row == 0), before, left)
    ahead = pltpu.roll(frac, lanes - 1, 1)
    right = jnp.where(lane == lanes - 1, pltpu.roll(ahead, rows - 1, 0), ahead)
    right = jnp.where((lane == lanes - 1) & (row == rows - 1), after, right)
    new_frac = (aperture * frac + inflow + left + right) / (aperture + total + 2.0)
    new_sat = sat + TAU_STEP * gained / (aperture + total)
    return new_frac, new_sat


def chain_ends(ends_ref, row, members):
    me = lax.axis_index("frac")
    lanes = ends_ref.shape[2]
    prior = ends_ref[jnp.maximum(me - 1, 0), row : row + 1, :]
    later = ends_ref[jnp.minimum(me + 1, members - 1), row : row + 1, :]
    before = jnp.where(me > 0, prior[:, lanes - 1 :], 0.0)
    after = jnp.where(me < members - 1, later[:, 0:1], 0.0)
    return before, after


def partial_residual(pressure, couple, source, inverse):
    rows, columns = pressure.shape
    row, col = iota((rows, columns), 0), iota((rows, columns), 1)
    beside = jnp.where(row == 0, 0.0, pltpu.roll(pressure, 1, 0))
    beside += jnp.where(row == rows - 1, 0.0, pltpu.roll(pressure, rows - 1, 0))
    beside += jnp.where(col == 0, 0.0, pltpu.roll(pressure, 1, 1))
    beside += jnp.where(col == columns - 1, 0.0, pltpu.roll(pressure, columns - 1, 1))
    return inverse * (source - (4.0 + couple) * pressure + beside)


def pack_low(q, inv, p, at, axis):
    return jnp.where(
        at < DEPTH, q, jnp.where(at < 2 * DEPTH, pltpu.roll(inv, DEPTH, axis), pltpu.roll(p, 2 * DEPTH, axis))
    )


def pack_high(q, inv, p, at, axis):
    size = q.shape[axis]
    return jnp.where(
        at >= size - DEPTH,
        q,
        jnp.where(
            at >= size - 2 * DEPTH,
            pltpu.roll(inv, size - DEPTH, axis),
            pltpu.roll(p, size - 2 * DEPTH, axis),
        ),
    )


def send_halo(out_ref, q, inv, p, groups, members):
    rows, columns = q.shape
    g, f = lax.axis_index("grp"), lax.axis_index("frac")
    here = g * members + f
    sub = iota((SUB, columns), 0)
    top = pack_low(q[:SUB], inv[:SUB], p[:SUB], sub, 0)
    bottom = pack_high(q[rows - SUB :], inv[rows - SUB :], p[rows - SUB :], sub, 0)
    lane = iota((rows, LANES), 1)
    low = pack_low(q[:, :LANES], inv[:, :LANES], p[:, :LANES], lane, 1)
    high = pack_high(q[:, columns - LANES :], inv[:, columns - LANES :], p[:, columns - LANES :], lane, 1)
    turned = jnp.transpose(jnp.where(lane < LANES // 2, low, high))
    left, right = turned[:SUB], turned[LANES - SUB :]
    p_top, p_bottom = p[:SUB], p[rows - SUB :]

    for step, strip, p_strip in ((-1, top, p_top), (1, bottom, p_bottom)):
        inside = (g + step >= 0) & (g + step < groups)
        base = here + step * members

        @pl.when(inside)
        def _():
            out_ref[base] = strip

        @pl.when(inside & (f > 0))
        def _():
            out_ref[base - 1, :, 0:LANES] = strip[:, :LANES]
            out_ref[base - 1, :, LANES : 2 * LANES] = p_strip[:, :LANES]

        @pl.when(inside & (f < members - 1))
        def _():
            out_ref[base + 1, :, 0:LANES] = strip[:, columns - LANES :]
            out_ref[base + 1, :, LANES : 2 * LANES] = p_strip[:, columns - LANES :]

    @pl.when(f > 0)
    def _():
        out_ref[here - 1, :, 0:LANES] = left

    @pl.when(f < members - 1)
    def _():
        out_ref[here + 1, :, 0:LANES] = right


def chebyshev(in_ref, q, inv, p, q_ext, inv_ext, p_ext, groups, members):
    rows, columns = q.shape
    g, f = lax.axis_index("grp"), lax.axis_index("frac")
    here = g * members + f
    last = groups * members - 1

    def block(dg, df):
        ok = (g + dg >= 0) & (g + dg < groups) & (f + df >= 0) & (f + df < members)
        at = jnp.clip(here + dg * members + df, 0, last)
        return jnp.where(ok, in_ref[at], 0.0)

    sub = iota((SUB, columns), 0)
    below, above = block(1, 0), block(-1, 0)

    def both(low, high, at, count, size):
        return jnp.where(at < count, low, jnp.where(at >= size - count, high, 0.0))

    q_ext[0:rows, 0:columns] = q
    inv_ext[0:rows, 0:columns] = inv
    p_ext[0:rows, 0:columns] = p
    q_ext[rows : rows + SUB, 0:columns] = both(below, above, sub, DEPTH, SUB)
    inv_ext[rows : rows + SUB, 0:columns] = both(
        pltpu.roll(below, SUB - DEPTH, 0), pltpu.roll(above, DEPTH, 0), sub, DEPTH, SUB
    )
    p_ext[rows : rows + SUB, 0:columns] = both(
        pltpu.roll(below, SUB - 2 * DEPTH, 0), pltpu.roll(above, 2 * DEPTH, 0), sub, 2, SUB
    )
    right, left = block(0, 1)[:, :LANES], block(0, -1)[:, :LANES]
    turned = jnp.transpose(
        jnp.concatenate([right, jnp.zeros((LANES - 2 * SUB, rows), F32), left], axis=0)
    )
    lane = iota((rows, LANES), 1)
    side = slice(columns, columns + LANES)
    q_ext[0:rows, side] = both(turned, turned, lane, DEPTH, LANES)
    inv_ext[0:rows, side] = both(
        pltpu.roll(turned, LANES - DEPTH, 1), pltpu.roll(turned, DEPTH, 1), lane, DEPTH, LANES
    )
    p_ext[0:rows, side] = both(
        pltpu.roll(turned, LANES - 2 * DEPTH, 1), pltpu.roll(turned, 2 * DEPTH, 1), lane, 2, LANES
    )
    sub = iota((SUB, LANES), 0)
    lane = iota((SUB, LANES), 1)
    low_right, low_left = block(1, 1), block(1, -1)
    high_right, high_left = block(-1, 1), block(-1, -1)
    low = both(low_right, low_left, iota((SUB, 2 * LANES), 1) % LANES, DEPTH, LANES)
    high = both(high_right, high_left, iota((SUB, 2 * LANES), 1) % LANES, DEPTH, LANES)
    corner = slice(rows, rows + SUB)
    q_ext[corner, side] = both(low[:, :LANES], high[:, :LANES], sub, DEPTH, SUB)
    inv_ext[corner, side] = both(
        pltpu.roll(low[:, :LANES], SUB - DEPTH, 0), pltpu.roll(high[:, :LANES], DEPTH, 0), sub, DEPTH, SUB
    )
    p_ext[corner, side] = both(low[:, LANES:], high[:, LANES:], sub, DEPTH, SUB)

    shape = (rows + SUB, columns + LANES)
    for here_row, there_row in ((0, shape[0] - 1), (shape[0] - 1, 0), (rows - 1, rows), (rows, rows - 1)):
        q_ext[here_row : here_row + 1, :] += (
            inv_ext[here_row : here_row + 1, :] * p_ext[there_row : there_row + 1, :]
        )
    lane = iota((shape[0], LANES), 1)
    first, final = slice(0, LANES), slice(columns - LANES, columns)
    p_side = p_ext[:, side]
    from_left, from_right = pltpu.roll(p_side, 1, 1), pltpu.roll(p_side, LANES - 1, 1)
    q_ext[:, first] += inv_ext[:, first] * jnp.where(lane == 0, from_left, 0.0)
    q_ext[:, final] += inv_ext[:, final] * jnp.where(lane == LANES - 1, from_right, 0.0)
    q_ext[:, side] += inv_ext[:, side] * jnp.where(
        lane == 0,
        pltpu.roll(p_ext[:, final], 1, 1),
        jnp.where(lane == LANES - 1, pltpu.roll(p_ext[:, first], LANES - 1, 1), 0.0),
    )
    inverse = inv_ext[...]
    start = q_ext[...]

    centre = 0.5 * (HIGH_BOUND + LOW_BOUND)
    half_width = 0.5 * (HIGH_BOUND - LOW_BOUND)
    scale_ratio = centre / half_width
    ratio_now = 1.0 / scale_ratio
    update = start / centre if centre != 1.0 else start
    change = update
    for _ in range(SWEEPS - 1):
        beside = (
            pltpu.roll(change, 1, 0)
            + pltpu.roll(change, shape[0] - 1, 0)
            + pltpu.roll(change, 1, 1)
            + pltpu.roll(change, shape[1] - 1, 1)
        )
        residual = start - change + inverse * beside
        ratio_next = 1.0 / (2.0 * scale_ratio - ratio_now)
        update = ratio_next * ratio_now * update + (2.0 * ratio_next / half_width) * residual
        ratio_now = ratio_next
        change = change + update
    return p + change[0:rows, 0:columns]


ROW_SEG = 0
ROW_TRANS = 1
ROW_UP = 2
ROW_P = ROW_UP + ITERS
ROW_S = ROW_P + 1
ROW_ENDS = ROW_S + 1


def first_kernel(
    members, cell_any, seg_any, trans_any, count_any, up_any, state_any, frac_any,
    out_ref, hot_ref, row_hot_ref, cell_ref, seg_ref, trans_ref, count_ref, up_ref, state_ref, ends_ref, sem,
):
    _, rows, columns = state_ref.shape
    width = cell_ref.shape[1]
    seg_rows = frac_any.shape[1]
    copies = [
        pltpu.make_async_copy(source, target, sem.at[i])
        for i, (source, target) in enumerate(
            [
                (cell_any, cell_ref),
                (state_any, state_ref),
                (seg_any, seg_ref),
                (trans_any, trans_ref),
                (count_any, count_ref),
                (up_any, up_ref),
                (frac_any.at[0, 0:SUB], ends_ref.at[0]),
                (frac_any.at[0, seg_rows - SUB : seg_rows], ends_ref.at[1]),
            ]
        )
    ]
    for copy in copies:
        copy.start()
    copies[0].wait()
    for o in range(members):
        row, col = cell_parts(cell_ref[o : o + 1, :], columns)
        at = slice(o * width, (o + 1) * width)
        hot_ref[:, at] = one_hot(col, columns)
        row_hot_ref[:, at] = one_hot(row, rows)
    copies[1].wait()
    table = table_of([state_ref[0], state_ref[1]])
    for copy in copies[2:]:
        copy.wait()
    ends = jnp.concatenate([ends_ref[0, 0:1], ends_ref[1, SUB - 1 : SUB]], axis=1)
    for o in range(members):
        one = slice(o, o + 1)
        row, _ = cell_parts(cell_ref[one, :], columns)
        cell_p, cell_s = pick(table, 2, rows, row, hot_ref[:, o * width : (o + 1) * width])
        live = iota((1, width), 1) < count_ref[0, o]
        out_ref[o, ROW_SEG : ROW_SEG + 1, :] = seg_ref[one, :].astype(F32)
        out_ref[o, ROW_TRANS : ROW_TRANS + 1, :] = jnp.where(live, trans_ref[one, :], 0.0)
        for t in range(ITERS):
            out_ref[o, ROW_UP + t : ROW_UP + t + 1, :] = up_ref[t, one, :].astype(F32)
        out_ref[o, ROW_P : ROW_P + 1, :] = cell_p
        out_ref[o, ROW_S : ROW_S + 1, :] = cell_s
        out_ref[o, ROW_ENDS : ROW_ENDS + 1, :] = ends


def seg_parts(slot_ref, s):
    seg = slot_ref[s, ROW_SEG : ROW_SEG + 1, :].astype(jnp.int32)
    return seg // LANES, seg % LANES


def seg_hots(slot_ref, hot_ref, row_hot_ref, members, width):
    for s in range(members):
        row, lane = seg_parts(slot_ref, s)
        at = slice(s * width, (s + 1) * width)
        hot_ref[:, at] = one_hot(lane, LANES)
        row_hot_ref[:, at] = one_hot(row, row_hot_ref.shape[0])


def seg_gather(slot_ref, hot_ref, fields, s, width, table):
    return pick(table, 2, fields, seg_parts(slot_ref, s)[0], hot_ref[:, s * width : (s + 1) * width])


def owner_start_kernel(
    members, slot_ref, frac_ref, aperture_ref, out_ref, new_ref, hot_ref, row_hot_ref, left_ref
):
    width = slot_ref.shape[2]
    rows = frac_ref.shape[1]
    frac, sat = frac_ref[0], frac_ref[1]
    seg_hots(slot_ref, hot_ref, row_hot_ref, members, width)
    table = table_of([frac, sat])
    for s in range(members):
        seg_p, seg_s = seg_gather(slot_ref, hot_ref, rows, s, width, table)
        out_ref[s, 0:1, :] = seg_p
        out_ref[s, 1:2, :] = seg_s
        slot = slot_ref[s]
        cell_p = slot[ROW_P : ROW_P + 1]
        weight, water = flow(
            slot[ROW_TRANS : ROW_TRANS + 1],
            slot[ROW_UP : ROW_UP + 1],
            cell_p,
            slot[ROW_S : ROW_S + 1],
            seg_p,
            seg_s,
        )
        spread(left_ref, row_hot_ref, s, [weight * cell_p, weight, water])
    inflow, total, gained = gathered_sum(left_ref, hot_ref, 3, rows)
    before, after = chain_ends(slot_ref, ROW_ENDS, members)
    new_frac, new_sat = frac_step(frac, sat, aperture_ref[...], before, after, inflow, total, gained)
    new_ref[0] = new_frac
    new_ref[1] = new_sat
    table = table_of([new_frac, new_sat])
    ends = ends_of(new_frac)
    for s in range(members):
        seg_p, seg_s = seg_gather(slot_ref, hot_ref, rows, s, width, table)
        out_ref[s, 2:3, :] = seg_p
        out_ref[s, 3:4, :] = seg_s
        out_ref[s, 4:5, :] = ends


def cell_update(
    members, t, hot_ref, row_hot_ref, sent_ref, cell_rows, seg_rows, pressure, saturation, perm, left_ref
):
    rows = pressure.shape[0]
    for o in range(members):
        seg_p, seg_s = seg_rows(o)
        cell_p, cell_s = cell_rows(o)
        weight, water = flow(
            sent_ref[o, ROW_TRANS : ROW_TRANS + 1, :],
            sent_ref[o, ROW_UP + t : ROW_UP + t + 1, :],
            cell_p,
            cell_s,
            seg_p,
            seg_s,
        )
        spread(left_ref, row_hot_ref, o, [weight, weight * seg_p, water])
    couple, source, lost = gathered_sum(left_ref, hot_ref, 3, rows)
    inverse = 1.0 / (4.0 + perm + couple)
    new_saturation = saturation - TAU_STEP * lost / (perm + couple)
    return new_saturation, partial_residual(pressure, couple, source, inverse), inverse


def source_start_kernel(
    groups, members, hot_ref, row_hot_ref, sent_ref, seg_ref, state_ref, perm_ref, out_ref, keep_ref, left_ref
):
    pressure = state_ref[0]
    new_saturation, q, inv = cell_update(
        members,
        0,
        hot_ref,
        row_hot_ref,
        sent_ref,
        lambda o: (sent_ref[o, ROW_P : ROW_P + 1, :], sent_ref[o, ROW_S : ROW_S + 1, :]),
        lambda o: (seg_ref[o, 0:1, :], seg_ref[o, 1:2, :]),
        pressure,
        state_ref[1],
        perm_ref[...],
        left_ref,
    )
    keep_ref[0] = pressure
    keep_ref[1] = new_saturation
    keep_ref[2] = q
    keep_ref[3] = inv
    send_halo(out_ref, q, inv, pressure, groups, members)


def cell_gather(members, cell_ref, hot_ref, fields, put):
    rows, columns = fields[0].shape
    width = cell_ref.shape[1]
    table = table_of(fields)
    for o in range(members):
        row, _ = cell_parts(cell_ref[o : o + 1, :], columns)
        put(o, *pick(table, len(fields), rows, row, hot_ref[:, o * width : (o + 1) * width]))


def middle_kernel(
    groups, members, halo_ref, cell_ref, hot_ref, row_hot_ref, sent_ref, seg_ref, kept_ref, perm_ref,
    out_ref, keep_ref, slots_ref, left_ref, q_ext, inv_ext, p_ext,
):
    pressure = chebyshev(
        halo_ref, kept_ref[2], kept_ref[3], kept_ref[0], q_ext, inv_ext, p_ext, groups, members
    )
    saturation = kept_ref[1]
    g = lax.axis_index("grp")

    def put(o, cell_p, cell_s):
        slots_ref[o, 0:1, :] = cell_p
        slots_ref[o, 1:2, :] = cell_s
        for half in range(2):
            at = slice(half * LANES, (half + 1) * LANES)
            out_ref[g * members + o, half : half + 1, LANES : 2 * LANES] = cell_p[:, at]
            out_ref[g * members + o, 2 + half : 3 + half, LANES : 2 * LANES] = cell_s[:, at]

    cell_gather(members, cell_ref, hot_ref, [pressure, saturation], put)
    new_saturation, q, inv = cell_update(
        members,
        1,
        hot_ref,
        row_hot_ref,
        sent_ref,
        lambda o: (slots_ref[o, 0:1, :], slots_ref[o, 1:2, :]),
        lambda o: (seg_ref[o, 2:3, :], seg_ref[o, 3:4, :]),
        pressure,
        saturation,
        perm_ref[...],
        left_ref,
    )
    keep_ref[0] = pressure
    keep_ref[1] = new_saturation
    keep_ref[2] = q
    keep_ref[3] = inv
    send_halo(out_ref, q, inv, pressure, groups, members)


def owner_update(
    members, t, slot_ref, cell_rows, seg_rows, frac, sat, aperture, ends, hot_ref, row_hot_ref, left_ref
):
    rows = frac.shape[0]
    for s in range(members):
        cell_p, cell_s = cell_rows(s)
        weight, water = flow(
            slot_ref[s, ROW_TRANS : ROW_TRANS + 1, :],
            slot_ref[s, ROW_UP + t : ROW_UP + t + 1, :],
            cell_p,
            cell_s,
            *seg_rows(s),
        )
        spread(left_ref, row_hot_ref, s, [weight * cell_p, weight, water])
    inflow, total, gained = gathered_sum(left_ref, hot_ref, 3, rows)
    return frac_step(frac, sat, aperture, *ends, inflow, total, gained)


def exchange_kernel(
    groups, members, halo_ref, cell_ref, cell_hot_ref, slot_ref, hot_ref, row_hot_ref, ends_ref, own_ref,
    frac_ref, aperture_ref, kept_ref, out_ref, new_ref, pressure_ref, left_ref, q_ext, inv_ext, p_ext,
):
    width = slot_ref.shape[2]
    rows = frac_ref.shape[1]
    g = lax.axis_index("grp")

    def cell_rows(s):
        block = halo_ref[g * members + s]
        half = block[:, LANES : 2 * LANES]
        return (
            jnp.concatenate([half[0:1], half[1:2]], axis=1),
            jnp.concatenate([half[2:3], half[3:4]], axis=1),
        )

    new_frac, new_sat = owner_update(
        members,
        1,
        slot_ref,
        cell_rows,
        lambda s: (own_ref[s, 2:3, :], own_ref[s, 3:4, :]),
        frac_ref[0],
        frac_ref[1],
        aperture_ref[...],
        chain_ends(ends_ref, 4, members),
        hot_ref,
        row_hot_ref,
        left_ref,
    )
    new_ref[0] = new_frac
    new_ref[1] = new_sat
    table = table_of([new_frac, new_sat])
    ends = ends_of(new_frac)
    for s in range(members):
        seg_p, seg_s = seg_gather(slot_ref, hot_ref, rows, s, width, table)
        out_ref[s, 2:3, :] = seg_p
        out_ref[s, 3:4, :] = seg_s
        out_ref[s, 4:5, :] = ends

    pressure = chebyshev(
        halo_ref, kept_ref[2], kept_ref[3], kept_ref[0], q_ext, inv_ext, p_ext, groups, members
    )
    pressure_ref[...] = pressure

    def put(o, cell_p, cell_s):
        out_ref[o, 0:1, :] = cell_p
        out_ref[o, 1:2, :] = cell_s

    cell_gather(members, cell_ref, cell_hot_ref, [pressure, kept_ref[1]], put)


def source_last_kernel(
    groups, members, hot_ref, row_hot_ref, sent_ref, own_ref, seg_ref, pressure_ref, kept_ref, perm_ref,
    out_ref, keep_ref, left_ref,
):
    pressure = pressure_ref[...]
    new_saturation, q, inv = cell_update(
        members,
        2,
        hot_ref,
        row_hot_ref,
        sent_ref,
        lambda o: (own_ref[o, 0:1, :], own_ref[o, 1:2, :]),
        lambda o: (seg_ref[o, 2:3, :], seg_ref[o, 3:4, :]),
        pressure,
        kept_ref[1],
        perm_ref[...],
        left_ref,
    )
    keep_ref[0] = new_saturation
    keep_ref[1] = q
    keep_ref[2] = inv
    send_halo(out_ref, q, inv, pressure, groups, members)


def owner_last_kernel(
    members, slot_ref, hot_ref, row_hot_ref, own_ref, seg_ref, frac_ref, aperture_ref, out_ref, left_ref
):
    new_frac, new_sat = owner_update(
        members,
        2,
        slot_ref,
        lambda s: (seg_ref[s, 0:1, :], seg_ref[s, 1:2, :]),
        lambda s: (own_ref[s, 2:3, :], own_ref[s, 3:4, :]),
        frac_ref[0],
        frac_ref[1],
        aperture_ref[...],
        chain_ends(seg_ref, 4, members),
        hot_ref,
        row_hot_ref,
        left_ref,
    )
    out_ref[0] = new_frac
    out_ref[1] = new_sat


def final_kernel(groups, members, halo_ref, pressure_ref, kept_ref, out_ref, q_ext, inv_ext, p_ext):
    out_ref[0] = chebyshev(
        halo_ref, kept_ref[1], kept_ref[2], pressure_ref[...], q_ext, inv_ext, p_ext, groups, members
    )
    out_ref[1] = kept_ref[0]


VMEM = pl.BlockSpec(memory_space=pltpu.VMEM)
HBM = pl.BlockSpec(memory_space=pltpu.HBM)


def call(kernel, statics, outs, scratch, *args, spec=VMEM):
    outs = [o if hasattr(o, "dtype") else jax.ShapeDtypeStruct(o, F32) for o in outs]
    return pl.pallas_call(
        functools.partial(kernel, *statics),
        out_shape=outs,
        in_specs=[spec] * len(args),
        out_specs=[VMEM] * len(outs),
        scratch_shapes=scratch,
        compiler_params=pltpu.CompilerParams(vmem_limit_bytes=32 * 1024 * 1024),
        name=kernel.__name__,
    )(*args)


def on_device(
    matrix_state,
    matrix_perm,
    frac_state,
    frac_aperture,
    link_cell,
    link_seg,
    link_trans,
    link_count,
    link_upwind,
):
    groups, members = lax.axis_size("grp"), lax.axis_size("frac")
    both = (groups, members)
    devices = groups * members
    cells = link_cell[0, 0]
    width = cells.shape[1]
    _, rows, columns = matrix_state.shape
    seg_dev = frac_state.shape[2]
    seg_rows = seg_dev // LANES
    frac = frac_state.reshape(2, seg_rows, LANES)
    aperture = frac_aperture.reshape(seg_rows, LANES)

    every = members * width
    slots = (members, SUB, width)
    halo = (devices, SUB, columns)
    left_cell = pltpu.VMEM((3 * PARTS * rows, every), BF16)
    left_seg = pltpu.VMEM((3 * PARTS * seg_rows, every), BF16)
    ext = [pltpu.VMEM((rows + SUB, columns + LANES), F32)] * 3

    def to_group(x):
        return lax.all_to_all(x, "frac", split_axis=0, concat_axis=0, tiled=True)

    def to_all(x):
        return lax.all_to_all(x, ("grp", "frac"), split_axis=0, concat_axis=0, tiled=True)

    def hots(*sizes):
        return [jax.ShapeDtypeStruct((n, every), BF16) for n in sizes]

    sent, cell_hot, cell_row_hot = call(
        first_kernel,
        (members,),
        [slots] + hots(columns, rows),
        [
            pltpu.VMEM((members, width), jnp.int32),
            pltpu.VMEM((members, width), jnp.int32),
            pltpu.VMEM((members, width), F32),
            pltpu.SMEM((1, members), jnp.int32),
            pltpu.VMEM((ITERS, members, width), jnp.int32),
            pltpu.VMEM(matrix_state.shape, F32),
            pltpu.VMEM((2, SUB, LANES), F32),
            pltpu.SemaphoreType.DMA((8,)),
        ],
        cells, link_seg[0, 0], link_trans[0, 0], link_count[0], link_upwind[:, 0, 0], matrix_state, frac,
        spec=HBM,
    )
    slot = to_group(sent)
    own, frac1, hot, row_hot = call(
        owner_start_kernel, (members,), [slots, frac.shape] + hots(LANES, seg_rows), [left_seg],
        slot, frac, aperture,
    )
    segs = to_group(own)
    edge, kept = call(
        source_start_kernel, both, [halo, (4, rows, columns)], [left_cell],
        cell_hot, cell_row_hot, sent, segs, matrix_state, matrix_perm,
    )
    around = to_all(edge)
    edge, kept = call(
        middle_kernel, both, [halo, (4, rows, columns)], [pltpu.VMEM(slots, F32), left_cell] + ext,
        around, cells, cell_hot, cell_row_hot, sent, segs, kept, matrix_perm,
    )
    around = to_all(edge)
    own, frac2, pressure = call(
        exchange_kernel, both, [slots, frac.shape, (rows, columns)], [left_seg] + ext,
        around, cells, cell_hot, slot, hot, row_hot, segs, own, frac1, aperture, kept,
    )
    segs = to_group(own)
    edge, kept = call(
        source_last_kernel, both, [halo, (3, rows, columns)], [left_cell],
        cell_hot, cell_row_hot, sent, own, segs, pressure, kept, matrix_perm,
    )
    around = to_all(edge)
    (frac3,) = call(
        owner_last_kernel, (members,), [frac.shape], [left_seg], slot, hot, row_hot, own, segs, frac2, aperture
    )
    (matrix_out,) = call(final_kernel, both, [matrix_state.shape], ext, around, pressure, kept)
    return matrix_out, frac3.reshape(frac_state.shape)


def solution(mesh):
    return jax.shard_map(
        on_device,
        mesh=mesh,
        in_specs=(
            P(None, "grp", "frac"),
            P("grp", "frac"),
            P(None, "grp", "frac"),
            P("grp", "frac"),
            P("grp", "frac", None, None),
            P("grp", "frac", None, None),
            P("grp", "frac", None, None),
            P("grp", "frac", None),
            P(None, "grp", "frac", None, None),
        ),
        out_specs=(P(None, "grp", "frac"), P(None, "grp", "frac")),
        check_vma=False,
    )
```

```python
import functools

import jax
import jax.numpy as jnp
from jax import lax
from jax.experimental import pallas as pl
from jax.experimental.pallas import tpu as pltpu
from jax.sharding import PartitionSpec as P

ITERS = 3
SWEEPS = 4

LOW_BOUND = 0.02
HIGH_BOUND = 1.98
TAU_STEP = 0.5
MOBILITY_FLOOR = 0.2

F32 = jnp.float32
BF16 = jnp.bfloat16
LANES = 128
SUB = 8
DEPTH = SWEEPS - 1


def iota(shape, dim):
    return lax.broadcasted_iota(jnp.int32, shape, dim)


def parts_of(x):
    high = x.astype(BF16).astype(F32)
    return high, x - high


PARTS = 2


def table_of(fields):
    split = [parts_of(f) for f in fields]
    return jnp.concatenate([s[p] for p in range(PARTS) for s in split], axis=0).astype(BF16)


def one_hot(index_row, count):
    hit = iota((count, index_row.shape[1]), 0) == index_row
    return jnp.where(hit, 1.0, 0.0).astype(BF16)


def pick(table, fields, rows, row_index, hot):
    wide = jnp.dot(table, hot, preferred_element_type=F32)
    hit = iota((rows, row_index.shape[1]), 0) == row_index
    found = []
    for f in range(fields):
        total = sum(wide[(p * fields + f) * rows : (p * fields + f + 1) * rows] for p in range(PARTS))
        found.append(jnp.sum(jnp.where(hit, total, 0.0), axis=0, keepdims=True))
    return found


def spread(left_ref, row_hot_ref, block, values):
    rows = row_hot_ref.shape[0]
    width = values[0].shape[1]
    at = slice(block * width, (block + 1) * width)
    hot = row_hot_ref[:, at]
    for f, value in enumerate(values):
        for p, part in enumerate(parts_of(value)):
            row = (p * len(values) + f) * rows
            left_ref[row : row + rows, at] = hot * part.astype(BF16)


def gathered_sum(left_ref, hot_ref, fields, rows):
    wide = lax.dot_general(
        left_ref[...], hot_ref[...], (((1,), (1,)), ((), ())), preferred_element_type=F32
    )
    return [
        sum(wide[(p * fields + f) * rows : (p * fields + f + 1) * rows] for p in range(PARTS))
        for f in range(fields)
    ]


def flow(trans, upwind, cell_p, cell_s, seg_p, seg_s):
    u = jnp.where(upwind > 0.5, cell_s, seg_s)
    weight = trans * (MOBILITY_FLOOR + u * u)
    water = weight * (cell_p - seg_p) * u
    return weight, water


def cell_parts(cell_row, columns):
    return cell_row // columns, cell_row % columns


def ends_of(frac):
    rows = frac.shape[0]
    return jnp.concatenate([frac[0:1], frac[rows - 1 : rows]], axis=1)


def frac_step(frac, sat, aperture, before, after, inflow, total, gained):
    rows, lanes = frac.shape
    row, lane = iota((rows, lanes), 0), iota((rows, lanes), 1)
    back = pltpu.roll(frac, 1, 1)
    left = jnp.where(lane == 0, pltpu.roll(back, 1, 0), back)
    left = jnp.where((lane == 0) & (row == 0), before, left)
    ahead = pltpu.roll(frac, lanes - 1, 1)
    right = jnp.where(lane == lanes - 1, pltpu.roll(ahead, rows - 1, 0), ahead)
    right = jnp.where((lane == lanes - 1) & (row == rows - 1), after, right)
    new_frac = (aperture * frac + inflow + left + right) / (aperture + total + 2.0)
    new_sat = sat + TAU_STEP * gained / (aperture + total)
    return new_frac, new_sat


def chain_ends(ends_ref, row, members):
    me = lax.axis_index("frac")
    lanes = ends_ref.shape[2]
    prior = ends_ref[jnp.maximum(me - 1, 0), row : row + 1, :]
    later = ends_ref[jnp.minimum(me + 1, members - 1), row : row + 1, :]
    before = jnp.where(me > 0, prior[:, lanes - 1 :], 0.0)
    after = jnp.where(me < members - 1, later[:, 0:1], 0.0)
    return before, after


def partial_residual(pressure, couple, source, inverse):
    rows, columns = pressure.shape
    row, col = iota((rows, columns), 0), iota((rows, columns), 1)
    beside = jnp.where(row == 0, 0.0, pltpu.roll(pressure, 1, 0))
    beside += jnp.where(row == rows - 1, 0.0, pltpu.roll(pressure, rows - 1, 0))
    beside += jnp.where(col == 0, 0.0, pltpu.roll(pressure, 1, 1))
    beside += jnp.where(col == columns - 1, 0.0, pltpu.roll(pressure, columns - 1, 1))
    return inverse * (source - (4.0 + couple) * pressure + beside)


def pack_low(q, inv, p, at, axis):
    return jnp.where(
        at < DEPTH, q, jnp.where(at < 2 * DEPTH, pltpu.roll(inv, DEPTH, axis), pltpu.roll(p, 2 * DEPTH, axis))
    )


def pack_high(q, inv, p, at, axis):
    size = q.shape[axis]
    return jnp.where(
        at >= size - DEPTH,
        q,
        jnp.where(
            at >= size - 2 * DEPTH,
            pltpu.roll(inv, size - DEPTH, axis),
            pltpu.roll(p, size - 2 * DEPTH, axis),
        ),
    )


def send_halo(out_ref, q, inv, p, groups, members):
    rows, columns = q.shape
    g, f = lax.axis_index("grp"), lax.axis_index("frac")
    here = g * members + f
    sub = iota((SUB, columns), 0)
    top = pack_low(q[:SUB], inv[:SUB], p[:SUB], sub, 0)
    bottom = pack_high(q[rows - SUB :], inv[rows - SUB :], p[rows - SUB :], sub, 0)
    lane = iota((rows, LANES), 1)
    low = pack_low(q[:, :LANES], inv[:, :LANES], p[:, :LANES], lane, 1)
    high = pack_high(q[:, columns - LANES :], inv[:, columns - LANES :], p[:, columns - LANES :], lane, 1)
    turned = jnp.transpose(jnp.where(lane < LANES // 2, low, high))
    left, right = turned[:SUB], turned[LANES - SUB :]
    p_top, p_bottom = p[:SUB], p[rows - SUB :]

    for step, strip, p_strip in ((-1, top, p_top), (1, bottom, p_bottom)):
        inside = (g + step >= 0) & (g + step < groups)
        base = here + step * members

        @pl.when(inside)
        def _():
            out_ref[base] = strip

        @pl.when(inside & (f > 0))
        def _():
            out_ref[base - 1, :, 0:LANES] = strip[:, :LANES]
            out_ref[base - 1, :, LANES : 2 * LANES] = p_strip[:, :LANES]

        @pl.when(inside & (f < members - 1))
        def _():
            out_ref[base + 1, :, 0:LANES] = strip[:, columns - LANES :]
            out_ref[base + 1, :, LANES : 2 * LANES] = p_strip[:, columns - LANES :]

    @pl.when(f > 0)
    def _():
        out_ref[here - 1, :, 0:LANES] = left

    @pl.when(f < members - 1)
    def _():
        out_ref[here + 1, :, 0:LANES] = right


def chebyshev(in_ref, q, inv, p, q_ext, inv_ext, p_ext, groups, members):
    rows, columns = q.shape
    g, f = lax.axis_index("grp"), lax.axis_index("frac")
    here = g * members + f
    last = groups * members - 1

    def block(dg, df):
        ok = (g + dg >= 0) & (g + dg < groups) & (f + df >= 0) & (f + df < members)
        at = jnp.clip(here + dg * members + df, 0, last)
        return jnp.where(ok, in_ref[at], 0.0)

    sub = iota((SUB, columns), 0)
    below, above = block(1, 0), block(-1, 0)

    def both(low, high, at, count, size):
        return jnp.where(at < count, low, jnp.where(at >= size - count, high, 0.0))

    q_ext[0:rows, 0:columns] = q
    inv_ext[0:rows, 0:columns] = inv
    p_ext[0:rows, 0:columns] = p
    q_ext[rows : rows + SUB, 0:columns] = both(below, above, sub, DEPTH, SUB)
    inv_ext[rows : rows + SUB, 0:columns] = both(
        pltpu.roll(below, SUB - DEPTH, 0), pltpu.roll(above, DEPTH, 0), sub, DEPTH, SUB
    )
    p_ext[rows : rows + SUB, 0:columns] = both(
        pltpu.roll(below, SUB - 2 * DEPTH, 0), pltpu.roll(above, 2 * DEPTH, 0), sub, 2, SUB
    )
    right, left = block(0, 1)[:, :LANES], block(0, -1)[:, :LANES]
    turned = jnp.transpose(
        jnp.concatenate([right, jnp.zeros((LANES - 2 * SUB, rows), F32), left], axis=0)
    )
    lane = iota((rows, LANES), 1)
    side = slice(columns, columns + LANES)
    q_ext[0:rows, side] = both(turned, turned, lane, DEPTH, LANES)
    inv_ext[0:rows, side] = both(
        pltpu.roll(turned, LANES - DEPTH, 1), pltpu.roll(turned, DEPTH, 1), lane, DEPTH, LANES
    )
    p_ext[0:rows, side] = both(
        pltpu.roll(turned, LANES - 2 * DEPTH, 1), pltpu.roll(turned, 2 * DEPTH, 1), lane, 2, LANES
    )
    sub = iota((SUB, LANES), 0)
    lane = iota((SUB, LANES), 1)
    low_right, low_left = block(1, 1), block(1, -1)
    high_right, high_left = block(-1, 1), block(-1, -1)
    low = both(low_right, low_left, iota((SUB, 2 * LANES), 1) % LANES, DEPTH, LANES)
    high = both(high_right, high_left, iota((SUB, 2 * LANES), 1) % LANES, DEPTH, LANES)
    corner = slice(rows, rows + SUB)
    q_ext[corner, side] = both(low[:, :LANES], high[:, :LANES], sub, DEPTH, SUB)
    inv_ext[corner, side] = both(
        pltpu.roll(low[:, :LANES], SUB - DEPTH, 0), pltpu.roll(high[:, :LANES], DEPTH, 0), sub, DEPTH, SUB
    )
    p_ext[corner, side] = both(low[:, LANES:], high[:, LANES:], sub, DEPTH, SUB)

    shape = (rows + SUB, columns + LANES)
    for here_row, there_row in ((0, shape[0] - 1), (shape[0] - 1, 0), (rows - 1, rows), (rows, rows - 1)):
        q_ext[here_row : here_row + 1, :] += (
            inv_ext[here_row : here_row + 1, :] * p_ext[there_row : there_row + 1, :]
        )
    lane = iota((shape[0], LANES), 1)
    first, final = slice(0, LANES), slice(columns - LANES, columns)
    p_side = p_ext[:, side]
    from_left, from_right = pltpu.roll(p_side, 1, 1), pltpu.roll(p_side, LANES - 1, 1)
    q_ext[:, first] += inv_ext[:, first] * jnp.where(lane == 0, from_left, 0.0)
    q_ext[:, final] += inv_ext[:, final] * jnp.where(lane == LANES - 1, from_right, 0.0)
    q_ext[:, side] += inv_ext[:, side] * jnp.where(
        lane == 0,
        pltpu.roll(p_ext[:, final], 1, 1),
        jnp.where(lane == LANES - 1, pltpu.roll(p_ext[:, first], LANES - 1, 1), 0.0),
    )
    inverse = inv_ext[...]
    start = q_ext[...]

    centre = 0.5 * (HIGH_BOUND + LOW_BOUND)
    half_width = 0.5 * (HIGH_BOUND - LOW_BOUND)
    scale_ratio = centre / half_width
    ratio_now = 1.0 / scale_ratio
    update = start / centre if centre != 1.0 else start
    change = update
    for _ in range(SWEEPS - 1):
        beside = (
            pltpu.roll(change, 1, 0)
            + pltpu.roll(change, shape[0] - 1, 0)
            + pltpu.roll(change, 1, 1)
            + pltpu.roll(change, shape[1] - 1, 1)
        )
        residual = start - change + inverse * beside
        ratio_next = 1.0 / (2.0 * scale_ratio - ratio_now)
        update = ratio_next * ratio_now * update + (2.0 * ratio_next / half_width) * residual
        ratio_now = ratio_next
        change = change + update
    return p + change[0:rows, 0:columns]


ROW_SEG = 0
ROW_TRANS = 1
ROW_UP = 2
ROW_P = ROW_UP + ITERS
ROW_S = ROW_P + 1
ROW_ENDS = ROW_S + 1


def first_kernel(
    members, cell_any, seg_any, trans_any, count_any, up_any, state_any, frac_any,
    out_ref, hot_ref, row_hot_ref, cell_ref, seg_ref, trans_ref, count_ref, up_ref, state_ref, ends_ref, sem,
):
    _, rows, columns = state_ref.shape
    width = cell_ref.shape[1]
    seg_rows = frac_any.shape[1]
    copies = [
        pltpu.make_async_copy(source, target, sem.at[i])
        for i, (source, target) in enumerate(
            [
                (cell_any, cell_ref),
                (state_any, state_ref),
                (seg_any, seg_ref),
                (trans_any, trans_ref),
                (count_any, count_ref),
                (up_any, up_ref),
                (frac_any.at[0, 0:SUB], ends_ref.at[0]),
                (frac_any.at[0, seg_rows - SUB : seg_rows], ends_ref.at[1]),
            ]
        )
    ]
    for copy in copies:
        copy.start()
    copies[0].wait()
    for o in range(members):
        row, col = cell_parts(cell_ref[o : o + 1, :], columns)
        at = slice(o * width, (o + 1) * width)
        hot_ref[:, at] = one_hot(col, columns)
        row_hot_ref[:, at] = one_hot(row, rows)
    copies[1].wait()
    table = table_of([state_ref[0], state_ref[1]])
    for copy in copies[2:]:
        copy.wait()
    ends = jnp.concatenate([ends_ref[0, 0:1], ends_ref[1, SUB - 1 : SUB]], axis=1)
    for o in range(members):
        one = slice(o, o + 1)
        row, _ = cell_parts(cell_ref[one, :], columns)
        cell_p, cell_s = pick(table, 2, rows, row, hot_ref[:, o * width : (o + 1) * width])
        live = iota((1, width), 1) < count_ref[0, o]
        out_ref[o, ROW_SEG : ROW_SEG + 1, :] = seg_ref[one, :].astype(F32)
        out_ref[o, ROW_TRANS : ROW_TRANS + 1, :] = jnp.where(live, trans_ref[one, :], 0.0)
        for t in range(ITERS):
            out_ref[o, ROW_UP + t : ROW_UP + t + 1, :] = up_ref[t, one, :].astype(F32)
        out_ref[o, ROW_P : ROW_P + 1, :] = cell_p
        out_ref[o, ROW_S : ROW_S + 1, :] = cell_s
        out_ref[o, ROW_ENDS : ROW_ENDS + 1, :] = ends


def seg_parts(slot_ref, s):
    seg = slot_ref[s, ROW_SEG : ROW_SEG + 1, :].astype(jnp.int32)
    return seg // LANES, seg % LANES


def seg_hots(slot_ref, hot_ref, row_hot_ref, members, width):
    for s in range(members):
        row, lane = seg_parts(slot_ref, s)
        at = slice(s * width, (s + 1) * width)
        hot_ref[:, at] = one_hot(lane, LANES)
        row_hot_ref[:, at] = one_hot(row, row_hot_ref.shape[0])


def seg_gather(slot_ref, hot_ref, fields, s, width, table):
    return pick(table, 2, fields, seg_parts(slot_ref, s)[0], hot_ref[:, s * width : (s + 1) * width])


def owner_start_kernel(
    members, slot_ref, frac_ref, aperture_ref, out_ref, new_ref, hot_ref, row_hot_ref, left_ref
):
    width = slot_ref.shape[2]
    rows = frac_ref.shape[1]
    frac, sat = frac_ref[0], frac_ref[1]
    seg_hots(slot_ref, hot_ref, row_hot_ref, members, width)
    table = table_of([frac, sat])
    for s in range(members):
        seg_p, seg_s = seg_gather(slot_ref, hot_ref, rows, s, width, table)
        out_ref[s, 0:1, :] = seg_p
        out_ref[s, 1:2, :] = seg_s
        slot = slot_ref[s]
        cell_p = slot[ROW_P : ROW_P + 1]
        weight, water = flow(
            slot[ROW_TRANS : ROW_TRANS + 1],
            slot[ROW_UP : ROW_UP + 1],
            cell_p,
            slot[ROW_S : ROW_S + 1],
            seg_p,
            seg_s,
        )
        spread(left_ref, row_hot_ref, s, [weight * cell_p, weight, water])
    inflow, total, gained = gathered_sum(left_ref, hot_ref, 3, rows)
    before, after = chain_ends(slot_ref, ROW_ENDS, members)
    new_frac, new_sat = frac_step(frac, sat, aperture_ref[...], before, after, inflow, total, gained)
    new_ref[0] = new_frac
    new_ref[1] = new_sat
    table = table_of([new_frac, new_sat])
    ends = ends_of(new_frac)
    for s in range(members):
        seg_p, seg_s = seg_gather(slot_ref, hot_ref, rows, s, width, table)
        out_ref[s, 2:3, :] = seg_p
        out_ref[s, 3:4, :] = seg_s
        out_ref[s, 4:5, :] = ends


def cell_update(
    members, t, hot_ref, row_hot_ref, sent_ref, cell_rows, seg_rows, pressure, saturation, perm, left_ref
):
    rows = pressure.shape[0]
    for o in range(members):
        seg_p, seg_s = seg_rows(o)
        cell_p, cell_s = cell_rows(o)
        weight, water = flow(
            sent_ref[o, ROW_TRANS : ROW_TRANS + 1, :],
            sent_ref[o, ROW_UP + t : ROW_UP + t + 1, :],
            cell_p,
            cell_s,
            seg_p,
            seg_s,
        )
        spread(left_ref, row_hot_ref, o, [weight, weight * seg_p, water])
    couple, source, lost = gathered_sum(left_ref, hot_ref, 3, rows)
    inverse = 1.0 / (4.0 + perm + couple)
    new_saturation = saturation - TAU_STEP * lost / (perm + couple)
    return new_saturation, partial_residual(pressure, couple, source, inverse), inverse


def source_start_kernel(
    groups, members, hot_ref, row_hot_ref, sent_ref, seg_ref, state_ref, perm_ref, out_ref, keep_ref, left_ref
):
    pressure = state_ref[0]
    new_saturation, q, inv = cell_update(
        members,
        0,
        hot_ref,
        row_hot_ref,
        sent_ref,
        lambda o: (sent_ref[o, ROW_P : ROW_P + 1, :], sent_ref[o, ROW_S : ROW_S + 1, :]),
        lambda o: (seg_ref[o, 0:1, :], seg_ref[o, 1:2, :]),
        pressure,
        state_ref[1],
        perm_ref[...],
        left_ref,
    )
    keep_ref[0] = pressure
    keep_ref[1] = new_saturation
    keep_ref[2] = q
    keep_ref[3] = inv
    send_halo(out_ref, q, inv, pressure, groups, members)


def cell_gather(members, cell_ref, hot_ref, fields, put):
    rows, columns = fields[0].shape
    width = cell_ref.shape[1]
    table = table_of(fields)
    for o in range(members):
        row, _ = cell_parts(cell_ref[o : o + 1, :], columns)
        put(o, *pick(table, len(fields), rows, row, hot_ref[:, o * width : (o + 1) * width]))


def middle_kernel(
    groups, members, halo_ref, cell_ref, hot_ref, row_hot_ref, sent_ref, seg_ref, kept_ref, perm_ref,
    out_ref, keep_ref, slots_ref, left_ref, q_ext, inv_ext, p_ext,
):
    pressure = chebyshev(
        halo_ref, kept_ref[2], kept_ref[3], kept_ref[0], q_ext, inv_ext, p_ext, groups, members
    )
    saturation = kept_ref[1]
    g = lax.axis_index("grp")

    def put(o, cell_p, cell_s):
        slots_ref[o, 0:1, :] = cell_p
        slots_ref[o, 1:2, :] = cell_s
        for half in range(2):
            at = slice(half * LANES, (half + 1) * LANES)
            out_ref[g * members + o, half : half + 1, LANES : 2 * LANES] = cell_p[:, at]
            out_ref[g * members + o, 2 + half : 3 + half, LANES : 2 * LANES] = cell_s[:, at]

    cell_gather(members, cell_ref, hot_ref, [pressure, saturation], put)
    new_saturation, q, inv = cell_update(
        members,
        1,
        hot_ref,
        row_hot_ref,
        sent_ref,
        lambda o: (slots_ref[o, 0:1, :], slots_ref[o, 1:2, :]),
        lambda o: (seg_ref[o, 2:3, :], seg_ref[o, 3:4, :]),
        pressure,
        saturation,
        perm_ref[...],
        left_ref,
    )
    keep_ref[0] = pressure
    keep_ref[1] = new_saturation
    keep_ref[2] = q
    keep_ref[3] = inv
    send_halo(out_ref, q, inv, pressure, groups, members)


def owner_update(
    members, t, slot_ref, cell_rows, seg_rows, frac, sat, aperture, ends, hot_ref, row_hot_ref, left_ref
):
    rows = frac.shape[0]
    for s in range(members):
        cell_p, cell_s = cell_rows(s)
        weight, water = flow(
            slot_ref[s, ROW_TRANS : ROW_TRANS + 1, :],
            slot_ref[s, ROW_UP + t : ROW_UP + t + 1, :],
            cell_p,
            cell_s,
            *seg_rows(s),
        )
        spread(left_ref, row_hot_ref, s, [weight * cell_p, weight, water])
    inflow, total, gained = gathered_sum(left_ref, hot_ref, 3, rows)
    return frac_step(frac, sat, aperture, *ends, inflow, total, gained)


def exchange_kernel(
    groups, members, halo_ref, cell_ref, cell_hot_ref, slot_ref, hot_ref, row_hot_ref, ends_ref, own_ref,
    frac_ref, aperture_ref, kept_ref, out_ref, new_ref, pressure_ref, left_ref, q_ext, inv_ext, p_ext,
):
    width = slot_ref.shape[2]
    rows = frac_ref.shape[1]
    g = lax.axis_index("grp")

    def cell_rows(s):
        block = halo_ref[g * members + s]
        half = block[:, LANES : 2 * LANES]
        return (
            jnp.concatenate([half[0:1], half[1:2]], axis=1),
            jnp.concatenate([half[2:3], half[3:4]], axis=1),
        )

    new_frac, new_sat = owner_update(
        members,
        1,
        slot_ref,
        cell_rows,
        lambda s: (own_ref[s, 2:3, :], own_ref[s, 3:4, :]),
        frac_ref[0],
        frac_ref[1],
        aperture_ref[...],
        chain_ends(ends_ref, 4, members),
        hot_ref,
        row_hot_ref,
        left_ref,
    )
    new_ref[0] = new_frac
    new_ref[1] = new_sat
    table = table_of([new_frac, new_sat])
    ends = ends_of(new_frac)
    for s in range(members):
        seg_p, seg_s = seg_gather(slot_ref, hot_ref, rows, s, width, table)
        out_ref[s, 2:3, :] = seg_p
        out_ref[s, 3:4, :] = seg_s
        out_ref[s, 4:5, :] = ends

    pressure = chebyshev(
        halo_ref, kept_ref[2], kept_ref[3], kept_ref[0], q_ext, inv_ext, p_ext, groups, members
    )
    pressure_ref[...] = pressure

    def put(o, cell_p, cell_s):
        out_ref[o, 0:1, :] = cell_p
        out_ref[o, 1:2, :] = cell_s

    cell_gather(members, cell_ref, cell_hot_ref, [pressure, kept_ref[1]], put)


def source_last_kernel(
    groups, members, hot_ref, row_hot_ref, sent_ref, own_ref, seg_ref, pressure_ref, kept_ref, perm_ref,
    out_ref, keep_ref, left_ref,
):
    pressure = pressure_ref[...]
    new_saturation, q, inv = cell_update(
        members,
        2,
        hot_ref,
        row_hot_ref,
        sent_ref,
        lambda o: (own_ref[o, 0:1, :], own_ref[o, 1:2, :]),
        lambda o: (seg_ref[o, 2:3, :], seg_ref[o, 3:4, :]),
        pressure,
        kept_ref[1],
        perm_ref[...],
        left_ref,
    )
    keep_ref[0] = new_saturation
    keep_ref[1] = q
    keep_ref[2] = inv
    send_halo(out_ref, q, inv, pressure, groups, members)


def owner_last_kernel(
    members, slot_ref, hot_ref, row_hot_ref, own_ref, seg_ref, frac_ref, aperture_ref, out_ref, left_ref
):
    new_frac, new_sat = owner_update(
        members,
        2,
        slot_ref,
        lambda s: (seg_ref[s, 0:1, :], seg_ref[s, 1:2, :]),
        lambda s: (own_ref[s, 2:3, :], own_ref[s, 3:4, :]),
        frac_ref[0],
        frac_ref[1],
        aperture_ref[...],
        chain_ends(seg_ref, 4, members),
        hot_ref,
        row_hot_ref,
        left_ref,
    )
    out_ref[0] = new_frac
    out_ref[1] = new_sat


def final_kernel(groups, members, halo_ref, pressure_ref, kept_ref, out_ref, q_ext, inv_ext, p_ext):
    out_ref[0] = chebyshev(
        halo_ref, kept_ref[1], kept_ref[2], pressure_ref[...], q_ext, inv_ext, p_ext, groups, members
    )
    out_ref[1] = kept_ref[0]


VMEM = pl.BlockSpec(memory_space=pltpu.VMEM)
HBM = pl.BlockSpec(memory_space=pltpu.HBM)


def call(kernel, statics, outs, scratch, *args, spec=VMEM):
    outs = [o if hasattr(o, "dtype") else jax.ShapeDtypeStruct(o, F32) for o in outs]
    return pl.pallas_call(
        functools.partial(kernel, *statics),
        out_shape=outs,
        in_specs=[spec] * len(args),
        out_specs=[VMEM] * len(outs),
        scratch_shapes=scratch,
        compiler_params=pltpu.CompilerParams(vmem_limit_bytes=32 * 1024 * 1024),
        name=kernel.__name__,
    )(*args)


def on_device(
    matrix_state,
    matrix_perm,
    frac_state,
    frac_aperture,
    link_cell,
    link_seg,
    link_trans,
    link_count,
    link_upwind,
):
    groups, members = lax.axis_size("grp"), lax.axis_size("frac")
    both = (groups, members)
    devices = groups * members
    cells = link_cell[0, 0]
    width = cells.shape[1]
    _, rows, columns = matrix_state.shape
    seg_dev = frac_state.shape[2]
    seg_rows = seg_dev // LANES
    frac = frac_state.reshape(2, seg_rows, LANES)
    aperture = frac_aperture.reshape(seg_rows, LANES)

    every = members * width
    slots = (members, SUB, width)
    halo = (devices, SUB, columns)
    left_cell = pltpu.VMEM((3 * PARTS * rows, every), BF16)
    left_seg = pltpu.VMEM((3 * PARTS * seg_rows, every), BF16)
    ext = [pltpu.VMEM((rows + SUB, columns + LANES), F32)] * 3

    def to_group(x):
        return lax.all_to_all(x, "frac", split_axis=0, concat_axis=0, tiled=True)

    def to_all(x):
        return lax.all_to_all(x, ("grp", "frac"), split_axis=0, concat_axis=0, tiled=True)

    def hots(*sizes):
        return [jax.ShapeDtypeStruct((n, every), BF16) for n in sizes]

    sent, cell_hot, cell_row_hot = call(
        first_kernel,
        (members,),
        [slots] + hots(columns, rows),
        [
            pltpu.VMEM((members, width), jnp.int32),
            pltpu.VMEM((members, width), jnp.int32),
            pltpu.VMEM((members, width), F32),
            pltpu.SMEM((1, members), jnp.int32),
            pltpu.VMEM((ITERS, members, width), jnp.int32),
            pltpu.VMEM(matrix_state.shape, F32),
            pltpu.VMEM((2, SUB, LANES), F32),
            pltpu.SemaphoreType.DMA((8,)),
        ],
        *[
            pltpu.with_memory_space_constraint(x, pltpu.HBM)
            for x in (
                cells, link_seg[0, 0], link_trans[0, 0], link_count[0], link_upwind[:, 0, 0], matrix_state, frac
            )
        ],
        spec=HBM,
    )
    slot = to_group(sent)
    own, frac1, hot, row_hot = call(
        owner_start_kernel, (members,), [slots, frac.shape] + hots(LANES, seg_rows), [left_seg],
        slot, frac, aperture,
    )
    segs = to_group(own)
    edge, kept = call(
        source_start_kernel, both, [halo, (4, rows, columns)], [left_cell],
        cell_hot, cell_row_hot, sent, segs, matrix_state, matrix_perm,
    )
    around = to_all(edge)
    edge, kept = call(
        middle_kernel, both, [halo, (4, rows, columns)], [pltpu.VMEM(slots, F32), left_cell] + ext,
        around, cells, cell_hot, cell_row_hot, sent, segs, kept, matrix_perm,
    )
    around = to_all(edge)
    own, frac2, pressure = call(
        exchange_kernel, both, [slots, frac.shape, (rows, columns)], [left_seg] + ext,
        around, cells, cell_hot, slot, hot, row_hot, segs, own, frac1, aperture, kept,
    )
    segs = to_group(own)
    edge, kept = call(
        source_last_kernel, both, [halo, (3, rows, columns)], [left_cell],
        cell_hot, cell_row_hot, sent, own, segs, pressure, kept, matrix_perm,
    )
    around = to_all(edge)
    (frac3,) = call(
        owner_last_kernel, (members,), [frac.shape], [left_seg], slot, hot, row_hot, own, segs, frac2, aperture
    )
    (matrix_out,) = call(final_kernel, both, [matrix_state.shape], ext, around, pressure, kept)
    return matrix_out, frac3.reshape(frac_state.shape)


def solution(mesh):
    return jax.shard_map(
        on_device,
        mesh=mesh,
        in_specs=(
            P(None, "grp", "frac"),
            P("grp", "frac"),
            P(None, "grp", "frac"),
            P("grp", "frac"),
            P("grp", "frac", None, None),
            P("grp", "frac", None, None),
            P("grp", "frac", None, None),
            P("grp", "frac", None),
            P(None, "grp", "frac", None, None),
        ),
        out_specs=(P(None, "grp", "frac"), P(None, "grp", "frac")),
        check_vma=False,
    )
```

```python
import functools

import jax
import jax.numpy as jnp
from jax import lax
from jax.experimental import pallas as pl
from jax.experimental.pallas import tpu as pltpu
from jax.sharding import PartitionSpec as P

ITERS = 3
SWEEPS = 4

LOW_BOUND = 0.02
HIGH_BOUND = 1.98
TAU_STEP = 0.5
MOBILITY_FLOOR = 0.2

F32 = jnp.float32
BF16 = jnp.bfloat16
LANES = 128
SUB = 8
DEPTH = SWEEPS - 1


def iota(shape, dim):
    return lax.broadcasted_iota(jnp.int32, shape, dim)


def parts_of(x):
    high = x.astype(BF16).astype(F32)
    return high, x - high


PARTS = 2


def table_of(fields):
    split = [parts_of(f) for f in fields]
    return jnp.concatenate([s[p] for p in range(PARTS) for s in split], axis=0).astype(BF16)


def one_hot(index_row, count):
    hit = iota((count, index_row.shape[1]), 0) == index_row
    return jnp.where(hit, 1.0, 0.0).astype(BF16)


def pick(table, fields, rows, row_index, hot):
    wide = jnp.dot(table, hot, preferred_element_type=F32)
    hit = iota((rows, row_index.shape[1]), 0) == row_index
    found = []
    for f in range(fields):
        total = sum(wide[(p * fields + f) * rows : (p * fields + f + 1) * rows] for p in range(PARTS))
        found.append(jnp.sum(jnp.where(hit, total, 0.0), axis=0, keepdims=True))
    return found


def spread(left_ref, row_hot_ref, block, values):
    rows = row_hot_ref.shape[0]
    width = values[0].shape[1]
    at = slice(block * width, (block + 1) * width)
    hot = row_hot_ref[:, at]
    for f, value in enumerate(values):
        for p, part in enumerate(parts_of(value)):
            row = (p * len(values) + f) * rows
            left_ref[row : row + rows, at] = hot * part.astype(BF16)


def gathered_sum(left_ref, hot_ref, fields, rows):
    wide = lax.dot_general(
        left_ref[...], hot_ref[...], (((1,), (1,)), ((), ())), preferred_element_type=F32
    )
    return [
        sum(wide[(p * fields + f) * rows : (p * fields + f + 1) * rows] for p in range(PARTS))
        for f in range(fields)
    ]


def flow(trans, upwind, cell_p, cell_s, seg_p, seg_s):
    u = jnp.where(upwind > 0.5, cell_s, seg_s)
    weight = trans * (MOBILITY_FLOOR + u * u)
    water = weight * (cell_p - seg_p) * u
    return weight, water


def cell_parts(cell_row, columns):
    return cell_row // columns, cell_row % columns


def ends_of(frac):
    rows = frac.shape[0]
    return jnp.concatenate([frac[0:1], frac[rows - 1 : rows]], axis=1)


def frac_step(frac, sat, aperture, before, after, inflow, total, gained):
    rows, lanes = frac.shape
    row, lane = iota((rows, lanes), 0), iota((rows, lanes), 1)
    back = pltpu.roll(frac, 1, 1)
    left = jnp.where(lane == 0, pltpu.roll(back, 1, 0), back)
    left = jnp.where((lane == 0) & (row == 0), before, left)
    ahead = pltpu.roll(frac, lanes - 1, 1)
    right = jnp.where(lane == lanes - 1, pltpu.roll(ahead, rows - 1, 0), ahead)
    right = jnp.where((lane == lanes - 1) & (row == rows - 1), after, right)
    new_frac = (aperture * frac + inflow + left + right) / (aperture + total + 2.0)
    new_sat = sat + TAU_STEP * gained / (aperture + total)
    return new_frac, new_sat


def chain_ends(ends_ref, row, members):
    me = lax.axis_index("frac")
    lanes = ends_ref.shape[2]
    prior = ends_ref[jnp.maximum(me - 1, 0), row : row + 1, :]
    later = ends_ref[jnp.minimum(me + 1, members - 1), row : row + 1, :]
    before = jnp.where(me > 0, prior[:, lanes - 1 :], 0.0)
    after = jnp.where(me < members - 1, later[:, 0:1], 0.0)
    return before, after


def partial_residual(pressure, couple, source, inverse):
    rows, columns = pressure.shape
    row, col = iota((rows, columns), 0), iota((rows, columns), 1)
    beside = jnp.where(row == 0, 0.0, pltpu.roll(pressure, 1, 0))
    beside += jnp.where(row == rows - 1, 0.0, pltpu.roll(pressure, rows - 1, 0))
    beside += jnp.where(col == 0, 0.0, pltpu.roll(pressure, 1, 1))
    beside += jnp.where(col == columns - 1, 0.0, pltpu.roll(pressure, columns - 1, 1))
    return inverse * (source - (4.0 + couple) * pressure + beside)


def pack_low(q, inv, p, at, axis):
    return jnp.where(
        at < DEPTH, q, jnp.where(at < 2 * DEPTH, pltpu.roll(inv, DEPTH, axis), pltpu.roll(p, 2 * DEPTH, axis))
    )


def pack_high(q, inv, p, at, axis):
    size = q.shape[axis]
    return jnp.where(
        at >= size - DEPTH,
        q,
        jnp.where(
            at >= size - 2 * DEPTH,
            pltpu.roll(inv, size - DEPTH, axis),
            pltpu.roll(p, size - 2 * DEPTH, axis),
        ),
    )


def block_rows(columns, width):
    vertical = 2 * DEPTH * (columns // LANES) + 1
    lateral = SUB + 2 * (width // LANES) + 1
    return max(vertical, lateral)


def put_rows(out_ref, at, values):
    for k in range(values.shape[0]):
        out_ref[at + k] = values[k : k + 1]


def get_rows(in_ref, at, count):
    return jnp.concatenate([in_ref[at + k] for k in range(count)], axis=0)


def send_slots(out_ref, at, first, second):
    halves = first.shape[1] // LANES
    for i, value in enumerate((first, second)):
        for h in range(halves):
            out_ref[at + SUB + i * halves + h] = value[:, h * LANES : (h + 1) * LANES]


def got_slots(in_ref, at, width):
    halves = width // LANES
    return [
        jnp.concatenate([in_ref[at + SUB + i * halves + h] for h in range(halves)], axis=1) for i in range(2)
    ]


def send_halo(out_ref, q, inv, p, groups, members, size):
    rows, columns = q.shape
    halves = columns // LANES
    g, f = lax.axis_index("grp"), lax.axis_index("frac")
    here = g * members + f
    lane = iota((rows, LANES), 1)
    low = pack_low(q[:, :LANES], inv[:, :LANES], p[:, :LANES], lane, 1)
    high = pack_high(q[:, columns - LANES :], inv[:, columns - LANES :], p[:, columns - LANES :], lane, 1)
    turned = jnp.transpose(jnp.where(lane < LANES // 2, low, high))
    left, right = turned[:SUB], turned[LANES - SUB :]
    lane = iota((1, LANES), 1)

    for step in (-1, 1):
        layer = (lambda k: k) if step < 0 else (lambda k: rows - 1 - k)

        def span(field, count, at):
            start = 0 if step < 0 else rows - count
            return field[start : start + count, at]

        inside = (g + step >= 0) & (g + step < groups)
        base = here + step * members
        tiles = [slice(h * LANES, (h + 1) * LANES) for h in range(halves)]

        @pl.when(inside)
        def _():
            at = base * size
            for h, tile in enumerate(tiles):
                put_rows(out_ref, at + h * DEPTH, span(q, DEPTH, tile))
                put_rows(out_ref, at + halves * DEPTH + h * (DEPTH - 1), span(inv, DEPTH - 1, tile))
                put_rows(out_ref, at + halves * (2 * DEPTH - 1) + h, span(p, 1, tile))
            deep, next_p = layer(DEPTH - 1), layer(1)
            extra = jnp.where(
                lane == 0,
                inv[deep : deep + 1, tiles[0]],
                jnp.where(
                    lane == LANES - 1,
                    inv[deep : deep + 1, tiles[-1]],
                    jnp.where(
                        lane == 1,
                        pltpu.roll(p[next_p : next_p + 1, tiles[0]], 1, 1),
                        pltpu.roll(p[next_p : next_p + 1, tiles[-1]], LANES - 1, 1),
                    ),
                ),
            )
            out_ref[at + halves * 2 * DEPTH] = extra

        for side, tile, there in ((-1, tiles[0], f > 0), (1, tiles[-1], f < members - 1)):

            @pl.when(inside & there)
            def _(side=side, tile=tile):
                at = (base + side) * size
                for i, field in enumerate((q, inv, p)):
                    put_rows(out_ref, at + i * DEPTH, span(field, DEPTH, tile))

    @pl.when(f > 0)
    def _():
        put_rows(out_ref, (here - 1) * size, left)

    @pl.when(f < members - 1)
    def _():
        put_rows(out_ref, (here + 1) * size, right)


def chebyshev(in_ref, q, inv, p, q_ext, inv_ext, p_ext, groups, members, size):
    rows, columns = q.shape
    halves = columns // LANES
    g, f = lax.axis_index("grp"), lax.axis_index("frac")
    here = g * members + f
    last = groups * members - 1

    def taker(dg, df):
        ok = (g + dg >= 0) & (g + dg < groups) & (f + df >= 0) & (f + df < members)
        at = jnp.clip(here + dg * members + df, 0, last) * size
        return lambda start, count: jnp.where(ok, get_rows(in_ref, at + start, count), 0.0)

    def both(low, high, at, count, size):
        return jnp.where(at < count, low, jnp.where(at >= size - count, high, 0.0))

    q_ext[0:rows, 0:columns] = q
    inv_ext[0:rows, 0:columns] = inv
    p_ext[0:rows, 0:columns] = p
    below, above = taker(1, 0), taker(-1, 0)
    lane = iota((1, LANES), 1)
    low_extra, high_extra = below(halves * 2 * DEPTH, 1), above(halves * 2 * DEPTH, 1)

    def filler(count):
        return jnp.zeros((count, LANES), F32)

    for h in range(halves):
        tile = slice(h * LANES, (h + 1) * LANES)
        edge = (lane == 0) & (h == 0) | (lane == LANES - 1) & (h == halves - 1)

        def at_edge(row, turn):
            return jnp.where(edge, pltpu.roll(row, turn, 1) if turn else row, 0.0)

        turn = LANES - 1 if h == 0 else 1
        at = h * DEPTH
        q_ext[rows : rows + SUB, tile] = jnp.concatenate(
            [below(at, DEPTH), filler(SUB - 2 * DEPTH), above(at, DEPTH)], axis=0
        )
        at = halves * DEPTH + h * (DEPTH - 1)
        inv_ext[rows : rows + SUB, tile] = jnp.concatenate(
            [
                below(at, DEPTH - 1),
                at_edge(low_extra, 0),
                filler(SUB - 2 * DEPTH),
                at_edge(high_extra, 0),
                above(at, DEPTH - 1),
            ],
            axis=0,
        )
        at = halves * (2 * DEPTH - 1) + h
        p_ext[rows : rows + SUB, tile] = jnp.concatenate(
            [
                below(at, 1),
                at_edge(low_extra, turn),
                filler(SUB - 4),
                at_edge(high_extra, turn),
                above(at, 1),
            ],
            axis=0,
        )
    right, left = taker(0, 1)(0, SUB), taker(0, -1)(0, SUB)
    turned = jnp.transpose(
        jnp.concatenate([right, jnp.zeros((LANES - 2 * SUB, rows), F32), left], axis=0)
    )
    lane = iota((rows, LANES), 1)
    side = slice(columns, columns + LANES)
    q_ext[0:rows, side] = both(turned, turned, lane, DEPTH, LANES)
    inv_ext[0:rows, side] = both(
        pltpu.roll(turned, LANES - DEPTH, 1), pltpu.roll(turned, DEPTH, 1), lane, DEPTH, LANES
    )
    p_ext[0:rows, side] = both(
        pltpu.roll(turned, LANES - 2 * DEPTH, 1), pltpu.roll(turned, 2 * DEPTH, 1), lane, 2, LANES
    )
    lane = iota((DEPTH, LANES), 1)
    corner = slice(rows, rows + SUB)
    low_right, low_left, high_right, high_left = taker(1, 1), taker(1, -1), taker(-1, 1), taker(-1, -1)
    for i, ext in enumerate((q_ext, inv_ext, p_ext)):
        at = i * DEPTH
        ext[corner, side] = jnp.concatenate(
            [
                both(low_right(at, DEPTH), low_left(at, DEPTH), lane, DEPTH, LANES),
                filler(SUB - 2 * DEPTH),
                both(high_right(at, DEPTH), high_left(at, DEPTH), lane, DEPTH, LANES),
            ],
            axis=0,
        )

    shape = (rows + SUB, columns + LANES)
    for here_row, there_row in ((0, shape[0] - 1), (shape[0] - 1, 0), (rows - 1, rows), (rows, rows - 1)):
        q_ext[here_row : here_row + 1, :] += (
            inv_ext[here_row : here_row + 1, :] * p_ext[there_row : there_row + 1, :]
        )
    lane = iota((shape[0], LANES), 1)
    first, final = slice(0, LANES), slice(columns - LANES, columns)
    p_side = p_ext[:, side]
    from_left, from_right = pltpu.roll(p_side, 1, 1), pltpu.roll(p_side, LANES - 1, 1)
    q_ext[:, first] += inv_ext[:, first] * jnp.where(lane == 0, from_left, 0.0)
    q_ext[:, final] += inv_ext[:, final] * jnp.where(lane == LANES - 1, from_right, 0.0)
    q_ext[:, side] += inv_ext[:, side] * jnp.where(
        lane == 0,
        pltpu.roll(p_ext[:, final], 1, 1),
        jnp.where(lane == LANES - 1, pltpu.roll(p_ext[:, first], LANES - 1, 1), 0.0),
    )
    inverse = inv_ext[...]
    start = q_ext[...]

    centre = 0.5 * (HIGH_BOUND + LOW_BOUND)
    half_width = 0.5 * (HIGH_BOUND - LOW_BOUND)
    scale_ratio = centre / half_width
    ratio_now = 1.0 / scale_ratio
    update = start / centre if centre != 1.0 else start
    change = update
    for _ in range(SWEEPS - 1):
        beside = (
            pltpu.roll(change, 1, 0)
            + pltpu.roll(change, shape[0] - 1, 0)
            + pltpu.roll(change, 1, 1)
            + pltpu.roll(change, shape[1] - 1, 1)
        )
        residual = start - change + inverse * beside
        ratio_next = 1.0 / (2.0 * scale_ratio - ratio_now)
        update = ratio_next * ratio_now * update + (2.0 * ratio_next / half_width) * residual
        ratio_now = ratio_next
        change = change + update
    return p + change[0:rows, 0:columns]


ROW_SEG = 0
ROW_TRANS = 1
ROW_UP = 2
ROW_P = ROW_UP + ITERS
ROW_S = ROW_P + 1
ROW_ENDS = ROW_S + 1


def first_kernel(
    members, cell_any, seg_any, trans_any, count_any, up_any, state_any, frac_any,
    out_ref, hot_ref, row_hot_ref, cell_ref, seg_ref, trans_ref, count_ref, up_ref, state_ref, frac_ref, sem,
):
    _, rows, columns = state_ref.shape
    width = cell_ref.shape[1]
    seg_rows = frac_ref.shape[1]
    copies = [
        pltpu.make_async_copy(source, target, sem.at[i])
        for i, (source, target) in enumerate(
            [
                (cell_any, cell_ref),
                (state_any, state_ref),
                (seg_any, seg_ref),
                (trans_any, trans_ref),
                (count_any, count_ref),
                (up_any, up_ref),
                (frac_any, frac_ref),
            ]
        )
    ]
    for copy in copies:
        copy.start()
    copies[0].wait()
    for o in range(members):
        row, col = cell_parts(cell_ref[o : o + 1, :], columns)
        at = slice(o * width, (o + 1) * width)
        hot_ref[:, at] = one_hot(col, columns)
        row_hot_ref[:, at] = one_hot(row, rows)
    copies[1].wait()
    table = table_of([state_ref[0], state_ref[1]])
    for copy in copies[2:]:
        copy.wait()
    ends = ends_of(frac_ref[0])
    whole = jnp.concatenate([frac_ref[0], frac_ref[1]], axis=1)
    for o in range(members):
        one = slice(o, o + 1)
        row, _ = cell_parts(cell_ref[one, :], columns)
        cell_p, cell_s = pick(table, 2, rows, row, hot_ref[:, o * width : (o + 1) * width])
        live = iota((1, width), 1) < count_ref[0, o]
        out_ref[o, ROW_SEG : ROW_SEG + 1, :] = seg_ref[one, :].astype(F32)
        out_ref[o, ROW_TRANS : ROW_TRANS + 1, :] = jnp.where(live, trans_ref[one, :], 0.0)
        for t in range(ITERS):
            out_ref[o, ROW_UP + t : ROW_UP + t + 1, :] = up_ref[t, one, :].astype(F32)
        out_ref[o, ROW_P : ROW_P + 1, :] = cell_p
        out_ref[o, ROW_S : ROW_S + 1, :] = cell_s
        out_ref[o, ROW_ENDS : ROW_ENDS + 1, :] = ends
        out_ref[o, SUB : SUB + seg_rows, :] = whole


def seg_parts(slot_ref, s):
    seg = slot_ref[s, ROW_SEG : ROW_SEG + 1, :].astype(jnp.int32)
    return seg // LANES, seg % LANES


def seg_hots(slot_ref, hot_ref, row_hot_ref, members, width):
    for s in range(members):
        row, lane = seg_parts(slot_ref, s)
        at = slice(s * width, (s + 1) * width)
        hot_ref[:, at] = one_hot(lane, LANES)
        row_hot_ref[:, at] = one_hot(row, row_hot_ref.shape[0])


def seg_gather(slot_ref, hot_ref, fields, s, width, table):
    return pick(table, 2, fields, seg_parts(slot_ref, s)[0], hot_ref[:, s * width : (s + 1) * width])


def cell_update(
    members, t, hot_ref, row_hot_ref, sent_ref, cell_rows, seg_rows, pressure, saturation, perm, left_ref
):
    rows = pressure.shape[0]
    for o in range(members):
        seg_p, seg_s = seg_rows(o)
        cell_p, cell_s = cell_rows(o)
        weight, water = flow(
            sent_ref[o, ROW_TRANS : ROW_TRANS + 1, :],
            sent_ref[o, ROW_UP + t : ROW_UP + t + 1, :],
            cell_p,
            cell_s,
            seg_p,
            seg_s,
        )
        spread(left_ref, row_hot_ref, o, [weight, weight * seg_p, water])
    couple, source, lost = gathered_sum(left_ref, hot_ref, 3, rows)
    inverse = 1.0 / (4.0 + perm + couple)
    new_saturation = saturation - TAU_STEP * lost / (perm + couple)
    return new_saturation, partial_residual(pressure, couple, source, inverse), inverse


def start_kernel(
    groups, members, size, slot_ref, sent_ref, cell_hot_ref, cell_row_hot_ref, frac_ref, aperture_ref,
    state_ref, perm_ref, out_ref, keep_ref, own_ref, new_ref, hot_ref, row_hot_ref,
    left_seg_ref, left_ref, found_ref,
):
    width = slot_ref.shape[2]
    rows = frac_ref.shape[1]
    g = lax.axis_index("grp")
    frac, sat = frac_ref[0], frac_ref[1]
    seg_hots(slot_ref, hot_ref, row_hot_ref, members, width)
    table = table_of([frac, sat])
    for s in range(members):
        seg_p, seg_s = seg_gather(slot_ref, hot_ref, rows, s, width, table)
        cell_p = slot_ref[s, ROW_P : ROW_P + 1, :]
        weight, water = flow(
            slot_ref[s, ROW_TRANS : ROW_TRANS + 1, :],
            slot_ref[s, ROW_UP : ROW_UP + 1, :],
            cell_p,
            slot_ref[s, ROW_S : ROW_S + 1, :],
            seg_p,
            seg_s,
        )
        spread(left_seg_ref, row_hot_ref, s, [weight * cell_p, weight, water])
    inflow, total, gained = gathered_sum(left_seg_ref, hot_ref, 3, rows)
    before, after = chain_ends(slot_ref, ROW_ENDS, members)
    new_frac, new_sat = frac_step(frac, sat, aperture_ref[...], before, after, inflow, total, gained)
    new_ref[0] = new_frac
    new_ref[1] = new_sat
    table = table_of([new_frac, new_sat])
    lane = iota((1, LANES), 1)
    ends = jnp.where(lane < LANES // 2, new_frac[0:1], new_frac[rows - 1 : rows])
    for s in range(members):
        seg_p, seg_s = seg_gather(slot_ref, hot_ref, rows, s, width, table)
        own_ref[s, 0:1, :] = seg_p
        own_ref[s, 1:2, :] = seg_s
        at = (g * members + s) * size
        send_slots(out_ref, at, seg_p, seg_s)
        out_ref[at + size - 1] = ends
    for o in range(members):
        row, lane = seg_parts(sent_ref, o)
        table = table_of([slot_ref[o, SUB : SUB + rows, 0:LANES], slot_ref[o, SUB : SUB + rows, LANES : 2 * LANES]])
        seg_p, seg_s = pick(table, 2, rows, row, one_hot(lane, LANES))
        found_ref[o, 0:1, :] = seg_p
        found_ref[o, 1:2, :] = seg_s
    pressure = state_ref[0]
    new_saturation, q, inv = cell_update(
        members,
        0,
        cell_hot_ref,
        cell_row_hot_ref,
        sent_ref,
        lambda o: (sent_ref[o, ROW_P : ROW_P + 1, :], sent_ref[o, ROW_S : ROW_S + 1, :]),
        lambda o: (found_ref[o, 0:1, :], found_ref[o, 1:2, :]),
        pressure,
        state_ref[1],
        perm_ref[...],
        left_ref,
    )
    keep_ref[0] = pressure
    keep_ref[1] = new_saturation
    keep_ref[2] = q
    keep_ref[3] = inv
    send_halo(out_ref, q, inv, pressure, groups, members, size)


def cell_gather(members, cell_ref, hot_ref, fields, put):
    rows, columns = fields[0].shape
    width = cell_ref.shape[1]
    table = table_of(fields)
    for o in range(members):
        row, _ = cell_parts(cell_ref[o : o + 1, :], columns)
        put(o, *pick(table, len(fields), rows, row, hot_ref[:, o * width : (o + 1) * width]))


def middle_kernel(
    groups, members, size, halo_ref, cell_ref, hot_ref, row_hot_ref, sent_ref, kept_ref, perm_ref,
    out_ref, keep_ref, slots_ref, left_ref, q_ext, inv_ext, p_ext,
):
    pressure = chebyshev(
        halo_ref, kept_ref[2], kept_ref[3], kept_ref[0], q_ext, inv_ext, p_ext, groups, members, size
    )
    saturation = kept_ref[1]
    g = lax.axis_index("grp")

    def put(o, cell_p, cell_s):
        slots_ref[o, 0:1, :] = cell_p
        slots_ref[o, 1:2, :] = cell_s
        send_slots(out_ref, (g * members + o) * size, cell_p, cell_s)

    cell_gather(members, cell_ref, hot_ref, [pressure, saturation], put)
    new_saturation, q, inv = cell_update(
        members,
        1,
        hot_ref,
        row_hot_ref,
        sent_ref,
        lambda o: (slots_ref[o, 0:1, :], slots_ref[o, 1:2, :]),
        lambda o: got_slots(halo_ref, (g * members + o) * size, cell_ref.shape[1]),
        pressure,
        saturation,
        perm_ref[...],
        left_ref,
    )
    keep_ref[0] = pressure
    keep_ref[1] = new_saturation
    keep_ref[2] = q
    keep_ref[3] = inv
    send_halo(out_ref, q, inv, pressure, groups, members, size)


def owner_update(
    members, t, slot_ref, cell_rows, seg_rows, frac, sat, aperture, ends, hot_ref, row_hot_ref, left_ref
):
    rows = frac.shape[0]
    for s in range(members):
        cell_p, cell_s = cell_rows(s)
        weight, water = flow(
            slot_ref[s, ROW_TRANS : ROW_TRANS + 1, :],
            slot_ref[s, ROW_UP + t : ROW_UP + t + 1, :],
            cell_p,
            cell_s,
            *seg_rows(s),
        )
        spread(left_ref, row_hot_ref, s, [weight * cell_p, weight, water])
    inflow, total, gained = gathered_sum(left_ref, hot_ref, 3, rows)
    return frac_step(frac, sat, aperture, *ends, inflow, total, gained)


def exchange_kernel(
    groups, members, size, halo_ref, cell_ref, cell_hot_ref, slot_ref, hot_ref, row_hot_ref, ends_ref, own_ref,
    frac_ref, aperture_ref, kept_ref, out_ref, new_ref, pressure_ref, left_ref, q_ext, inv_ext, p_ext,
):
    width = slot_ref.shape[2]
    rows = frac_ref.shape[1]
    g = lax.axis_index("grp")

    def cell_rows(s):
        return got_slots(halo_ref, (g * members + s) * size, width)

    me = lax.axis_index("frac")
    prior = ends_ref[(g * members + jnp.maximum(me - 1, 0)) * size + size - 1]
    later = ends_ref[(g * members + jnp.minimum(me + 1, members - 1)) * size + size - 1]
    before = jnp.where(me > 0, prior[:, LANES - 1 :], 0.0)
    after = jnp.where(me < members - 1, later[:, 0:1], 0.0)

    new_frac, new_sat = owner_update(
        members,
        1,
        slot_ref,
        cell_rows,
        lambda s: (own_ref[s, 0:1, :], own_ref[s, 1:2, :]),
        frac_ref[0],
        frac_ref[1],
        aperture_ref[...],
        (before, after),
        hot_ref,
        row_hot_ref,
        left_ref,
    )
    new_ref[0] = new_frac
    new_ref[1] = new_sat
    table = table_of([new_frac, new_sat])
    ends = ends_of(new_frac)
    for s in range(members):
        seg_p, seg_s = seg_gather(slot_ref, hot_ref, rows, s, width, table)
        out_ref[s, 2:3, :] = seg_p
        out_ref[s, 3:4, :] = seg_s
        out_ref[s, 4:5, :] = ends

    pressure = chebyshev(
        halo_ref, kept_ref[2], kept_ref[3], kept_ref[0], q_ext, inv_ext, p_ext, groups, members, size
    )
    pressure_ref[...] = pressure

    def put(o, cell_p, cell_s):
        out_ref[o, 0:1, :] = cell_p
        out_ref[o, 1:2, :] = cell_s

    cell_gather(members, cell_ref, cell_hot_ref, [pressure, kept_ref[1]], put)


def source_last_kernel(
    groups, members, size, hot_ref, row_hot_ref, sent_ref, own_ref, seg_ref, pressure_ref, kept_ref, perm_ref,
    out_ref, keep_ref, left_ref,
):
    pressure = pressure_ref[...]
    new_saturation, q, inv = cell_update(
        members,
        2,
        hot_ref,
        row_hot_ref,
        sent_ref,
        lambda o: (own_ref[o, 0:1, :], own_ref[o, 1:2, :]),
        lambda o: (seg_ref[o, 2:3, :], seg_ref[o, 3:4, :]),
        pressure,
        kept_ref[1],
        perm_ref[...],
        left_ref,
    )
    keep_ref[0] = new_saturation
    keep_ref[1] = q
    keep_ref[2] = inv
    send_halo(out_ref, q, inv, pressure, groups, members, size)


def owner_last_kernel(
    members, slot_ref, hot_ref, row_hot_ref, own_ref, seg_ref, frac_ref, aperture_ref, out_ref, left_ref
):
    new_frac, new_sat = owner_update(
        members,
        2,
        slot_ref,
        lambda s: (seg_ref[s, 0:1, :], seg_ref[s, 1:2, :]),
        lambda s: (own_ref[s, 2:3, :], own_ref[s, 3:4, :]),
        frac_ref[0],
        frac_ref[1],
        aperture_ref[...],
        chain_ends(seg_ref, 4, members),
        hot_ref,
        row_hot_ref,
        left_ref,
    )
    out_ref[0] = new_frac
    out_ref[1] = new_sat


def final_kernel(groups, members, size, halo_ref, pressure_ref, kept_ref, out_ref, q_ext, inv_ext, p_ext):
    out_ref[0] = chebyshev(
        halo_ref, kept_ref[1], kept_ref[2], pressure_ref[...], q_ext, inv_ext, p_ext, groups, members, size
    )
    out_ref[1] = kept_ref[0]


VMEM = pl.BlockSpec(memory_space=pltpu.VMEM)
HBM = pl.BlockSpec(memory_space=pltpu.HBM)


def call(kernel, statics, outs, scratch, *args, spec=VMEM):
    outs = [o if hasattr(o, "dtype") else jax.ShapeDtypeStruct(o, F32) for o in outs]
    return pl.pallas_call(
        functools.partial(kernel, *statics),
        out_shape=outs,
        in_specs=[spec] * len(args),
        out_specs=[VMEM] * len(outs),
        scratch_shapes=scratch,
        compiler_params=pltpu.CompilerParams(vmem_limit_bytes=32 * 1024 * 1024),
        name=kernel.__name__,
    )(*args)


def on_device(
    matrix_state,
    matrix_perm,
    frac_state,
    frac_aperture,
    link_cell,
    link_seg,
    link_trans,
    link_count,
    link_upwind,
):
    groups, members = lax.axis_size("grp"), lax.axis_size("frac")
    devices = groups * members
    cells = link_cell[0, 0]
    width = cells.shape[1]
    _, rows, columns = matrix_state.shape
    seg_dev = frac_state.shape[2]
    seg_rows = seg_dev // LANES
    frac = frac_state.reshape(2, seg_rows, LANES)
    aperture = frac_aperture.reshape(seg_rows, LANES)

    every = members * width
    slots = (members, SUB, width)
    size = block_rows(columns, width)
    both = (groups, members, size)
    halo = (devices * size, 1, LANES)
    left_cell = pltpu.VMEM((3 * PARTS * rows, every), BF16)
    left_seg = pltpu.VMEM((3 * PARTS * seg_rows, every), BF16)
    ext = [pltpu.VMEM((rows + SUB, columns + LANES), F32)] * 3

    def to_group(x):
        return lax.all_to_all(x, "frac", split_axis=0, concat_axis=0, tiled=True)

    def to_all(x):
        return lax.all_to_all(x, ("grp", "frac"), split_axis=0, concat_axis=0, tiled=True)

    def hots(*sizes):
        return [jax.ShapeDtypeStruct((n, every), BF16) for n in sizes]

    sent, cell_hot, cell_row_hot = call(
        first_kernel,
        (members,),
        [(members, SUB + seg_rows, width)] + hots(columns, rows),
        [
            pltpu.VMEM((members, width), jnp.int32),
            pltpu.VMEM((members, width), jnp.int32),
            pltpu.VMEM((members, width), F32),
            pltpu.SMEM((1, members), jnp.int32),
            pltpu.VMEM((ITERS, members, width), jnp.int32),
            pltpu.VMEM(matrix_state.shape, F32),
            pltpu.VMEM(frac.shape, F32),
            pltpu.SemaphoreType.DMA((7,)),
        ],
        *[
            pltpu.with_memory_space_constraint(x, pltpu.HBM)
            for x in (
                cells, link_seg[0, 0], link_trans[0, 0], link_count[0], link_upwind[:, 0, 0], matrix_state, frac
            )
        ],
        spec=HBM,
    )
    slot = to_group(sent)
    edge, kept, own, frac1, hot, row_hot = call(
        start_kernel,
        both,
        [halo, (4, rows, columns), (members, 2, width), frac.shape] + hots(LANES, seg_rows),
        [left_seg, left_cell, pltpu.VMEM((members, 2, width), F32)],
        slot, sent, cell_hot, cell_row_hot, frac, aperture, matrix_state, matrix_perm,
    )
    before = to_all(edge)
    edge, kept = call(
        middle_kernel, both, [halo, (4, rows, columns)], [pltpu.VMEM((members, 2, width), F32), left_cell] + ext,
        before, cells, cell_hot, cell_row_hot, sent, kept, matrix_perm,
    )
    around = to_all(edge)
    own, frac2, pressure = call(
        exchange_kernel, both, [slots, frac.shape, (rows, columns)], [left_seg] + ext,
        around, cells, cell_hot, slot, hot, row_hot, before, own, frac1, aperture, kept,
    )
    segs = to_group(own)
    edge, kept = call(
        source_last_kernel, both, [halo, (3, rows, columns)], [left_cell],
        cell_hot, cell_row_hot, sent, own, segs, pressure, kept, matrix_perm,
    )
    around = to_all(edge)
    (frac3,) = call(
        owner_last_kernel, (members,), [frac.shape], [left_seg], slot, hot, row_hot, own, segs, frac2, aperture
    )
    (matrix_out,) = call(final_kernel, both, [matrix_state.shape], ext, around, pressure, kept)
    return matrix_out, frac3.reshape(frac_state.shape)


def solution(mesh):
    return jax.shard_map(
        on_device,
        mesh=mesh,
        in_specs=(
            P(None, "grp", "frac"),
            P("grp", "frac"),
            P(None, "grp", "frac"),
            P("grp", "frac"),
            P("grp", "frac", None, None),
            P("grp", "frac", None, None),
            P("grp", "frac", None, None),
            P("grp", "frac", None),
            P(None, "grp", "frac", None, None),
        ),
        out_specs=(P(None, "grp", "frac"), P(None, "grp", "frac")),
        check_vma=False,
    )
```

```python
import functools

import jax
import jax.numpy as jnp
from jax import lax
from jax.experimental import pallas as pl
from jax.experimental.pallas import tpu as pltpu
from jax.sharding import PartitionSpec as P

ITERS = 3
SWEEPS = 4

LOW_BOUND = 0.02
HIGH_BOUND = 1.98
TAU_STEP = 0.5
MOBILITY_FLOOR = 0.2

F32 = jnp.float32
BF16 = jnp.bfloat16
LANES = 128
SUB = 8
SEG_COLUMNS = 2 * LANES
DEPTH = SWEEPS - 1


def iota(shape, dim):
    return lax.broadcasted_iota(jnp.int32, shape, dim)


def parts_of(x):
    high = x.astype(BF16).astype(F32)
    return high, x - high


PARTS = 2


def table_of(fields):
    split = [parts_of(f) for f in fields]
    return jnp.concatenate([s[p] for p in range(PARTS) for s in split], axis=0).astype(BF16)


def one_hot(index_row, count):
    shape = (count, index_row.shape[1])
    hit = iota(shape, 0).astype(F32).astype(BF16) == index_row.astype(F32).astype(BF16)
    return jnp.where(hit, jnp.ones(shape, BF16), jnp.zeros(shape, BF16))


def pick(table, fields, rows, row_index, hot):
    wide = jnp.dot(table, hot, preferred_element_type=F32)
    hit = iota((rows, row_index.shape[1]), 0) == row_index
    found = []
    for f in range(fields):
        total = sum(wide[(p * fields + f) * rows : (p * fields + f + 1) * rows] for p in range(PARTS))
        found.append(jnp.sum(jnp.where(hit, total, 0.0), axis=0, keepdims=True))
    return found


def spread(left_ref, row_hot_ref, block, values):
    rows = row_hot_ref.shape[0]
    width = values[0].shape[1]
    at = slice(block * width, (block + 1) * width)
    hot = row_hot_ref[:, at]
    for f, value in enumerate(values):
        for p, part in enumerate(parts_of(value)):
            row = (p * len(values) + f) * rows
            left_ref[row : row + rows, at] = hot * part.astype(BF16)


def gathered_sum(left_ref, hot_ref, fields, rows):
    wide = lax.dot_general(
        left_ref[...], hot_ref[...], (((1,), (1,)), ((), ())), preferred_element_type=F32
    )
    return [
        sum(wide[(p * fields + f) * rows : (p * fields + f + 1) * rows] for p in range(PARTS))
        for f in range(fields)
    ]


def flow(trans, upwind, cell_p, cell_s, seg_p, seg_s):
    u = jnp.where(upwind > 0.5, cell_s, seg_s)
    weight = trans * (MOBILITY_FLOOR + u * u)
    water = weight * (cell_p - seg_p) * u
    return weight, water


def cell_parts(cell_row, columns):
    return cell_row // columns, cell_row % columns


def load_segs(ref, *lead):
    rows = ref.shape[-2] // 2
    return jnp.concatenate([ref[(*lead, pl.ds(h, rows, 2), slice(None))] for h in range(2)], axis=1)


def store_segs(ref, lead, value):
    rows = value.shape[0]
    for h in range(2):
        ref[lead, pl.ds(h, rows, 2), :] = value[:, h * LANES : (h + 1) * LANES]


def ends_of(frac):
    rows, columns = frac.shape
    lane = iota((1, columns), 1)
    return jnp.where(lane < columns // 2, frac[0:1], frac[rows - 1 : rows])


def frac_step(frac, sat, aperture, before, after, inflow, total, gained):
    rows, lanes = frac.shape
    row, lane = iota((rows, lanes), 0), iota((rows, lanes), 1)
    back = pltpu.roll(frac, 1, 1)
    left = jnp.where(lane == 0, pltpu.roll(back, 1, 0), back)
    left = jnp.where((lane == 0) & (row == 0), before, left)
    ahead = pltpu.roll(frac, lanes - 1, 1)
    right = jnp.where(lane == lanes - 1, pltpu.roll(ahead, rows - 1, 0), ahead)
    right = jnp.where((lane == lanes - 1) & (row == rows - 1), after, right)
    new_frac = (aperture * frac + inflow + left + right) / (aperture + total + 2.0)
    new_sat = sat + TAU_STEP * gained / (aperture + total)
    return new_frac, new_sat


def chain_ends(ends_ref, row, members):
    me = lax.axis_index("frac")
    lanes = ends_ref.shape[2]
    prior = ends_ref[jnp.maximum(me - 1, 0), row : row + 1, :]
    later = ends_ref[jnp.minimum(me + 1, members - 1), row : row + 1, :]
    before = jnp.where(me > 0, prior[:, lanes - 1 :], 0.0)
    after = jnp.where(me < members - 1, later[:, 0:1], 0.0)
    return before, after


def partial_residual(pressure, couple, source, inverse):
    rows, columns = pressure.shape
    row, col = iota((rows, columns), 0), iota((rows, columns), 1)
    beside = jnp.where(row == 0, 0.0, pltpu.roll(pressure, 1, 0))
    beside += jnp.where(row == rows - 1, 0.0, pltpu.roll(pressure, rows - 1, 0))
    beside += jnp.where(col == 0, 0.0, pltpu.roll(pressure, 1, 1))
    beside += jnp.where(col == columns - 1, 0.0, pltpu.roll(pressure, columns - 1, 1))
    return inverse * (source - (4.0 + couple) * pressure + beside)


def pack_low(q, inv, p, at, axis):
    return jnp.where(
        at < DEPTH, q, jnp.where(at < 2 * DEPTH, pltpu.roll(inv, DEPTH, axis), pltpu.roll(p, 2 * DEPTH, axis))
    )


def pack_high(q, inv, p, at, axis):
    size = q.shape[axis]
    return jnp.where(
        at >= size - DEPTH,
        q,
        jnp.where(
            at >= size - 2 * DEPTH,
            pltpu.roll(inv, size - DEPTH, axis),
            pltpu.roll(p, size - 2 * DEPTH, axis),
        ),
    )


def block_rows(columns, width):
    vertical = 2 * DEPTH * (columns // LANES) + 1
    lateral = SUB + 2 * (width // LANES) + 1
    return max(vertical, lateral)


def put_rows(out_ref, at, values):
    for k in range(values.shape[0]):
        out_ref[at + k] = values[k : k + 1]


def get_rows(in_ref, at, count):
    return jnp.concatenate([in_ref[at + k] for k in range(count)], axis=0)


def send_slots(out_ref, at, first, second):
    halves = first.shape[1] // LANES
    for i, value in enumerate((first, second)):
        for h in range(halves):
            out_ref[at + SUB + i * halves + h] = value[:, h * LANES : (h + 1) * LANES]


def got_slots(in_ref, at, width):
    halves = width // LANES
    return [
        jnp.concatenate([in_ref[at + SUB + i * halves + h] for h in range(halves)], axis=1) for i in range(2)
    ]


def send_halo(out_ref, q, inv, p, groups, members, size):
    rows, columns = q.shape
    halves = columns // LANES
    g, f = lax.axis_index("grp"), lax.axis_index("frac")
    here = g * members + f
    lane = iota((rows, LANES), 1)
    low = pack_low(q[:, :LANES], inv[:, :LANES], p[:, :LANES], lane, 1)
    high = pack_high(q[:, columns - LANES :], inv[:, columns - LANES :], p[:, columns - LANES :], lane, 1)
    turned = jnp.transpose(jnp.where(lane < LANES // 2, low, high))
    left, right = turned[:SUB], turned[LANES - SUB :]
    lane = iota((1, LANES), 1)

    for step in (-1, 1):
        layer = (lambda k: k) if step < 0 else (lambda k: rows - 1 - k)

        def span(field, count, at):
            start = 0 if step < 0 else rows - count
            return field[start : start + count, at]

        inside = (g + step >= 0) & (g + step < groups)
        base = here + step * members
        tiles = [slice(h * LANES, (h + 1) * LANES) for h in range(halves)]

        @pl.when(inside)
        def _():
            at = base * size
            for h, tile in enumerate(tiles):
                put_rows(out_ref, at + h * DEPTH, span(q, DEPTH, tile))
                put_rows(out_ref, at + halves * DEPTH + h * (DEPTH - 1), span(inv, DEPTH - 1, tile))
                put_rows(out_ref, at + halves * (2 * DEPTH - 1) + h, span(p, 1, tile))
            deep, next_p = layer(DEPTH - 1), layer(1)
            extra = jnp.where(
                lane == 0,
                inv[deep : deep + 1, tiles[0]],
                jnp.where(
                    lane == LANES - 1,
                    inv[deep : deep + 1, tiles[-1]],
                    jnp.where(
                        lane == 1,
                        pltpu.roll(p[next_p : next_p + 1, tiles[0]], 1, 1),
                        pltpu.roll(p[next_p : next_p + 1, tiles[-1]], LANES - 1, 1),
                    ),
                ),
            )
            out_ref[at + halves * 2 * DEPTH] = extra

        for side, tile, there in ((-1, tiles[0], f > 0), (1, tiles[-1], f < members - 1)):

            @pl.when(inside & there)
            def _(side=side, tile=tile):
                at = (base + side) * size
                for i, field in enumerate((q, inv, p)):
                    put_rows(out_ref, at + i * DEPTH, span(field, DEPTH, tile))

    @pl.when(f > 0)
    def _():
        put_rows(out_ref, (here - 1) * size, left)

    @pl.when(f < members - 1)
    def _():
        put_rows(out_ref, (here + 1) * size, right)


def chebyshev(in_ref, q, inv, p, q_ext, inv_ext, p_ext, groups, members, size):
    rows, columns = q.shape
    halves = columns // LANES
    g, f = lax.axis_index("grp"), lax.axis_index("frac")
    here = g * members + f
    last = groups * members - 1

    def taker(dg, df):
        ok = (g + dg >= 0) & (g + dg < groups) & (f + df >= 0) & (f + df < members)
        at = jnp.clip(here + dg * members + df, 0, last) * size
        return lambda start, count: jnp.where(ok, get_rows(in_ref, at + start, count), 0.0)

    def both(low, high, at, count, size):
        return jnp.where(at < count, low, jnp.where(at >= size - count, high, 0.0))

    q_ext[0:rows, 0:columns] = q
    inv_ext[0:rows, 0:columns] = inv
    p_ext[0:rows, 0:columns] = p
    below, above = taker(1, 0), taker(-1, 0)
    lane = iota((1, LANES), 1)
    low_extra, high_extra = below(halves * 2 * DEPTH, 1), above(halves * 2 * DEPTH, 1)

    def filler(count):
        return jnp.zeros((count, LANES), F32)

    for h in range(halves):
        tile = slice(h * LANES, (h + 1) * LANES)
        edge = (lane == 0) & (h == 0) | (lane == LANES - 1) & (h == halves - 1)

        def at_edge(row, turn):
            return jnp.where(edge, pltpu.roll(row, turn, 1) if turn else row, 0.0)

        turn = LANES - 1 if h == 0 else 1
        at = h * DEPTH
        q_ext[rows : rows + SUB, tile] = jnp.concatenate(
            [below(at, DEPTH), filler(SUB - 2 * DEPTH), above(at, DEPTH)], axis=0
        )
        at = halves * DEPTH + h * (DEPTH - 1)
        inv_ext[rows : rows + SUB, tile] = jnp.concatenate(
            [
                below(at, DEPTH - 1),
                at_edge(low_extra, 0),
                filler(SUB - 2 * DEPTH),
                at_edge(high_extra, 0),
                above(at, DEPTH - 1),
            ],
            axis=0,
        )
        at = halves * (2 * DEPTH - 1) + h
        p_ext[rows : rows + SUB, tile] = jnp.concatenate(
            [
                below(at, 1),
                at_edge(low_extra, turn),
                filler(SUB - 4),
                at_edge(high_extra, turn),
                above(at, 1),
            ],
            axis=0,
        )
    right, left = taker(0, 1)(0, SUB), taker(0, -1)(0, SUB)
    turned = jnp.transpose(
        jnp.concatenate([right, jnp.zeros((LANES - 2 * SUB, rows), F32), left], axis=0)
    )
    lane = iota((rows, LANES), 1)
    side = slice(columns, columns + LANES)
    q_ext[0:rows, side] = both(turned, turned, lane, DEPTH, LANES)
    inv_ext[0:rows, side] = both(
        pltpu.roll(turned, LANES - DEPTH, 1), pltpu.roll(turned, DEPTH, 1), lane, DEPTH, LANES
    )
    p_ext[0:rows, side] = both(
        pltpu.roll(turned, LANES - 2 * DEPTH, 1), pltpu.roll(turned, 2 * DEPTH, 1), lane, 2, LANES
    )
    lane = iota((DEPTH, LANES), 1)
    corner = slice(rows, rows + SUB)
    low_right, low_left, high_right, high_left = taker(1, 1), taker(1, -1), taker(-1, 1), taker(-1, -1)
    for i, ext in enumerate((q_ext, inv_ext, p_ext)):
        at = i * DEPTH
        ext[corner, side] = jnp.concatenate(
            [
                both(low_right(at, DEPTH), low_left(at, DEPTH), lane, DEPTH, LANES),
                filler(SUB - 2 * DEPTH),
                both(high_right(at, DEPTH), high_left(at, DEPTH), lane, DEPTH, LANES),
            ],
            axis=0,
        )

    shape = (rows + SUB, columns + LANES)
    for here_row, there_row in ((0, shape[0] - 1), (shape[0] - 1, 0), (rows - 1, rows), (rows, rows - 1)):
        q_ext[here_row : here_row + 1, :] += (
            inv_ext[here_row : here_row + 1, :] * p_ext[there_row : there_row + 1, :]
        )
    lane = iota((shape[0], LANES), 1)
    first, final = slice(0, LANES), slice(columns - LANES, columns)
    p_side = p_ext[:, side]
    from_left, from_right = pltpu.roll(p_side, 1, 1), pltpu.roll(p_side, LANES - 1, 1)
    q_ext[:, first] += inv_ext[:, first] * jnp.where(lane == 0, from_left, 0.0)
    q_ext[:, final] += inv_ext[:, final] * jnp.where(lane == LANES - 1, from_right, 0.0)
    q_ext[:, side] += inv_ext[:, side] * jnp.where(
        lane == 0,
        pltpu.roll(p_ext[:, final], 1, 1),
        jnp.where(lane == LANES - 1, pltpu.roll(p_ext[:, first], LANES - 1, 1), 0.0),
    )
    inverse = inv_ext[...]
    start = q_ext[...]

    centre = 0.5 * (HIGH_BOUND + LOW_BOUND)
    half_width = 0.5 * (HIGH_BOUND - LOW_BOUND)
    scale_ratio = centre / half_width
    ratio_now = 1.0 / scale_ratio
    update = start / centre if centre != 1.0 else start
    change = update
    for _ in range(SWEEPS - 1):
        beside = (
            pltpu.roll(change, 1, 0)
            + pltpu.roll(change, shape[0] - 1, 0)
            + pltpu.roll(change, 1, 1)
            + pltpu.roll(change, shape[1] - 1, 1)
        )
        residual = start - change + inverse * beside
        ratio_next = 1.0 / (2.0 * scale_ratio - ratio_now)
        update = ratio_next * ratio_now * update + (2.0 * ratio_next / half_width) * residual
        ratio_now = ratio_next
        change = change + update
    return p + change[0:rows, 0:columns]


ROW_SEG = 0
ROW_TRANS = 1
ROW_UP = 2
ROW_P = ROW_UP + ITERS
ROW_S = ROW_P + 1
ROW_ENDS = ROW_S + 1


def first_kernel(
    members, cell_any, seg_any, trans_any, count_any, up_any, state_any, frac_any,
    out_ref, hot_ref, row_hot_ref, cell_ref, seg_ref, trans_ref, count_ref, up_ref, state_ref, frac_ref, sem,
):
    _, rows, columns = state_ref.shape
    width = cell_ref.shape[1]
    copies = [
        pltpu.make_async_copy(source, target, sem.at[i])
        for i, (source, target) in enumerate(
            [
                (cell_any, cell_ref),
                (state_any, state_ref),
                (seg_any, seg_ref),
                (trans_any, trans_ref),
                (count_any, count_ref),
                (up_any, up_ref),
                (frac_any, frac_ref),
            ]
        )
    ]
    for copy in copies:
        copy.start()
    copies[0].wait()
    for o in range(members):
        row, col = cell_parts(cell_ref[o : o + 1, :], columns)
        at = slice(o * width, (o + 1) * width)
        hot_ref[:, at] = one_hot(col, columns)
        row_hot_ref[:, at] = one_hot(row, rows)
    copies[1].wait()
    table = table_of([state_ref[0], state_ref[1]])
    for copy in copies[2:]:
        copy.wait()
    frac = load_segs(frac_ref, 0)
    ends = ends_of(frac)
    whole = jnp.concatenate([frac, load_segs(frac_ref, 1)], axis=0)
    for o in range(members):
        one = slice(o, o + 1)
        row, _ = cell_parts(cell_ref[one, :], columns)
        cell_p, cell_s = pick(table, 2, rows, row, hot_ref[:, o * width : (o + 1) * width])
        live = iota((1, width), 1) < count_ref[0, o]
        out_ref[o, ROW_SEG : ROW_SEG + 1, :] = seg_ref[one, :].astype(F32)
        out_ref[o, ROW_TRANS : ROW_TRANS + 1, :] = jnp.where(live, trans_ref[one, :], 0.0)
        for t in range(ITERS):
            out_ref[o, ROW_UP + t : ROW_UP + t + 1, :] = up_ref[t, one, :].astype(F32)
        out_ref[o, ROW_P : ROW_P + 1, :] = cell_p
        out_ref[o, ROW_S : ROW_S + 1, :] = cell_s
        out_ref[o, ROW_ENDS : ROW_ENDS + 1, :] = ends
        out_ref[o, SUB:, :] = whole


def seg_parts(slot_ref, s):
    seg = slot_ref[s, ROW_SEG : ROW_SEG + 1, :].astype(jnp.int32)
    return seg // SEG_COLUMNS, seg % SEG_COLUMNS


def seg_hots(slot_ref, hot_ref, row_hot_ref, members, width):
    for s in range(members):
        row, lane = seg_parts(slot_ref, s)
        at = slice(s * width, (s + 1) * width)
        hot_ref[:, at] = one_hot(lane, SEG_COLUMNS)
        row_hot_ref[:, at] = one_hot(row, row_hot_ref.shape[0])


def seg_gather(slot_ref, hot_ref, fields, s, width, table):
    return pick(table, 2, fields, seg_parts(slot_ref, s)[0], hot_ref[:, s * width : (s + 1) * width])


def cell_update(
    members, t, hot_ref, row_hot_ref, sent_ref, cell_rows, seg_rows, pressure, saturation, perm, left_ref
):
    rows = pressure.shape[0]
    for o in range(members):
        seg_p, seg_s = seg_rows(o)
        cell_p, cell_s = cell_rows(o)
        weight, water = flow(
            sent_ref[o, ROW_TRANS : ROW_TRANS + 1, :],
            sent_ref[o, ROW_UP + t : ROW_UP + t + 1, :],
            cell_p,
            cell_s,
            seg_p,
            seg_s,
        )
        spread(left_ref, row_hot_ref, o, [weight, weight * seg_p, water])
    couple, source, lost = gathered_sum(left_ref, hot_ref, 3, rows)
    inverse = 1.0 / (4.0 + perm + couple)
    new_saturation = saturation - TAU_STEP * lost / (perm + couple)
    return new_saturation, partial_residual(pressure, couple, source, inverse), inverse


def start_kernel(
    groups, members, size, slot_ref, sent_ref, cell_hot_ref, cell_row_hot_ref, frac_ref, aperture_ref,
    state_ref, perm_ref, out_ref, keep_ref, own_ref, new_ref, hot_ref, row_hot_ref,
    left_seg_ref, left_ref, found_ref,
):
    width = slot_ref.shape[2]
    rows = new_ref.shape[1]
    g = lax.axis_index("grp")
    frac, sat = load_segs(frac_ref, 0), load_segs(frac_ref, 1)
    seg_hots(slot_ref, hot_ref, row_hot_ref, members, width)
    table = table_of([frac, sat])
    for s in range(members):
        seg_p, seg_s = seg_gather(slot_ref, hot_ref, rows, s, width, table)
        cell_p = slot_ref[s, ROW_P : ROW_P + 1, :]
        weight, water = flow(
            slot_ref[s, ROW_TRANS : ROW_TRANS + 1, :],
            slot_ref[s, ROW_UP : ROW_UP + 1, :],
            cell_p,
            slot_ref[s, ROW_S : ROW_S + 1, :],
            seg_p,
            seg_s,
        )
        spread(left_seg_ref, row_hot_ref, s, [weight * cell_p, weight, water])
    inflow, total, gained = gathered_sum(left_seg_ref, hot_ref, 3, rows)
    before, after = chain_ends(slot_ref, ROW_ENDS, members)
    new_frac, new_sat = frac_step(frac, sat, load_segs(aperture_ref), before, after, inflow, total, gained)
    new_ref[0] = new_frac
    new_ref[1] = new_sat
    table = table_of([new_frac, new_sat])
    ends = ends_of(new_frac)
    ends = jnp.where(iota((1, LANES), 1) < LANES // 2, ends[:, :LANES], ends[:, SEG_COLUMNS - LANES :])
    for s in range(members):
        seg_p, seg_s = seg_gather(slot_ref, hot_ref, rows, s, width, table)
        own_ref[s, 0:1, :] = seg_p
        own_ref[s, 1:2, :] = seg_s
        at = (g * members + s) * size
        send_slots(out_ref, at, seg_p, seg_s)
        out_ref[at + size - 1] = ends
    for o in range(members):
        row, lane = seg_parts(sent_ref, o)
        table = table_of([slot_ref[o, SUB : SUB + rows, :], slot_ref[o, SUB + rows :, :]])
        seg_p, seg_s = pick(table, 2, rows, row, one_hot(lane, SEG_COLUMNS))
        found_ref[o, 0:1, :] = seg_p
        found_ref[o, 1:2, :] = seg_s
    pressure = state_ref[0]
    new_saturation, q, inv = cell_update(
        members,
        0,
        cell_hot_ref,
        cell_row_hot_ref,
        sent_ref,
        lambda o: (sent_ref[o, ROW_P : ROW_P + 1, :], sent_ref[o, ROW_S : ROW_S + 1, :]),
        lambda o: (found_ref[o, 0:1, :], found_ref[o, 1:2, :]),
        pressure,
        state_ref[1],
        perm_ref[...],
        left_ref,
    )
    keep_ref[0] = pressure
    keep_ref[1] = new_saturation
    keep_ref[2] = q
    keep_ref[3] = inv
    send_halo(out_ref, q, inv, pressure, groups, members, size)


def cell_gather(members, cell_ref, hot_ref, fields, put):
    rows, columns = fields[0].shape
    width = cell_ref.shape[1]
    table = table_of(fields)
    for o in range(members):
        row, _ = cell_parts(cell_ref[o : o + 1, :], columns)
        put(o, *pick(table, len(fields), rows, row, hot_ref[:, o * width : (o + 1) * width]))


def middle_kernel(
    groups, members, size, halo_ref, cell_ref, hot_ref, row_hot_ref, sent_ref, kept_ref, perm_ref,
    out_ref, keep_ref, slots_ref, left_ref, q_ext, inv_ext, p_ext,
):
    pressure = chebyshev(
        halo_ref, kept_ref[2], kept_ref[3], kept_ref[0], q_ext, inv_ext, p_ext, groups, members, size
    )
    saturation = kept_ref[1]
    g = lax.axis_index("grp")

    def put(o, cell_p, cell_s):
        slots_ref[o, 0:1, :] = cell_p
        slots_ref[o, 1:2, :] = cell_s
        send_slots(out_ref, (g * members + o) * size, cell_p, cell_s)

    cell_gather(members, cell_ref, hot_ref, [pressure, saturation], put)
    new_saturation, q, inv = cell_update(
        members,
        1,
        hot_ref,
        row_hot_ref,
        sent_ref,
        lambda o: (slots_ref[o, 0:1, :], slots_ref[o, 1:2, :]),
        lambda o: got_slots(halo_ref, (g * members + o) * size, cell_ref.shape[1]),
        pressure,
        saturation,
        perm_ref[...],
        left_ref,
    )
    keep_ref[0] = pressure
    keep_ref[1] = new_saturation
    keep_ref[2] = q
    keep_ref[3] = inv
    send_halo(out_ref, q, inv, pressure, groups, members, size)


def owner_update(
    members, t, slot_ref, cell_rows, seg_rows, frac, sat, aperture, ends, hot_ref, row_hot_ref, left_ref
):
    rows = frac.shape[0]
    for s in range(members):
        cell_p, cell_s = cell_rows(s)
        weight, water = flow(
            slot_ref[s, ROW_TRANS : ROW_TRANS + 1, :],
            slot_ref[s, ROW_UP + t : ROW_UP + t + 1, :],
            cell_p,
            cell_s,
            *seg_rows(s),
        )
        spread(left_ref, row_hot_ref, s, [weight * cell_p, weight, water])
    inflow, total, gained = gathered_sum(left_ref, hot_ref, 3, rows)
    return frac_step(frac, sat, aperture, *ends, inflow, total, gained)


def exchange_kernel(
    groups, members, size, halo_ref, cell_ref, cell_hot_ref, slot_ref, hot_ref, row_hot_ref, ends_ref, own_ref,
    frac_ref, aperture_ref, kept_ref, out_ref, new_ref, pressure_ref, left_ref, q_ext, inv_ext, p_ext,
):
    width = slot_ref.shape[2]
    rows = frac_ref.shape[1]
    g = lax.axis_index("grp")

    def cell_rows(s):
        return got_slots(halo_ref, (g * members + s) * size, width)

    me = lax.axis_index("frac")
    prior = ends_ref[(g * members + jnp.maximum(me - 1, 0)) * size + size - 1]
    later = ends_ref[(g * members + jnp.minimum(me + 1, members - 1)) * size + size - 1]
    before = jnp.where(me > 0, prior[:, LANES - 1 :], 0.0)
    after = jnp.where(me < members - 1, later[:, 0:1], 0.0)

    new_frac, new_sat = owner_update(
        members,
        1,
        slot_ref,
        cell_rows,
        lambda s: (own_ref[s, 0:1, :], own_ref[s, 1:2, :]),
        frac_ref[0],
        frac_ref[1],
        load_segs(aperture_ref),
        (before, after),
        hot_ref,
        row_hot_ref,
        left_ref,
    )
    new_ref[0] = new_frac
    new_ref[1] = new_sat
    table = table_of([new_frac, new_sat])
    ends = ends_of(new_frac)
    for s in range(members):
        seg_p, seg_s = seg_gather(slot_ref, hot_ref, rows, s, width, table)
        out_ref[s, 2:3, :] = seg_p
        out_ref[s, 3:4, :] = seg_s
        out_ref[s, 4:5, :] = ends

    pressure = chebyshev(
        halo_ref, kept_ref[2], kept_ref[3], kept_ref[0], q_ext, inv_ext, p_ext, groups, members, size
    )
    pressure_ref[...] = pressure

    def put(o, cell_p, cell_s):
        out_ref[o, 0:1, :] = cell_p
        out_ref[o, 1:2, :] = cell_s

    cell_gather(members, cell_ref, cell_hot_ref, [pressure, kept_ref[1]], put)


def source_last_kernel(
    groups, members, size, hot_ref, row_hot_ref, sent_ref, own_ref, seg_ref, pressure_ref, kept_ref, perm_ref,
    out_ref, keep_ref, left_ref,
):
    pressure = pressure_ref[...]
    new_saturation, q, inv = cell_update(
        members,
        2,
        hot_ref,
        row_hot_ref,
        sent_ref,
        lambda o: (own_ref[o, 0:1, :], own_ref[o, 1:2, :]),
        lambda o: (seg_ref[o, 2:3, :], seg_ref[o, 3:4, :]),
        pressure,
        kept_ref[1],
        perm_ref[...],
        left_ref,
    )
    keep_ref[0] = new_saturation
    keep_ref[1] = q
    keep_ref[2] = inv
    send_halo(out_ref, q, inv, pressure, groups, members, size)


def owner_last_kernel(
    members, slot_ref, hot_ref, row_hot_ref, own_ref, seg_ref, frac_ref, aperture_ref, out_ref, left_ref
):
    new_frac, new_sat = owner_update(
        members,
        2,
        slot_ref,
        lambda s: (seg_ref[s, 0:1, :], seg_ref[s, 1:2, :]),
        lambda s: (own_ref[s, 2:3, :], own_ref[s, 3:4, :]),
        frac_ref[0],
        frac_ref[1],
        load_segs(aperture_ref),
        chain_ends(seg_ref, 4, members),
        hot_ref,
        row_hot_ref,
        left_ref,
    )
    store_segs(out_ref, 0, new_frac)
    store_segs(out_ref, 1, new_sat)


def final_kernel(groups, members, size, halo_ref, pressure_ref, kept_ref, out_ref, q_ext, inv_ext, p_ext):
    out_ref[0] = chebyshev(
        halo_ref, kept_ref[1], kept_ref[2], pressure_ref[...], q_ext, inv_ext, p_ext, groups, members, size
    )
    out_ref[1] = kept_ref[0]


VMEM = pl.BlockSpec(memory_space=pltpu.VMEM)
HBM = pl.BlockSpec(memory_space=pltpu.HBM)


def call(kernel, statics, outs, scratch, *args, spec=VMEM):
    outs = [o if hasattr(o, "dtype") else jax.ShapeDtypeStruct(o, F32) for o in outs]
    return pl.pallas_call(
        functools.partial(kernel, *statics),
        out_shape=outs,
        in_specs=[spec] * len(args),
        out_specs=[VMEM] * len(outs),
        scratch_shapes=scratch,
        compiler_params=pltpu.CompilerParams(vmem_limit_bytes=32 * 1024 * 1024),
        name=kernel.__name__,
    )(*args)


def on_device(
    matrix_state,
    matrix_perm,
    frac_state,
    frac_aperture,
    link_cell,
    link_seg,
    link_trans,
    link_count,
    link_upwind,
):
    groups, members = lax.axis_size("grp"), lax.axis_size("frac")
    devices = groups * members
    cells = link_cell[0, 0]
    width = cells.shape[1]
    _, rows, columns = matrix_state.shape
    seg_dev = frac_state.shape[2]
    seg_rows = seg_dev // LANES
    frac = frac_state.reshape(2, seg_rows, LANES)
    aperture = frac_aperture.reshape(seg_rows, LANES)

    every = members * width
    slots = (members, SUB, width)
    size = block_rows(columns, width)
    both = (groups, members, size)
    halo = (devices * size, 1, LANES)
    left_cell = pltpu.VMEM((3 * PARTS * rows, every), BF16)
    seg_wide = seg_dev // SEG_COLUMNS
    segs_wide = (2, seg_wide, SEG_COLUMNS)
    left_seg = pltpu.VMEM((3 * PARTS * seg_wide, every), BF16)
    ext = [pltpu.VMEM((rows + SUB, columns + LANES), F32)] * 3

    def to_group(x):
        return lax.all_to_all(x, "frac", split_axis=0, concat_axis=0, tiled=True)

    def to_all(x):
        return lax.all_to_all(x, ("grp", "frac"), split_axis=0, concat_axis=0, tiled=True)

    def hots(*sizes):
        return [jax.ShapeDtypeStruct((n, every), BF16) for n in sizes]

    sent, cell_hot, cell_row_hot = call(
        first_kernel,
        (members,),
        [(members, SUB + 2 * seg_wide, SEG_COLUMNS)] + hots(columns, rows),
        [
            pltpu.VMEM((members, width), jnp.int32),
            pltpu.VMEM((members, width), jnp.int32),
            pltpu.VMEM((members, width), F32),
            pltpu.SMEM((1, members), jnp.int32),
            pltpu.VMEM((ITERS, members, width), jnp.int32),
            pltpu.VMEM(matrix_state.shape, F32),
            pltpu.VMEM(frac.shape, F32),
            pltpu.SemaphoreType.DMA((7,)),
        ],
        *[
            pltpu.with_memory_space_constraint(x, pltpu.HBM)
            for x in (
                cells, link_seg[0, 0], link_trans[0, 0], link_count[0], link_upwind[:, 0, 0], matrix_state, frac
            )
        ],
        spec=HBM,
    )
    slot = to_group(sent)
    edge, kept, own, frac1, hot, row_hot = call(
        start_kernel,
        both,
        [halo, (4, rows, columns), (members, 2, width), segs_wide] + hots(SEG_COLUMNS, seg_wide),
        [left_seg, left_cell, pltpu.VMEM((members, 2, width), F32)],
        slot, sent, cell_hot, cell_row_hot, frac, aperture, matrix_state, matrix_perm,
    )
    before = to_all(edge)
    edge, kept = call(
        middle_kernel, both, [halo, (4, rows, columns)], [pltpu.VMEM((members, 2, width), F32), left_cell] + ext,
        before, cells, cell_hot, cell_row_hot, sent, kept, matrix_perm,
    )
    around = to_all(edge)
    own, frac2, pressure = call(
        exchange_kernel, both, [slots, segs_wide, (rows, columns)], [left_seg] + ext,
        around, cells, cell_hot, slot, hot, row_hot, before, own, frac1, aperture, kept,
    )
    segs = to_group(own)
    edge, kept = call(
        source_last_kernel, both, [halo, (3, rows, columns)], [left_cell],
        cell_hot, cell_row_hot, sent, own, segs, pressure, kept, matrix_perm,
    )
    around = to_all(edge)
    (frac3,) = call(
        owner_last_kernel, (members,), [frac.shape], [left_seg], slot, hot, row_hot, own, segs, frac2, aperture
    )
    (matrix_out,) = call(final_kernel, both, [matrix_state.shape], ext, around, pressure, kept)
    return matrix_out, frac3.reshape(frac_state.shape)


def solution(mesh):
    return jax.shard_map(
        on_device,
        mesh=mesh,
        in_specs=(
            P(None, "grp", "frac"),
            P("grp", "frac"),
            P(None, "grp", "frac"),
            P("grp", "frac"),
            P("grp", "frac", None, None),
            P("grp", "frac", None, None),
            P("grp", "frac", None, None),
            P("grp", "frac", None),
            P(None, "grp", "frac", None, None),
        ),
        out_specs=(P(None, "grp", "frac"), P(None, "grp", "frac")),
        check_vma=False,
    )
```

```python
import functools

import jax
import jax.numpy as jnp
from jax import lax
from jax.experimental import pallas as pl
from jax.experimental.pallas import tpu as pltpu
from jax.sharding import PartitionSpec as P

ITERS = 3
SWEEPS = 4

LOW_BOUND = 0.02
HIGH_BOUND = 1.98
TAU_STEP = 0.5
MOBILITY_FLOOR = 0.2

F32 = jnp.float32
BF16 = jnp.bfloat16
LANES = 128
SUB = 8
SEG_COLUMNS = 2 * LANES
DEPTH = SWEEPS - 1


def iota(shape, dim):
    return lax.broadcasted_iota(jnp.int32, shape, dim)


def parts_of(x):
    high = x.astype(BF16).astype(F32)
    return high, x - high


PARTS = 2


def table_of(fields):
    split = [parts_of(f) for f in fields]
    return jnp.concatenate([s[p] for p in range(PARTS) for s in split], axis=0).astype(BF16)


def one_hot(index_row, count):
    shape = (count, index_row.shape[1])
    hit = iota(shape, 0).astype(F32).astype(BF16) == index_row.astype(F32).astype(BF16)
    return jnp.where(hit, jnp.ones(shape, BF16), jnp.zeros(shape, BF16))


def pick(table, fields, rows, row_index, hot):
    wide = jnp.dot(table, hot, preferred_element_type=F32)
    hit = iota((rows, row_index.shape[1]), 0) == row_index
    found = []
    for f in range(fields):
        total = sum(wide[(p * fields + f) * rows : (p * fields + f + 1) * rows] for p in range(PARTS))
        found.append(jnp.sum(jnp.where(hit, total, 0.0), axis=0, keepdims=True))
    return found


def spread(left_ref, row_hot_ref, block, values):
    rows = row_hot_ref.shape[0]
    width = values[0].shape[1]
    at = slice(block * width, (block + 1) * width)
    hot = row_hot_ref[:, at]
    for f, value in enumerate(values):
        for p, part in enumerate(parts_of(value)):
            row = (p * len(values) + f) * rows
            left_ref[row : row + rows, at] = hot * part.astype(BF16)


def gathered_sum(left_ref, hot_ref, fields, rows):
    wide = lax.dot_general(
        left_ref[...], hot_ref[...], (((1,), (1,)), ((), ())), preferred_element_type=F32
    )
    return [
        sum(wide[(p * fields + f) * rows : (p * fields + f + 1) * rows] for p in range(PARTS))
        for f in range(fields)
    ]


def flow(trans, upwind, cell_p, cell_s, seg_p, seg_s):
    u = jnp.where(upwind > 0.5, cell_s, seg_s)
    weight = trans * (MOBILITY_FLOOR + u * u)
    water = weight * (cell_p - seg_p) * u
    return weight, water


def cell_parts(cell_row, columns):
    return cell_row // columns, cell_row % columns


def load_segs(ref, *lead):
    rows = ref.shape[-2] // 2
    return jnp.concatenate([ref[(*lead, pl.ds(h, rows, 2), slice(None))] for h in range(2)], axis=1)


def store_segs(ref, lead, value):
    rows = value.shape[0]
    for h in range(2):
        ref[lead, pl.ds(h, rows, 2), :] = value[:, h * LANES : (h + 1) * LANES]


def ends_of(frac):
    rows, columns = frac.shape
    lane = iota((1, columns), 1)
    return jnp.where(lane < columns // 2, frac[0:1], frac[rows - 1 : rows])


def frac_step(frac, sat, aperture, before, after, inflow, total, gained):
    rows, lanes = frac.shape
    row, lane = iota((rows, lanes), 0), iota((rows, lanes), 1)
    back = pltpu.roll(frac, 1, 1)
    left = jnp.where(lane == 0, pltpu.roll(back, 1, 0), back)
    left = jnp.where((lane == 0) & (row == 0), before, left)
    ahead = pltpu.roll(frac, lanes - 1, 1)
    right = jnp.where(lane == lanes - 1, pltpu.roll(ahead, rows - 1, 0), ahead)
    right = jnp.where((lane == lanes - 1) & (row == rows - 1), after, right)
    new_frac = (aperture * frac + inflow + left + right) / (aperture + total + 2.0)
    new_sat = sat + TAU_STEP * gained / (aperture + total)
    return new_frac, new_sat


def chain_ends(ends_ref, row, members):
    me = lax.axis_index("frac")
    lanes = ends_ref.shape[2]
    prior = ends_ref[jnp.maximum(me - 1, 0), row : row + 1, :]
    later = ends_ref[jnp.minimum(me + 1, members - 1), row : row + 1, :]
    before = jnp.where(me > 0, prior[:, lanes - 1 :], 0.0)
    after = jnp.where(me < members - 1, later[:, 0:1], 0.0)
    return before, after


def partial_residual(pressure, couple, source, inverse):
    rows, columns = pressure.shape
    row, col = iota((rows, columns), 0), iota((rows, columns), 1)
    beside = jnp.where(row == 0, 0.0, pltpu.roll(pressure, 1, 0))
    beside += jnp.where(row == rows - 1, 0.0, pltpu.roll(pressure, rows - 1, 0))
    beside += jnp.where(col == 0, 0.0, pltpu.roll(pressure, 1, 1))
    beside += jnp.where(col == columns - 1, 0.0, pltpu.roll(pressure, columns - 1, 1))
    return inverse * (source - (4.0 + couple) * pressure + beside)


def pack_low(q, inv, p, at, axis):
    return jnp.where(
        at < DEPTH, q, jnp.where(at < 2 * DEPTH, pltpu.roll(inv, DEPTH, axis), pltpu.roll(p, 2 * DEPTH, axis))
    )


def pack_high(q, inv, p, at, axis):
    size = q.shape[axis]
    return jnp.where(
        at >= size - DEPTH,
        q,
        jnp.where(
            at >= size - 2 * DEPTH,
            pltpu.roll(inv, size - DEPTH, axis),
            pltpu.roll(p, size - 2 * DEPTH, axis),
        ),
    )


def block_rows(columns, width):
    vertical = 2 * DEPTH * (columns // LANES) + 1
    lateral = SUB + 2 * (width // LANES) + 1
    return max(vertical, lateral)


def put_rows(out_ref, at, values):
    for k in range(values.shape[0]):
        out_ref[at + k] = values[k : k + 1]


def get_rows(in_ref, at, count):
    return jnp.concatenate([in_ref[at + k] for k in range(count)], axis=0)


def send_slots(out_ref, at, first, second):
    halves = first.shape[1] // LANES
    for i, value in enumerate((first, second)):
        for h in range(halves):
            out_ref[at + SUB + i * halves + h] = value[:, h * LANES : (h + 1) * LANES]


def got_slots(in_ref, at, width):
    halves = width // LANES
    return [
        jnp.concatenate([in_ref[at + SUB + i * halves + h] for h in range(halves)], axis=1) for i in range(2)
    ]


def send_halo(out_ref, q, inv, p, groups, members, size):
    rows, columns = q.shape
    halves = columns // LANES
    g, f = lax.axis_index("grp"), lax.axis_index("frac")
    here = g * members + f
    lane = iota((rows, LANES), 1)
    low = pack_low(q[:, :LANES], inv[:, :LANES], p[:, :LANES], lane, 1)
    high = pack_high(q[:, columns - LANES :], inv[:, columns - LANES :], p[:, columns - LANES :], lane, 1)
    turned = jnp.transpose(jnp.where(lane < LANES // 2, low, high))
    left, right = turned[:SUB], turned[LANES - SUB :]
    lane = iota((1, LANES), 1)

    for step in (-1, 1):
        layer = (lambda k: k) if step < 0 else (lambda k: rows - 1 - k)

        def span(field, count, at):
            start = 0 if step < 0 else rows - count
            return field[start : start + count, at]

        inside = (g + step >= 0) & (g + step < groups)
        base = here + step * members
        tiles = [slice(h * LANES, (h + 1) * LANES) for h in range(halves)]

        @pl.when(inside)
        def _():
            at = base * size
            for h, tile in enumerate(tiles):
                put_rows(out_ref, at + h * DEPTH, span(q, DEPTH, tile))
                put_rows(out_ref, at + halves * DEPTH + h * (DEPTH - 1), span(inv, DEPTH - 1, tile))
                put_rows(out_ref, at + halves * (2 * DEPTH - 1) + h, span(p, 1, tile))
            deep, next_p = layer(DEPTH - 1), layer(1)
            extra = jnp.where(
                lane == 0,
                inv[deep : deep + 1, tiles[0]],
                jnp.where(
                    lane == LANES - 1,
                    inv[deep : deep + 1, tiles[-1]],
                    jnp.where(
                        lane == 1,
                        pltpu.roll(p[next_p : next_p + 1, tiles[0]], 1, 1),
                        pltpu.roll(p[next_p : next_p + 1, tiles[-1]], LANES - 1, 1),
                    ),
                ),
            )
            out_ref[at + halves * 2 * DEPTH] = extra

        for side, tile, there in ((-1, tiles[0], f > 0), (1, tiles[-1], f < members - 1)):

            @pl.when(inside & there)
            def _(side=side, tile=tile):
                at = (base + side) * size
                for i, field in enumerate((q, inv, p)):
                    put_rows(out_ref, at + i * DEPTH, span(field, DEPTH, tile))

    @pl.when(f > 0)
    def _():
        put_rows(out_ref, (here - 1) * size, left)

    @pl.when(f < members - 1)
    def _():
        put_rows(out_ref, (here + 1) * size, right)


def chebyshev(in_ref, q_ref, inv_ref, p_ref, target, scratch, groups, members, size):
    q_ext, inv_ext, p_ext, update_ref, even_ref, odd_ref = scratch
    rows, columns = target.shape
    halves = columns // LANES
    side = halves
    g, f = lax.axis_index("grp"), lax.axis_index("frac")
    here = g * members + f
    last = groups * members - 1

    def taker(dg, df):
        ok = (g + dg >= 0) & (g + dg < groups) & (f + df >= 0) & (f + df < members)
        at = jnp.clip(here + dg * members + df, 0, last) * size
        return lambda start, count: jnp.where(ok, get_rows(in_ref, at + start, count), 0.0)

    def both(low, high, at, count, size):
        return jnp.where(at < count, low, jnp.where(at >= size - count, high, 0.0))

    def filler(count):
        return jnp.zeros((count, LANES), F32)

    for h in range(halves):
        for ext, ref in ((q_ext, q_ref), (inv_ext, inv_ref), (p_ext, p_ref)):
            ext[h, 0:rows, :] = ref[:, h * LANES : (h + 1) * LANES]
    outer = slice(rows, rows + SUB)
    below, above = taker(1, 0), taker(-1, 0)
    lane = iota((1, LANES), 1)
    low_extra, high_extra = below(halves * 2 * DEPTH, 1), above(halves * 2 * DEPTH, 1)
    for h in range(halves):
        edge = (lane == 0) & (h == 0) | (lane == LANES - 1) & (h == halves - 1)

        def at_edge(row, turn):
            return jnp.where(edge, pltpu.roll(row, turn, 1) if turn else row, 0.0)

        turn = LANES - 1 if h == 0 else 1
        at = h * DEPTH
        q_ext[h, outer, :] = jnp.concatenate(
            [below(at, DEPTH), filler(SUB - 2 * DEPTH), above(at, DEPTH)], axis=0
        )
        at = halves * DEPTH + h * (DEPTH - 1)
        inv_ext[h, outer, :] = jnp.concatenate(
            [
                below(at, DEPTH - 1),
                at_edge(low_extra, 0),
                filler(SUB - 2 * DEPTH),
                at_edge(high_extra, 0),
                above(at, DEPTH - 1),
            ],
            axis=0,
        )
        at = halves * (2 * DEPTH - 1) + h
        p_ext[h, outer, :] = jnp.concatenate(
            [
                below(at, 1),
                at_edge(low_extra, turn),
                filler(SUB - 4),
                at_edge(high_extra, turn),
                above(at, 1),
            ],
            axis=0,
        )
    right, left = taker(0, 1)(0, SUB), taker(0, -1)(0, SUB)
    turned = jnp.transpose(
        jnp.concatenate([right, jnp.zeros((LANES - 2 * SUB, rows), F32), left], axis=0)
    )
    lane = iota((rows, LANES), 1)
    q_ext[side, 0:rows, :] = both(turned, turned, lane, DEPTH, LANES)
    inv_ext[side, 0:rows, :] = both(
        pltpu.roll(turned, LANES - DEPTH, 1), pltpu.roll(turned, DEPTH, 1), lane, DEPTH, LANES
    )
    p_ext[side, 0:rows, :] = both(
        pltpu.roll(turned, LANES - 2 * DEPTH, 1), pltpu.roll(turned, 2 * DEPTH, 1), lane, 2, LANES
    )
    lane = iota((DEPTH, LANES), 1)
    low_right, low_left, high_right, high_left = taker(1, 1), taker(1, -1), taker(-1, 1), taker(-1, -1)
    for i, ext in enumerate((q_ext, inv_ext, p_ext)):
        at = i * DEPTH
        ext[side, outer, :] = jnp.concatenate(
            [
                both(low_right(at, DEPTH), low_left(at, DEPTH), lane, DEPTH, LANES),
                filler(SUB - 2 * DEPTH),
                both(high_right(at, DEPTH), high_left(at, DEPTH), lane, DEPTH, LANES),
            ],
            axis=0,
        )

    end = rows + SUB - 1
    for own, other in ((0, end), (end, 0), (rows - 1, rows), (rows, rows - 1)):
        for c in range(halves + 1):
            q_ext[c, own : own + 1, :] += inv_ext[c, own : own + 1, :] * p_ext[c, other : other + 1, :]
    centre = 0.5 * (HIGH_BOUND + LOW_BOUND)
    half_width = 0.5 * (HIGH_BOUND - LOW_BOUND)
    scale_ratio = centre / half_width
    ratio_now = 1.0 / scale_ratio
    lane = iota((SUB, LANES), 1)
    count = rows // SUB + 1

    def keep(ref, c, r, value):
        at = (r + 1) * SUB
        ref[c, at : at + SUB, :] = value
        if r == count - 1:
            ref[c, 0:SUB, :] = value
        if r == 0:
            at = (count + 1) * SUB
            ref[c, at : at + SUB, :] = value

    for r in range(count):
        at = slice(r * SUB, (r + 1) * SUB)
        p_side, p_first, p_final = p_ext[side, at, :], p_ext[0, at, :], p_ext[halves - 1, at, :]
        missing = [0.0] * (halves + 1)
        missing[0] += jnp.where(lane == 0, pltpu.roll(p_side, 1, 1), 0.0)
        missing[halves - 1] += jnp.where(lane == LANES - 1, pltpu.roll(p_side, LANES - 1, 1), 0.0)
        missing[side] = jnp.where(
            lane == 0,
            pltpu.roll(p_final, 1, 1),
            jnp.where(lane == LANES - 1, pltpu.roll(p_first, LANES - 1, 1), 0.0),
        )
        for c in range(halves + 1):
            start = q_ext[c, at, :] + inv_ext[c, at, :] * missing[c]
            q_ext[c, at, :] = start
            keep(even_ref, c, r, start / centre if centre != 1.0 else start)
    now_ref, next_ref = even_ref, odd_ref
    for sweep in range(1, SWEEPS):
        ratio_next = 1.0 / (2.0 * scale_ratio - ratio_now)
        final = sweep == SWEEPS - 1
        for r in range(count - 1 if final else count):
            at = slice(r * SUB, (r + 1) * SUB)
            mids = [now_ref[c, (r + 1) * SUB : (r + 2) * SUB, :] for c in range(halves + 1)]
            after = [pltpu.roll(m, 1, 1) for m in mids]
            ahead = [pltpu.roll(m, LANES - 1, 1) for m in mids]
            for c in range(halves if final else halves + 1):
                beside = now_ref[c, (r + 1) * SUB - 1 : (r + 2) * SUB - 1, :]
                beside += now_ref[c, (r + 1) * SUB + 1 : (r + 2) * SUB + 1, :]
                beside += jnp.where(lane == 0, after[(c - 1) % (halves + 1)], after[c])
                beside += jnp.where(lane == LANES - 1, ahead[(c + 1) % (halves + 1)], ahead[c])
                residual = q_ext[c, at, :] - mids[c] + inv_ext[c, at, :] * beside
                old = mids[c] if sweep == 1 else update_ref[c, at, :]
                update = ratio_next * ratio_now * old + (2.0 * ratio_next / half_width) * residual
                if final:
                    tile = slice(c * LANES, (c + 1) * LANES)
                    target[at, tile] = p_ref[at, tile] + mids[c] + update
                else:
                    update_ref[c, at, :] = update
                    keep(next_ref, c, r, mids[c] + update)
        ratio_now = ratio_next
        now_ref, next_ref = next_ref, now_ref


ROW_SEG = 0
ROW_TRANS = 1
ROW_UP = 2
ROW_P = ROW_UP + ITERS
ROW_S = ROW_P + 1
ROW_ENDS = ROW_S + 1


def first_kernel(
    members, cell_any, seg_any, trans_any, count_any, up_any, state_any, frac_any,
    out_ref, hot_ref, row_hot_ref, cell_ref, seg_ref, trans_ref, count_ref, up_ref, state_ref, frac_ref, sem,
):
    _, rows, columns = state_ref.shape
    width = cell_ref.shape[1]
    copies = [
        pltpu.make_async_copy(source, target, sem.at[i])
        for i, (source, target) in enumerate(
            [
                (cell_any, cell_ref),
                (state_any, state_ref),
                (seg_any, seg_ref),
                (trans_any, trans_ref),
                (count_any, count_ref),
                (up_any, up_ref),
                (frac_any, frac_ref),
            ]
        )
    ]
    for copy in copies:
        copy.start()
    copies[0].wait()
    for o in range(members):
        row, col = cell_parts(cell_ref[o : o + 1, :], columns)
        at = slice(o * width, (o + 1) * width)
        hot_ref[:, at] = one_hot(col, columns)
        row_hot_ref[:, at] = one_hot(row, rows)
    copies[1].wait()
    table = table_of([state_ref[0], state_ref[1]])
    for copy in copies[2:]:
        copy.wait()
    frac = load_segs(frac_ref, 0)
    ends = ends_of(frac)
    whole = jnp.concatenate([frac, load_segs(frac_ref, 1)], axis=0)
    for o in range(members):
        one = slice(o, o + 1)
        row, _ = cell_parts(cell_ref[one, :], columns)
        cell_p, cell_s = pick(table, 2, rows, row, hot_ref[:, o * width : (o + 1) * width])
        live = iota((1, width), 1) < count_ref[0, o]
        out_ref[o, ROW_SEG : ROW_SEG + 1, :] = seg_ref[one, :].astype(F32)
        out_ref[o, ROW_TRANS : ROW_TRANS + 1, :] = jnp.where(live, trans_ref[one, :], 0.0)
        for t in range(ITERS):
            out_ref[o, ROW_UP + t : ROW_UP + t + 1, :] = up_ref[t, one, :].astype(F32)
        out_ref[o, ROW_P : ROW_P + 1, :] = cell_p
        out_ref[o, ROW_S : ROW_S + 1, :] = cell_s
        out_ref[o, ROW_ENDS : ROW_ENDS + 1, :] = ends
        out_ref[o, SUB:, :] = whole


def seg_parts(slot_ref, s):
    seg = slot_ref[s, ROW_SEG : ROW_SEG + 1, :].astype(jnp.int32)
    return seg // SEG_COLUMNS, seg % SEG_COLUMNS


def seg_hots(slot_ref, hot_ref, row_hot_ref, members, width):
    for s in range(members):
        row, lane = seg_parts(slot_ref, s)
        at = slice(s * width, (s + 1) * width)
        hot_ref[:, at] = one_hot(lane, SEG_COLUMNS)
        row_hot_ref[:, at] = one_hot(row, row_hot_ref.shape[0])


def seg_gather(slot_ref, hot_ref, fields, s, width, table):
    return pick(table, 2, fields, seg_parts(slot_ref, s)[0], hot_ref[:, s * width : (s + 1) * width])


def cell_update(
    members, t, hot_ref, row_hot_ref, sent_ref, cell_rows, seg_rows, pressure, saturation, perm, left_ref
):
    rows = pressure.shape[0]
    for o in range(members):
        seg_p, seg_s = seg_rows(o)
        cell_p, cell_s = cell_rows(o)
        weight, water = flow(
            sent_ref[o, ROW_TRANS : ROW_TRANS + 1, :],
            sent_ref[o, ROW_UP + t : ROW_UP + t + 1, :],
            cell_p,
            cell_s,
            seg_p,
            seg_s,
        )
        spread(left_ref, row_hot_ref, o, [weight, weight * seg_p, water])
    couple, source, lost = gathered_sum(left_ref, hot_ref, 3, rows)
    inverse = 1.0 / (4.0 + perm + couple)
    new_saturation = saturation - TAU_STEP * lost / (perm + couple)
    return new_saturation, partial_residual(pressure, couple, source, inverse), inverse


def start_kernel(
    groups, members, size, slot_ref, sent_ref, cell_hot_ref, cell_row_hot_ref, frac_ref, aperture_ref,
    state_ref, perm_ref, out_ref, keep_ref, own_ref, new_ref, hot_ref, row_hot_ref,
    left_seg_ref, left_ref, found_ref,
):
    width = slot_ref.shape[2]
    rows = new_ref.shape[1]
    g = lax.axis_index("grp")
    frac, sat = load_segs(frac_ref, 0), load_segs(frac_ref, 1)
    seg_hots(slot_ref, hot_ref, row_hot_ref, members, width)
    table = table_of([frac, sat])
    for s in range(members):
        seg_p, seg_s = seg_gather(slot_ref, hot_ref, rows, s, width, table)
        cell_p = slot_ref[s, ROW_P : ROW_P + 1, :]
        weight, water = flow(
            slot_ref[s, ROW_TRANS : ROW_TRANS + 1, :],
            slot_ref[s, ROW_UP : ROW_UP + 1, :],
            cell_p,
            slot_ref[s, ROW_S : ROW_S + 1, :],
            seg_p,
            seg_s,
        )
        spread(left_seg_ref, row_hot_ref, s, [weight * cell_p, weight, water])
    inflow, total, gained = gathered_sum(left_seg_ref, hot_ref, 3, rows)
    before, after = chain_ends(slot_ref, ROW_ENDS, members)
    new_frac, new_sat = frac_step(frac, sat, load_segs(aperture_ref), before, after, inflow, total, gained)
    new_ref[0] = new_frac
    new_ref[1] = new_sat
    table = table_of([new_frac, new_sat])
    ends = ends_of(new_frac)
    ends = jnp.where(iota((1, LANES), 1) < LANES // 2, ends[:, :LANES], ends[:, SEG_COLUMNS - LANES :])
    for s in range(members):
        seg_p, seg_s = seg_gather(slot_ref, hot_ref, rows, s, width, table)
        own_ref[s, 0:1, :] = seg_p
        own_ref[s, 1:2, :] = seg_s
        at = (g * members + s) * size
        send_slots(out_ref, at, seg_p, seg_s)
        out_ref[at + size - 1] = ends
    for o in range(members):
        row, lane = seg_parts(sent_ref, o)
        table = table_of([slot_ref[o, SUB : SUB + rows, :], slot_ref[o, SUB + rows :, :]])
        seg_p, seg_s = pick(table, 2, rows, row, one_hot(lane, SEG_COLUMNS))
        found_ref[o, 0:1, :] = seg_p
        found_ref[o, 1:2, :] = seg_s
    pressure = state_ref[0]
    new_saturation, q, inv = cell_update(
        members,
        0,
        cell_hot_ref,
        cell_row_hot_ref,
        sent_ref,
        lambda o: (sent_ref[o, ROW_P : ROW_P + 1, :], sent_ref[o, ROW_S : ROW_S + 1, :]),
        lambda o: (found_ref[o, 0:1, :], found_ref[o, 1:2, :]),
        pressure,
        state_ref[1],
        perm_ref[...],
        left_ref,
    )
    keep_ref[0] = pressure
    keep_ref[1] = new_saturation
    keep_ref[2] = q
    keep_ref[3] = inv
    send_halo(out_ref, q, inv, pressure, groups, members, size)


def cell_gather(members, cell_ref, hot_ref, fields, put):
    rows, columns = fields[0].shape
    width = cell_ref.shape[1]
    table = table_of(fields)
    for o in range(members):
        row, _ = cell_parts(cell_ref[o : o + 1, :], columns)
        put(o, *pick(table, len(fields), rows, row, hot_ref[:, o * width : (o + 1) * width]))


def middle_kernel(
    groups, members, size, halo_ref, cell_ref, hot_ref, row_hot_ref, sent_ref, kept_ref, perm_ref,
    out_ref, keep_ref, slots_ref, left_ref, *scratch,
):
    chebyshev(
        halo_ref, kept_ref.at[2], kept_ref.at[3], kept_ref.at[0], keep_ref.at[0], scratch, groups, members, size
    )
    pressure = keep_ref[0]
    saturation = kept_ref[1]
    g = lax.axis_index("grp")

    def put(o, cell_p, cell_s):
        slots_ref[o, 0:1, :] = cell_p
        slots_ref[o, 1:2, :] = cell_s
        send_slots(out_ref, (g * members + o) * size, cell_p, cell_s)

    cell_gather(members, cell_ref, hot_ref, [pressure, saturation], put)
    new_saturation, q, inv = cell_update(
        members,
        1,
        hot_ref,
        row_hot_ref,
        sent_ref,
        lambda o: (slots_ref[o, 0:1, :], slots_ref[o, 1:2, :]),
        lambda o: got_slots(halo_ref, (g * members + o) * size, cell_ref.shape[1]),
        pressure,
        saturation,
        perm_ref[...],
        left_ref,
    )
    keep_ref[1] = new_saturation
    keep_ref[2] = q
    keep_ref[3] = inv
    send_halo(out_ref, q, inv, pressure, groups, members, size)


def owner_update(
    members, t, slot_ref, cell_rows, seg_rows, frac, sat, aperture, ends, hot_ref, row_hot_ref, left_ref
):
    rows = frac.shape[0]
    for s in range(members):
        cell_p, cell_s = cell_rows(s)
        weight, water = flow(
            slot_ref[s, ROW_TRANS : ROW_TRANS + 1, :],
            slot_ref[s, ROW_UP + t : ROW_UP + t + 1, :],
            cell_p,
            cell_s,
            *seg_rows(s),
        )
        spread(left_ref, row_hot_ref, s, [weight * cell_p, weight, water])
    inflow, total, gained = gathered_sum(left_ref, hot_ref, 3, rows)
    return frac_step(frac, sat, aperture, *ends, inflow, total, gained)


def exchange_kernel(
    groups, members, size, halo_ref, cell_ref, cell_hot_ref, slot_ref, hot_ref, row_hot_ref, ends_ref, own_ref,
    frac_ref, aperture_ref, kept_ref, out_ref, new_ref, pressure_ref, left_ref, *scratch,
):
    width = slot_ref.shape[2]
    rows = frac_ref.shape[1]
    g = lax.axis_index("grp")

    def cell_rows(s):
        return got_slots(halo_ref, (g * members + s) * size, width)

    me = lax.axis_index("frac")
    prior = ends_ref[(g * members + jnp.maximum(me - 1, 0)) * size + size - 1]
    later = ends_ref[(g * members + jnp.minimum(me + 1, members - 1)) * size + size - 1]
    before = jnp.where(me > 0, prior[:, LANES - 1 :], 0.0)
    after = jnp.where(me < members - 1, later[:, 0:1], 0.0)

    new_frac, new_sat = owner_update(
        members,
        1,
        slot_ref,
        cell_rows,
        lambda s: (own_ref[s, 0:1, :], own_ref[s, 1:2, :]),
        frac_ref[0],
        frac_ref[1],
        load_segs(aperture_ref),
        (before, after),
        hot_ref,
        row_hot_ref,
        left_ref,
    )
    new_ref[0] = new_frac
    new_ref[1] = new_sat
    table = table_of([new_frac, new_sat])
    ends = ends_of(new_frac)
    for s in range(members):
        seg_p, seg_s = seg_gather(slot_ref, hot_ref, rows, s, width, table)
        out_ref[s, 2:3, :] = seg_p
        out_ref[s, 3:4, :] = seg_s
        out_ref[s, 4:5, :] = ends

    chebyshev(
        halo_ref, kept_ref.at[2], kept_ref.at[3], kept_ref.at[0], pressure_ref, scratch, groups, members, size
    )
    pressure = pressure_ref[...]

    def put(o, cell_p, cell_s):
        out_ref[o, 0:1, :] = cell_p
        out_ref[o, 1:2, :] = cell_s

    cell_gather(members, cell_ref, cell_hot_ref, [pressure, kept_ref[1]], put)


def source_last_kernel(
    groups, members, size, hot_ref, row_hot_ref, sent_ref, own_ref, seg_ref, pressure_ref, kept_ref, perm_ref,
    out_ref, keep_ref, left_ref,
):
    pressure = pressure_ref[...]
    new_saturation, q, inv = cell_update(
        members,
        2,
        hot_ref,
        row_hot_ref,
        sent_ref,
        lambda o: (own_ref[o, 0:1, :], own_ref[o, 1:2, :]),
        lambda o: (seg_ref[o, 2:3, :], seg_ref[o, 3:4, :]),
        pressure,
        kept_ref[1],
        perm_ref[...],
        left_ref,
    )
    keep_ref[0] = new_saturation
    keep_ref[1] = q
    keep_ref[2] = inv
    send_halo(out_ref, q, inv, pressure, groups, members, size)


def owner_last_kernel(
    members, slot_ref, hot_ref, row_hot_ref, own_ref, seg_ref, frac_ref, aperture_ref, out_ref, left_ref
):
    new_frac, new_sat = owner_update(
        members,
        2,
        slot_ref,
        lambda s: (seg_ref[s, 0:1, :], seg_ref[s, 1:2, :]),
        lambda s: (own_ref[s, 2:3, :], own_ref[s, 3:4, :]),
        frac_ref[0],
        frac_ref[1],
        load_segs(aperture_ref),
        chain_ends(seg_ref, 4, members),
        hot_ref,
        row_hot_ref,
        left_ref,
    )
    store_segs(out_ref, 0, new_frac)
    store_segs(out_ref, 1, new_sat)


def final_kernel(groups, members, size, halo_ref, pressure_ref, kept_ref, out_ref, *scratch):
    chebyshev(
        halo_ref, kept_ref.at[1], kept_ref.at[2], pressure_ref, out_ref.at[0], scratch, groups, members, size
    )
    out_ref[1] = kept_ref[0]


VMEM = pl.BlockSpec(memory_space=pltpu.VMEM)
HBM = pl.BlockSpec(memory_space=pltpu.HBM)


def call(kernel, statics, outs, scratch, *args, spec=VMEM):
    outs = [o if hasattr(o, "dtype") else jax.ShapeDtypeStruct(o, F32) for o in outs]
    return pl.pallas_call(
        functools.partial(kernel, *statics),
        out_shape=outs,
        in_specs=[spec] * len(args),
        out_specs=[VMEM] * len(outs),
        scratch_shapes=scratch,
        compiler_params=pltpu.CompilerParams(vmem_limit_bytes=32 * 1024 * 1024),
        name=kernel.__name__,
    )(*args)


def on_device(
    matrix_state,
    matrix_perm,
    frac_state,
    frac_aperture,
    link_cell,
    link_seg,
    link_trans,
    link_count,
    link_upwind,
):
    groups, members = lax.axis_size("grp"), lax.axis_size("frac")
    devices = groups * members
    cells = link_cell[0, 0]
    width = cells.shape[1]
    _, rows, columns = matrix_state.shape
    seg_dev = frac_state.shape[2]
    seg_rows = seg_dev // LANES
    frac = frac_state.reshape(2, seg_rows, LANES)
    aperture = frac_aperture.reshape(seg_rows, LANES)

    every = members * width
    slots = (members, SUB, width)
    size = block_rows(columns, width)
    both = (groups, members, size)
    halo = (devices * size, 1, LANES)
    left_cell = pltpu.VMEM((3 * PARTS * rows, every), BF16)
    seg_wide = seg_dev // SEG_COLUMNS
    segs_wide = (2, seg_wide, SEG_COLUMNS)
    left_seg = pltpu.VMEM((3 * PARTS * seg_wide, every), BF16)
    tiles = columns // LANES + 1
    ext = [pltpu.VMEM((tiles, rows + SUB, LANES), F32)] * 4 + [pltpu.VMEM((tiles, rows + 3 * SUB, LANES), F32)] * 2

    def to_group(x):
        return lax.all_to_all(x, "frac", split_axis=0, concat_axis=0, tiled=True)

    def to_all(x):
        return lax.all_to_all(x, ("grp", "frac"), split_axis=0, concat_axis=0, tiled=True)

    def hots(*sizes):
        return [jax.ShapeDtypeStruct((n, every), BF16) for n in sizes]

    sent, cell_hot, cell_row_hot = call(
        first_kernel,
        (members,),
        [(members, SUB + 2 * seg_wide, SEG_COLUMNS)] + hots(columns, rows),
        [
            pltpu.VMEM((members, width), jnp.int32),
            pltpu.VMEM((members, width), jnp.int32),
            pltpu.VMEM((members, width), F32),
            pltpu.SMEM((1, members), jnp.int32),
            pltpu.VMEM((ITERS, members, width), jnp.int32),
            pltpu.VMEM(matrix_state.shape, F32),
            pltpu.VMEM(frac.shape, F32),
            pltpu.SemaphoreType.DMA((7,)),
        ],
        *[
            pltpu.with_memory_space_constraint(x, pltpu.HBM)
            for x in (
                cells, link_seg[0, 0], link_trans[0, 0], link_count[0], link_upwind[:, 0, 0], matrix_state, frac
            )
        ],
        spec=HBM,
    )
    slot = to_group(sent)
    edge, kept, own, frac1, hot, row_hot = call(
        start_kernel,
        both,
        [halo, (4, rows, columns), (members, 2, width), segs_wide] + hots(SEG_COLUMNS, seg_wide),
        [left_seg, left_cell, pltpu.VMEM((members, 2, width), F32)],
        slot, sent, cell_hot, cell_row_hot, frac, aperture, matrix_state, matrix_perm,
    )
    before = to_all(edge)
    edge, kept = call(
        middle_kernel, both, [halo, (4, rows, columns)], [pltpu.VMEM((members, 2, width), F32), left_cell] + ext,
        before, cells, cell_hot, cell_row_hot, sent, kept, matrix_perm,
    )
    around = to_all(edge)
    own, frac2, pressure = call(
        exchange_kernel, both, [slots, segs_wide, (rows, columns)], [left_seg] + ext,
        around, cells, cell_hot, slot, hot, row_hot, before, own, frac1, aperture, kept,
    )
    segs = to_group(own)
    edge, kept = call(
        source_last_kernel, both, [halo, (3, rows, columns)], [left_cell],
        cell_hot, cell_row_hot, sent, own, segs, pressure, kept, matrix_perm,
    )
    around = to_all(edge)
    (frac3,) = call(
        owner_last_kernel, (members,), [frac.shape], [left_seg], slot, hot, row_hot, own, segs, frac2, aperture
    )
    (matrix_out,) = call(final_kernel, both, [matrix_state.shape], ext, around, pressure, kept)
    return matrix_out, frac3.reshape(frac_state.shape)


def solution(mesh):
    return jax.shard_map(
        on_device,
        mesh=mesh,
        in_specs=(
            P(None, "grp", "frac"),
            P("grp", "frac"),
            P(None, "grp", "frac"),
            P("grp", "frac"),
            P("grp", "frac", None, None),
            P("grp", "frac", None, None),
            P("grp", "frac", None, None),
            P("grp", "frac", None),
            P(None, "grp", "frac", None, None),
        ),
        out_specs=(P(None, "grp", "frac"), P(None, "grp", "frac")),
        check_vma=False,
    )
```

```python
import functools

import jax
import jax.numpy as jnp
from jax import lax
from jax.experimental import pallas as pl
from jax.experimental.pallas import tpu as pltpu
from jax.sharding import PartitionSpec as P

ITERS = 3
SWEEPS = 4

LOW_BOUND = 0.02
HIGH_BOUND = 1.98
TAU_STEP = 0.5
MOBILITY_FLOOR = 0.2

F32 = jnp.float32
BF16 = jnp.bfloat16
LANES = 128
SUB = 8
SEG_COLUMNS = 2 * LANES
DEPTH = SWEEPS - 1


def iota(shape, dim):
    return lax.broadcasted_iota(jnp.int32, shape, dim)


def parts_of(x):
    high = x.astype(BF16).astype(F32)
    return high, x - high


PARTS = 2


def table_of(fields):
    split = [parts_of(f) for f in fields]
    return jnp.concatenate([s[p] for p in range(PARTS) for s in split], axis=0).astype(BF16)


def one_hot(index_row, count):
    shape = (count, index_row.shape[1])
    hit = iota(shape, 0).astype(F32).astype(BF16) == index_row.astype(F32).astype(BF16)
    return jnp.where(hit, jnp.ones(shape, BF16), jnp.zeros(shape, BF16))


def pick(table, fields, rows, row_index, hot):
    wide = jnp.dot(table, hot, preferred_element_type=F32)
    hit = iota((rows, row_index.shape[1]), 0) == row_index
    found = []
    for f in range(fields):
        total = sum(wide[(p * fields + f) * rows : (p * fields + f + 1) * rows] for p in range(PARTS))
        found.append(jnp.sum(jnp.where(hit, total, 0.0), axis=0, keepdims=True))
    return found


def spread(left_ref, row_hot_ref, block, values):
    rows = row_hot_ref.shape[0]
    width = values[0].shape[1]
    at = slice(block * width, (block + 1) * width)
    hot = row_hot_ref[:, at]
    for f, value in enumerate(values):
        for p, part in enumerate(parts_of(value)):
            row = (p * len(values) + f) * rows
            left_ref[row : row + rows, at] = hot * part.astype(BF16)


def gathered_sum(left_ref, hot_ref, fields, rows):
    wide = lax.dot_general(
        left_ref[...], hot_ref[...], (((1,), (1,)), ((), ())), preferred_element_type=F32
    )
    return [
        sum(wide[(p * fields + f) * rows : (p * fields + f + 1) * rows] for p in range(PARTS))
        for f in range(fields)
    ]


def flow(trans, upwind, cell_p, cell_s, seg_p, seg_s):
    u = jnp.where(upwind > 0.5, cell_s, seg_s)
    weight = trans * (MOBILITY_FLOOR + u * u)
    water = weight * (cell_p - seg_p) * u
    return weight, water


def cell_parts(cell_row, columns):
    return cell_row // columns, cell_row % columns


def load_segs(ref, *lead):
    rows = ref.shape[-2] // 2
    return jnp.concatenate([ref[(*lead, pl.ds(h, rows, 2), slice(None))] for h in range(2)], axis=1)


def store_segs(ref, lead, value):
    rows = value.shape[0]
    for h in range(2):
        ref[lead, pl.ds(h, rows, 2), :] = value[:, h * LANES : (h + 1) * LANES]


def ends_of(frac):
    rows, columns = frac.shape
    lane = iota((1, columns), 1)
    return jnp.where(lane < columns // 2, frac[0:1], frac[rows - 1 : rows])


def frac_step(frac, sat, aperture, before, after, inflow, total, gained):
    rows, lanes = frac.shape
    row, lane = iota((rows, lanes), 0), iota((rows, lanes), 1)
    back = pltpu.roll(frac, 1, 1)
    left = jnp.where(lane == 0, pltpu.roll(back, 1, 0), back)
    left = jnp.where((lane == 0) & (row == 0), before, left)
    ahead = pltpu.roll(frac, lanes - 1, 1)
    right = jnp.where(lane == lanes - 1, pltpu.roll(ahead, rows - 1, 0), ahead)
    right = jnp.where((lane == lanes - 1) & (row == rows - 1), after, right)
    new_frac = (aperture * frac + inflow + left + right) / (aperture + total + 2.0)
    new_sat = sat + TAU_STEP * gained / (aperture + total)
    return new_frac, new_sat


def chain_ends(ends_ref, row, members):
    me = lax.axis_index("frac")
    lanes = ends_ref.shape[2]
    prior = ends_ref[jnp.maximum(me - 1, 0), row : row + 1, :]
    later = ends_ref[jnp.minimum(me + 1, members - 1), row : row + 1, :]
    before = jnp.where(me > 0, prior[:, lanes - 1 :], 0.0)
    after = jnp.where(me < members - 1, later[:, 0:1], 0.0)
    return before, after


def partial_residual(pressure, couple, source, inverse):
    rows, columns = pressure.shape
    row, col = iota((rows, columns), 0), iota((rows, columns), 1)
    beside = jnp.where(row == 0, 0.0, pltpu.roll(pressure, 1, 0))
    beside += jnp.where(row == rows - 1, 0.0, pltpu.roll(pressure, rows - 1, 0))
    beside += jnp.where(col == 0, 0.0, pltpu.roll(pressure, 1, 1))
    beside += jnp.where(col == columns - 1, 0.0, pltpu.roll(pressure, columns - 1, 1))
    return inverse * (source - (4.0 + couple) * pressure + beside)


def pack_low(q, inv, p, at, axis):
    return jnp.where(
        at < DEPTH, q, jnp.where(at < 2 * DEPTH, pltpu.roll(inv, DEPTH, axis), pltpu.roll(p, 2 * DEPTH, axis))
    )


def pack_high(q, inv, p, at, axis):
    size = q.shape[axis]
    return jnp.where(
        at >= size - DEPTH,
        q,
        jnp.where(
            at >= size - 2 * DEPTH,
            pltpu.roll(inv, size - DEPTH, axis),
            pltpu.roll(p, size - 2 * DEPTH, axis),
        ),
    )


def block_rows(columns, width):
    vertical = 2 * DEPTH * (columns // LANES) + 1
    lateral = SUB + 2 * (width // LANES) + 1
    return max(vertical, lateral)


def put_rows(out_ref, at, values):
    for k in range(values.shape[0]):
        out_ref[at + k] = values[k : k + 1]


def get_rows(in_ref, at, count):
    return jnp.concatenate([in_ref[at + k] for k in range(count)], axis=0)


def send_slots(out_ref, at, first, second):
    halves = first.shape[1] // LANES
    for i, value in enumerate((first, second)):
        for h in range(halves):
            out_ref[at + SUB + i * halves + h] = value[:, h * LANES : (h + 1) * LANES]


def got_slots(in_ref, at, width):
    halves = width // LANES
    return [
        jnp.concatenate([in_ref[at + SUB + i * halves + h] for h in range(halves)], axis=1) for i in range(2)
    ]


def send_halo(out_ref, q, inv, p, groups, members, size):
    rows, columns = q.shape
    halves = columns // LANES
    g, f = lax.axis_index("grp"), lax.axis_index("frac")
    here = g * members + f
    lane = iota((rows, LANES), 1)
    low = pack_low(q[:, :LANES], inv[:, :LANES], p[:, :LANES], lane, 1)
    high = pack_high(q[:, columns - LANES :], inv[:, columns - LANES :], p[:, columns - LANES :], lane, 1)
    turned = jnp.transpose(jnp.where(lane < LANES // 2, low, high))
    left, right = turned[:SUB], turned[LANES - SUB :]
    lane = iota((1, LANES), 1)

    for step in (-1, 1):
        layer = (lambda k: k) if step < 0 else (lambda k: rows - 1 - k)

        def span(field, count, at):
            start = 0 if step < 0 else rows - count
            return field[start : start + count, at]

        inside = (g + step >= 0) & (g + step < groups)
        base = here + step * members
        tiles = [slice(h * LANES, (h + 1) * LANES) for h in range(halves)]

        @pl.when(inside)
        def _():
            at = base * size
            for h, tile in enumerate(tiles):
                put_rows(out_ref, at + h * DEPTH, span(q, DEPTH, tile))
                put_rows(out_ref, at + halves * DEPTH + h * (DEPTH - 1), span(inv, DEPTH - 1, tile))
                put_rows(out_ref, at + halves * (2 * DEPTH - 1) + h, span(p, 1, tile))
            deep, next_p = layer(DEPTH - 1), layer(1)
            extra = jnp.where(
                lane == 0,
                inv[deep : deep + 1, tiles[0]],
                jnp.where(
                    lane == LANES - 1,
                    inv[deep : deep + 1, tiles[-1]],
                    jnp.where(
                        lane == 1,
                        pltpu.roll(p[next_p : next_p + 1, tiles[0]], 1, 1),
                        pltpu.roll(p[next_p : next_p + 1, tiles[-1]], LANES - 1, 1),
                    ),
                ),
            )
            out_ref[at + halves * 2 * DEPTH] = extra

        for side, tile, there in ((-1, tiles[0], f > 0), (1, tiles[-1], f < members - 1)):

            @pl.when(inside & there)
            def _(side=side, tile=tile):
                at = (base + side) * size
                for i, field in enumerate((q, inv, p)):
                    put_rows(out_ref, at + i * DEPTH, span(field, DEPTH, tile))

    @pl.when(f > 0)
    def _():
        put_rows(out_ref, (here - 1) * size, left)

    @pl.when(f < members - 1)
    def _():
        put_rows(out_ref, (here + 1) * size, right)


def chebyshev(in_ref, q_ref, inv_ref, p_ref, target, scratch, groups, members, size, ready=None):
    q_ext, inv_ext, p_ext, update_ref, even_ref, odd_ref = scratch
    rows, columns = target.shape
    halves = columns // LANES
    side = halves
    g, f = lax.axis_index("grp"), lax.axis_index("frac")
    here = g * members + f
    last = groups * members - 1

    def taker(dg, df):
        ok = (g + dg >= 0) & (g + dg < groups) & (f + df >= 0) & (f + df < members)
        at = jnp.clip(here + dg * members + df, 0, last) * size
        return lambda start, count: jnp.where(ok, get_rows(in_ref, at + start, count), 0.0)

    def both(low, high, at, count, size):
        return jnp.where(at < count, low, jnp.where(at >= size - count, high, 0.0))

    def filler(count):
        return jnp.zeros((count, LANES), F32)

    for h in range(halves):
        for ext, ref in ((q_ext, q_ref), (inv_ext, inv_ref), (p_ext, p_ref)):
            ext[h, 0:rows, :] = ref[:, h * LANES : (h + 1) * LANES]
    outer = slice(rows, rows + SUB)
    below, above = taker(1, 0), taker(-1, 0)
    lane = iota((1, LANES), 1)
    low_extra, high_extra = below(halves * 2 * DEPTH, 1), above(halves * 2 * DEPTH, 1)
    for h in range(halves):
        edge = (lane == 0) & (h == 0) | (lane == LANES - 1) & (h == halves - 1)

        def at_edge(row, turn):
            return jnp.where(edge, pltpu.roll(row, turn, 1) if turn else row, 0.0)

        turn = LANES - 1 if h == 0 else 1
        at = h * DEPTH
        q_ext[h, outer, :] = jnp.concatenate(
            [below(at, DEPTH), filler(SUB - 2 * DEPTH), above(at, DEPTH)], axis=0
        )
        at = halves * DEPTH + h * (DEPTH - 1)
        inv_ext[h, outer, :] = jnp.concatenate(
            [
                below(at, DEPTH - 1),
                at_edge(low_extra, 0),
                filler(SUB - 2 * DEPTH),
                at_edge(high_extra, 0),
                above(at, DEPTH - 1),
            ],
            axis=0,
        )
        at = halves * (2 * DEPTH - 1) + h
        p_ext[h, outer, :] = jnp.concatenate(
            [
                below(at, 1),
                at_edge(low_extra, turn),
                filler(SUB - 4),
                at_edge(high_extra, turn),
                above(at, 1),
            ],
            axis=0,
        )
    right, left = taker(0, 1)(0, SUB), taker(0, -1)(0, SUB)
    turned = jnp.transpose(
        jnp.concatenate([right, jnp.zeros((LANES - 2 * SUB, rows), F32), left], axis=0)
    )
    lane = iota((rows, LANES), 1)
    q_ext[side, 0:rows, :] = both(turned, turned, lane, DEPTH, LANES)
    inv_ext[side, 0:rows, :] = both(
        pltpu.roll(turned, LANES - DEPTH, 1), pltpu.roll(turned, DEPTH, 1), lane, DEPTH, LANES
    )
    p_ext[side, 0:rows, :] = both(
        pltpu.roll(turned, LANES - 2 * DEPTH, 1), pltpu.roll(turned, 2 * DEPTH, 1), lane, 2, LANES
    )
    lane = iota((DEPTH, LANES), 1)
    low_right, low_left, high_right, high_left = taker(1, 1), taker(1, -1), taker(-1, 1), taker(-1, -1)
    for i, ext in enumerate((q_ext, inv_ext, p_ext)):
        at = i * DEPTH
        ext[side, outer, :] = jnp.concatenate(
            [
                both(low_right(at, DEPTH), low_left(at, DEPTH), lane, DEPTH, LANES),
                filler(SUB - 2 * DEPTH),
                both(high_right(at, DEPTH), high_left(at, DEPTH), lane, DEPTH, LANES),
            ],
            axis=0,
        )

    end = rows + SUB - 1
    for own, other in ((0, end), (end, 0), (rows - 1, rows), (rows, rows - 1)):
        for c in range(halves + 1):
            q_ext[c, own : own + 1, :] += inv_ext[c, own : own + 1, :] * p_ext[c, other : other + 1, :]
    centre = 0.5 * (HIGH_BOUND + LOW_BOUND)
    half_width = 0.5 * (HIGH_BOUND - LOW_BOUND)
    scale_ratio = centre / half_width
    ratio_now = 1.0 / scale_ratio
    lane = iota((SUB, LANES), 1)
    count = rows // SUB + 1

    def keep(ref, c, r, value):
        at = (r + 1) * SUB
        ref[c, at : at + SUB, :] = value
        if r == count - 1:
            ref[c, 0:SUB, :] = value
        if r == 0:
            at = (count + 1) * SUB
            ref[c, at : at + SUB, :] = value

    for r in range(count):
        at = slice(r * SUB, (r + 1) * SUB)
        p_side, p_first, p_final = p_ext[side, at, :], p_ext[0, at, :], p_ext[halves - 1, at, :]
        missing = [0.0] * (halves + 1)
        missing[0] += jnp.where(lane == 0, pltpu.roll(p_side, 1, 1), 0.0)
        missing[halves - 1] += jnp.where(lane == LANES - 1, pltpu.roll(p_side, LANES - 1, 1), 0.0)
        missing[side] = jnp.where(
            lane == 0,
            pltpu.roll(p_final, 1, 1),
            jnp.where(lane == LANES - 1, pltpu.roll(p_first, LANES - 1, 1), 0.0),
        )
        for c in range(halves + 1):
            start = q_ext[c, at, :] + inv_ext[c, at, :] * missing[c]
            q_ext[c, at, :] = start
            keep(even_ref, c, r, start / centre if centre != 1.0 else start)
    now_ref, next_ref = even_ref, odd_ref
    for sweep in range(1, SWEEPS):
        ratio_next = 1.0 / (2.0 * scale_ratio - ratio_now)
        final = sweep == SWEEPS - 1
        for r in range(count - 1 if final else count):
            at = slice(r * SUB, (r + 1) * SUB)
            mids = [now_ref[c, (r + 1) * SUB : (r + 2) * SUB, :] for c in range(halves + 1)]
            after = [pltpu.roll(m, 1, 1) for m in mids]
            ahead = [pltpu.roll(m, LANES - 1, 1) for m in mids]
            for c in range(halves if final else halves + 1):
                beside = now_ref[c, (r + 1) * SUB - 1 : (r + 2) * SUB - 1, :]
                beside += now_ref[c, (r + 1) * SUB + 1 : (r + 2) * SUB + 1, :]
                beside += jnp.where(lane == 0, after[(c - 1) % (halves + 1)], after[c])
                beside += jnp.where(lane == LANES - 1, ahead[(c + 1) % (halves + 1)], ahead[c])
                residual = q_ext[c, at, :] - mids[c] + inv_ext[c, at, :] * beside
                old = mids[c] if sweep == 1 else update_ref[c, at, :]
                update = ratio_next * ratio_now * old + (2.0 * ratio_next / half_width) * residual
                if final:
                    tile = slice(c * LANES, (c + 1) * LANES)
                    target[at, tile] = p_ref[at, tile] + mids[c] + update
                else:
                    update_ref[c, at, :] = update
                    keep(next_ref, c, r, mids[c] + update)
            if final and ready is not None:
                ready(r + 1)
        ratio_now = ratio_next
        now_ref, next_ref = next_ref, now_ref


ROW_SEG = 0
ROW_TRANS = 1
ROW_UP = 2
ROW_P = ROW_UP + ITERS
ROW_S = ROW_P + 1
ROW_ENDS = ROW_S + 1


def first_kernel(
    members, cell_any, seg_any, trans_any, count_any, up_any, state_any, frac_any,
    out_ref, hot_ref, row_hot_ref, cell_ref, seg_ref, trans_ref, count_ref, up_ref, state_ref, frac_ref, sem,
):
    _, rows, columns = state_ref.shape
    width = cell_ref.shape[1]
    copies = [
        pltpu.make_async_copy(source, target, sem.at[i])
        for i, (source, target) in enumerate(
            [
                (cell_any, cell_ref),
                (state_any, state_ref),
                (seg_any, seg_ref),
                (trans_any, trans_ref),
                (count_any, count_ref),
                (up_any, up_ref),
                (frac_any, frac_ref),
            ]
        )
    ]
    for copy in copies:
        copy.start()
    copies[0].wait()
    copies[1].wait()
    table = table_of([state_ref[0], state_ref[1]])
    for copy in copies[2:]:
        copy.wait()
    frac = load_segs(frac_ref, 0)
    ends = ends_of(frac)
    whole = jnp.concatenate([frac, load_segs(frac_ref, 1)], axis=0)
    for o in range(members):
        one = slice(o, o + 1)
        at = slice(o * width, (o + 1) * width)
        row, col = cell_parts(cell_ref[one, :], columns)
        hot = one_hot(col, columns)
        hot_ref[:, at] = hot
        row_hot_ref[:, at] = one_hot(row, rows)
        cell_p, cell_s = pick(table, 2, rows, row, hot)
        live = iota((1, width), 1) < count_ref[0, o]
        out_ref[o, ROW_SEG : ROW_SEG + 1, :] = seg_ref[one, :].astype(F32)
        out_ref[o, ROW_TRANS : ROW_TRANS + 1, :] = jnp.where(live, trans_ref[one, :], 0.0)
        for t in range(ITERS):
            out_ref[o, ROW_UP + t : ROW_UP + t + 1, :] = up_ref[t, one, :].astype(F32)
        out_ref[o, ROW_P : ROW_P + 1, :] = cell_p
        out_ref[o, ROW_S : ROW_S + 1, :] = cell_s
        out_ref[o, ROW_ENDS : ROW_ENDS + 1, :] = ends
        out_ref[o, SUB:, :] = whole


def seg_parts(slot_ref, s):
    seg = slot_ref[s, ROW_SEG : ROW_SEG + 1, :].astype(jnp.int32)
    return seg // SEG_COLUMNS, seg % SEG_COLUMNS


def seg_hots(slot_ref, hot_ref, row_hot_ref, members, width):
    for s in range(members):
        row, lane = seg_parts(slot_ref, s)
        at = slice(s * width, (s + 1) * width)
        hot_ref[:, at] = one_hot(lane, SEG_COLUMNS)
        row_hot_ref[:, at] = one_hot(row, row_hot_ref.shape[0])


def seg_gather(slot_ref, hot_ref, fields, s, width, table):
    return pick(table, 2, fields, seg_parts(slot_ref, s)[0], hot_ref[:, s * width : (s + 1) * width])


def cell_update(
    members, t, hot_ref, row_hot_ref, sent_ref, cell_rows, seg_rows, pressure, saturation, perm, left_ref
):
    rows = pressure.shape[0]
    for o in range(members):
        seg_p, seg_s = seg_rows(o)
        cell_p, cell_s = cell_rows(o)
        weight, water = flow(
            sent_ref[o, ROW_TRANS : ROW_TRANS + 1, :],
            sent_ref[o, ROW_UP + t : ROW_UP + t + 1, :],
            cell_p,
            cell_s,
            seg_p,
            seg_s,
        )
        spread(left_ref, row_hot_ref, o, [weight, weight * seg_p, water])
    couple, source, lost = gathered_sum(left_ref, hot_ref, 3, rows)
    inverse = 1.0 / (4.0 + perm + couple)
    new_saturation = saturation - TAU_STEP * lost / (perm + couple)
    return new_saturation, partial_residual(pressure, couple, source, inverse), inverse


def start_kernel(
    groups, members, size, slot_ref, sent_ref, cell_hot_ref, cell_row_hot_ref, frac_ref, aperture_ref,
    state_ref, perm_ref, out_ref, keep_ref, own_ref, new_ref, hot_ref, row_hot_ref,
    left_seg_ref, left_ref, found_ref,
):
    width = slot_ref.shape[2]
    rows = new_ref.shape[1]
    g = lax.axis_index("grp")
    frac, sat = load_segs(frac_ref, 0), load_segs(frac_ref, 1)
    seg_hots(slot_ref, hot_ref, row_hot_ref, members, width)
    table = table_of([frac, sat])
    for s in range(members):
        seg_p, seg_s = seg_gather(slot_ref, hot_ref, rows, s, width, table)
        cell_p = slot_ref[s, ROW_P : ROW_P + 1, :]
        weight, water = flow(
            slot_ref[s, ROW_TRANS : ROW_TRANS + 1, :],
            slot_ref[s, ROW_UP : ROW_UP + 1, :],
            cell_p,
            slot_ref[s, ROW_S : ROW_S + 1, :],
            seg_p,
            seg_s,
        )
        spread(left_seg_ref, row_hot_ref, s, [weight * cell_p, weight, water])
    inflow, total, gained = gathered_sum(left_seg_ref, hot_ref, 3, rows)
    before, after = chain_ends(slot_ref, ROW_ENDS, members)
    new_frac, new_sat = frac_step(frac, sat, load_segs(aperture_ref), before, after, inflow, total, gained)
    new_ref[0] = new_frac
    new_ref[1] = new_sat
    table = table_of([new_frac, new_sat])
    ends = ends_of(new_frac)
    ends = jnp.where(iota((1, LANES), 1) < LANES // 2, ends[:, :LANES], ends[:, SEG_COLUMNS - LANES :])
    for s in range(members):
        seg_p, seg_s = seg_gather(slot_ref, hot_ref, rows, s, width, table)
        own_ref[s, 0:1, :] = seg_p
        own_ref[s, 1:2, :] = seg_s
        at = (g * members + s) * size
        send_slots(out_ref, at, seg_p, seg_s)
        out_ref[at + size - 1] = ends
    for o in range(members):
        row, lane = seg_parts(sent_ref, o)
        table = table_of([slot_ref[o, SUB : SUB + rows, :], slot_ref[o, SUB + rows :, :]])
        seg_p, seg_s = pick(table, 2, rows, row, one_hot(lane, SEG_COLUMNS))
        found_ref[o, 0:1, :] = seg_p
        found_ref[o, 1:2, :] = seg_s
    pressure = state_ref[0]
    new_saturation, q, inv = cell_update(
        members,
        0,
        cell_hot_ref,
        cell_row_hot_ref,
        sent_ref,
        lambda o: (sent_ref[o, ROW_P : ROW_P + 1, :], sent_ref[o, ROW_S : ROW_S + 1, :]),
        lambda o: (found_ref[o, 0:1, :], found_ref[o, 1:2, :]),
        pressure,
        state_ref[1],
        perm_ref[...],
        left_ref,
    )
    keep_ref[0] = pressure
    keep_ref[1] = new_saturation
    keep_ref[2] = q
    keep_ref[3] = inv
    send_halo(out_ref, q, inv, pressure, groups, members, size)


def cell_gather(members, cell_ref, hot_ref, fields, put):
    rows, columns = fields[0].shape
    width = cell_ref.shape[1]
    table = table_of(fields)
    for o in range(members):
        row, _ = cell_parts(cell_ref[o : o + 1, :], columns)
        put(o, *pick(table, len(fields), rows, row, hot_ref[:, o * width : (o + 1) * width]))


def middle_kernel(
    groups, members, size, halo_ref, cell_ref, hot_ref, row_hot_ref, sent_ref, kept_ref, perm_ref,
    out_ref, keep_ref, slots_ref, left_ref, *scratch,
):
    saturation = kept_ref[1]
    g = lax.axis_index("grp")

    def put_s(o, cell_s):
        slots_ref[o, 1:2, :] = cell_s

    cell_gather(members, cell_ref, hot_ref, [saturation], put_s)
    chebyshev(
        halo_ref, kept_ref.at[2], kept_ref.at[3], kept_ref.at[0], keep_ref.at[0], scratch, groups, members, size
    )
    pressure = keep_ref[0]

    def put_p(o, cell_p):
        slots_ref[o, 0:1, :] = cell_p
        send_slots(out_ref, (g * members + o) * size, cell_p, slots_ref[o, 1:2, :])

    cell_gather(members, cell_ref, hot_ref, [pressure], put_p)
    new_saturation, q, inv = cell_update(
        members,
        1,
        hot_ref,
        row_hot_ref,
        sent_ref,
        lambda o: (slots_ref[o, 0:1, :], slots_ref[o, 1:2, :]),
        lambda o: got_slots(halo_ref, (g * members + o) * size, cell_ref.shape[1]),
        pressure,
        saturation,
        perm_ref[...],
        left_ref,
    )
    keep_ref[1] = new_saturation
    keep_ref[2] = q
    keep_ref[3] = inv
    send_halo(out_ref, q, inv, pressure, groups, members, size)


def owner_update(
    members, t, slot_ref, cell_rows, seg_rows, frac, sat, aperture, ends, hot_ref, row_hot_ref, left_ref
):
    rows = frac.shape[0]
    for s in range(members):
        cell_p, cell_s = cell_rows(s)
        weight, water = flow(
            slot_ref[s, ROW_TRANS : ROW_TRANS + 1, :],
            slot_ref[s, ROW_UP + t : ROW_UP + t + 1, :],
            cell_p,
            cell_s,
            *seg_rows(s),
        )
        spread(left_ref, row_hot_ref, s, [weight * cell_p, weight, water])
    inflow, total, gained = gathered_sum(left_ref, hot_ref, 3, rows)
    return frac_step(frac, sat, aperture, *ends, inflow, total, gained)


def exchange_kernel(
    groups, members, size, halo_ref, cell_ref, cell_hot_ref, slot_ref, hot_ref, row_hot_ref, ends_ref, own_ref,
    frac_ref, aperture_ref, kept_ref, out_ref, new_ref, pressure_ref, left_ref, *scratch,
):
    width = slot_ref.shape[2]
    rows = frac_ref.shape[1]
    g = lax.axis_index("grp")

    def cell_rows(s):
        return got_slots(halo_ref, (g * members + s) * size, width)

    me = lax.axis_index("frac")
    prior = ends_ref[(g * members + jnp.maximum(me - 1, 0)) * size + size - 1]
    later = ends_ref[(g * members + jnp.minimum(me + 1, members - 1)) * size + size - 1]
    before = jnp.where(me > 0, prior[:, LANES - 1 :], 0.0)
    after = jnp.where(me < members - 1, later[:, 0:1], 0.0)

    new_frac, new_sat = owner_update(
        members,
        1,
        slot_ref,
        cell_rows,
        lambda s: (own_ref[s, 0:1, :], own_ref[s, 1:2, :]),
        frac_ref[0],
        frac_ref[1],
        load_segs(aperture_ref),
        (before, after),
        hot_ref,
        row_hot_ref,
        left_ref,
    )
    new_ref[0] = new_frac
    new_ref[1] = new_sat
    table = table_of([new_frac, new_sat])
    ends = ends_of(new_frac)
    for s in range(members):
        seg_p, seg_s = seg_gather(slot_ref, hot_ref, rows, s, width, table)
        out_ref[s, 2:3, :] = seg_p
        out_ref[s, 3:4, :] = seg_s
        out_ref[s, 4:5, :] = ends

    chebyshev(
        halo_ref, kept_ref.at[2], kept_ref.at[3], kept_ref.at[0], pressure_ref, scratch, groups, members, size
    )
    pressure = pressure_ref[...]

    def put(o, cell_p, cell_s):
        out_ref[o, 0:1, :] = cell_p
        out_ref[o, 1:2, :] = cell_s

    cell_gather(members, cell_ref, cell_hot_ref, [pressure, kept_ref[1]], put)


def source_last_kernel(
    groups, members, size, hot_ref, row_hot_ref, sent_ref, own_ref, seg_ref, pressure_ref, kept_ref, perm_ref,
    out_any, keep_ref, left_ref, out_ref, sem,
):
    pressure = pressure_ref[...]
    new_saturation, q, inv = cell_update(
        members,
        2,
        hot_ref,
        row_hot_ref,
        sent_ref,
        lambda o: (own_ref[o, 0:1, :], own_ref[o, 1:2, :]),
        lambda o: (seg_ref[o, 2:3, :], seg_ref[o, 3:4, :]),
        pressure,
        kept_ref[1],
        perm_ref[...],
        left_ref,
    )
    keep_ref[0] = new_saturation
    keep_ref[1] = q
    keep_ref[2] = inv
    send_halo(out_ref, q, inv, pressure, groups, members, size)
    g, f = lax.axis_index("grp"), lax.axis_index("frac")
    runs = []
    for i, step in enumerate((-1, 0, 1)):
        at = jnp.clip((g + step) * members + f - 1, 0, groups * members - 3) * size
        run = pltpu.make_async_copy(out_ref.at[pl.ds(at, 3 * size)], out_any.at[pl.ds(at, 3 * size)], sem.at[i])
        runs.append(((g + step >= 0) & (g + step < groups), run))
    for inside, run in runs:
        pl.when(inside)(run.start)
    for inside, run in runs:
        pl.when(inside)(run.wait)


def owner_last_kernel(
    members, slot_ref, hot_ref, row_hot_ref, own_ref, seg_ref, frac_ref, aperture_ref, out_ref, left_ref
):
    new_frac, new_sat = owner_update(
        members,
        2,
        slot_ref,
        lambda s: (seg_ref[s, 0:1, :], seg_ref[s, 1:2, :]),
        lambda s: (own_ref[s, 2:3, :], own_ref[s, 3:4, :]),
        frac_ref[0],
        frac_ref[1],
        load_segs(aperture_ref),
        chain_ends(seg_ref, 4, members),
        hot_ref,
        row_hot_ref,
        left_ref,
    )
    store_segs(out_ref, 0, new_frac)
    store_segs(out_ref, 1, new_sat)


def final_kernel(groups, members, size, halo_ref, pressure_ref, kept_ref, out_any, new_ref, sem, *scratch):
    rows = pressure_ref.shape[0]
    chunk = rows // 2
    copies = [pltpu.make_async_copy(kept_ref.at[0], out_any.at[1], sem.at[0])]
    copies[0].start()

    def ready(tiles):
        if tiles * SUB % chunk == 0:
            at = pl.ds(tiles * SUB - chunk, chunk)
            copies.append(pltpu.make_async_copy(new_ref.at[at], out_any.at[0, at], sem.at[len(copies)]))
            copies[-1].start()

    chebyshev(
        halo_ref, kept_ref.at[1], kept_ref.at[2], pressure_ref, new_ref, scratch, groups, members, size, ready
    )
    for copy in copies:
        copy.wait()


VMEM = pl.BlockSpec(memory_space=pltpu.VMEM)
HBM = pl.BlockSpec(memory_space=pltpu.HBM)


def call(kernel, statics, outs, scratch, *args, spec=VMEM, away=()):
    outs = [o if hasattr(o, "dtype") else jax.ShapeDtypeStruct(o, F32) for o in outs]
    return pl.pallas_call(
        functools.partial(kernel, *statics),
        out_shape=outs,
        in_specs=[spec] * len(args),
        out_specs=[HBM if i in away else VMEM for i in range(len(outs))],
        scratch_shapes=scratch,
        compiler_params=pltpu.CompilerParams(vmem_limit_bytes=32 * 1024 * 1024),
        name=kernel.__name__,
    )(*args)


def on_device(
    matrix_state,
    matrix_perm,
    frac_state,
    frac_aperture,
    link_cell,
    link_seg,
    link_trans,
    link_count,
    link_upwind,
):
    groups, members = lax.axis_size("grp"), lax.axis_size("frac")
    devices = groups * members
    cells = link_cell[0, 0]
    width = cells.shape[1]
    _, rows, columns = matrix_state.shape
    seg_dev = frac_state.shape[2]
    seg_rows = seg_dev // LANES
    frac = frac_state.reshape(2, seg_rows, LANES)
    aperture = frac_aperture.reshape(seg_rows, LANES)

    every = members * width
    slots = (members, SUB, width)
    size = block_rows(columns, width)
    both = (groups, members, size)
    halo = (devices * size, 1, LANES)
    left_cell = pltpu.VMEM((3 * PARTS * rows, every), BF16)
    seg_wide = seg_dev // SEG_COLUMNS
    segs_wide = (2, seg_wide, SEG_COLUMNS)
    left_seg = pltpu.VMEM((3 * PARTS * seg_wide, every), BF16)
    tiles = columns // LANES + 1
    ext = [pltpu.VMEM((tiles, rows + SUB, LANES), F32)] * 4 + [pltpu.VMEM((tiles, rows + 3 * SUB, LANES), F32)] * 2

    def to_group(x):
        return lax.all_to_all(x, "frac", split_axis=0, concat_axis=0, tiled=True)

    def to_all(x):
        return lax.all_to_all(x, ("grp", "frac"), split_axis=0, concat_axis=0, tiled=True)

    def hots(*sizes):
        return [jax.ShapeDtypeStruct((n, every), BF16) for n in sizes]

    sent, cell_hot, cell_row_hot = call(
        first_kernel,
        (members,),
        [(members, SUB + 2 * seg_wide, SEG_COLUMNS)] + hots(columns, rows),
        [
            pltpu.VMEM((members, width), jnp.int32),
            pltpu.VMEM((members, width), jnp.int32),
            pltpu.VMEM((members, width), F32),
            pltpu.SMEM((1, members), jnp.int32),
            pltpu.VMEM((ITERS, members, width), jnp.int32),
            pltpu.VMEM(matrix_state.shape, F32),
            pltpu.VMEM(frac.shape, F32),
            pltpu.SemaphoreType.DMA((7,)),
        ],
        *[
            pltpu.with_memory_space_constraint(x, pltpu.HBM)
            for x in (
                cells, link_seg[0, 0], link_trans[0, 0], link_count[0], link_upwind[:, 0, 0], matrix_state, frac
            )
        ],
        spec=HBM,
    )
    slot = to_group(sent)
    edge, kept, own, frac1, hot, row_hot = call(
        start_kernel,
        both,
        [halo, (4, rows, columns), (members, 2, width), segs_wide] + hots(SEG_COLUMNS, seg_wide),
        [left_seg, left_cell, pltpu.VMEM((members, 2, width), F32)],
        slot, sent, cell_hot, cell_row_hot, frac, aperture, matrix_state, matrix_perm,
    )
    before = to_all(edge)
    edge, kept = call(
        middle_kernel, both, [halo, (4, rows, columns)], [pltpu.VMEM((members, 2, width), F32), left_cell] + ext,
        before, cells, cell_hot, cell_row_hot, sent, kept, matrix_perm,
    )
    around = to_all(edge)
    own, frac2, pressure = call(
        exchange_kernel, both, [slots, segs_wide, (rows, columns)], [left_seg] + ext,
        around, cells, cell_hot, slot, hot, row_hot, before, own, frac1, aperture, kept,
    )
    segs = to_group(own)
    edge, kept = call(
        source_last_kernel,
        both,
        [halo, (3, rows, columns)],
        [left_cell, pltpu.VMEM(halo, F32), pltpu.SemaphoreType.DMA((3,))],
        cell_hot, cell_row_hot, sent, own, segs, pressure, kept, matrix_perm,
        away=(0,),
    )
    around = to_all(edge)
    (frac3,) = call(
        owner_last_kernel, (members,), [frac.shape], [left_seg], slot, hot, row_hot, own, segs, frac2, aperture
    )
    (matrix_out,) = call(
        final_kernel,
        both,
        [matrix_state.shape],
        [pltpu.VMEM((rows, columns), F32), pltpu.SemaphoreType.DMA((3,))] + ext,
        around, pressure, kept,
        away=(0,),
    )
    return matrix_out, frac3.reshape(frac_state.shape)


def solution(mesh):
    return jax.shard_map(
        on_device,
        mesh=mesh,
        in_specs=(
            P(None, "grp", "frac"),
            P("grp", "frac"),
            P(None, "grp", "frac"),
            P("grp", "frac"),
            P("grp", "frac", None, None),
            P("grp", "frac", None, None),
            P("grp", "frac", None, None),
            P("grp", "frac", None),
            P(None, "grp", "frac", None, None),
        ),
        out_specs=(P(None, "grp", "frac"), P(None, "grp", "frac")),
        check_vma=False,
    )
```

```python
import functools

import jax
import jax.numpy as jnp
from jax import lax
from jax.experimental import pallas as pl
from jax.experimental.pallas import tpu as pltpu
from jax.sharding import PartitionSpec as P

ITERS = 3
SWEEPS = 4

LOW_BOUND = 0.02
HIGH_BOUND = 1.98
TAU_STEP = 0.5
MOBILITY_FLOOR = 0.2

F32 = jnp.float32
BF16 = jnp.bfloat16
LANES = 128
SUB = 8
SEG_COLUMNS = 2 * LANES
DEPTH = SWEEPS - 1


def iota(shape, dim):
    return lax.broadcasted_iota(jnp.int32, shape, dim)


def parts_of(x):
    high = x.astype(BF16).astype(F32)
    return high, x - high


PARTS = 2


def table_of(fields):
    split = [parts_of(f) for f in fields]
    return jnp.concatenate([s[p] for p in range(PARTS) for s in split], axis=0).astype(BF16)


def one_hot(index_row, count):
    shape = (count, index_row.shape[1])
    hit = iota(shape, 0).astype(F32).astype(BF16) == index_row.astype(F32).astype(BF16)
    return jnp.where(hit, jnp.ones(shape, BF16), jnp.zeros(shape, BF16))


def pick(table, fields, rows, row_index, hot):
    wide = jnp.dot(table, hot, preferred_element_type=F32)
    hit = iota((rows, row_index.shape[1]), 0) == row_index
    found = []
    for f in range(fields):
        total = sum(wide[(p * fields + f) * rows : (p * fields + f + 1) * rows] for p in range(PARTS))
        found.append(jnp.sum(jnp.where(hit, total, 0.0), axis=0, keepdims=True))
    return found


def spread(left_ref, row_hot_ref, block, values):
    rows = row_hot_ref.shape[0]
    width = values[0].shape[1]
    at = slice(block * width, (block + 1) * width)
    hot = row_hot_ref[:, at]
    for f, value in enumerate(values):
        for p, part in enumerate(parts_of(value)):
            row = (p * len(values) + f) * rows
            left_ref[row : row + rows, at] = hot * part.astype(BF16)


def gathered_sum(left_ref, hot_ref, fields, rows):
    wide = lax.dot_general(
        left_ref[...], hot_ref[...], (((1,), (1,)), ((), ())), preferred_element_type=F32
    )
    return [
        sum(wide[(p * fields + f) * rows : (p * fields + f + 1) * rows] for p in range(PARTS))
        for f in range(fields)
    ]


def flow(trans, upwind, cell_p, cell_s, seg_p, seg_s):
    u = jnp.where(upwind > 0.5, cell_s, seg_s)
    weight = trans * (MOBILITY_FLOOR + u * u)
    water = weight * (cell_p - seg_p) * u
    return weight, water


def cell_parts(cell_row, columns):
    return cell_row // columns, cell_row % columns


def load_segs(ref, *lead):
    rows = ref.shape[-2] // 2
    return jnp.concatenate([ref[(*lead, pl.ds(h, rows, 2), slice(None))] for h in range(2)], axis=1)


def store_segs(ref, lead, value):
    rows = value.shape[0]
    for h in range(2):
        ref[lead, pl.ds(h, rows, 2), :] = value[:, h * LANES : (h + 1) * LANES]


def ends_of(frac):
    rows, columns = frac.shape
    lane = iota((1, columns), 1)
    return jnp.where(lane < columns // 2, frac[0:1], frac[rows - 1 : rows])


def frac_step(frac, sat, aperture, before, after, inflow, total, gained):
    rows, lanes = frac.shape
    row, lane = iota((rows, lanes), 0), iota((rows, lanes), 1)
    back = pltpu.roll(frac, 1, 1)
    left = jnp.where(lane == 0, pltpu.roll(back, 1, 0), back)
    left = jnp.where((lane == 0) & (row == 0), before, left)
    ahead = pltpu.roll(frac, lanes - 1, 1)
    right = jnp.where(lane == lanes - 1, pltpu.roll(ahead, rows - 1, 0), ahead)
    right = jnp.where((lane == lanes - 1) & (row == rows - 1), after, right)
    new_frac = (aperture * frac + inflow + left + right) / (aperture + total + 2.0)
    new_sat = sat + TAU_STEP * gained / (aperture + total)
    return new_frac, new_sat


def chain_ends(ends_ref, row, members):
    me = lax.axis_index("frac")
    lanes = ends_ref.shape[2]
    prior = ends_ref[jnp.maximum(me - 1, 0), row : row + 1, :]
    later = ends_ref[jnp.minimum(me + 1, members - 1), row : row + 1, :]
    before = jnp.where(me > 0, prior[:, lanes - 1 :], 0.0)
    after = jnp.where(me < members - 1, later[:, 0:1], 0.0)
    return before, after


def partial_residual(pressure, couple, source, inverse):
    rows, columns = pressure.shape
    row, col = iota((rows, columns), 0), iota((rows, columns), 1)
    beside = jnp.where(row == 0, 0.0, pltpu.roll(pressure, 1, 0))
    beside += jnp.where(row == rows - 1, 0.0, pltpu.roll(pressure, rows - 1, 0))
    beside += jnp.where(col == 0, 0.0, pltpu.roll(pressure, 1, 1))
    beside += jnp.where(col == columns - 1, 0.0, pltpu.roll(pressure, columns - 1, 1))
    return inverse * (source - (4.0 + couple) * pressure + beside)


def pack_low(q, inv, p, at, axis):
    return jnp.where(
        at < DEPTH, q, jnp.where(at < 2 * DEPTH, pltpu.roll(inv, DEPTH, axis), pltpu.roll(p, 2 * DEPTH, axis))
    )


def pack_high(q, inv, p, at, axis):
    size = q.shape[axis]
    return jnp.where(
        at >= size - DEPTH,
        q,
        jnp.where(
            at >= size - 2 * DEPTH,
            pltpu.roll(inv, size - DEPTH, axis),
            pltpu.roll(p, size - 2 * DEPTH, axis),
        ),
    )


def block_rows(columns, width):
    vertical = 2 * DEPTH * (columns // LANES) + 1
    lateral = SUB + 2 * (width // LANES) + 1
    return max(vertical, lateral)


def put_rows(out_ref, at, values):
    for k in range(values.shape[0]):
        out_ref[at + k] = values[k : k + 1]


def get_rows(in_ref, at, count):
    return jnp.concatenate([in_ref[at + k] for k in range(count)], axis=0)


def send_slots(out_ref, at, first, second):
    halves = first.shape[1] // LANES
    for i, value in enumerate((first, second)):
        for h in range(halves):
            out_ref[at + SUB + i * halves + h] = value[:, h * LANES : (h + 1) * LANES]


def got_slots(in_ref, at, width):
    halves = width // LANES
    return [
        jnp.concatenate([in_ref[at + SUB + i * halves + h] for h in range(halves)], axis=1) for i in range(2)
    ]


def send_halo(out_ref, q, inv, p, groups, members, size):
    rows, columns = q.shape
    halves = columns // LANES
    g, f = lax.axis_index("grp"), lax.axis_index("frac")
    here = g * members + f
    lane = iota((rows, LANES), 1)
    low = pack_low(q[:, :LANES], inv[:, :LANES], p[:, :LANES], lane, 1)
    high = pack_high(q[:, columns - LANES :], inv[:, columns - LANES :], p[:, columns - LANES :], lane, 1)
    turned = jnp.transpose(jnp.where(lane < LANES // 2, low, high))
    left, right = turned[:SUB], turned[LANES - SUB :]
    lane = iota((1, LANES), 1)
    spare = jnp.where(g + 2 < groups, here + 2 * members, here - 2 * members)

    for step in (-1, 1):
        layer = (lambda k: k) if step < 0 else (lambda k: rows - 1 - k)

        def span(field, count, at):
            start = 0 if step < 0 else rows - count
            return field[start : start + count, at]

        inside = (g + step >= 0) & (g + step < groups)
        base = here + step * members
        tiles = [slice(h * LANES, (h + 1) * LANES) for h in range(halves)]

        at = jnp.where(inside, base, spare) * size
        for h, tile in enumerate(tiles):
            put_rows(out_ref, at + h * DEPTH, span(q, DEPTH, tile))
            put_rows(out_ref, at + halves * DEPTH + h * (DEPTH - 1), span(inv, DEPTH - 1, tile))
            put_rows(out_ref, at + halves * (2 * DEPTH - 1) + h, span(p, 1, tile))
        deep, next_p = layer(DEPTH - 1), layer(1)
        extra = jnp.where(
            lane == 0,
            inv[deep : deep + 1, tiles[0]],
            jnp.where(
                lane == LANES - 1,
                inv[deep : deep + 1, tiles[-1]],
                jnp.where(
                    lane == 1,
                    pltpu.roll(p[next_p : next_p + 1, tiles[0]], 1, 1),
                    pltpu.roll(p[next_p : next_p + 1, tiles[-1]], LANES - 1, 1),
                ),
            ),
        )
        out_ref[at + halves * 2 * DEPTH] = extra

        for side, tile, there in ((-1, tiles[0], f > 0), (1, tiles[-1], f < members - 1)):
            at = jnp.where(inside & there, base + side, spare) * size
            for i, field in enumerate((q, inv, p)):
                put_rows(out_ref, at + i * DEPTH, span(field, DEPTH, tile))

    put_rows(out_ref, jnp.where(f > 0, here - 1, spare) * size, left)
    put_rows(out_ref, jnp.where(f < members - 1, here + 1, spare) * size, right)


def chebyshev(in_ref, q_ref, inv_ref, p_ref, target, scratch, groups, members, size):
    q_ext, inv_ext, p_ext, update_ref, even_ref, odd_ref = scratch
    rows, columns = target.shape
    halves = columns // LANES
    side = halves
    g, f = lax.axis_index("grp"), lax.axis_index("frac")
    here = g * members + f
    last = groups * members - 1

    def taker(dg, df):
        ok = (g + dg >= 0) & (g + dg < groups) & (f + df >= 0) & (f + df < members)
        at = jnp.clip(here + dg * members + df, 0, last) * size
        return lambda start, count: jnp.where(ok, get_rows(in_ref, at + start, count), 0.0)

    def both(low, high, at, count, size):
        return jnp.where(at < count, low, jnp.where(at >= size - count, high, 0.0))

    def filler(count):
        return jnp.zeros((count, LANES), F32)

    for h in range(halves):
        for ext, ref in ((q_ext, q_ref), (inv_ext, inv_ref), (p_ext, p_ref)):
            ext[h, 0:rows, :] = ref[:, h * LANES : (h + 1) * LANES]
    outer = slice(rows, rows + SUB)
    below, above = taker(1, 0), taker(-1, 0)
    lane = iota((1, LANES), 1)
    low_extra, high_extra = below(halves * 2 * DEPTH, 1), above(halves * 2 * DEPTH, 1)
    for h in range(halves):
        edge = (lane == 0) & (h == 0) | (lane == LANES - 1) & (h == halves - 1)

        def at_edge(row, turn):
            return jnp.where(edge, pltpu.roll(row, turn, 1) if turn else row, 0.0)

        turn = LANES - 1 if h == 0 else 1
        at = h * DEPTH
        q_ext[h, outer, :] = jnp.concatenate(
            [below(at, DEPTH), filler(SUB - 2 * DEPTH), above(at, DEPTH)], axis=0
        )
        at = halves * DEPTH + h * (DEPTH - 1)
        inv_ext[h, outer, :] = jnp.concatenate(
            [
                below(at, DEPTH - 1),
                at_edge(low_extra, 0),
                filler(SUB - 2 * DEPTH),
                at_edge(high_extra, 0),
                above(at, DEPTH - 1),
            ],
            axis=0,
        )
        at = halves * (2 * DEPTH - 1) + h
        p_ext[h, outer, :] = jnp.concatenate(
            [
                below(at, 1),
                at_edge(low_extra, turn),
                filler(SUB - 4),
                at_edge(high_extra, turn),
                above(at, 1),
            ],
            axis=0,
        )
    right, left = taker(0, 1)(0, SUB), taker(0, -1)(0, SUB)
    turned = jnp.transpose(
        jnp.concatenate([right, jnp.zeros((LANES - 2 * SUB, rows), F32), left], axis=0)
    )
    lane = iota((rows, LANES), 1)
    q_ext[side, 0:rows, :] = both(turned, turned, lane, DEPTH, LANES)
    inv_ext[side, 0:rows, :] = both(
        pltpu.roll(turned, LANES - DEPTH, 1), pltpu.roll(turned, DEPTH, 1), lane, DEPTH, LANES
    )
    p_ext[side, 0:rows, :] = both(
        pltpu.roll(turned, LANES - 2 * DEPTH, 1), pltpu.roll(turned, 2 * DEPTH, 1), lane, 2, LANES
    )
    lane = iota((DEPTH, LANES), 1)
    low_right, low_left, high_right, high_left = taker(1, 1), taker(1, -1), taker(-1, 1), taker(-1, -1)
    for i, ext in enumerate((q_ext, inv_ext, p_ext)):
        at = i * DEPTH
        ext[side, outer, :] = jnp.concatenate(
            [
                both(low_right(at, DEPTH), low_left(at, DEPTH), lane, DEPTH, LANES),
                filler(SUB - 2 * DEPTH),
                both(high_right(at, DEPTH), high_left(at, DEPTH), lane, DEPTH, LANES),
            ],
            axis=0,
        )

    end = rows + SUB - 1
    for own, other in ((0, end), (end, 0), (rows - 1, rows), (rows, rows - 1)):
        for c in range(halves + 1):
            q_ext[c, own : own + 1, :] += inv_ext[c, own : own + 1, :] * p_ext[c, other : other + 1, :]
    centre = 0.5 * (HIGH_BOUND + LOW_BOUND)
    half_width = 0.5 * (HIGH_BOUND - LOW_BOUND)
    scale_ratio = centre / half_width
    ratio_now = 1.0 / scale_ratio
    lane = iota((SUB, LANES), 1)
    count = rows // SUB + 1

    def keep(ref, c, r, value):
        at = (r + 1) * SUB
        ref[c, at : at + SUB, :] = value
        if r == count - 1:
            ref[c, 0:SUB, :] = value
        if r == 0:
            at = (count + 1) * SUB
            ref[c, at : at + SUB, :] = value

    for r in range(count):
        at = slice(r * SUB, (r + 1) * SUB)
        p_side, p_first, p_final = p_ext[side, at, :], p_ext[0, at, :], p_ext[halves - 1, at, :]
        missing = [0.0] * (halves + 1)
        missing[0] += jnp.where(lane == 0, pltpu.roll(p_side, 1, 1), 0.0)
        missing[halves - 1] += jnp.where(lane == LANES - 1, pltpu.roll(p_side, LANES - 1, 1), 0.0)
        missing[side] = jnp.where(
            lane == 0,
            pltpu.roll(p_final, 1, 1),
            jnp.where(lane == LANES - 1, pltpu.roll(p_first, LANES - 1, 1), 0.0),
        )
        for c in range(halves + 1):
            start = q_ext[c, at, :] + inv_ext[c, at, :] * missing[c]
            q_ext[c, at, :] = start
            keep(even_ref, c, r, start / centre if centre != 1.0 else start)
    now_ref, next_ref = even_ref, odd_ref
    for sweep in range(1, SWEEPS):
        ratio_next = 1.0 / (2.0 * scale_ratio - ratio_now)
        final = sweep == SWEEPS - 1
        for r in range(count - 1 if final else count):
            at = slice(r * SUB, (r + 1) * SUB)
            mids = [now_ref[c, (r + 1) * SUB : (r + 2) * SUB, :] for c in range(halves + 1)]
            after = [pltpu.roll(m, 1, 1) for m in mids]
            ahead = [pltpu.roll(m, LANES - 1, 1) for m in mids]
            for c in range(halves if final else halves + 1):
                beside = now_ref[c, (r + 1) * SUB - 1 : (r + 2) * SUB - 1, :]
                beside += now_ref[c, (r + 1) * SUB + 1 : (r + 2) * SUB + 1, :]
                beside += jnp.where(lane == 0, after[(c - 1) % (halves + 1)], after[c])
                beside += jnp.where(lane == LANES - 1, ahead[(c + 1) % (halves + 1)], ahead[c])
                residual = q_ext[c, at, :] - mids[c] + inv_ext[c, at, :] * beside
                old = mids[c] if sweep == 1 else update_ref[c, at, :]
                update = ratio_next * ratio_now * old + (2.0 * ratio_next / half_width) * residual
                if final:
                    tile = slice(c * LANES, (c + 1) * LANES)
                    target[at, tile] = p_ref[at, tile] + mids[c] + update
                else:
                    update_ref[c, at, :] = update
                    keep(next_ref, c, r, mids[c] + update)
        ratio_now = ratio_next
        now_ref, next_ref = next_ref, now_ref


ROW_SEG = 0
ROW_TRANS = 1
ROW_UP = 2
ROW_P = ROW_UP + ITERS
ROW_S = ROW_P + 1
ROW_ENDS = ROW_S + 1


def first_kernel(
    members, cell_any, seg_any, trans_any, count_any, up_any, state_any, frac_any,
    out_ref, hot_ref, row_hot_ref, cell_ref, seg_ref, trans_ref, count_ref, up_ref, state_ref, frac_ref, sem,
):
    _, rows, columns = state_ref.shape
    width = cell_ref.shape[1]
    copies = [
        pltpu.make_async_copy(source, target, sem.at[i])
        for i, (source, target) in enumerate(
            [
                (cell_any, cell_ref),
                (state_any, state_ref),
                (seg_any, seg_ref),
                (trans_any, trans_ref),
                (count_any, count_ref),
                (up_any, up_ref),
                (frac_any, frac_ref),
            ]
        )
    ]
    for copy in copies:
        copy.start()
    copies[0].wait()
    for o in range(members):
        row, col = cell_parts(cell_ref[o : o + 1, :], columns)
        at = slice(o * width, (o + 1) * width)
        hot_ref[:, at] = one_hot(col, columns)
        row_hot_ref[:, at] = one_hot(row, rows)
    copies[1].wait()
    table = table_of([state_ref[0], state_ref[1]])
    for copy in copies[2:]:
        copy.wait()
    frac = load_segs(frac_ref, 0)
    ends = ends_of(frac)
    whole = jnp.concatenate([frac, load_segs(frac_ref, 1)], axis=0)
    for o in range(members):
        one = slice(o, o + 1)
        row, _ = cell_parts(cell_ref[one, :], columns)
        cell_p, cell_s = pick(table, 2, rows, row, hot_ref[:, o * width : (o + 1) * width])
        live = iota((1, width), 1) < count_ref[0, o]
        out_ref[o, ROW_SEG : ROW_SEG + 1, :] = seg_ref[one, :].astype(F32)
        out_ref[o, ROW_TRANS : ROW_TRANS + 1, :] = jnp.where(live, trans_ref[one, :], 0.0)
        for t in range(ITERS):
            out_ref[o, ROW_UP + t : ROW_UP + t + 1, :] = up_ref[t, one, :].astype(F32)
        out_ref[o, ROW_P : ROW_P + 1, :] = cell_p
        out_ref[o, ROW_S : ROW_S + 1, :] = cell_s
        out_ref[o, ROW_ENDS : ROW_ENDS + 1, :] = ends
        out_ref[o, SUB:, :] = whole


def seg_parts(slot_ref, s):
    seg = slot_ref[s, ROW_SEG : ROW_SEG + 1, :].astype(jnp.int32)
    return seg // SEG_COLUMNS, seg % SEG_COLUMNS


def seg_hots(slot_ref, hot_ref, row_hot_ref, members, width):
    for s in range(members):
        row, lane = seg_parts(slot_ref, s)
        at = slice(s * width, (s + 1) * width)
        hot_ref[:, at] = one_hot(lane, SEG_COLUMNS)
        row_hot_ref[:, at] = one_hot(row, row_hot_ref.shape[0])


def seg_gather(slot_ref, hot_ref, fields, s, width, table):
    return pick(table, 2, fields, seg_parts(slot_ref, s)[0], hot_ref[:, s * width : (s + 1) * width])


def cell_update(
    members, t, hot_ref, row_hot_ref, sent_ref, cell_rows, seg_rows, pressure, saturation, perm, left_ref
):
    rows = pressure.shape[0]
    for o in range(members):
        seg_p, seg_s = seg_rows(o)
        cell_p, cell_s = cell_rows(o)
        weight, water = flow(
            sent_ref[o, ROW_TRANS : ROW_TRANS + 1, :],
            sent_ref[o, ROW_UP + t : ROW_UP + t + 1, :],
            cell_p,
            cell_s,
            seg_p,
            seg_s,
        )
        spread(left_ref, row_hot_ref, o, [weight, weight * seg_p, water])
    couple, source, lost = gathered_sum(left_ref, hot_ref, 3, rows)
    inverse = 1.0 / (4.0 + perm + couple)
    new_saturation = saturation - TAU_STEP * lost / (perm + couple)
    return new_saturation, partial_residual(pressure, couple, source, inverse), inverse


def start_kernel(
    groups, members, size, slot_ref, sent_ref, cell_hot_ref, cell_row_hot_ref, frac_ref, aperture_ref,
    state_ref, perm_ref, out_ref, keep_ref, own_ref, new_ref, hot_ref, row_hot_ref,
    left_seg_ref, left_ref, found_ref,
):
    width = slot_ref.shape[2]
    rows = new_ref.shape[1]
    g = lax.axis_index("grp")
    frac, sat = load_segs(frac_ref, 0), load_segs(frac_ref, 1)
    seg_hots(slot_ref, hot_ref, row_hot_ref, members, width)
    table = table_of([frac, sat])
    for s in range(members):
        seg_p, seg_s = seg_gather(slot_ref, hot_ref, rows, s, width, table)
        cell_p = slot_ref[s, ROW_P : ROW_P + 1, :]
        weight, water = flow(
            slot_ref[s, ROW_TRANS : ROW_TRANS + 1, :],
            slot_ref[s, ROW_UP : ROW_UP + 1, :],
            cell_p,
            slot_ref[s, ROW_S : ROW_S + 1, :],
            seg_p,
            seg_s,
        )
        spread(left_seg_ref, row_hot_ref, s, [weight * cell_p, weight, water])
    inflow, total, gained = gathered_sum(left_seg_ref, hot_ref, 3, rows)
    before, after = chain_ends(slot_ref, ROW_ENDS, members)
    new_frac, new_sat = frac_step(frac, sat, load_segs(aperture_ref), before, after, inflow, total, gained)
    new_ref[0] = new_frac
    new_ref[1] = new_sat
    table = table_of([new_frac, new_sat])
    ends = ends_of(new_frac)
    ends = jnp.where(iota((1, LANES), 1) < LANES // 2, ends[:, :LANES], ends[:, SEG_COLUMNS - LANES :])
    for s in range(members):
        seg_p, seg_s = seg_gather(slot_ref, hot_ref, rows, s, width, table)
        own_ref[s, 0:1, :] = seg_p
        own_ref[s, 1:2, :] = seg_s
        at = (g * members + s) * size
        send_slots(out_ref, at, seg_p, seg_s)
        out_ref[at + size - 1] = ends
    for o in range(members):
        row, lane = seg_parts(sent_ref, o)
        table = table_of([slot_ref[o, SUB : SUB + rows, :], slot_ref[o, SUB + rows :, :]])
        seg_p, seg_s = pick(table, 2, rows, row, one_hot(lane, SEG_COLUMNS))
        found_ref[o, 0:1, :] = seg_p
        found_ref[o, 1:2, :] = seg_s
    pressure = state_ref[0]
    new_saturation, q, inv = cell_update(
        members,
        0,
        cell_hot_ref,
        cell_row_hot_ref,
        sent_ref,
        lambda o: (sent_ref[o, ROW_P : ROW_P + 1, :], sent_ref[o, ROW_S : ROW_S + 1, :]),
        lambda o: (found_ref[o, 0:1, :], found_ref[o, 1:2, :]),
        pressure,
        state_ref[1],
        perm_ref[...],
        left_ref,
    )
    keep_ref[0] = pressure
    keep_ref[1] = new_saturation
    keep_ref[2] = q
    keep_ref[3] = inv
    send_halo(out_ref, q, inv, pressure, groups, members, size)


def cell_gather(members, cell_ref, hot_ref, fields, put):
    rows, columns = fields[0].shape
    width = cell_ref.shape[1]
    table = table_of(fields)
    for o in range(members):
        row, _ = cell_parts(cell_ref[o : o + 1, :], columns)
        put(o, *pick(table, len(fields), rows, row, hot_ref[:, o * width : (o + 1) * width]))


def middle_kernel(
    groups, members, size, halo_ref, cell_ref, hot_ref, row_hot_ref, sent_ref, kept_ref, perm_ref,
    out_ref, keep_ref, slots_ref, left_ref, *scratch,
):
    saturation = kept_ref[1]
    g = lax.axis_index("grp")

    def put_s(o, cell_s):
        slots_ref[o, 1:2, :] = cell_s

    cell_gather(members, cell_ref, hot_ref, [saturation], put_s)
    chebyshev(
        halo_ref, kept_ref.at[2], kept_ref.at[3], kept_ref.at[0], keep_ref.at[0], scratch, groups, members, size
    )
    pressure = keep_ref[0]

    def put_p(o, cell_p):
        slots_ref[o, 0:1, :] = cell_p
        send_slots(out_ref, (g * members + o) * size, cell_p, slots_ref[o, 1:2, :])

    cell_gather(members, cell_ref, hot_ref, [pressure], put_p)
    new_saturation, q, inv = cell_update(
        members,
        1,
        hot_ref,
        row_hot_ref,
        sent_ref,
        lambda o: (slots_ref[o, 0:1, :], slots_ref[o, 1:2, :]),
        lambda o: got_slots(halo_ref, (g * members + o) * size, cell_ref.shape[1]),
        pressure,
        saturation,
        perm_ref[...],
        left_ref,
    )
    keep_ref[1] = new_saturation
    keep_ref[2] = q
    keep_ref[3] = inv
    send_halo(out_ref, q, inv, pressure, groups, members, size)


def owner_update(
    members, t, slot_ref, cell_rows, seg_rows, frac, sat, aperture, ends, hot_ref, row_hot_ref, left_ref
):
    rows = frac.shape[0]
    for s in range(members):
        cell_p, cell_s = cell_rows(s)
        weight, water = flow(
            slot_ref[s, ROW_TRANS : ROW_TRANS + 1, :],
            slot_ref[s, ROW_UP + t : ROW_UP + t + 1, :],
            cell_p,
            cell_s,
            *seg_rows(s),
        )
        spread(left_ref, row_hot_ref, s, [weight * cell_p, weight, water])
    inflow, total, gained = gathered_sum(left_ref, hot_ref, 3, rows)
    return frac_step(frac, sat, aperture, *ends, inflow, total, gained)


def exchange_kernel(
    groups, members, size, halo_ref, cell_ref, cell_hot_ref, slot_ref, hot_ref, row_hot_ref, ends_ref, own_ref,
    frac_ref, aperture_ref, kept_ref, out_ref, new_ref, pressure_ref, left_ref, *scratch,
):
    width = slot_ref.shape[2]
    rows = frac_ref.shape[1]
    g = lax.axis_index("grp")

    def cell_rows(s):
        return got_slots(halo_ref, (g * members + s) * size, width)

    me = lax.axis_index("frac")
    prior = ends_ref[(g * members + jnp.maximum(me - 1, 0)) * size + size - 1]
    later = ends_ref[(g * members + jnp.minimum(me + 1, members - 1)) * size + size - 1]
    before = jnp.where(me > 0, prior[:, LANES - 1 :], 0.0)
    after = jnp.where(me < members - 1, later[:, 0:1], 0.0)

    new_frac, new_sat = owner_update(
        members,
        1,
        slot_ref,
        cell_rows,
        lambda s: (own_ref[s, 0:1, :], own_ref[s, 1:2, :]),
        frac_ref[0],
        frac_ref[1],
        load_segs(aperture_ref),
        (before, after),
        hot_ref,
        row_hot_ref,
        left_ref,
    )
    new_ref[0] = new_frac
    new_ref[1] = new_sat
    table = table_of([new_frac, new_sat])
    ends = ends_of(new_frac)
    for s in range(members):
        seg_p, seg_s = seg_gather(slot_ref, hot_ref, rows, s, width, table)
        out_ref[s, 2:3, :] = seg_p
        out_ref[s, 3:4, :] = seg_s
        out_ref[s, 4:5, :] = ends

    chebyshev(
        halo_ref, kept_ref.at[2], kept_ref.at[3], kept_ref.at[0], pressure_ref, scratch, groups, members, size
    )
    pressure = pressure_ref[...]

    def put(o, cell_p, cell_s):
        out_ref[o, 0:1, :] = cell_p
        out_ref[o, 1:2, :] = cell_s

    cell_gather(members, cell_ref, cell_hot_ref, [pressure, kept_ref[1]], put)


def source_last_kernel(
    groups, members, size, hot_ref, row_hot_ref, sent_ref, own_ref, seg_ref, pressure_ref, kept_ref, perm_ref,
    out_ref, keep_ref, left_ref,
):
    pressure = pressure_ref[...]
    new_saturation, q, inv = cell_update(
        members,
        2,
        hot_ref,
        row_hot_ref,
        sent_ref,
        lambda o: (own_ref[o, 0:1, :], own_ref[o, 1:2, :]),
        lambda o: (seg_ref[o, 2:3, :], seg_ref[o, 3:4, :]),
        pressure,
        kept_ref[1],
        perm_ref[...],
        left_ref,
    )
    keep_ref[0] = new_saturation
    keep_ref[1] = q
    keep_ref[2] = inv
    send_halo(out_ref, q, inv, pressure, groups, members, size)


def owner_last_kernel(
    members, slot_ref, hot_ref, row_hot_ref, own_ref, seg_ref, frac_ref, aperture_ref, out_ref, left_ref
):
    new_frac, new_sat = owner_update(
        members,
        2,
        slot_ref,
        lambda s: (seg_ref[s, 0:1, :], seg_ref[s, 1:2, :]),
        lambda s: (own_ref[s, 2:3, :], own_ref[s, 3:4, :]),
        frac_ref[0],
        frac_ref[1],
        load_segs(aperture_ref),
        chain_ends(seg_ref, 4, members),
        hot_ref,
        row_hot_ref,
        left_ref,
    )
    store_segs(out_ref, 0, new_frac)
    store_segs(out_ref, 1, new_sat)


def final_kernel(groups, members, size, halo_ref, pressure_ref, kept_ref, out_ref, *scratch):
    chebyshev(
        halo_ref, kept_ref.at[1], kept_ref.at[2], pressure_ref, out_ref.at[0], scratch, groups, members, size
    )
    out_ref[1] = kept_ref[0]


VMEM = pl.BlockSpec(memory_space=pltpu.VMEM)
HBM = pl.BlockSpec(memory_space=pltpu.HBM)


def call(kernel, statics, outs, scratch, *args, spec=VMEM):
    outs = [o if hasattr(o, "dtype") else jax.ShapeDtypeStruct(o, F32) for o in outs]
    return pl.pallas_call(
        functools.partial(kernel, *statics),
        out_shape=outs,
        in_specs=[spec] * len(args),
        out_specs=[VMEM] * len(outs),
        scratch_shapes=scratch,
        compiler_params=pltpu.CompilerParams(vmem_limit_bytes=32 * 1024 * 1024),
        name=kernel.__name__,
    )(*args)


def on_device(
    matrix_state,
    matrix_perm,
    frac_state,
    frac_aperture,
    link_cell,
    link_seg,
    link_trans,
    link_count,
    link_upwind,
):
    groups, members = lax.axis_size("grp"), lax.axis_size("frac")
    devices = groups * members
    cells = link_cell[0, 0]
    width = cells.shape[1]
    _, rows, columns = matrix_state.shape
    seg_dev = frac_state.shape[2]
    seg_rows = seg_dev // LANES
    frac = frac_state.reshape(2, seg_rows, LANES)
    aperture = frac_aperture.reshape(seg_rows, LANES)

    every = members * width
    slots = (members, SUB, width)
    size = block_rows(columns, width)
    both = (groups, members, size)
    halo = (devices * size, 1, LANES)
    left_cell = pltpu.VMEM((3 * PARTS * rows, every), BF16)
    seg_wide = seg_dev // SEG_COLUMNS
    segs_wide = (2, seg_wide, SEG_COLUMNS)
    left_seg = pltpu.VMEM((3 * PARTS * seg_wide, every), BF16)
    tiles = columns // LANES + 1
    ext = [pltpu.VMEM((tiles, rows + SUB, LANES), F32)] * 4 + [pltpu.VMEM((tiles, rows + 3 * SUB, LANES), F32)] * 2

    def to_group(x):
        return lax.all_to_all(x, "frac", split_axis=0, concat_axis=0, tiled=True)

    def to_all(x):
        return lax.all_to_all(x, ("grp", "frac"), split_axis=0, concat_axis=0, tiled=True)

    def hots(*sizes):
        return [jax.ShapeDtypeStruct((n, every), BF16) for n in sizes]

    sent, cell_hot, cell_row_hot = call(
        first_kernel,
        (members,),
        [(members, SUB + 2 * seg_wide, SEG_COLUMNS)] + hots(columns, rows),
        [
            pltpu.VMEM((members, width), jnp.int32),
            pltpu.VMEM((members, width), jnp.int32),
            pltpu.VMEM((members, width), F32),
            pltpu.SMEM((1, members), jnp.int32),
            pltpu.VMEM((ITERS, members, width), jnp.int32),
            pltpu.VMEM(matrix_state.shape, F32),
            pltpu.VMEM(frac.shape, F32),
            pltpu.SemaphoreType.DMA((7,)),
        ],
        *[
            pltpu.with_memory_space_constraint(x, pltpu.HBM)
            for x in (
                cells, link_seg[0, 0], link_trans[0, 0], link_count[0], link_upwind[:, 0, 0], matrix_state, frac
            )
        ],
        spec=HBM,
    )
    slot = to_group(sent)
    edge, kept, own, frac1, hot, row_hot = call(
        start_kernel,
        both,
        [halo, (4, rows, columns), (members, 2, width), segs_wide] + hots(SEG_COLUMNS, seg_wide),
        [left_seg, left_cell, pltpu.VMEM((members, 2, width), F32)],
        slot, sent, cell_hot, cell_row_hot, frac, aperture, matrix_state, matrix_perm,
    )
    before = to_all(edge)
    edge, kept = call(
        middle_kernel, both, [halo, (4, rows, columns)], [pltpu.VMEM((members, 2, width), F32), left_cell] + ext,
        before, cells, cell_hot, cell_row_hot, sent, kept, matrix_perm,
    )
    around = to_all(edge)
    own, frac2, pressure = call(
        exchange_kernel, both, [slots, segs_wide, (rows, columns)], [left_seg] + ext,
        around, cells, cell_hot, slot, hot, row_hot, before, own, frac1, aperture, kept,
    )
    segs = to_group(own)
    edge, kept = call(
        source_last_kernel, both, [halo, (3, rows, columns)], [left_cell],
        cell_hot, cell_row_hot, sent, own, segs, pressure, kept, matrix_perm,
    )
    around = to_all(edge)
    (frac3,) = call(
        owner_last_kernel, (members,), [frac.shape], [left_seg], slot, hot, row_hot, own, segs, frac2, aperture
    )
    (matrix_out,) = call(final_kernel, both, [matrix_state.shape], ext, around, pressure, kept)
    return matrix_out, frac3.reshape(frac_state.shape)


def solution(mesh):
    return jax.shard_map(
        on_device,
        mesh=mesh,
        in_specs=(
            P(None, "grp", "frac"),
            P("grp", "frac"),
            P(None, "grp", "frac"),
            P("grp", "frac"),
            P("grp", "frac", None, None),
            P("grp", "frac", None, None),
            P("grp", "frac", None, None),
            P("grp", "frac", None),
            P(None, "grp", "frac", None, None),
        ),
        out_specs=(P(None, "grp", "frac"), P(None, "grp", "frac")),
        check_vma=False,
    )
```

```python
import functools

import jax
import jax.numpy as jnp
from jax import lax
from jax.experimental import pallas as pl
from jax.experimental.pallas import tpu as pltpu
from jax.sharding import PartitionSpec as P

ITERS = 3
SWEEPS = 4

LOW_BOUND = 0.02
HIGH_BOUND = 1.98
TAU_STEP = 0.5
MOBILITY_FLOOR = 0.2

F32 = jnp.float32
BF16 = jnp.bfloat16
LANES = 128
SUB = 8
SEG_COLUMNS = 2 * LANES
DEPTH = SWEEPS - 1


def iota(shape, dim):
    return lax.broadcasted_iota(jnp.int32, shape, dim)


def parts_of(x):
    high = x.astype(BF16).astype(F32)
    return high, x - high


PARTS = 2


def table_of(fields):
    split = [parts_of(f) for f in fields]
    return jnp.concatenate([s[p] for p in range(PARTS) for s in split], axis=0).astype(BF16)


def one_hot(index_row, count):
    shape = (count, index_row.shape[1])
    hit = iota(shape, 0).astype(F32).astype(BF16) == index_row.astype(F32).astype(BF16)
    return jnp.where(hit, jnp.ones(shape, BF16), jnp.zeros(shape, BF16))


def pick(table, fields, rows, row_index, hot):
    wide = jnp.dot(table, hot, preferred_element_type=F32)
    hit = iota((rows, row_index.shape[1]), 0) == row_index
    found = []
    for f in range(fields):
        total = sum(wide[(p * fields + f) * rows : (p * fields + f + 1) * rows] for p in range(PARTS))
        found.append(jnp.sum(jnp.where(hit, total, 0.0), axis=0, keepdims=True))
    return found


def spread(left_ref, row_hot_ref, block, values):
    rows = row_hot_ref.shape[0]
    width = values[0].shape[1]
    at = slice(block * width, (block + 1) * width)
    hot = row_hot_ref[:, at]
    for f, value in enumerate(values):
        for p, part in enumerate(parts_of(value)):
            row = (p * len(values) + f) * rows
            left_ref[row : row + rows, at] = hot * part.astype(BF16)


def gathered_sum(left_ref, hot_ref, fields, rows):
    wide = lax.dot_general(
        left_ref[...], hot_ref[...], (((1,), (1,)), ((), ())), preferred_element_type=F32
    )
    return [
        sum(wide[(p * fields + f) * rows : (p * fields + f + 1) * rows] for p in range(PARTS))
        for f in range(fields)
    ]


def flow(trans, upwind, cell_p, cell_s, seg_p, seg_s):
    u = jnp.where(upwind > 0.5, cell_s, seg_s)
    weight = trans * (MOBILITY_FLOOR + u * u)
    water = weight * (cell_p - seg_p) * u
    return weight, water


def cell_parts(cell_row, columns):
    return cell_row // columns, cell_row % columns


def load_segs(ref, *lead):
    rows = ref.shape[-2] // 2
    return jnp.concatenate([ref[(*lead, pl.ds(h, rows, 2), slice(None))] for h in range(2)], axis=1)


def store_segs(ref, lead, value):
    rows = value.shape[0]
    for h in range(2):
        ref[lead, pl.ds(h, rows, 2), :] = value[:, h * LANES : (h + 1) * LANES]


def ends_of(frac):
    rows, columns = frac.shape
    lane = iota((1, columns), 1)
    return jnp.where(lane < columns // 2, frac[0:1], frac[rows - 1 : rows])


def frac_step(frac, sat, aperture, before, after, inflow, total, gained):
    rows, lanes = frac.shape
    row, lane = iota((rows, lanes), 0), iota((rows, lanes), 1)
    back = pltpu.roll(frac, 1, 1)
    left = jnp.where(lane == 0, pltpu.roll(back, 1, 0), back)
    left = jnp.where((lane == 0) & (row == 0), before, left)
    ahead = pltpu.roll(frac, lanes - 1, 1)
    right = jnp.where(lane == lanes - 1, pltpu.roll(ahead, rows - 1, 0), ahead)
    right = jnp.where((lane == lanes - 1) & (row == rows - 1), after, right)
    new_frac = (aperture * frac + inflow + left + right) / (aperture + total + 2.0)
    new_sat = sat + TAU_STEP * gained / (aperture + total)
    return new_frac, new_sat


def chain_ends(ends_ref, row, members):
    me = lax.axis_index("frac")
    lanes = ends_ref.shape[2]
    prior = ends_ref[jnp.maximum(me - 1, 0), row : row + 1, :]
    later = ends_ref[jnp.minimum(me + 1, members - 1), row : row + 1, :]
    before = jnp.where(me > 0, prior[:, lanes - 1 :], 0.0)
    after = jnp.where(me < members - 1, later[:, 0:1], 0.0)
    return before, after


def partial_residual(pressure, couple, source, inverse):
    rows, columns = pressure.shape
    row, col = iota((rows, columns), 0), iota((rows, columns), 1)
    beside = jnp.where(row == 0, 0.0, pltpu.roll(pressure, 1, 0))
    beside += jnp.where(row == rows - 1, 0.0, pltpu.roll(pressure, rows - 1, 0))
    beside += jnp.where(col == 0, 0.0, pltpu.roll(pressure, 1, 1))
    beside += jnp.where(col == columns - 1, 0.0, pltpu.roll(pressure, columns - 1, 1))
    return inverse * (source - (4.0 + couple) * pressure + beside)


def pack_low(q, inv, p, at, axis):
    return jnp.where(
        at < DEPTH, q, jnp.where(at < 2 * DEPTH, pltpu.roll(inv, DEPTH, axis), pltpu.roll(p, 2 * DEPTH, axis))
    )


def pack_high(q, inv, p, at, axis):
    size = q.shape[axis]
    return jnp.where(
        at >= size - DEPTH,
        q,
        jnp.where(
            at >= size - 2 * DEPTH,
            pltpu.roll(inv, size - DEPTH, axis),
            pltpu.roll(p, size - 2 * DEPTH, axis),
        ),
    )


def block_rows(columns, width):
    vertical = 2 * DEPTH * (columns // LANES) + 1
    lateral = SUB + 2 * (width // LANES) + 1
    return max(vertical, lateral)


def put_rows(out_ref, at, values):
    for k in range(values.shape[0]):
        out_ref[at + k] = values[k : k + 1]


def get_rows(in_ref, at, count):
    return jnp.concatenate([in_ref[at + k] for k in range(count)], axis=0)


def send_slots(out_ref, at, first, second):
    halves = first.shape[1] // LANES
    for i, value in enumerate((first, second)):
        for h in range(halves):
            out_ref[at + SUB + i * halves + h] = value[:, h * LANES : (h + 1) * LANES]


def got_slots(in_ref, at, width):
    halves = width // LANES
    return [
        jnp.concatenate([in_ref[at + SUB + i * halves + h] for h in range(halves)], axis=1) for i in range(2)
    ]


def send_halo(out_ref, q, inv, p, groups, members, size):
    rows, columns = q.shape
    halves = columns // LANES
    g, f = lax.axis_index("grp"), lax.axis_index("frac")
    here = g * members + f
    lane = iota((rows, LANES), 1)
    low = pack_low(q[:, :LANES], inv[:, :LANES], p[:, :LANES], lane, 1)
    high = pack_high(q[:, columns - LANES :], inv[:, columns - LANES :], p[:, columns - LANES :], lane, 1)
    turned = jnp.transpose(jnp.where(lane < LANES // 2, low, high))
    left, right = turned[:SUB], turned[LANES - SUB :]
    lane = iota((1, LANES), 1)
    spare = jnp.where(g + 2 < groups, here + 2 * members, here - 2 * members)

    for step in (-1, 1):
        layer = (lambda k: k) if step < 0 else (lambda k: rows - 1 - k)

        def span(field, count, at):
            start = 0 if step < 0 else rows - count
            return field[start : start + count, at]

        inside = (g + step >= 0) & (g + step < groups)
        base = here + step * members
        tiles = [slice(h * LANES, (h + 1) * LANES) for h in range(halves)]

        at = jnp.where(inside, base, spare) * size
        for h, tile in enumerate(tiles):
            put_rows(out_ref, at + h * DEPTH, span(q, DEPTH, tile))
            put_rows(out_ref, at + halves * DEPTH + h * (DEPTH - 1), span(inv, DEPTH - 1, tile))
            put_rows(out_ref, at + halves * (2 * DEPTH - 1) + h, span(p, 1, tile))
        deep, next_p = layer(DEPTH - 1), layer(1)
        extra = jnp.where(
            lane == 0,
            inv[deep : deep + 1, tiles[0]],
            jnp.where(
                lane == LANES - 1,
                inv[deep : deep + 1, tiles[-1]],
                jnp.where(
                    lane == 1,
                    pltpu.roll(p[next_p : next_p + 1, tiles[0]], 1, 1),
                    pltpu.roll(p[next_p : next_p + 1, tiles[-1]], LANES - 1, 1),
                ),
            ),
        )
        out_ref[at + halves * 2 * DEPTH] = extra

        for side, tile, there in ((-1, tiles[0], f > 0), (1, tiles[-1], f < members - 1)):
            at = jnp.where(inside & there, base + side, spare) * size
            for i, field in enumerate((q, inv, p)):
                put_rows(out_ref, at + i * DEPTH, span(field, DEPTH, tile))

    put_rows(out_ref, jnp.where(f > 0, here - 1, spare) * size, left)
    put_rows(out_ref, jnp.where(f < members - 1, here + 1, spare) * size, right)


def chebyshev(in_ref, q_ref, inv_ref, p_ref, target, scratch, groups, members, size):
    q_ext, inv_ext, p_ext, update_ref, even_ref, odd_ref = scratch
    rows, columns = target.shape
    halves = columns // LANES
    side = halves
    g, f = lax.axis_index("grp"), lax.axis_index("frac")
    here = g * members + f
    last = groups * members - 1

    def taker(dg, df):
        ok = (g + dg >= 0) & (g + dg < groups) & (f + df >= 0) & (f + df < members)
        at = jnp.clip(here + dg * members + df, 0, last) * size
        return lambda start, count: jnp.where(ok, get_rows(in_ref, at + start, count), 0.0)

    def both(low, high, at, count, size):
        return jnp.where(at < count, low, jnp.where(at >= size - count, high, 0.0))

    def filler(count):
        return jnp.zeros((count, LANES), F32)

    for h in range(halves):
        for ext, ref in ((q_ext, q_ref), (inv_ext, inv_ref), (p_ext, p_ref)):
            ext[h, 0:rows, :] = ref[:, h * LANES : (h + 1) * LANES]
    outer = slice(rows, rows + SUB)
    below, above = taker(1, 0), taker(-1, 0)
    lane = iota((1, LANES), 1)
    low_extra, high_extra = below(halves * 2 * DEPTH, 1), above(halves * 2 * DEPTH, 1)
    for h in range(halves):
        edge = (lane == 0) & (h == 0) | (lane == LANES - 1) & (h == halves - 1)

        def at_edge(row, turn):
            return jnp.where(edge, pltpu.roll(row, turn, 1) if turn else row, 0.0)

        turn = LANES - 1 if h == 0 else 1
        at = h * DEPTH
        q_ext[h, outer, :] = jnp.concatenate(
            [below(at, DEPTH), filler(SUB - 2 * DEPTH), above(at, DEPTH)], axis=0
        )
        at = halves * DEPTH + h * (DEPTH - 1)
        inv_ext[h, outer, :] = jnp.concatenate(
            [
                below(at, DEPTH - 1),
                at_edge(low_extra, 0),
                filler(SUB - 2 * DEPTH),
                at_edge(high_extra, 0),
                above(at, DEPTH - 1),
            ],
            axis=0,
        )
        at = halves * (2 * DEPTH - 1) + h
        p_ext[h, outer, :] = jnp.concatenate(
            [
                below(at, 1),
                at_edge(low_extra, turn),
                filler(SUB - 4),
                at_edge(high_extra, turn),
                above(at, 1),
            ],
            axis=0,
        )
    right, left = taker(0, 1)(0, SUB), taker(0, -1)(0, SUB)
    turned = jnp.transpose(
        jnp.concatenate([right, jnp.zeros((LANES - 2 * SUB, rows), F32), left], axis=0)
    )
    lane = iota((rows, LANES), 1)
    q_ext[side, 0:rows, :] = both(turned, turned, lane, DEPTH, LANES)
    inv_ext[side, 0:rows, :] = both(
        pltpu.roll(turned, LANES - DEPTH, 1), pltpu.roll(turned, DEPTH, 1), lane, DEPTH, LANES
    )
    p_ext[side, 0:rows, :] = both(
        pltpu.roll(turned, LANES - 2 * DEPTH, 1), pltpu.roll(turned, 2 * DEPTH, 1), lane, 2, LANES
    )
    lane = iota((DEPTH, LANES), 1)
    low_right, low_left, high_right, high_left = taker(1, 1), taker(1, -1), taker(-1, 1), taker(-1, -1)
    for i, ext in enumerate((q_ext, inv_ext, p_ext)):
        at = i * DEPTH
        ext[side, outer, :] = jnp.concatenate(
            [
                both(low_right(at, DEPTH), low_left(at, DEPTH), lane, DEPTH, LANES),
                filler(SUB - 2 * DEPTH),
                both(high_right(at, DEPTH), high_left(at, DEPTH), lane, DEPTH, LANES),
            ],
            axis=0,
        )

    end = rows + SUB - 1
    for own, other in ((0, end), (end, 0), (rows - 1, rows), (rows, rows - 1)):
        for c in range(halves + 1):
            q_ext[c, own : own + 1, :] += inv_ext[c, own : own + 1, :] * p_ext[c, other : other + 1, :]
    centre = 0.5 * (HIGH_BOUND + LOW_BOUND)
    half_width = 0.5 * (HIGH_BOUND - LOW_BOUND)
    scale_ratio = centre / half_width
    ratio_now = 1.0 / scale_ratio
    lane = iota((SUB, LANES), 1)
    count = rows // SUB + 1

    def keep(ref, c, r, value):
        at = (r + 1) * SUB
        ref[c, at : at + SUB, :] = value
        if r == count - 1:
            ref[c, 0:SUB, :] = value
        if r == 0:
            at = (count + 1) * SUB
            ref[c, at : at + SUB, :] = value

    for r in range(count):
        at = slice(r * SUB, (r + 1) * SUB)
        p_side, p_first, p_final = p_ext[side, at, :], p_ext[0, at, :], p_ext[halves - 1, at, :]
        missing = [0.0] * (halves + 1)
        missing[0] += jnp.where(lane == 0, pltpu.roll(p_side, 1, 1), 0.0)
        missing[halves - 1] += jnp.where(lane == LANES - 1, pltpu.roll(p_side, LANES - 1, 1), 0.0)
        missing[side] = jnp.where(
            lane == 0,
            pltpu.roll(p_final, 1, 1),
            jnp.where(lane == LANES - 1, pltpu.roll(p_first, LANES - 1, 1), 0.0),
        )
        for c in range(halves + 1):
            start = q_ext[c, at, :] + inv_ext[c, at, :] * missing[c]
            q_ext[c, at, :] = start
            keep(even_ref, c, r, start / centre if centre != 1.0 else start)
    now_ref, next_ref = even_ref, odd_ref
    for sweep in range(1, SWEEPS):
        ratio_next = 1.0 / (2.0 * scale_ratio - ratio_now)
        final = sweep == SWEEPS - 1
        for r in range(count - 1 if final else count):
            at = slice(r * SUB, (r + 1) * SUB)
            mids = [now_ref[c, (r + 1) * SUB : (r + 2) * SUB, :] for c in range(halves + 1)]
            after = [pltpu.roll(m, 1, 1) for m in mids]
            ahead = [pltpu.roll(m, LANES - 1, 1) for m in mids]
            for c in range(halves if final else halves + 1):
                beside = now_ref[c, (r + 1) * SUB - 1 : (r + 2) * SUB - 1, :]
                beside += now_ref[c, (r + 1) * SUB + 1 : (r + 2) * SUB + 1, :]
                beside += jnp.where(lane == 0, after[(c - 1) % (halves + 1)], after[c])
                beside += jnp.where(lane == LANES - 1, ahead[(c + 1) % (halves + 1)], ahead[c])
                residual = q_ext[c, at, :] - mids[c] + inv_ext[c, at, :] * beside
                old = mids[c] if sweep == 1 else update_ref[c, at, :]
                update = ratio_next * ratio_now * old + (2.0 * ratio_next / half_width) * residual
                if final:
                    tile = slice(c * LANES, (c + 1) * LANES)
                    target[at, tile] = p_ref[at, tile] + mids[c] + update
                else:
                    update_ref[c, at, :] = update
                    keep(next_ref, c, r, mids[c] + update)
        ratio_now = ratio_next
        now_ref, next_ref = next_ref, now_ref


ROW_SEG = 0
ROW_TRANS = 1
ROW_UP = 2
ROW_P = ROW_UP + ITERS
ROW_S = ROW_P + 1
ROW_ENDS = ROW_S + 1


def first_kernel(
    members, cell_any, seg_any, trans_any, count_any, up_any, state_any, frac_any,
    out_ref, hot_ref, row_hot_ref, cell_ref, seg_ref, trans_ref, count_ref, up_ref, state_ref, frac_ref, sem,
):
    _, rows, columns = state_ref.shape
    width = cell_ref.shape[1]
    copies = [
        pltpu.make_async_copy(source, target, sem.at[i])
        for i, (source, target) in enumerate(
            [
                (cell_any, cell_ref),
                (state_any, state_ref),
                (seg_any, seg_ref),
                (trans_any, trans_ref),
                (count_any, count_ref),
                (up_any, up_ref),
                (frac_any, frac_ref),
            ]
        )
    ]
    for copy in copies:
        copy.start()
    copies[0].wait()
    for o in range(members):
        row, col = cell_parts(cell_ref[o : o + 1, :], columns)
        at = slice(o * width, (o + 1) * width)
        hot_ref[:, at] = one_hot(col, columns)
        row_hot_ref[:, at] = one_hot(row, rows)
    copies[1].wait()
    table = table_of([state_ref[0], state_ref[1]])
    for copy in copies[2:]:
        copy.wait()
    frac = load_segs(frac_ref, 0)
    ends = ends_of(frac)
    whole = jnp.concatenate([frac, load_segs(frac_ref, 1)], axis=0)
    for o in range(members):
        one = slice(o, o + 1)
        row, _ = cell_parts(cell_ref[one, :], columns)
        cell_p, cell_s = pick(table, 2, rows, row, hot_ref[:, o * width : (o + 1) * width])
        live = iota((1, width), 1) < count_ref[0, o]
        out_ref[o, ROW_SEG : ROW_SEG + 1, :] = seg_ref[one, :].astype(F32)
        out_ref[o, ROW_TRANS : ROW_TRANS + 1, :] = jnp.where(live, trans_ref[one, :], 0.0)
        for t in range(ITERS):
            out_ref[o, ROW_UP + t : ROW_UP + t + 1, :] = up_ref[t, one, :].astype(F32)
        out_ref[o, ROW_P : ROW_P + 1, :] = cell_p
        out_ref[o, ROW_S : ROW_S + 1, :] = cell_s
        out_ref[o, ROW_ENDS : ROW_ENDS + 1, :] = ends
        out_ref[o, SUB:, :] = whole


def seg_parts(slot_ref, s):
    seg = slot_ref[s, ROW_SEG : ROW_SEG + 1, :].astype(jnp.int32)
    return seg // SEG_COLUMNS, seg % SEG_COLUMNS


def seg_hots(slot_ref, hot_ref, row_hot_ref, members, width):
    for s in range(members):
        row, lane = seg_parts(slot_ref, s)
        at = slice(s * width, (s + 1) * width)
        hot_ref[:, at] = one_hot(lane, SEG_COLUMNS)
        row_hot_ref[:, at] = one_hot(row, row_hot_ref.shape[0])


def seg_gather(slot_ref, hot_ref, fields, s, width, table):
    return pick(table, 2, fields, seg_parts(slot_ref, s)[0], hot_ref[:, s * width : (s + 1) * width])


def cell_update(
    members, t, hot_ref, row_hot_ref, sent_ref, cell_rows, seg_rows, pressure, saturation, perm, left_ref
):
    rows = pressure.shape[0]
    for o in range(members):
        seg_p, seg_s = seg_rows(o)
        cell_p, cell_s = cell_rows(o)
        weight, water = flow(
            sent_ref[o, ROW_TRANS : ROW_TRANS + 1, :],
            sent_ref[o, ROW_UP + t : ROW_UP + t + 1, :],
            cell_p,
            cell_s,
            seg_p,
            seg_s,
        )
        spread(left_ref, row_hot_ref, o, [weight, weight * seg_p, water])
    couple, source, lost = gathered_sum(left_ref, hot_ref, 3, rows)
    inverse = 1.0 / (4.0 + perm + couple)
    new_saturation = saturation - TAU_STEP * lost / (perm + couple)
    return new_saturation, partial_residual(pressure, couple, source, inverse), inverse


def start_kernel(
    groups, members, size, slot_ref, sent_ref, cell_hot_ref, cell_row_hot_ref, frac_ref, aperture_ref,
    state_ref, perm_ref, out_ref, keep_ref, own_ref, new_ref, hot_ref, row_hot_ref,
    left_seg_ref, left_ref, found_ref,
):
    width = slot_ref.shape[2]
    rows = new_ref.shape[1]
    g = lax.axis_index("grp")
    frac, sat = load_segs(frac_ref, 0), load_segs(frac_ref, 1)
    seg_hots(slot_ref, hot_ref, row_hot_ref, members, width)
    table = table_of([frac, sat])
    for s in range(members):
        seg_p, seg_s = seg_gather(slot_ref, hot_ref, rows, s, width, table)
        cell_p = slot_ref[s, ROW_P : ROW_P + 1, :]
        weight, water = flow(
            slot_ref[s, ROW_TRANS : ROW_TRANS + 1, :],
            slot_ref[s, ROW_UP : ROW_UP + 1, :],
            cell_p,
            slot_ref[s, ROW_S : ROW_S + 1, :],
            seg_p,
            seg_s,
        )
        spread(left_seg_ref, row_hot_ref, s, [weight * cell_p, weight, water])
    inflow, total, gained = gathered_sum(left_seg_ref, hot_ref, 3, rows)
    before, after = chain_ends(slot_ref, ROW_ENDS, members)
    new_frac, new_sat = frac_step(frac, sat, load_segs(aperture_ref), before, after, inflow, total, gained)
    new_ref[0] = new_frac
    new_ref[1] = new_sat
    table = table_of([new_frac, new_sat])
    ends = ends_of(new_frac)
    ends = jnp.where(iota((1, LANES), 1) < LANES // 2, ends[:, :LANES], ends[:, SEG_COLUMNS - LANES :])
    for s in range(members):
        seg_p, seg_s = seg_gather(slot_ref, hot_ref, rows, s, width, table)
        own_ref[s, 0:1, :] = seg_p
        own_ref[s, 1:2, :] = seg_s
        at = (g * members + s) * size
        send_slots(out_ref, at, seg_p, seg_s)
        out_ref[at + size - 1] = ends
    for o in range(members):
        row, lane = seg_parts(sent_ref, o)
        table = table_of([slot_ref[o, SUB : SUB + rows, :], slot_ref[o, SUB + rows :, :]])
        seg_p, seg_s = pick(table, 2, rows, row, one_hot(lane, SEG_COLUMNS))
        found_ref[o, 0:1, :] = seg_p
        found_ref[o, 1:2, :] = seg_s
    pressure = state_ref[0]
    new_saturation, q, inv = cell_update(
        members,
        0,
        cell_hot_ref,
        cell_row_hot_ref,
        sent_ref,
        lambda o: (sent_ref[o, ROW_P : ROW_P + 1, :], sent_ref[o, ROW_S : ROW_S + 1, :]),
        lambda o: (found_ref[o, 0:1, :], found_ref[o, 1:2, :]),
        pressure,
        state_ref[1],
        perm_ref[...],
        left_ref,
    )
    keep_ref[0] = pressure
    keep_ref[1] = new_saturation
    keep_ref[2] = q
    keep_ref[3] = inv
    send_halo(out_ref, q, inv, pressure, groups, members, size)


def cell_gather(members, cell_ref, hot_ref, fields, put):
    rows, columns = fields[0].shape
    width = cell_ref.shape[1]
    table = table_of(fields)
    for o in range(members):
        row, _ = cell_parts(cell_ref[o : o + 1, :], columns)
        put(o, *pick(table, len(fields), rows, row, hot_ref[:, o * width : (o + 1) * width]))


def middle_kernel(
    groups, members, size, halo_ref, cell_ref, hot_ref, row_hot_ref, sent_ref, kept_ref, perm_ref,
    out_ref, keep_ref, slots_ref, left_ref, *scratch,
):
    saturation = kept_ref[1]
    g = lax.axis_index("grp")

    def put_s(o, cell_s):
        slots_ref[o, 1:2, :] = cell_s

    cell_gather(members, cell_ref, hot_ref, [saturation], put_s)
    chebyshev(
        halo_ref, kept_ref.at[2], kept_ref.at[3], kept_ref.at[0], keep_ref.at[0], scratch, groups, members, size
    )
    pressure = keep_ref[0]

    def put_p(o, cell_p):
        slots_ref[o, 0:1, :] = cell_p
        send_slots(out_ref, (g * members + o) * size, cell_p, slots_ref[o, 1:2, :])

    cell_gather(members, cell_ref, hot_ref, [pressure], put_p)
    new_saturation, q, inv = cell_update(
        members,
        1,
        hot_ref,
        row_hot_ref,
        sent_ref,
        lambda o: (slots_ref[o, 0:1, :], slots_ref[o, 1:2, :]),
        lambda o: got_slots(halo_ref, (g * members + o) * size, cell_ref.shape[1]),
        pressure,
        saturation,
        perm_ref[...],
        left_ref,
    )
    keep_ref[1] = new_saturation
    keep_ref[2] = q
    keep_ref[3] = inv
    send_halo(out_ref, q, inv, pressure, groups, members, size)


def owner_spread(members, t, slot_ref, cell_rows, seg_rows, row_hot_ref, left_ref):
    for s in range(members):
        cell_p, cell_s = cell_rows(s)
        weight, water = flow(
            slot_ref[s, ROW_TRANS : ROW_TRANS + 1, :],
            slot_ref[s, ROW_UP + t : ROW_UP + t + 1, :],
            cell_p,
            cell_s,
            *seg_rows(s),
        )
        spread(left_ref, row_hot_ref, s, [weight * cell_p, weight, water])


def owner_update(
    members, t, slot_ref, cell_rows, seg_rows, frac, sat, aperture, ends, hot_ref, row_hot_ref, left_ref
):
    owner_spread(members, t, slot_ref, cell_rows, seg_rows, row_hot_ref, left_ref)
    inflow, total, gained = gathered_sum(left_ref, hot_ref, 3, frac.shape[0])
    return frac_step(frac, sat, aperture, *ends, inflow, total, gained)


def exchange_kernel(
    groups, members, size, halo_ref, cell_ref, cell_hot_ref, slot_ref, hot_ref, row_hot_ref, ends_ref, own_ref,
    frac_ref, aperture_ref, kept_ref, out_ref, new_ref, pressure_ref, left_ref, *scratch,
):
    width = slot_ref.shape[2]
    g = lax.axis_index("grp")

    def cell_rows(s):
        return got_slots(halo_ref, (g * members + s) * size, width)

    me = lax.axis_index("frac")
    prior = ends_ref[(g * members + jnp.maximum(me - 1, 0)) * size + size - 1]
    later = ends_ref[(g * members + jnp.minimum(me + 1, members - 1)) * size + size - 1]
    before = jnp.where(me > 0, prior[:, LANES - 1 :], 0.0)
    after = jnp.where(me < members - 1, later[:, 0:1], 0.0)

    rows, columns = pressure_ref.shape
    seg_wide = frac_ref.shape[1]
    owner_spread(
        members,
        1,
        slot_ref,
        cell_rows,
        lambda s: (own_ref[s, 0:1, :], own_ref[s, 1:2, :]),
        row_hot_ref,
        left_ref,
    )
    chebyshev(
        halo_ref, kept_ref.at[2], kept_ref.at[3], kept_ref.at[0], pressure_ref, scratch, groups, members, size
    )
    inflow, total, gained = gathered_sum(left_ref, hot_ref, 3, seg_wide)
    new_frac, new_sat = frac_step(
        frac_ref[0], frac_ref[1], load_segs(aperture_ref), before, after, inflow, total, gained
    )
    new_ref[0] = new_frac
    new_ref[1] = new_sat
    seg_table = table_of([new_frac, new_sat])
    ends = ends_of(new_frac)
    table = table_of([pressure_ref[...], kept_ref[1]])
    for o in range(members):
        at = slice(o * width, (o + 1) * width)
        row, _ = cell_parts(cell_ref[o : o + 1, :], columns)
        cell_p, cell_s = pick(table, 2, rows, row, cell_hot_ref[:, at])
        out_ref[o, 0:1, :] = cell_p
        out_ref[o, 1:2, :] = cell_s
        seg_p, seg_s = pick(seg_table, 2, seg_wide, seg_parts(slot_ref, o)[0], hot_ref[:, at])
        out_ref[o, 2:3, :] = seg_p
        out_ref[o, 3:4, :] = seg_s
        out_ref[o, 4:5, :] = ends


def source_last_kernel(
    groups, members, size, hot_ref, row_hot_ref, sent_ref, own_ref, seg_ref, pressure_ref, kept_ref, perm_ref,
    out_ref, keep_ref, left_ref,
):
    pressure = pressure_ref[...]
    new_saturation, q, inv = cell_update(
        members,
        2,
        hot_ref,
        row_hot_ref,
        sent_ref,
        lambda o: (own_ref[o, 0:1, :], own_ref[o, 1:2, :]),
        lambda o: (seg_ref[o, 2:3, :], seg_ref[o, 3:4, :]),
        pressure,
        kept_ref[1],
        perm_ref[...],
        left_ref,
    )
    keep_ref[0] = new_saturation
    keep_ref[1] = q
    keep_ref[2] = inv
    send_halo(out_ref, q, inv, pressure, groups, members, size)


def final_kernel(
    groups, members, size, halo_ref, pressure_ref, kept_ref, slot_ref, hot_ref, row_hot_ref, own_ref, seg_ref,
    frac_ref, aperture_ref, out_ref, new_ref, left_ref, *scratch,
):
    new_frac, new_sat = owner_update(
        members,
        2,
        slot_ref,
        lambda s: (seg_ref[s, 0:1, :], seg_ref[s, 1:2, :]),
        lambda s: (own_ref[s, 2:3, :], own_ref[s, 3:4, :]),
        frac_ref[0],
        frac_ref[1],
        load_segs(aperture_ref),
        chain_ends(seg_ref, 4, members),
        hot_ref,
        row_hot_ref,
        left_ref,
    )
    store_segs(new_ref, 0, new_frac)
    store_segs(new_ref, 1, new_sat)
    chebyshev(
        halo_ref, kept_ref.at[1], kept_ref.at[2], pressure_ref, out_ref.at[0], scratch, groups, members, size
    )
    out_ref[1] = kept_ref[0]


VMEM = pl.BlockSpec(memory_space=pltpu.VMEM)
HBM = pl.BlockSpec(memory_space=pltpu.HBM)


def call(kernel, statics, outs, scratch, *args, spec=VMEM):
    outs = [o if hasattr(o, "dtype") else jax.ShapeDtypeStruct(o, F32) for o in outs]
    return pl.pallas_call(
        functools.partial(kernel, *statics),
        out_shape=outs,
        in_specs=[spec] * len(args),
        out_specs=[VMEM] * len(outs),
        scratch_shapes=scratch,
        compiler_params=pltpu.CompilerParams(vmem_limit_bytes=32 * 1024 * 1024),
        name=kernel.__name__,
    )(*args)


def on_device(
    matrix_state,
    matrix_perm,
    frac_state,
    frac_aperture,
    link_cell,
    link_seg,
    link_trans,
    link_count,
    link_upwind,
):
    groups, members = lax.axis_size("grp"), lax.axis_size("frac")
    devices = groups * members
    cells = link_cell[0, 0]
    width = cells.shape[1]
    _, rows, columns = matrix_state.shape
    seg_dev = frac_state.shape[2]
    seg_rows = seg_dev // LANES
    frac = frac_state.reshape(2, seg_rows, LANES)
    aperture = frac_aperture.reshape(seg_rows, LANES)

    every = members * width
    slots = (members, SUB, width)
    size = block_rows(columns, width)
    both = (groups, members, size)
    halo = (devices * size, 1, LANES)
    left_cell = pltpu.VMEM((3 * PARTS * rows, every), BF16)
    seg_wide = seg_dev // SEG_COLUMNS
    segs_wide = (2, seg_wide, SEG_COLUMNS)
    left_seg = pltpu.VMEM((3 * PARTS * seg_wide, every), BF16)
    tiles = columns // LANES + 1
    ext = [pltpu.VMEM((tiles, rows + SUB, LANES), F32)] * 4 + [pltpu.VMEM((tiles, rows + 3 * SUB, LANES), F32)] * 2

    def to_group(x):
        return lax.all_to_all(x, "frac", split_axis=0, concat_axis=0, tiled=True)

    def to_all(x):
        return lax.all_to_all(x, ("grp", "frac"), split_axis=0, concat_axis=0, tiled=True)

    def hots(*sizes):
        return [jax.ShapeDtypeStruct((n, every), BF16) for n in sizes]

    sent, cell_hot, cell_row_hot = call(
        first_kernel,
        (members,),
        [(members, SUB + 2 * seg_wide, SEG_COLUMNS)] + hots(columns, rows),
        [
            pltpu.VMEM((members, width), jnp.int32),
            pltpu.VMEM((members, width), jnp.int32),
            pltpu.VMEM((members, width), F32),
            pltpu.SMEM((1, members), jnp.int32),
            pltpu.VMEM((ITERS, members, width), jnp.int32),
            pltpu.VMEM(matrix_state.shape, F32),
            pltpu.VMEM(frac.shape, F32),
            pltpu.SemaphoreType.DMA((7,)),
        ],
        *[
            pltpu.with_memory_space_constraint(x, pltpu.HBM)
            for x in (
                cells, link_seg[0, 0], link_trans[0, 0], link_count[0], link_upwind[:, 0, 0], matrix_state, frac
            )
        ],
        spec=HBM,
    )
    slot = to_group(sent)
    edge, kept, own, frac1, hot, row_hot = call(
        start_kernel,
        both,
        [halo, (4, rows, columns), (members, 2, width), segs_wide] + hots(SEG_COLUMNS, seg_wide),
        [left_seg, left_cell, pltpu.VMEM((members, 2, width), F32)],
        slot, sent, cell_hot, cell_row_hot, frac, aperture, matrix_state, matrix_perm,
    )
    before = to_all(edge)
    edge, kept = call(
        middle_kernel, both, [halo, (4, rows, columns)], [pltpu.VMEM((members, 2, width), F32), left_cell] + ext,
        before, cells, cell_hot, cell_row_hot, sent, kept, matrix_perm,
    )
    around = to_all(edge)
    own, frac2, pressure = call(
        exchange_kernel, both, [slots, segs_wide, (rows, columns)], [left_seg] + ext,
        around, cells, cell_hot, slot, hot, row_hot, before, own, frac1, aperture, kept,
    )
    segs = to_group(own)
    edge, kept = call(
        source_last_kernel, both, [halo, (3, rows, columns)], [left_cell],
        cell_hot, cell_row_hot, sent, own, segs, pressure, kept, matrix_perm,
    )
    around = to_all(edge)
    matrix_out, frac3 = call(
        final_kernel,
        both,
        [matrix_state.shape, frac.shape],
        [left_seg] + ext,
        around, pressure, kept, slot, hot, row_hot, own, segs, frac2, aperture,
    )
    return matrix_out, frac3.reshape(frac_state.shape)


def solution(mesh):
    return jax.shard_map(
        on_device,
        mesh=mesh,
        in_specs=(
            P(None, "grp", "frac"),
            P("grp", "frac"),
            P(None, "grp", "frac"),
            P("grp", "frac"),
            P("grp", "frac", None, None),
            P("grp", "frac", None, None),
            P("grp", "frac", None, None),
            P("grp", "frac", None),
            P(None, "grp", "frac", None, None),
        ),
        out_specs=(P(None, "grp", "frac"), P(None, "grp", "frac")),
        check_vma=False,
    )
```

```python
import functools

import jax
import jax.numpy as jnp
from jax import lax
from jax.experimental import pallas as pl
from jax.experimental.pallas import tpu as pltpu
from jax.sharding import PartitionSpec as P

ITERS = 3
SWEEPS = 4

LOW_BOUND = 0.02
HIGH_BOUND = 1.98
TAU_STEP = 0.5
MOBILITY_FLOOR = 0.2

F32 = jnp.float32
BF16 = jnp.bfloat16
LANES = 128
SUB = 8
SEG_COLUMNS = 2 * LANES
DEPTH = SWEEPS - 1


def iota(shape, dim):
    return lax.broadcasted_iota(jnp.int32, shape, dim)


def parts_of(x):
    high = x.astype(BF16).astype(F32)
    return high, x - high


PARTS = 2


def table_of(fields):
    split = [parts_of(f) for f in fields]
    return jnp.concatenate([s[p] for p in range(PARTS) for s in split], axis=0).astype(BF16)


def one_hot(index_row, count):
    shape = (count, index_row.shape[1])
    hit = iota(shape, 0).astype(F32).astype(BF16) == index_row.astype(F32).astype(BF16)
    return jnp.where(hit, jnp.ones(shape, BF16), jnp.zeros(shape, BF16))


def pick(table, fields, rows, row_index, hot):
    wide = jnp.dot(table, hot, preferred_element_type=F32)
    hit = iota((rows, row_index.shape[1]), 0) == row_index
    found = []
    for f in range(fields):
        total = sum(wide[(p * fields + f) * rows : (p * fields + f + 1) * rows] for p in range(PARTS))
        found.append(jnp.sum(jnp.where(hit, total, 0.0), axis=0, keepdims=True))
    return found


def spread(left_ref, row_hot_ref, block, values):
    rows = row_hot_ref.shape[0]
    width = values[0].shape[1]
    at = slice(block * width, (block + 1) * width)
    hot = row_hot_ref[:, at]
    for f, value in enumerate(values):
        for p, part in enumerate(parts_of(value)):
            row = (p * len(values) + f) * rows
            left_ref[row : row + rows, at] = hot * part.astype(BF16)


def gathered_sum(left_ref, hot_ref, fields, rows):
    wide = lax.dot_general(
        left_ref[...], hot_ref[...], (((1,), (1,)), ((), ())), preferred_element_type=F32
    )
    return [
        sum(wide[(p * fields + f) * rows : (p * fields + f + 1) * rows] for p in range(PARTS))
        for f in range(fields)
    ]


def flow(trans, upwind, cell_p, cell_s, seg_p, seg_s):
    u = jnp.where(upwind > 0.5, cell_s, seg_s)
    weight = trans * (MOBILITY_FLOOR + u * u)
    water = weight * (cell_p - seg_p) * u
    return weight, water


def cell_parts(cell_row, columns):
    return cell_row // columns, cell_row % columns


def load_segs(ref, *lead):
    rows = ref.shape[-2] // 2
    return jnp.concatenate([ref[(*lead, pl.ds(h, rows, 2), slice(None))] for h in range(2)], axis=1)


def store_segs(ref, lead, value):
    rows = value.shape[0]
    for h in range(2):
        ref[lead, pl.ds(h, rows, 2), :] = value[:, h * LANES : (h + 1) * LANES]


def ends_of(frac):
    rows, columns = frac.shape
    lane = iota((1, columns), 1)
    return jnp.where(lane < columns // 2, frac[0:1], frac[rows - 1 : rows])


def frac_step(frac, sat, aperture, before, after, inflow, total, gained):
    rows, lanes = frac.shape
    row, lane = iota((rows, lanes), 0), iota((rows, lanes), 1)
    back = pltpu.roll(frac, 1, 1)
    left = jnp.where(lane == 0, pltpu.roll(back, 1, 0), back)
    left = jnp.where((lane == 0) & (row == 0), before, left)
    ahead = pltpu.roll(frac, lanes - 1, 1)
    right = jnp.where(lane == lanes - 1, pltpu.roll(ahead, rows - 1, 0), ahead)
    right = jnp.where((lane == lanes - 1) & (row == rows - 1), after, right)
    new_frac = (aperture * frac + inflow + left + right) / (aperture + total + 2.0)
    new_sat = sat + TAU_STEP * gained / (aperture + total)
    return new_frac, new_sat


def chain_ends(ends_ref, row, members):
    me = lax.axis_index("frac")
    lanes = ends_ref.shape[2]
    prior = ends_ref[jnp.maximum(me - 1, 0), row : row + 1, :]
    later = ends_ref[jnp.minimum(me + 1, members - 1), row : row + 1, :]
    before = jnp.where(me > 0, prior[:, lanes - 1 :], 0.0)
    after = jnp.where(me < members - 1, later[:, 0:1], 0.0)
    return before, after


def partial_residual(pressure, couple, source, inverse, ring):
    rows, columns = pressure.shape
    row, col = iota((rows, columns), 0), iota((rows, columns), 1)
    beside = jnp.where(row == 0, 0.0, pltpu.roll(pressure, 1, 0))
    beside += jnp.where(row == rows - 1, 0.0, pltpu.roll(pressure, rows - 1, 0))
    beside += jnp.where(col == 0, 0.0, pltpu.roll(pressure, 1, 1))
    beside += jnp.where(col == columns - 1, 0.0, pltpu.roll(pressure, columns - 1, 1))
    if ring is not None:
        beside += ring
    return inverse * (source - (4.0 + couple) * pressure + beside)


def edge_columns(p):
    rows, columns = p.shape
    lane = iota((rows, LANES), 1)
    turned = jnp.transpose(jnp.where(lane < LANES // 2, p[:, :LANES], p[:, columns - LANES :]))
    return turned[0:1], turned[LANES - 1 : LANES]


def ring_of(left, right, columns, members):
    f = lax.axis_index("frac")
    rows = left.shape[1]
    left = jnp.where(f > 0, left, 0.0)
    right = jnp.where(f < members - 1, right, 0.0)
    turned = jnp.transpose(jnp.concatenate([left, jnp.zeros((LANES - 2, rows), F32), right], axis=0))
    lane = iota((rows, LANES), 1)
    low = jnp.where(lane == 0, turned, 0.0)
    high = jnp.where(lane == LANES - 1, turned, 0.0)
    if columns == LANES:
        return low + high
    return jnp.concatenate([low] + [jnp.zeros((rows, LANES), F32)] * (columns // LANES - 2) + [high], axis=1)


def pack_low(q, inv, p, at, axis):
    return jnp.where(
        at < DEPTH, q, jnp.where(at < 2 * DEPTH, pltpu.roll(inv, DEPTH, axis), pltpu.roll(p, 2 * DEPTH, axis))
    )


def pack_high(q, inv, p, at, axis):
    size = q.shape[axis]
    return jnp.where(
        at >= size - DEPTH,
        q,
        jnp.where(
            at >= size - 2 * DEPTH,
            pltpu.roll(inv, size - DEPTH, axis),
            pltpu.roll(p, size - 2 * DEPTH, axis),
        ),
    )


def block_rows(columns, width, closed):
    vertical = 2 * DEPTH * (columns // LANES)
    lateral = SUB + 2 * (width // LANES)
    return max(vertical, lateral) + (0 if closed else 1)


def put_rows(out_ref, at, values):
    for k in range(values.shape[0]):
        out_ref[at + k] = values[k : k + 1]


def get_rows(in_ref, at, count):
    return jnp.concatenate([in_ref[at + k] for k in range(count)], axis=0)


def send_slots(out_ref, at, first, second):
    halves = first.shape[1] // LANES
    for i, value in enumerate((first, second)):
        for h in range(halves):
            out_ref[at + SUB + i * halves + h] = value[:, h * LANES : (h + 1) * LANES]


def got_slots(in_ref, at, width):
    halves = width // LANES
    return [
        jnp.concatenate([in_ref[at + SUB + i * halves + h] for h in range(halves)], axis=1) for i in range(2)
    ]


def send_halo(out_ref, q, inv, p, groups, members, size, closed, ends=None):
    rows, columns = q.shape
    halves = columns // LANES
    g, f = lax.axis_index("grp"), lax.axis_index("frac")
    here = g * members + f
    lane = iota((rows, LANES), 1)
    low = pack_low(q[:, :LANES], inv[:, :LANES], p[:, :LANES], lane, 1)
    high = pack_high(q[:, columns - LANES :], inv[:, columns - LANES :], p[:, columns - LANES :], lane, 1)
    turned = jnp.transpose(jnp.where(lane < LANES // 2, low, high))
    left, right = turned[:SUB], turned[LANES - SUB :]
    if ends is not None:
        sub, lane = iota((SUB, LANES), 0), iota((SUB, LANES), 1)
        left = jnp.where((sub == SUB - 1) & (lane == 1), ends[0], left)
        right = jnp.where((sub == 0) & (lane == LANES - 2), ends[1], right)
    lane = iota((1, LANES), 1)
    spare = jnp.where(g + 2 < groups, here + 2 * members, here - 2 * members)

    for step in (-1, 1):
        layer = (lambda k: k) if step < 0 else (lambda k: rows - 1 - k)

        def span(field, count, at):
            start = 0 if step < 0 else rows - count
            return field[start : start + count, at]

        inside = (g + step >= 0) & (g + step < groups)
        base = here + step * members
        tiles = [slice(h * LANES, (h + 1) * LANES) for h in range(halves)]

        at = jnp.where(inside, base, spare) * size
        for h, tile in enumerate(tiles):
            put_rows(out_ref, at + h * DEPTH, span(q, DEPTH, tile))
            put_rows(out_ref, at + halves * DEPTH + h * (DEPTH - 1), span(inv, DEPTH - 1, tile))
            put_rows(out_ref, at + halves * (2 * DEPTH - 1) + h, span(p, 1, tile))
        if not closed:
            deep, next_p = layer(DEPTH - 1), layer(1)
            extra = jnp.where(
                lane == 0,
                inv[deep : deep + 1, tiles[0]],
                jnp.where(
                    lane == LANES - 1,
                    inv[deep : deep + 1, tiles[-1]],
                    jnp.where(
                        lane == 1,
                        pltpu.roll(p[next_p : next_p + 1, tiles[0]], 1, 1),
                        pltpu.roll(p[next_p : next_p + 1, tiles[-1]], LANES - 1, 1),
                    ),
                ),
            )
            out_ref[at + halves * 2 * DEPTH] = extra

        for side, tile, there in ((-1, tiles[0], f > 0), (1, tiles[-1], f < members - 1)):
            at = jnp.where(inside & there, base + side, spare) * size
            for i, field in enumerate((q, inv, p)):
                put_rows(out_ref, at + i * DEPTH, span(field, DEPTH, tile))

    put_rows(out_ref, jnp.where(f > 0, here - 1, spare) * size, left)
    put_rows(out_ref, jnp.where(f < members - 1, here + 1, spare) * size, right)


def chebyshev(in_ref, q_ref, inv_ref, p_ref, target, scratch, groups, members, size, closed):
    q_ext, inv_ext, p_ext, update_ref, even_ref, odd_ref = scratch
    rows, columns = target.shape
    halves = columns // LANES
    side = halves
    g, f = lax.axis_index("grp"), lax.axis_index("frac")
    here = g * members + f
    last = groups * members - 1

    def taker(dg, df):
        ok = (g + dg >= 0) & (g + dg < groups) & (f + df >= 0) & (f + df < members)
        at = jnp.clip(here + dg * members + df, 0, last) * size
        return lambda start, count: jnp.where(ok, get_rows(in_ref, at + start, count), 0.0)

    def both(low, high, at, count, size):
        return jnp.where(at < count, low, jnp.where(at >= size - count, high, 0.0))

    def filler(count):
        return jnp.zeros((count, LANES), F32)

    for h in range(halves):
        for ext, ref in ((q_ext, q_ref), (inv_ext, inv_ref), (p_ext, p_ref)):
            ext[h, 0:rows, :] = ref[:, h * LANES : (h + 1) * LANES]
    outer = slice(rows, rows + SUB)
    below, above = taker(1, 0), taker(-1, 0)
    lane = iota((1, LANES), 1)
    if not closed:
        low_extra, high_extra = below(halves * 2 * DEPTH, 1), above(halves * 2 * DEPTH, 1)
    for h in range(halves):
        edge = (lane == 0) & (h == 0) | (lane == LANES - 1) & (h == halves - 1)

        def at_edge(high, turn):
            if closed:
                return filler(1)
            row = high_extra if high else low_extra
            return jnp.where(edge, pltpu.roll(row, turn, 1) if turn else row, 0.0)

        turn = LANES - 1 if h == 0 else 1
        at = h * DEPTH
        q_ext[h, outer, :] = jnp.concatenate(
            [below(at, DEPTH), filler(SUB - 2 * DEPTH), above(at, DEPTH)], axis=0
        )
        at = halves * DEPTH + h * (DEPTH - 1)
        inv_ext[h, outer, :] = jnp.concatenate(
            [
                below(at, DEPTH - 1),
                at_edge(False, 0),
                filler(SUB - 2 * DEPTH),
                at_edge(True, 0),
                above(at, DEPTH - 1),
            ],
            axis=0,
        )
        at = halves * (2 * DEPTH - 1) + h
        p_ext[h, outer, :] = jnp.concatenate(
            [
                below(at, 1),
                at_edge(False, turn),
                filler(SUB - 4),
                at_edge(True, turn),
                above(at, 1),
            ],
            axis=0,
        )
    right, left = taker(0, 1)(0, SUB), taker(0, -1)(0, SUB)
    turned = jnp.transpose(
        jnp.concatenate([right, jnp.zeros((LANES - 2 * SUB, rows), F32), left], axis=0)
    )
    lane = iota((rows, LANES), 1)
    q_ext[side, 0:rows, :] = both(turned, turned, lane, DEPTH, LANES)
    inv_ext[side, 0:rows, :] = both(
        pltpu.roll(turned, LANES - DEPTH, 1), pltpu.roll(turned, DEPTH, 1), lane, DEPTH, LANES
    )
    p_ext[side, 0:rows, :] = both(
        pltpu.roll(turned, LANES - 2 * DEPTH, 1), pltpu.roll(turned, 2 * DEPTH, 1), lane, 2, LANES
    )
    lane = iota((DEPTH, LANES), 1)
    low_right, low_left, high_right, high_left = taker(1, 1), taker(1, -1), taker(-1, 1), taker(-1, -1)
    for i, ext in enumerate((q_ext, inv_ext, p_ext)):
        at = i * DEPTH
        ext[side, outer, :] = jnp.concatenate(
            [
                both(low_right(at, DEPTH), low_left(at, DEPTH), lane, DEPTH, LANES),
                filler(SUB - 2 * DEPTH),
                both(high_right(at, DEPTH), high_left(at, DEPTH), lane, DEPTH, LANES),
            ],
            axis=0,
        )

    end = rows + SUB - 1
    for own, other in ((0, end), (end, 0), (rows - 1, rows), (rows, rows - 1)):
        for c in range(halves + 1):
            q_ext[c, own : own + 1, :] += inv_ext[c, own : own + 1, :] * p_ext[c, other : other + 1, :]
    centre = 0.5 * (HIGH_BOUND + LOW_BOUND)
    half_width = 0.5 * (HIGH_BOUND - LOW_BOUND)
    scale_ratio = centre / half_width
    ratio_now = 1.0 / scale_ratio
    lane = iota((SUB, LANES), 1)
    count = rows // SUB + 1

    def keep(ref, c, r, value):
        at = (r + 1) * SUB
        ref[c, at : at + SUB, :] = value
        if r == count - 1:
            ref[c, 0:SUB, :] = value
        if r == 0:
            at = (count + 1) * SUB
            ref[c, at : at + SUB, :] = value

    for r in range(count):
        at = slice(r * SUB, (r + 1) * SUB)
        if closed:
            for c in range(halves + 1):
                start = q_ext[c, at, :]
                keep(even_ref, c, r, start / centre if centre != 1.0 else start)
            continue
        p_side, p_first, p_final = p_ext[side, at, :], p_ext[0, at, :], p_ext[halves - 1, at, :]
        missing = [0.0] * (halves + 1)
        missing[0] += jnp.where(lane == 0, pltpu.roll(p_side, 1, 1), 0.0)
        missing[halves - 1] += jnp.where(lane == LANES - 1, pltpu.roll(p_side, LANES - 1, 1), 0.0)
        missing[side] = jnp.where(
            lane == 0,
            pltpu.roll(p_final, 1, 1),
            jnp.where(lane == LANES - 1, pltpu.roll(p_first, LANES - 1, 1), 0.0),
        )
        for c in range(halves + 1):
            start = q_ext[c, at, :] + inv_ext[c, at, :] * missing[c]
            q_ext[c, at, :] = start
            keep(even_ref, c, r, start / centre if centre != 1.0 else start)
    now_ref, next_ref = even_ref, odd_ref
    for sweep in range(1, SWEEPS):
        ratio_next = 1.0 / (2.0 * scale_ratio - ratio_now)
        final = sweep == SWEEPS - 1
        for r in range(count - 1 if final else count):
            at = slice(r * SUB, (r + 1) * SUB)
            mids = [now_ref[c, (r + 1) * SUB : (r + 2) * SUB, :] for c in range(halves + 1)]
            after = [pltpu.roll(m, 1, 1) for m in mids]
            ahead = [pltpu.roll(m, LANES - 1, 1) for m in mids]
            for c in range(halves if final else halves + 1):
                beside = now_ref[c, (r + 1) * SUB - 1 : (r + 2) * SUB - 1, :]
                beside += now_ref[c, (r + 1) * SUB + 1 : (r + 2) * SUB + 1, :]
                beside += jnp.where(lane == 0, after[(c - 1) % (halves + 1)], after[c])
                beside += jnp.where(lane == LANES - 1, ahead[(c + 1) % (halves + 1)], ahead[c])
                residual = q_ext[c, at, :] - mids[c] + inv_ext[c, at, :] * beside
                old = mids[c] if sweep == 1 else update_ref[c, at, :]
                update = ratio_next * ratio_now * old + (2.0 * ratio_next / half_width) * residual
                if final:
                    tile = slice(c * LANES, (c + 1) * LANES)
                    target[at, tile] = p_ref[at, tile] + mids[c] + update
                else:
                    update_ref[c, at, :] = update
                    keep(next_ref, c, r, mids[c] + update)
        ratio_now = ratio_next
        now_ref, next_ref = next_ref, now_ref


ROW_SEG = 0
ROW_TRANS = 1
ROW_UP = 2
ROW_P = ROW_UP + ITERS
ROW_S = ROW_P + 1
ROW_ENDS = ROW_S + 1


def first_kernel(
    members, cell_any, seg_any, trans_any, count_any, up_any, state_any, frac_any,
    out_ref, hot_ref, row_hot_ref, cell_ref, seg_ref, trans_ref, count_ref, up_ref, state_ref, frac_ref, sem,
):
    _, rows, columns = state_ref.shape
    width = cell_ref.shape[1]
    state_rows = [pl.ds(h * rows // 2, rows // 2) for h in range(2)]
    copies = [
        pltpu.make_async_copy(source, target, sem.at[i])
        for i, (source, target) in enumerate(
            [
                (cell_any, cell_ref),
                *[(state_any.at[k, at], state_ref.at[k, at]) for at in state_rows for k in range(2)],
                (seg_any, seg_ref),
                (trans_any, trans_ref),
                (count_any, count_ref),
                (up_any, up_ref),
                (frac_any, frac_ref),
            ]
        )
    ]
    for copy in copies:
        copy.start()
    copies[0].wait()

    def make_hots(o):
        row, col = cell_parts(cell_ref[o : o + 1, :], columns)
        at = slice(o * width, (o + 1) * width)
        hot_ref[:, at] = one_hot(col, columns)
        row_hot_ref[:, at] = one_hot(row, rows)

    early = members // 2
    for o in range(early):
        make_hots(o)
    for copy in copies[1:5]:
        copy.wait()
    table = table_of([state_ref[0], state_ref[1]])
    for copy in copies[5:]:
        copy.wait()
    frac = load_segs(frac_ref, 0)
    ends = ends_of(frac)
    left, right = edge_columns(state_ref[0])
    me = lax.axis_index("frac")
    to_left = jnp.concatenate([ends[:, :LANES], left], axis=1)
    to_right = jnp.concatenate([right, ends[:, LANES:]], axis=1)
    whole = jnp.concatenate([frac, load_segs(frac_ref, 1)], axis=0)
    for o in range(members):
        one = slice(o, o + 1)
        row, _ = cell_parts(cell_ref[one, :], columns)
        if o >= early:
            make_hots(o)
        cell_p, cell_s = pick(table, 2, rows, row, hot_ref[:, o * width : (o + 1) * width])
        live = iota((1, width), 1) < count_ref[0, o]
        out_ref[o, ROW_SEG : ROW_SEG + 1, :] = seg_ref[one, :].astype(F32)
        out_ref[o, ROW_TRANS : ROW_TRANS + 1, :] = jnp.where(live, trans_ref[one, :], 0.0)
        for t in range(ITERS):
            out_ref[o, ROW_UP + t : ROW_UP + t + 1, :] = up_ref[t, one, :].astype(F32)
        out_ref[o, ROW_P : ROW_P + 1, :] = cell_p
        out_ref[o, ROW_S : ROW_S + 1, :] = cell_s
        out_ref[o, ROW_ENDS : ROW_ENDS + 1, :] = jnp.where(me + 1 == o, to_right, to_left)
        out_ref[o, SUB:, :] = whole


def seg_parts(slot_ref, s):
    seg = slot_ref[s, ROW_SEG : ROW_SEG + 1, :].astype(jnp.int32)
    return seg // SEG_COLUMNS, seg % SEG_COLUMNS


def seg_hots(slot_ref, hot_ref, row_hot_ref, members, width):
    for s in range(members):
        row, lane = seg_parts(slot_ref, s)
        at = slice(s * width, (s + 1) * width)
        hot_ref[:, at] = one_hot(lane, SEG_COLUMNS)
        row_hot_ref[:, at] = one_hot(row, row_hot_ref.shape[0])


def seg_gather(slot_ref, hot_ref, fields, s, width, table):
    return pick(table, 2, fields, seg_parts(slot_ref, s)[0], hot_ref[:, s * width : (s + 1) * width])


def cell_update(
    members, t, hot_ref, row_hot_ref, sent_ref, cell_rows, seg_rows, pressure, saturation, perm, left_ref, ring
):
    rows = pressure.shape[0]
    for o in range(members):
        seg_p, seg_s = seg_rows(o)
        cell_p, cell_s = cell_rows(o)
        weight, water = flow(
            sent_ref[o, ROW_TRANS : ROW_TRANS + 1, :],
            sent_ref[o, ROW_UP + t : ROW_UP + t + 1, :],
            cell_p,
            cell_s,
            seg_p,
            seg_s,
        )
        spread(left_ref, row_hot_ref, o, [weight, weight * seg_p, water])
    couple, source, lost = gathered_sum(left_ref, hot_ref, 3, rows)
    inverse = 1.0 / (4.0 + perm + couple)
    new_saturation = saturation - TAU_STEP * lost / (perm + couple)
    return new_saturation, partial_residual(pressure, couple, source, inverse, ring), inverse


def start_kernel(
    groups, members, size, slot_ref, sent_ref, cell_hot_ref, cell_row_hot_ref, frac_ref, aperture_ref,
    state_ref, perm_ref, out_ref, keep_ref, own_ref, new_ref, hot_ref, row_hot_ref,
    left_seg_ref, left_ref, found_ref,
):
    width = slot_ref.shape[2]
    rows = new_ref.shape[1]
    g = lax.axis_index("grp")
    frac, sat = load_segs(frac_ref, 0), load_segs(frac_ref, 1)
    seg_hots(slot_ref, hot_ref, row_hot_ref, members, width)
    table = table_of([frac, sat])
    for s in range(members):
        seg_p, seg_s = seg_gather(slot_ref, hot_ref, rows, s, width, table)
        cell_p = slot_ref[s, ROW_P : ROW_P + 1, :]
        weight, water = flow(
            slot_ref[s, ROW_TRANS : ROW_TRANS + 1, :],
            slot_ref[s, ROW_UP : ROW_UP + 1, :],
            cell_p,
            slot_ref[s, ROW_S : ROW_S + 1, :],
            seg_p,
            seg_s,
        )
        spread(left_seg_ref, row_hot_ref, s, [weight * cell_p, weight, water])
    inflow, total, gained = gathered_sum(left_seg_ref, hot_ref, 3, rows)
    before, after = chain_ends(slot_ref, ROW_ENDS, members)
    new_frac, new_sat = frac_step(frac, sat, load_segs(aperture_ref), before, after, inflow, total, gained)
    new_ref[0] = new_frac
    new_ref[1] = new_sat
    table = table_of([new_frac, new_sat])
    for s in range(members):
        seg_p, seg_s = seg_gather(slot_ref, hot_ref, rows, s, width, table)
        own_ref[s, 0:1, :] = seg_p
        own_ref[s, 1:2, :] = seg_s
        at = (g * members + s) * size
        send_slots(out_ref, at, seg_p, seg_s)
    for o in range(members):
        row, lane = seg_parts(sent_ref, o)
        table = table_of([slot_ref[o, SUB : SUB + rows, :], slot_ref[o, SUB + rows :, :]])
        seg_p, seg_s = pick(table, 2, rows, row, one_hot(lane, SEG_COLUMNS))
        found_ref[o, 0:1, :] = seg_p
        found_ref[o, 1:2, :] = seg_s
    me = lax.axis_index("frac")
    pressure = state_ref[0]
    new_saturation, q, inv = cell_update(
        members,
        0,
        cell_hot_ref,
        cell_row_hot_ref,
        sent_ref,
        lambda o: (sent_ref[o, ROW_P : ROW_P + 1, :], sent_ref[o, ROW_S : ROW_S + 1, :]),
        lambda o: (found_ref[o, 0:1, :], found_ref[o, 1:2, :]),
        pressure,
        state_ref[1],
        perm_ref[...],
        left_ref,
        ring_of(
            slot_ref[jnp.maximum(me - 1, 0), ROW_ENDS : ROW_ENDS + 1, :][:, :LANES],
            slot_ref[jnp.minimum(me + 1, members - 1), ROW_ENDS : ROW_ENDS + 1, :][:, LANES:],
            state_ref.shape[2],
            members,
        ),
    )
    keep_ref[0] = pressure
    keep_ref[1] = new_saturation
    keep_ref[2] = q
    keep_ref[3] = inv
    ends = (new_frac[0:1, 0:1], new_frac[rows - 1 : rows, SEG_COLUMNS - 1 : SEG_COLUMNS])
    send_halo(out_ref, q, inv, pressure, groups, members, size, True, ends)


def cell_gather(members, cell_ref, hot_ref, fields, put):
    rows, columns = fields[0].shape
    width = cell_ref.shape[1]
    table = table_of(fields)
    for o in range(members):
        row, _ = cell_parts(cell_ref[o : o + 1, :], columns)
        put(o, *pick(table, len(fields), rows, row, hot_ref[:, o * width : (o + 1) * width]))


def middle_kernel(
    groups, members, size, open_size, halo_ref, cell_ref, hot_ref, row_hot_ref, sent_ref, kept_ref, perm_ref,
    out_ref, keep_ref, slots_ref, left_ref, *scratch,
):
    saturation = kept_ref[1]
    g = lax.axis_index("grp")

    def put_s(o, cell_s):
        slots_ref[o, 1:2, :] = cell_s

    cell_gather(members, cell_ref, hot_ref, [saturation], put_s)
    chebyshev(
        halo_ref, kept_ref.at[2], kept_ref.at[3], kept_ref.at[0], keep_ref.at[0], scratch, groups, members, size, True
    )
    pressure = keep_ref[0]

    def put_p(o, cell_p):
        slots_ref[o, 0:1, :] = cell_p
        send_slots(out_ref, (g * members + o) * open_size, cell_p, slots_ref[o, 1:2, :])

    cell_gather(members, cell_ref, hot_ref, [pressure], put_p)
    new_saturation, q, inv = cell_update(
        members,
        1,
        hot_ref,
        row_hot_ref,
        sent_ref,
        lambda o: (slots_ref[o, 0:1, :], slots_ref[o, 1:2, :]),
        lambda o: got_slots(halo_ref, (g * members + o) * size, cell_ref.shape[1]),
        pressure,
        saturation,
        perm_ref[...],
        left_ref,
        None,
    )
    keep_ref[1] = new_saturation
    keep_ref[2] = q
    keep_ref[3] = inv
    send_halo(out_ref, q, inv, pressure, groups, members, open_size, False)


def owner_spread(members, t, slot_ref, cell_rows, seg_rows, row_hot_ref, left_ref):
    for s in range(members):
        cell_p, cell_s = cell_rows(s)
        weight, water = flow(
            slot_ref[s, ROW_TRANS : ROW_TRANS + 1, :],
            slot_ref[s, ROW_UP + t : ROW_UP + t + 1, :],
            cell_p,
            cell_s,
            *seg_rows(s),
        )
        spread(left_ref, row_hot_ref, s, [weight * cell_p, weight, water])


def owner_update(
    members, t, slot_ref, cell_rows, seg_rows, frac, sat, aperture, ends, hot_ref, row_hot_ref, left_ref
):
    owner_spread(members, t, slot_ref, cell_rows, seg_rows, row_hot_ref, left_ref)
    inflow, total, gained = gathered_sum(left_ref, hot_ref, 3, frac.shape[0])
    return frac_step(frac, sat, aperture, *ends, inflow, total, gained)


def exchange_kernel(
    groups, members, closed_size, size, halo_ref, cell_ref, cell_hot_ref, slot_ref, hot_ref, row_hot_ref, ends_ref, own_ref,
    frac_ref, aperture_ref, kept_ref, out_ref, new_ref, pressure_ref, left_ref, *scratch,
):
    width = slot_ref.shape[2]
    g = lax.axis_index("grp")

    def cell_rows(s):
        return got_slots(halo_ref, (g * members + s) * size, width)

    me = lax.axis_index("frac")
    prior = ends_ref[(g * members + jnp.maximum(me - 1, 0)) * closed_size]
    later = ends_ref[(g * members + jnp.minimum(me + 1, members - 1)) * closed_size + SUB - 1]
    before = jnp.where(me > 0, prior[:, LANES - 2 : LANES - 1], 0.0)
    after = jnp.where(me < members - 1, later[:, 1:2], 0.0)

    rows, columns = pressure_ref.shape
    seg_wide = frac_ref.shape[1]
    owner_spread(
        members,
        1,
        slot_ref,
        cell_rows,
        lambda s: (own_ref[s, 0:1, :], own_ref[s, 1:2, :]),
        row_hot_ref,
        left_ref,
    )
    chebyshev(
        halo_ref, kept_ref.at[2], kept_ref.at[3], kept_ref.at[0], pressure_ref, scratch, groups, members, size, False
    )
    inflow, total, gained = gathered_sum(left_ref, hot_ref, 3, seg_wide)
    new_frac, new_sat = frac_step(
        frac_ref[0], frac_ref[1], load_segs(aperture_ref), before, after, inflow, total, gained
    )
    new_ref[0] = new_frac
    new_ref[1] = new_sat
    seg_table = table_of([new_frac, new_sat])
    ends = ends_of(new_frac)
    table = table_of([pressure_ref[...], kept_ref[1]])
    columns_row = jnp.concatenate(edge_columns(pressure_ref[...]), axis=1)
    for o in range(members):
        at = slice(o * width, (o + 1) * width)
        row, _ = cell_parts(cell_ref[o : o + 1, :], columns)
        cell_p, cell_s = pick(table, 2, rows, row, cell_hot_ref[:, at])
        out_ref[o, 0:1, :] = cell_p
        out_ref[o, 1:2, :] = cell_s
        seg_p, seg_s = pick(seg_table, 2, seg_wide, seg_parts(slot_ref, o)[0], hot_ref[:, at])
        out_ref[o, 2:3, :] = seg_p
        out_ref[o, 3:4, :] = seg_s
        out_ref[o, 4:5, :] = ends
        out_ref[o, 5:6, :] = columns_row


def source_last_kernel(
    groups, members, size, hot_ref, row_hot_ref, sent_ref, own_ref, seg_ref, pressure_ref, kept_ref, perm_ref,
    out_ref, keep_ref, left_ref,
):
    me = lax.axis_index("frac")
    pressure = pressure_ref[...]
    new_saturation, q, inv = cell_update(
        members,
        2,
        hot_ref,
        row_hot_ref,
        sent_ref,
        lambda o: (own_ref[o, 0:1, :], own_ref[o, 1:2, :]),
        lambda o: (seg_ref[o, 2:3, :], seg_ref[o, 3:4, :]),
        pressure,
        kept_ref[1],
        perm_ref[...],
        left_ref,
        ring_of(
            seg_ref[jnp.maximum(me - 1, 0), 5:6, :][:, LANES:],
            seg_ref[jnp.minimum(me + 1, members - 1), 5:6, :][:, :LANES],
            pressure_ref.shape[1],
            members,
        ),
    )
    keep_ref[0] = new_saturation
    keep_ref[1] = q
    keep_ref[2] = inv
    send_halo(out_ref, q, inv, pressure, groups, members, size, True)


def final_kernel(
    groups, members, size, halo_ref, pressure_ref, kept_ref, slot_ref, hot_ref, row_hot_ref, own_ref, seg_ref,
    frac_ref, aperture_ref, out_ref, new_ref, left_ref, *scratch,
):
    new_frac, new_sat = owner_update(
        members,
        2,
        slot_ref,
        lambda s: (seg_ref[s, 0:1, :], seg_ref[s, 1:2, :]),
        lambda s: (own_ref[s, 2:3, :], own_ref[s, 3:4, :]),
        frac_ref[0],
        frac_ref[1],
        load_segs(aperture_ref),
        chain_ends(seg_ref, 4, members),
        hot_ref,
        row_hot_ref,
        left_ref,
    )
    store_segs(new_ref, 0, new_frac)
    store_segs(new_ref, 1, new_sat)
    chebyshev(
        halo_ref, kept_ref.at[1], kept_ref.at[2], pressure_ref, out_ref.at[0], scratch, groups, members, size, True
    )
    out_ref[1] = kept_ref[0]


VMEM = pl.BlockSpec(memory_space=pltpu.VMEM)
HBM = pl.BlockSpec(memory_space=pltpu.HBM)


def call(kernel, statics, outs, scratch, *args, spec=VMEM):
    outs = [o if hasattr(o, "dtype") else jax.ShapeDtypeStruct(o, F32) for o in outs]
    return pl.pallas_call(
        functools.partial(kernel, *statics),
        out_shape=outs,
        in_specs=[spec] * len(args),
        out_specs=[VMEM] * len(outs),
        scratch_shapes=scratch,
        compiler_params=pltpu.CompilerParams(vmem_limit_bytes=32 * 1024 * 1024),
        name=kernel.__name__,
    )(*args)


def on_device(
    matrix_state,
    matrix_perm,
    frac_state,
    frac_aperture,
    link_cell,
    link_seg,
    link_trans,
    link_count,
    link_upwind,
):
    groups, members = lax.axis_size("grp"), lax.axis_size("frac")
    devices = groups * members
    cells = link_cell[0, 0]
    width = cells.shape[1]
    _, rows, columns = matrix_state.shape
    seg_dev = frac_state.shape[2]
    seg_rows = seg_dev // LANES
    frac = frac_state.reshape(2, seg_rows, LANES)
    aperture = frac_aperture.reshape(seg_rows, LANES)

    every = members * width
    slots = (members, SUB, width)
    closed_size, open_size = block_rows(columns, width, True), block_rows(columns, width, False)
    both = (groups, members, closed_size)
    halves = (groups, members, closed_size, open_size)
    halo, open_halo = (devices * closed_size, 1, LANES), (devices * open_size, 1, LANES)
    left_cell = pltpu.VMEM((3 * PARTS * rows, every), BF16)
    seg_wide = seg_dev // SEG_COLUMNS
    segs_wide = (2, seg_wide, SEG_COLUMNS)
    left_seg = pltpu.VMEM((3 * PARTS * seg_wide, every), BF16)
    tiles = columns // LANES + 1
    ext = [pltpu.VMEM((tiles, rows + SUB, LANES), F32)] * 4 + [pltpu.VMEM((tiles, rows + 3 * SUB, LANES), F32)] * 2

    def to_group(x):
        return lax.all_to_all(x, "frac", split_axis=0, concat_axis=0, tiled=True)

    def to_all(x):
        return lax.all_to_all(x, ("grp", "frac"), split_axis=0, concat_axis=0, tiled=True)

    def hots(*sizes):
        return [jax.ShapeDtypeStruct((n, every), BF16) for n in sizes]

    sent, cell_hot, cell_row_hot = call(
        first_kernel,
        (members,),
        [(members, SUB + 2 * seg_wide, SEG_COLUMNS)] + hots(columns, rows),
        [
            pltpu.VMEM((members, width), jnp.int32),
            pltpu.VMEM((members, width), jnp.int32),
            pltpu.VMEM((members, width), F32),
            pltpu.SMEM((1, members), jnp.int32),
            pltpu.VMEM((ITERS, members, width), jnp.int32),
            pltpu.VMEM(matrix_state.shape, F32),
            pltpu.VMEM(frac.shape, F32),
            pltpu.SemaphoreType.DMA((10,)),
        ],
        *[
            pltpu.with_memory_space_constraint(x, pltpu.HBM)
            for x in (
                cells, link_seg[0, 0], link_trans[0, 0], link_count[0], link_upwind[:, 0, 0], matrix_state, frac
            )
        ],
        spec=HBM,
    )
    slot = to_group(sent)
    edge, kept, own, frac1, hot, row_hot = call(
        start_kernel,
        both,
        [halo, (4, rows, columns), (members, 2, width), segs_wide] + hots(SEG_COLUMNS, seg_wide),
        [left_seg, left_cell, pltpu.VMEM((members, 2, width), F32)],
        slot, sent, cell_hot, cell_row_hot, frac, aperture, matrix_state, matrix_perm,
    )
    before = to_all(edge)
    edge, kept = call(
        middle_kernel, halves, [open_halo, (4, rows, columns)], [pltpu.VMEM((members, 2, width), F32), left_cell] + ext,
        before, cells, cell_hot, cell_row_hot, sent, kept, matrix_perm,
    )
    around = to_all(edge)
    own, frac2, pressure = call(
        exchange_kernel, halves, [slots, segs_wide, (rows, columns)], [left_seg] + ext,
        around, cells, cell_hot, slot, hot, row_hot, before, own, frac1, aperture, kept,
    )
    segs = to_group(own)
    edge, kept = call(
        source_last_kernel, both, [halo, (3, rows, columns)], [left_cell],
        cell_hot, cell_row_hot, sent, own, segs, pressure, kept, matrix_perm,
    )
    around = to_all(edge)
    matrix_out, frac3 = call(
        final_kernel,
        both,
        [matrix_state.shape, frac.shape],
        [left_seg] + ext,
        around, pressure, kept, slot, hot, row_hot, own, segs, frac2, aperture,
    )
    return matrix_out, frac3.reshape(frac_state.shape)


def solution(mesh):
    return jax.shard_map(
        on_device,
        mesh=mesh,
        in_specs=(
            P(None, "grp", "frac"),
            P("grp", "frac"),
            P(None, "grp", "frac"),
            P("grp", "frac"),
            P("grp", "frac", None, None),
            P("grp", "frac", None, None),
            P("grp", "frac", None, None),
            P("grp", "frac", None),
            P(None, "grp", "frac", None, None),
        ),
        out_specs=(P(None, "grp", "frac"), P(None, "grp", "frac")),
        check_vma=False,
    )
```

```python
import functools

import jax
import jax.numpy as jnp
from jax import lax
from jax.experimental import pallas as pl
from jax.experimental.pallas import tpu as pltpu
from jax.sharding import PartitionSpec as P

ITERS = 3
SWEEPS = 4

LOW_BOUND = 0.02
HIGH_BOUND = 1.98
TAU_STEP = 0.5
MOBILITY_FLOOR = 0.2

F32 = jnp.float32
BF16 = jnp.bfloat16
LANES = 128
SUB = 8
SEG_COLUMNS = 2 * LANES
DEPTH = SWEEPS - 1


def iota(shape, dim):
    return lax.broadcasted_iota(jnp.int32, shape, dim)


def parts_of(x):
    high = x.astype(BF16).astype(F32)
    return high, x - high


PARTS = 2


def table_of(fields):
    split = [parts_of(f) for f in fields]
    return jnp.concatenate([s[p] for p in range(PARTS) for s in split], axis=0).astype(BF16)


def one_hot(index_row, count):
    shape = (count, index_row.shape[1])
    hit = iota(shape, 0).astype(F32).astype(BF16) == index_row.astype(F32).astype(BF16)
    return jnp.where(hit, jnp.ones(shape, BF16), jnp.zeros(shape, BF16))


def pick(table, fields, rows, row_index, hot):
    wide = jnp.dot(table, hot, preferred_element_type=F32)
    hit = iota((rows, row_index.shape[1]), 0) == row_index
    found = []
    for f in range(fields):
        total = sum(wide[(p * fields + f) * rows : (p * fields + f + 1) * rows] for p in range(PARTS))
        found.append(jnp.sum(jnp.where(hit, total, 0.0), axis=0, keepdims=True))
    return found


def spread(left_ref, row_hot_ref, block, values):
    rows = row_hot_ref.shape[0]
    width = values[0].shape[1]
    at = slice(block * width, (block + 1) * width)
    hot = row_hot_ref[:, at]
    for f, value in enumerate(values):
        for p, part in enumerate(parts_of(value)):
            row = (p * len(values) + f) * rows
            left_ref[row : row + rows, at] = hot * part.astype(BF16)


def gathered_sum(left_ref, hot_ref, fields, rows):
    wide = lax.dot_general(
        left_ref[...], hot_ref[...], (((1,), (1,)), ((), ())), preferred_element_type=F32
    )
    return [
        sum(wide[(p * fields + f) * rows : (p * fields + f + 1) * rows] for p in range(PARTS))
        for f in range(fields)
    ]


def flow(trans, upwind, cell_p, cell_s, seg_p, seg_s):
    u = jnp.where(upwind > 0.5, cell_s, seg_s)
    weight = trans * (MOBILITY_FLOOR + u * u)
    water = weight * (cell_p - seg_p) * u
    return weight, water


def cell_parts(cell_row, columns):
    return cell_row // columns, cell_row % columns


def load_segs(ref, *lead):
    rows = ref.shape[-2] // 2
    return jnp.concatenate([ref[(*lead, pl.ds(h, rows, 2), slice(None))] for h in range(2)], axis=1)


def store_segs(ref, lead, value):
    rows = value.shape[0]
    for h in range(2):
        ref[lead, pl.ds(h, rows, 2), :] = value[:, h * LANES : (h + 1) * LANES]


def ends_of(frac):
    rows, columns = frac.shape
    lane = iota((1, columns), 1)
    return jnp.where(lane < columns // 2, frac[0:1], frac[rows - 1 : rows])


def frac_step(frac, sat, aperture, before, after, inflow, total, gained):
    rows, lanes = frac.shape
    row, lane = iota((rows, lanes), 0), iota((rows, lanes), 1)
    back = pltpu.roll(frac, 1, 1)
    left = jnp.where(lane == 0, pltpu.roll(back, 1, 0), back)
    left = jnp.where((lane == 0) & (row == 0), before, left)
    ahead = pltpu.roll(frac, lanes - 1, 1)
    right = jnp.where(lane == lanes - 1, pltpu.roll(ahead, rows - 1, 0), ahead)
    right = jnp.where((lane == lanes - 1) & (row == rows - 1), after, right)
    new_frac = (aperture * frac + inflow + left + right) / (aperture + total + 2.0)
    new_sat = sat + TAU_STEP * gained / (aperture + total)
    return new_frac, new_sat


def chain_ends(ends_ref, row, members):
    me = lax.axis_index("frac")
    lanes = ends_ref.shape[2]
    prior = ends_ref[jnp.maximum(me - 1, 0), row : row + 1, :]
    later = ends_ref[jnp.minimum(me + 1, members - 1), row : row + 1, :]
    before = jnp.where(me > 0, prior[:, lanes - 1 :], 0.0)
    after = jnp.where(me < members - 1, later[:, 0:1], 0.0)
    return before, after


def partial_residual(pressure, couple, source, inverse, ring):
    rows, columns = pressure.shape
    row, col = iota((rows, columns), 0), iota((rows, columns), 1)
    beside = jnp.where(row == 0, 0.0, pltpu.roll(pressure, 1, 0))
    beside += jnp.where(row == rows - 1, 0.0, pltpu.roll(pressure, rows - 1, 0))
    beside += jnp.where(col == 0, 0.0, pltpu.roll(pressure, 1, 1))
    beside += jnp.where(col == columns - 1, 0.0, pltpu.roll(pressure, columns - 1, 1))
    if ring is not None:
        beside += ring
    return inverse * (source - (4.0 + couple) * pressure + beside)


def edge_columns(p):
    rows, columns = p.shape
    lane = iota((rows, LANES), 1)
    turned = jnp.transpose(jnp.where(lane < LANES // 2, p[:, :LANES], p[:, columns - LANES :]))
    return turned[0:1], turned[LANES - 1 : LANES]


def ring_of(left, right, columns, members):
    f = lax.axis_index("frac")
    rows = left.shape[1]
    left = jnp.where(f > 0, left, 0.0)
    right = jnp.where(f < members - 1, right, 0.0)
    turned = jnp.transpose(jnp.concatenate([left, jnp.zeros((LANES - 2, rows), F32), right], axis=0))
    lane = iota((rows, LANES), 1)
    low = jnp.where(lane == 0, turned, 0.0)
    high = jnp.where(lane == LANES - 1, turned, 0.0)
    if columns == LANES:
        return low + high
    return jnp.concatenate([low] + [jnp.zeros((rows, LANES), F32)] * (columns // LANES - 2) + [high], axis=1)


def pack_low(q, inv, p, at, axis):
    return jnp.where(
        at < DEPTH, q, jnp.where(at < 2 * DEPTH, pltpu.roll(inv, DEPTH, axis), pltpu.roll(p, 2 * DEPTH, axis))
    )


def pack_high(q, inv, p, at, axis):
    size = q.shape[axis]
    return jnp.where(
        at >= size - DEPTH,
        q,
        jnp.where(
            at >= size - 2 * DEPTH,
            pltpu.roll(inv, size - DEPTH, axis),
            pltpu.roll(p, size - 2 * DEPTH, axis),
        ),
    )


def block_rows(columns, width, closed):
    vertical = 2 * DEPTH * (columns // LANES)
    lateral = SUB + 2 * (width // LANES)
    return max(vertical, lateral) + (0 if closed else 1)


def put_rows(out_ref, at, values):
    for k in range(values.shape[0]):
        out_ref[at + k] = values[k : k + 1]


def get_rows(in_ref, at, count):
    return jnp.concatenate([in_ref[at + k] for k in range(count)], axis=0)


def send_slots(out_ref, at, first, second):
    halves = first.shape[1] // LANES
    for i, value in enumerate((first, second)):
        for h in range(halves):
            out_ref[at + SUB + i * halves + h] = value[:, h * LANES : (h + 1) * LANES]


def got_slots(in_ref, at, width):
    halves = width // LANES
    return [
        jnp.concatenate([in_ref[at + SUB + i * halves + h] for h in range(halves)], axis=1) for i in range(2)
    ]


def send_halo(out_ref, q, inv, p, groups, members, size, closed, ends=None):
    rows, columns = q.shape
    halves = columns // LANES
    g, f = lax.axis_index("grp"), lax.axis_index("frac")
    here = g * members + f
    lane = iota((rows, LANES), 1)
    low = pack_low(q[:, :LANES], inv[:, :LANES], p[:, :LANES], lane, 1)
    high = pack_high(q[:, columns - LANES :], inv[:, columns - LANES :], p[:, columns - LANES :], lane, 1)
    turned = jnp.transpose(jnp.where(lane < LANES // 2, low, high))
    left, right = turned[:SUB], turned[LANES - SUB :]
    if ends is not None:
        sub, lane = iota((SUB, LANES), 0), iota((SUB, LANES), 1)
        left = jnp.where((sub == SUB - 1) & (lane == 1), ends[0], left)
        right = jnp.where((sub == 0) & (lane == LANES - 2), ends[1], right)
    lane = iota((1, LANES), 1)
    spare = jnp.where(g + 2 < groups, here + 2 * members, here - 2 * members)

    for step in (-1, 1):
        layer = (lambda k: k) if step < 0 else (lambda k: rows - 1 - k)

        def span(field, count, at):
            start = 0 if step < 0 else rows - count
            return field[start : start + count, at]

        inside = (g + step >= 0) & (g + step < groups)
        base = here + step * members
        tiles = [slice(h * LANES, (h + 1) * LANES) for h in range(halves)]

        at = jnp.where(inside, base, spare) * size
        for h, tile in enumerate(tiles):
            put_rows(out_ref, at + h * DEPTH, span(q, DEPTH, tile))
            put_rows(out_ref, at + halves * DEPTH + h * (DEPTH - 1), span(inv, DEPTH - 1, tile))
            put_rows(out_ref, at + halves * (2 * DEPTH - 1) + h, span(p, 1, tile))
        if not closed:
            deep, next_p = layer(DEPTH - 1), layer(1)
            extra = jnp.where(
                lane == 0,
                inv[deep : deep + 1, tiles[0]],
                jnp.where(
                    lane == LANES - 1,
                    inv[deep : deep + 1, tiles[-1]],
                    jnp.where(
                        lane == 1,
                        pltpu.roll(p[next_p : next_p + 1, tiles[0]], 1, 1),
                        pltpu.roll(p[next_p : next_p + 1, tiles[-1]], LANES - 1, 1),
                    ),
                ),
            )
            out_ref[at + halves * 2 * DEPTH] = extra

        for side, tile, there in ((-1, tiles[0], f > 0), (1, tiles[-1], f < members - 1)):
            at = jnp.where(inside & there, base + side, spare) * size
            for i, field in enumerate((q, inv, p)):
                put_rows(out_ref, at + i * DEPTH, span(field, DEPTH, tile))

    put_rows(out_ref, jnp.where(f > 0, here - 1, spare) * size, left)
    put_rows(out_ref, jnp.where(f < members - 1, here + 1, spare) * size, right)


def chebyshev(in_ref, q_ref, inv_ref, p_ref, target, scratch, groups, members, size, closed):
    q_ext, inv_ext, p_ext, update_ref, even_ref, odd_ref = scratch
    rows, columns = target.shape
    halves = columns // LANES
    side = halves
    g, f = lax.axis_index("grp"), lax.axis_index("frac")
    here = g * members + f
    last = groups * members - 1

    def taker(dg, df):
        ok = (g + dg >= 0) & (g + dg < groups) & (f + df >= 0) & (f + df < members)
        at = jnp.clip(here + dg * members + df, 0, last) * size
        return lambda start, count: jnp.where(ok, get_rows(in_ref, at + start, count), 0.0)

    def both(low, high, at, count, size):
        return jnp.where(at < count, low, jnp.where(at >= size - count, high, 0.0))

    def filler(count):
        return jnp.zeros((count, LANES), F32)

    for h in range(halves):
        for ext, ref in ((q_ext, q_ref), (inv_ext, inv_ref), (p_ext, p_ref)):
            ext[h, 0:rows, :] = ref[:, h * LANES : (h + 1) * LANES]
    outer = slice(rows, rows + SUB)
    below, above = taker(1, 0), taker(-1, 0)
    lane = iota((1, LANES), 1)
    if not closed:
        low_extra, high_extra = below(halves * 2 * DEPTH, 1), above(halves * 2 * DEPTH, 1)
    for h in range(halves):
        edge = (lane == 0) & (h == 0) | (lane == LANES - 1) & (h == halves - 1)

        def at_edge(high, turn):
            if closed:
                return filler(1)
            row = high_extra if high else low_extra
            return jnp.where(edge, pltpu.roll(row, turn, 1) if turn else row, 0.0)

        turn = LANES - 1 if h == 0 else 1
        at = h * DEPTH
        q_ext[h, outer, :] = jnp.concatenate(
            [below(at, DEPTH), filler(SUB - 2 * DEPTH), above(at, DEPTH)], axis=0
        )
        at = halves * DEPTH + h * (DEPTH - 1)
        inv_ext[h, outer, :] = jnp.concatenate(
            [
                below(at, DEPTH - 1),
                at_edge(False, 0),
                filler(SUB - 2 * DEPTH),
                at_edge(True, 0),
                above(at, DEPTH - 1),
            ],
            axis=0,
        )
        at = halves * (2 * DEPTH - 1) + h
        p_ext[h, outer, :] = jnp.concatenate(
            [
                below(at, 1),
                at_edge(False, turn),
                filler(SUB - 4),
                at_edge(True, turn),
                above(at, 1),
            ],
            axis=0,
        )
    right, left = taker(0, 1)(0, SUB), taker(0, -1)(0, SUB)
    turned = jnp.transpose(
        jnp.concatenate([right, jnp.zeros((LANES - 2 * SUB, rows), F32), left], axis=0)
    )
    lane = iota((rows, LANES), 1)
    q_ext[side, 0:rows, :] = both(turned, turned, lane, DEPTH, LANES)
    inv_ext[side, 0:rows, :] = both(
        pltpu.roll(turned, LANES - DEPTH, 1), pltpu.roll(turned, DEPTH, 1), lane, DEPTH, LANES
    )
    p_ext[side, 0:rows, :] = both(
        pltpu.roll(turned, LANES - 2 * DEPTH, 1), pltpu.roll(turned, 2 * DEPTH, 1), lane, 2, LANES
    )
    lane = iota((DEPTH, LANES), 1)
    low_right, low_left, high_right, high_left = taker(1, 1), taker(1, -1), taker(-1, 1), taker(-1, -1)
    for i, ext in enumerate((q_ext, inv_ext, p_ext)):
        at = i * DEPTH
        ext[side, outer, :] = jnp.concatenate(
            [
                both(low_right(at, DEPTH), low_left(at, DEPTH), lane, DEPTH, LANES),
                filler(SUB - 2 * DEPTH),
                both(high_right(at, DEPTH), high_left(at, DEPTH), lane, DEPTH, LANES),
            ],
            axis=0,
        )

    end = rows + SUB - 1
    for own, other in ((0, end), (end, 0), (rows - 1, rows), (rows, rows - 1)):
        for c in range(halves + 1):
            q_ext[c, own : own + 1, :] += inv_ext[c, own : own + 1, :] * p_ext[c, other : other + 1, :]
    centre = 0.5 * (HIGH_BOUND + LOW_BOUND)
    half_width = 0.5 * (HIGH_BOUND - LOW_BOUND)
    scale_ratio = centre / half_width
    ratio_now = 1.0 / scale_ratio
    lane = iota((SUB, LANES), 1)
    count = rows // SUB + 1

    def keep(ref, c, r, value):
        at = (r + 1) * SUB
        ref[c, at : at + SUB, :] = value
        if r == count - 1:
            ref[c, 0:SUB, :] = value
        if r == 0:
            at = (count + 1) * SUB
            ref[c, at : at + SUB, :] = value

    for r in range(count):
        at = slice(r * SUB, (r + 1) * SUB)
        if closed:
            for c in range(halves + 1):
                start = q_ext[c, at, :]
                keep(even_ref, c, r, start / centre if centre != 1.0 else start)
            continue
        p_side, p_first, p_final = p_ext[side, at, :], p_ext[0, at, :], p_ext[halves - 1, at, :]
        missing = [0.0] * (halves + 1)
        missing[0] += jnp.where(lane == 0, pltpu.roll(p_side, 1, 1), 0.0)
        missing[halves - 1] += jnp.where(lane == LANES - 1, pltpu.roll(p_side, LANES - 1, 1), 0.0)
        missing[side] = jnp.where(
            lane == 0,
            pltpu.roll(p_final, 1, 1),
            jnp.where(lane == LANES - 1, pltpu.roll(p_first, LANES - 1, 1), 0.0),
        )
        for c in range(halves + 1):
            start = q_ext[c, at, :] + inv_ext[c, at, :] * missing[c]
            q_ext[c, at, :] = start
            keep(even_ref, c, r, start / centre if centre != 1.0 else start)
    now_ref, next_ref = even_ref, odd_ref
    for sweep in range(1, SWEEPS):
        ratio_next = 1.0 / (2.0 * scale_ratio - ratio_now)
        final = sweep == SWEEPS - 1
        for r in range(count - 1 if final else count):
            at = slice(r * SUB, (r + 1) * SUB)
            mids = [now_ref[c, (r + 1) * SUB : (r + 2) * SUB, :] for c in range(halves + 1)]
            after = [pltpu.roll(m, 1, 1) for m in mids]
            ahead = [pltpu.roll(m, LANES - 1, 1) for m in mids]
            for c in range(halves if final else halves + 1):
                beside = now_ref[c, (r + 1) * SUB - 1 : (r + 2) * SUB - 1, :]
                beside += now_ref[c, (r + 1) * SUB + 1 : (r + 2) * SUB + 1, :]
                beside += jnp.where(lane == 0, after[(c - 1) % (halves + 1)], after[c])
                beside += jnp.where(lane == LANES - 1, ahead[(c + 1) % (halves + 1)], ahead[c])
                residual = q_ext[c, at, :] - mids[c] + inv_ext[c, at, :] * beside
                old = mids[c] if sweep == 1 else update_ref[c, at, :]
                update = ratio_next * ratio_now * old + (2.0 * ratio_next / half_width) * residual
                if final:
                    tile = slice(c * LANES, (c + 1) * LANES)
                    target[at, tile] = p_ref[at, tile] + mids[c] + update
                else:
                    update_ref[c, at, :] = update
                    keep(next_ref, c, r, mids[c] + update)
        ratio_now = ratio_next
        now_ref, next_ref = next_ref, now_ref


ROW_SEG = 0
ROW_TRANS = 1
ROW_UP = 2
ROW_P = ROW_UP + ITERS
ROW_S = ROW_P + 1
ROW_ENDS = ROW_S + 1


def first_kernel(
    members, cell_any, seg_any, trans_any, count_any, up_any, state_any, frac_any,
    out_ref, hot_ref, row_hot_ref, cell_ref, seg_ref, trans_ref, count_ref, up_ref, state_ref, frac_ref, sem,
):
    _, rows, columns = state_ref.shape
    width = cell_ref.shape[1]
    copies = [
        pltpu.make_async_copy(source, target, sem.at[i])
        for i, (source, target) in enumerate(
            [
                (cell_any, cell_ref),
                (state_any, state_ref),
                (seg_any, seg_ref),
                (trans_any, trans_ref),
                (count_any, count_ref),
                (up_any, up_ref),
                (frac_any, frac_ref),
            ]
        )
    ]
    for copy in copies:
        copy.start()
    copies[0].wait()

    def make_hots(o):
        row, col = cell_parts(cell_ref[o : o + 1, :], columns)
        at = slice(o * width, (o + 1) * width)
        hot_ref[:, at] = one_hot(col, columns)
        row_hot_ref[:, at] = one_hot(row, rows)

    for o in range(members):
        make_hots(o)
    copies[1].wait()
    table = table_of([state_ref[0], state_ref[1]])
    for copy in copies[2:]:
        copy.wait()
    frac = load_segs(frac_ref, 0)
    ends = ends_of(frac)
    left, right = edge_columns(state_ref[0])
    me = lax.axis_index("frac")
    to_left = jnp.concatenate([ends[:, :LANES], left], axis=1)
    to_right = jnp.concatenate([right, ends[:, LANES:]], axis=1)
    whole = jnp.concatenate([frac, load_segs(frac_ref, 1)], axis=0)
    for o in range(members):
        one = slice(o, o + 1)
        row, _ = cell_parts(cell_ref[one, :], columns)
        cell_p, cell_s = pick(table, 2, rows, row, hot_ref[:, o * width : (o + 1) * width])
        live = iota((1, width), 1) < count_ref[0, o]
        out_ref[o, ROW_SEG : ROW_SEG + 1, :] = seg_ref[one, :].astype(F32)
        out_ref[o, ROW_TRANS : ROW_TRANS + 1, :] = jnp.where(live, trans_ref[one, :], 0.0)
        for t in range(ITERS):
            out_ref[o, ROW_UP + t : ROW_UP + t + 1, :] = up_ref[t, one, :].astype(F32)
        out_ref[o, ROW_P : ROW_P + 1, :] = cell_p
        out_ref[o, ROW_S : ROW_S + 1, :] = cell_s
        out_ref[o, ROW_ENDS : ROW_ENDS + 1, :] = jnp.where(me + 1 == o, to_right, to_left)
        out_ref[o, SUB:, :] = whole


def seg_parts(slot_ref, s):
    seg = slot_ref[s, ROW_SEG : ROW_SEG + 1, :].astype(jnp.int32)
    return seg // SEG_COLUMNS, seg % SEG_COLUMNS


def seg_hots(slot_ref, hot_ref, row_hot_ref, members, width):
    for s in range(members):
        row, lane = seg_parts(slot_ref, s)
        at = slice(s * width, (s + 1) * width)
        hot_ref[:, at] = one_hot(lane, SEG_COLUMNS)
        row_hot_ref[:, at] = one_hot(row, row_hot_ref.shape[0])


def seg_gather(slot_ref, hot_ref, fields, s, width, table):
    return pick(table, 2, fields, seg_parts(slot_ref, s)[0], hot_ref[:, s * width : (s + 1) * width])


def cell_spread(t, o, row_hot_ref, sent_ref, cell_row, seg_row, left_ref):
    seg_p, seg_s = seg_row
    cell_p, cell_s = cell_row
    weight, water = flow(
        sent_ref[o, ROW_TRANS : ROW_TRANS + 1, :],
        sent_ref[o, ROW_UP + t : ROW_UP + t + 1, :],
        cell_p,
        cell_s,
        seg_p,
        seg_s,
    )
    spread(left_ref, row_hot_ref, o, [weight, weight * seg_p, water])


def cell_finish(hot_ref, pressure, saturation, perm, left_ref, ring):
    rows = pressure.shape[0]
    couple, source, lost = gathered_sum(left_ref, hot_ref, 3, rows)
    inverse = 1.0 / (4.0 + perm + couple)
    new_saturation = saturation - TAU_STEP * lost / (perm + couple)
    return new_saturation, partial_residual(pressure, couple, source, inverse, ring), inverse


def cell_update(
    members, t, hot_ref, row_hot_ref, sent_ref, cell_rows, seg_rows, pressure, saturation, perm, left_ref, ring
):
    for o in range(members):
        cell_spread(t, o, row_hot_ref, sent_ref, cell_rows(o), seg_rows(o), left_ref)
    return cell_finish(hot_ref, pressure, saturation, perm, left_ref, ring)


def start_kernel(
    groups, members, size, slot_ref, sent_ref, cell_hot_ref, cell_row_hot_ref, frac_ref, aperture_ref,
    state_ref, perm_ref, out_ref, keep_ref, own_ref, new_ref, hot_ref, row_hot_ref,
    left_seg_ref, left_ref,
):
    width = slot_ref.shape[2]
    rows = new_ref.shape[1]
    g = lax.axis_index("grp")
    frac, sat = load_segs(frac_ref, 0), load_segs(frac_ref, 1)
    seg_hots(slot_ref, hot_ref, row_hot_ref, members, width)
    table = table_of([frac, sat])
    for s in range(members):
        seg_p, seg_s = seg_gather(slot_ref, hot_ref, rows, s, width, table)
        cell_p = slot_ref[s, ROW_P : ROW_P + 1, :]
        weight, water = flow(
            slot_ref[s, ROW_TRANS : ROW_TRANS + 1, :],
            slot_ref[s, ROW_UP : ROW_UP + 1, :],
            cell_p,
            slot_ref[s, ROW_S : ROW_S + 1, :],
            seg_p,
            seg_s,
        )
        spread(left_seg_ref, row_hot_ref, s, [weight * cell_p, weight, water])
        o = s
        row, lane = seg_parts(sent_ref, o)
        whole = table_of([slot_ref[o, SUB : SUB + rows, :], slot_ref[o, SUB + rows :, :]])
        seg_p, seg_s = pick(whole, 2, rows, row, one_hot(lane, SEG_COLUMNS))
        cell_spread(
            0,
            o,
            cell_row_hot_ref,
            sent_ref,
            (sent_ref[o, ROW_P : ROW_P + 1, :], sent_ref[o, ROW_S : ROW_S + 1, :]),
            (seg_p, seg_s),
            left_ref,
        )
    inflow, total, gained = gathered_sum(left_seg_ref, hot_ref, 3, rows)
    before, after = chain_ends(slot_ref, ROW_ENDS, members)
    new_frac, new_sat = frac_step(frac, sat, load_segs(aperture_ref), before, after, inflow, total, gained)
    new_ref[0] = new_frac
    new_ref[1] = new_sat
    table = table_of([new_frac, new_sat])
    me = lax.axis_index("frac")
    pressure = state_ref[0]
    new_saturation, q, inv = cell_finish(
        cell_hot_ref,
        pressure,
        state_ref[1],
        perm_ref[...],
        left_ref,
        ring_of(
            slot_ref[jnp.maximum(me - 1, 0), ROW_ENDS : ROW_ENDS + 1, :][:, :LANES],
            slot_ref[jnp.minimum(me + 1, members - 1), ROW_ENDS : ROW_ENDS + 1, :][:, LANES:],
            state_ref.shape[2],
            members,
        ),
    )
    for s in range(members):
        seg_p, seg_s = seg_gather(slot_ref, hot_ref, rows, s, width, table)
        own_ref[s, 0:1, :] = seg_p
        own_ref[s, 1:2, :] = seg_s
        at = (g * members + s) * size
        send_slots(out_ref, at, seg_p, seg_s)
    keep_ref[0] = pressure
    keep_ref[1] = new_saturation
    keep_ref[2] = q
    keep_ref[3] = inv
    ends = (new_frac[0:1, 0:1], new_frac[rows - 1 : rows, SEG_COLUMNS - 1 : SEG_COLUMNS])
    send_halo(out_ref, q, inv, pressure, groups, members, size, True, ends)


def cell_gather(members, cell_ref, hot_ref, fields, put):
    rows, columns = fields[0].shape
    width = cell_ref.shape[1]
    table = table_of(fields)
    for o in range(members):
        row, _ = cell_parts(cell_ref[o : o + 1, :], columns)
        put(o, *pick(table, len(fields), rows, row, hot_ref[:, o * width : (o + 1) * width]))


def middle_kernel(
    groups, members, size, open_size, halo_ref, cell_ref, hot_ref, row_hot_ref, sent_ref, kept_ref, perm_ref,
    out_ref, keep_ref, slots_ref, left_ref, *scratch,
):
    saturation = kept_ref[1]
    g = lax.axis_index("grp")

    def put_s(o, cell_s):
        slots_ref[o, 1:2, :] = cell_s

    cell_gather(members, cell_ref, hot_ref, [saturation], put_s)
    chebyshev(
        halo_ref, kept_ref.at[2], kept_ref.at[3], kept_ref.at[0], keep_ref.at[0], scratch, groups, members, size, True
    )
    pressure = keep_ref[0]

    def put_p(o, cell_p):
        slots_ref[o, 0:1, :] = cell_p
        send_slots(out_ref, (g * members + o) * open_size, cell_p, slots_ref[o, 1:2, :])

    cell_gather(members, cell_ref, hot_ref, [pressure], put_p)
    new_saturation, q, inv = cell_update(
        members,
        1,
        hot_ref,
        row_hot_ref,
        sent_ref,
        lambda o: (slots_ref[o, 0:1, :], slots_ref[o, 1:2, :]),
        lambda o: got_slots(halo_ref, (g * members + o) * size, cell_ref.shape[1]),
        pressure,
        saturation,
        perm_ref[...],
        left_ref,
        None,
    )
    keep_ref[1] = new_saturation
    keep_ref[2] = q
    keep_ref[3] = inv
    send_halo(out_ref, q, inv, pressure, groups, members, open_size, False)


def owner_spread(members, t, slot_ref, cell_rows, seg_rows, row_hot_ref, left_ref):
    for s in range(members):
        cell_p, cell_s = cell_rows(s)
        weight, water = flow(
            slot_ref[s, ROW_TRANS : ROW_TRANS + 1, :],
            slot_ref[s, ROW_UP + t : ROW_UP + t + 1, :],
            cell_p,
            cell_s,
            *seg_rows(s),
        )
        spread(left_ref, row_hot_ref, s, [weight * cell_p, weight, water])


def owner_update(
    members, t, slot_ref, cell_rows, seg_rows, frac, sat, aperture, ends, hot_ref, row_hot_ref, left_ref
):
    owner_spread(members, t, slot_ref, cell_rows, seg_rows, row_hot_ref, left_ref)
    inflow, total, gained = gathered_sum(left_ref, hot_ref, 3, frac.shape[0])
    return frac_step(frac, sat, aperture, *ends, inflow, total, gained)


def exchange_kernel(
    groups, members, closed_size, size, halo_ref, cell_ref, cell_hot_ref, slot_ref, hot_ref, row_hot_ref, ends_ref, own_ref,
    frac_ref, aperture_ref, kept_ref, out_ref, new_ref, pressure_ref, left_ref, *scratch,
):
    width = slot_ref.shape[2]
    g = lax.axis_index("grp")

    def cell_rows(s):
        return got_slots(halo_ref, (g * members + s) * size, width)

    me = lax.axis_index("frac")
    prior = ends_ref[(g * members + jnp.maximum(me - 1, 0)) * closed_size]
    later = ends_ref[(g * members + jnp.minimum(me + 1, members - 1)) * closed_size + SUB - 1]
    before = jnp.where(me > 0, prior[:, LANES - 2 : LANES - 1], 0.0)
    after = jnp.where(me < members - 1, later[:, 1:2], 0.0)

    rows, columns = pressure_ref.shape
    seg_wide = frac_ref.shape[1]
    owner_spread(
        members,
        1,
        slot_ref,
        cell_rows,
        lambda s: (own_ref[s, 0:1, :], own_ref[s, 1:2, :]),
        row_hot_ref,
        left_ref,
    )
    chebyshev(
        halo_ref, kept_ref.at[2], kept_ref.at[3], kept_ref.at[0], pressure_ref, scratch, groups, members, size, False
    )
    inflow, total, gained = gathered_sum(left_ref, hot_ref, 3, seg_wide)
    new_frac, new_sat = frac_step(
        frac_ref[0], frac_ref[1], load_segs(aperture_ref), before, after, inflow, total, gained
    )
    new_ref[0] = new_frac
    new_ref[1] = new_sat
    seg_table = table_of([new_frac, new_sat])
    ends = ends_of(new_frac)
    table = table_of([pressure_ref[...], kept_ref[1]])
    columns_row = jnp.concatenate(edge_columns(pressure_ref[...]), axis=1)
    for o in range(members):
        at = slice(o * width, (o + 1) * width)
        row, _ = cell_parts(cell_ref[o : o + 1, :], columns)
        cell_p, cell_s = pick(table, 2, rows, row, cell_hot_ref[:, at])
        out_ref[o, 0:1, :] = cell_p
        out_ref[o, 1:2, :] = cell_s
        seg_p, seg_s = pick(seg_table, 2, seg_wide, seg_parts(slot_ref, o)[0], hot_ref[:, at])
        out_ref[o, 2:3, :] = seg_p
        out_ref[o, 3:4, :] = seg_s
        out_ref[o, 4:5, :] = ends
        out_ref[o, 5:6, :] = columns_row


def source_last_kernel(
    groups, members, size, hot_ref, row_hot_ref, sent_ref, own_ref, seg_ref, pressure_ref, kept_ref, perm_ref,
    out_ref, keep_ref, left_ref,
):
    me = lax.axis_index("frac")
    pressure = pressure_ref[...]
    new_saturation, q, inv = cell_update(
        members,
        2,
        hot_ref,
        row_hot_ref,
        sent_ref,
        lambda o: (own_ref[o, 0:1, :], own_ref[o, 1:2, :]),
        lambda o: (seg_ref[o, 2:3, :], seg_ref[o, 3:4, :]),
        pressure,
        kept_ref[1],
        perm_ref[...],
        left_ref,
        ring_of(
            seg_ref[jnp.maximum(me - 1, 0), 5:6, :][:, LANES:],
            seg_ref[jnp.minimum(me + 1, members - 1), 5:6, :][:, :LANES],
            pressure_ref.shape[1],
            members,
        ),
    )
    keep_ref[0] = new_saturation
    keep_ref[1] = q
    keep_ref[2] = inv
    send_halo(out_ref, q, inv, pressure, groups, members, size, True)


def final_kernel(
    groups, members, size, halo_ref, pressure_ref, kept_ref, slot_ref, hot_ref, row_hot_ref, own_ref, seg_ref,
    frac_ref, aperture_ref, out_ref, new_ref, left_ref, *scratch,
):
    new_frac, new_sat = owner_update(
        members,
        2,
        slot_ref,
        lambda s: (seg_ref[s, 0:1, :], seg_ref[s, 1:2, :]),
        lambda s: (own_ref[s, 2:3, :], own_ref[s, 3:4, :]),
        frac_ref[0],
        frac_ref[1],
        load_segs(aperture_ref),
        chain_ends(seg_ref, 4, members),
        hot_ref,
        row_hot_ref,
        left_ref,
    )
    store_segs(new_ref, 0, new_frac)
    store_segs(new_ref, 1, new_sat)
    chebyshev(
        halo_ref, kept_ref.at[1], kept_ref.at[2], pressure_ref, out_ref.at[0], scratch, groups, members, size, True
    )
    out_ref[1] = kept_ref[0]


VMEM = pl.BlockSpec(memory_space=pltpu.VMEM)
HBM = pl.BlockSpec(memory_space=pltpu.HBM)


def call(kernel, statics, outs, scratch, *args, spec=VMEM):
    outs = [o if hasattr(o, "dtype") else jax.ShapeDtypeStruct(o, F32) for o in outs]
    return pl.pallas_call(
        functools.partial(kernel, *statics),
        out_shape=outs,
        in_specs=[spec] * len(args),
        out_specs=[VMEM] * len(outs),
        scratch_shapes=scratch,
        compiler_params=pltpu.CompilerParams(vmem_limit_bytes=32 * 1024 * 1024),
        name=kernel.__name__,
    )(*args)


def on_device(
    matrix_state,
    matrix_perm,
    frac_state,
    frac_aperture,
    link_cell,
    link_seg,
    link_trans,
    link_count,
    link_upwind,
):
    groups, members = lax.axis_size("grp"), lax.axis_size("frac")
    devices = groups * members
    cells = link_cell[0, 0]
    width = cells.shape[1]
    _, rows, columns = matrix_state.shape
    seg_dev = frac_state.shape[2]
    seg_rows = seg_dev // LANES
    frac = frac_state.reshape(2, seg_rows, LANES)
    aperture = frac_aperture.reshape(seg_rows, LANES)

    every = members * width
    slots = (members, SUB, width)
    closed_size, open_size = block_rows(columns, width, True), block_rows(columns, width, False)
    both = (groups, members, closed_size)
    halves = (groups, members, closed_size, open_size)
    halo, open_halo = (devices * closed_size, 1, LANES), (devices * open_size, 1, LANES)
    left_cell = pltpu.VMEM((3 * PARTS * rows, every), BF16)
    seg_wide = seg_dev // SEG_COLUMNS
    segs_wide = (2, seg_wide, SEG_COLUMNS)
    left_seg = pltpu.VMEM((3 * PARTS * seg_wide, every), BF16)
    tiles = columns // LANES + 1
    ext = [pltpu.VMEM((tiles, rows + SUB, LANES), F32)] * 4 + [pltpu.VMEM((tiles, rows + 3 * SUB, LANES), F32)] * 2

    def to_group(x):
        return lax.all_to_all(x, "frac", split_axis=0, concat_axis=0, tiled=True)

    def to_all(x):
        return lax.all_to_all(x, ("grp", "frac"), split_axis=0, concat_axis=0, tiled=True)

    def hots(*sizes):
        return [jax.ShapeDtypeStruct((n, every), BF16) for n in sizes]

    sent, cell_hot, cell_row_hot = call(
        first_kernel,
        (members,),
        [(members, SUB + 2 * seg_wide, SEG_COLUMNS)] + hots(columns, rows),
        [
            pltpu.VMEM((members, width), jnp.int32),
            pltpu.VMEM((members, width), jnp.int32),
            pltpu.VMEM((members, width), F32),
            pltpu.SMEM((1, members), jnp.int32),
            pltpu.VMEM((ITERS, members, width), jnp.int32),
            pltpu.VMEM(matrix_state.shape, F32),
            pltpu.VMEM(frac.shape, F32),
            pltpu.SemaphoreType.DMA((7,)),
        ],
        *[
            pltpu.with_memory_space_constraint(x, pltpu.HBM)
            for x in (
                cells, link_seg[0, 0], link_trans[0, 0], link_count[0], link_upwind[:, 0, 0], matrix_state, frac
            )
        ],
        spec=HBM,
    )
    slot = to_group(sent)
    edge, kept, own, frac1, hot, row_hot = call(
        start_kernel,
        both,
        [halo, (4, rows, columns), (members, 2, width), segs_wide] + hots(SEG_COLUMNS, seg_wide),
        [left_seg, left_cell],
        slot, sent, cell_hot, cell_row_hot, frac, aperture, matrix_state, matrix_perm,
    )
    before = to_all(edge)
    edge, kept = call(
        middle_kernel, halves, [open_halo, (4, rows, columns)], [pltpu.VMEM((members, 2, width), F32), left_cell] + ext,
        before, cells, cell_hot, cell_row_hot, sent, kept, matrix_perm,
    )
    around = to_all(edge)
    own, frac2, pressure = call(
        exchange_kernel, halves, [slots, segs_wide, (rows, columns)], [left_seg] + ext,
        around, cells, cell_hot, slot, hot, row_hot, before, own, frac1, aperture, kept,
    )
    segs = to_group(own)
    edge, kept = call(
        source_last_kernel, both, [halo, (3, rows, columns)], [left_cell],
        cell_hot, cell_row_hot, sent, own, segs, pressure, kept, matrix_perm,
    )
    around = to_all(edge)
    matrix_out, frac3 = call(
        final_kernel,
        both,
        [matrix_state.shape, frac.shape],
        [left_seg] + ext,
        around, pressure, kept, slot, hot, row_hot, own, segs, frac2, aperture,
    )
    return matrix_out, frac3.reshape(frac_state.shape)


def solution(mesh):
    return jax.shard_map(
        on_device,
        mesh=mesh,
        in_specs=(
            P(None, "grp", "frac"),
            P("grp", "frac"),
            P(None, "grp", "frac"),
            P("grp", "frac"),
            P("grp", "frac", None, None),
            P("grp", "frac", None, None),
            P("grp", "frac", None, None),
            P("grp", "frac", None),
            P(None, "grp", "frac", None, None),
        ),
        out_specs=(P(None, "grp", "frac"), P(None, "grp", "frac")),
        check_vma=False,
    )
```

```python
import functools

import jax
import jax.numpy as jnp
from jax import lax
from jax.experimental import pallas as pl
from jax.experimental.pallas import tpu as pltpu
from jax.sharding import PartitionSpec as P

ITERS = 3
SWEEPS = 4

LOW_BOUND = 0.02
HIGH_BOUND = 1.98
TAU_STEP = 0.5
MOBILITY_FLOOR = 0.2

F32 = jnp.float32
BF16 = jnp.bfloat16
LANES = 128
SUB = 8
SEG_COLUMNS = 2 * LANES
DEPTH = SWEEPS - 1


def iota(shape, dim):
    return lax.broadcasted_iota(jnp.int32, shape, dim)


def parts_of(x):
    high = x.astype(BF16).astype(F32)
    return high, x - high


PARTS = 2


def table_of(fields):
    split = [parts_of(f) for f in fields]
    return jnp.concatenate([s[p] for p in range(PARTS) for s in split], axis=0).astype(BF16)


def one_hot(index_row, count):
    shape = (count, index_row.shape[1])
    hit = iota(shape, 0).astype(F32).astype(BF16) == index_row.astype(F32).astype(BF16)
    return jnp.where(hit, jnp.ones(shape, BF16), jnp.zeros(shape, BF16))


def pick(table, fields, rows, row_index, hot):
    wide = jnp.dot(table, hot, preferred_element_type=F32)
    hit = iota((rows, row_index.shape[1]), 0) == row_index
    found = []
    for f in range(fields):
        total = sum(wide[(p * fields + f) * rows : (p * fields + f + 1) * rows] for p in range(PARTS))
        found.append(jnp.sum(jnp.where(hit, total, 0.0), axis=0, keepdims=True))
    return found


def spread(left_ref, row_hot_ref, block, values):
    rows = row_hot_ref.shape[0]
    width = values[0].shape[1]
    at = slice(block * width, (block + 1) * width)
    hot = row_hot_ref[:, at]
    for f, value in enumerate(values):
        for p, part in enumerate(parts_of(value)):
            row = (p * len(values) + f) * rows
            left_ref[row : row + rows, at] = hot * part.astype(BF16)


def gathered_sum(left_ref, hot_ref, fields, rows):
    wide = lax.dot_general(
        left_ref[...], hot_ref[...], (((1,), (1,)), ((), ())), preferred_element_type=F32
    )
    return [
        sum(wide[(p * fields + f) * rows : (p * fields + f + 1) * rows] for p in range(PARTS))
        for f in range(fields)
    ]


def flow(trans, upwind, cell_p, cell_s, seg_p, seg_s):
    u = jnp.where(upwind > 0.5, cell_s, seg_s)
    weight = trans * (MOBILITY_FLOOR + u * u)
    water = weight * (cell_p - seg_p) * u
    return weight, water


def cell_parts(cell_row, columns):
    return cell_row // columns, cell_row % columns


def load_segs(ref, *lead):
    rows = ref.shape[-2] // 2
    return jnp.concatenate([ref[(*lead, pl.ds(h, rows, 2), slice(None))] for h in range(2)], axis=1)


def store_segs(ref, lead, value):
    rows = value.shape[0]
    for h in range(2):
        ref[lead, pl.ds(h, rows, 2), :] = value[:, h * LANES : (h + 1) * LANES]


def ends_of(frac):
    rows, columns = frac.shape
    lane = iota((1, columns), 1)
    return jnp.where(lane < columns // 2, frac[0:1], frac[rows - 1 : rows])


def frac_step(frac, sat, aperture, before, after, inflow, total, gained):
    rows, lanes = frac.shape
    row, lane = iota((rows, lanes), 0), iota((rows, lanes), 1)
    back = pltpu.roll(frac, 1, 1)
    left = jnp.where(lane == 0, pltpu.roll(back, 1, 0), back)
    left = jnp.where((lane == 0) & (row == 0), before, left)
    ahead = pltpu.roll(frac, lanes - 1, 1)
    right = jnp.where(lane == lanes - 1, pltpu.roll(ahead, rows - 1, 0), ahead)
    right = jnp.where((lane == lanes - 1) & (row == rows - 1), after, right)
    new_frac = (aperture * frac + inflow + left + right) / (aperture + total + 2.0)
    new_sat = sat + TAU_STEP * gained / (aperture + total)
    return new_frac, new_sat


def chain_ends(ends_ref, row, members):
    me = lax.axis_index("frac")
    lanes = ends_ref.shape[2]
    prior = ends_ref[jnp.maximum(me - 1, 0), row : row + 1, :]
    later = ends_ref[jnp.minimum(me + 1, members - 1), row : row + 1, :]
    before = jnp.where(me > 0, prior[:, lanes - 1 :], 0.0)
    after = jnp.where(me < members - 1, later[:, 0:1], 0.0)
    return before, after


def partial_residual(pressure, couple, source, inverse, ring):
    rows, columns = pressure.shape
    row, col = iota((rows, columns), 0), iota((rows, columns), 1)
    beside = jnp.where(row == 0, 0.0, pltpu.roll(pressure, 1, 0))
    beside += jnp.where(row == rows - 1, 0.0, pltpu.roll(pressure, rows - 1, 0))
    beside += jnp.where(col == 0, 0.0, pltpu.roll(pressure, 1, 1))
    beside += jnp.where(col == columns - 1, 0.0, pltpu.roll(pressure, columns - 1, 1))
    if ring is not None:
        beside += ring
    return inverse * (source - (4.0 + couple) * pressure + beside)


def edge_columns(p):
    rows, columns = p.shape
    lane = iota((rows, LANES), 1)
    turned = jnp.transpose(jnp.where(lane < LANES // 2, p[:, :LANES], p[:, columns - LANES :]))
    return turned[0:1], turned[LANES - 1 : LANES]


def ring_of(left, right, columns, members):
    f = lax.axis_index("frac")
    rows = left.shape[1]
    left = jnp.where(f > 0, left, 0.0)
    right = jnp.where(f < members - 1, right, 0.0)
    turned = jnp.transpose(jnp.concatenate([left, jnp.zeros((LANES - 2, rows), F32), right], axis=0))
    lane = iota((rows, LANES), 1)
    low = jnp.where(lane == 0, turned, 0.0)
    high = jnp.where(lane == LANES - 1, turned, 0.0)
    if columns == LANES:
        return low + high
    return jnp.concatenate([low] + [jnp.zeros((rows, LANES), F32)] * (columns // LANES - 2) + [high], axis=1)


def pack_low(q, inv, p, at, axis):
    return jnp.where(
        at < DEPTH, q, jnp.where(at < 2 * DEPTH, pltpu.roll(inv, DEPTH, axis), pltpu.roll(p, 2 * DEPTH, axis))
    )


def pack_high(q, inv, p, at, axis):
    size = q.shape[axis]
    return jnp.where(
        at >= size - DEPTH,
        q,
        jnp.where(
            at >= size - 2 * DEPTH,
            pltpu.roll(inv, size - DEPTH, axis),
            pltpu.roll(p, size - 2 * DEPTH, axis),
        ),
    )


def block_rows(columns, width, closed):
    vertical = 2 * DEPTH * (columns // LANES)
    lateral = SUB + 2 * (width // LANES)
    return max(vertical, lateral) + (0 if closed else 1)


def put_rows(out_ref, at, values):
    for k in range(values.shape[0]):
        out_ref[at + k] = values[k : k + 1]


def get_rows(in_ref, at, count):
    return jnp.concatenate([in_ref[at + k] for k in range(count)], axis=0)


def send_slots(out_ref, at, first, second):
    halves = first.shape[1] // LANES
    for i, value in enumerate((first, second)):
        for h in range(halves):
            out_ref[at + SUB + i * halves + h] = value[:, h * LANES : (h + 1) * LANES]


def got_slots(in_ref, at, width):
    halves = width // LANES
    return [
        jnp.concatenate([in_ref[at + SUB + i * halves + h] for h in range(halves)], axis=1) for i in range(2)
    ]


def send_halo(out_ref, q, inv, p, groups, members, size, closed, ends=None):
    rows, columns = q.shape
    halves = columns // LANES
    g, f = lax.axis_index("grp"), lax.axis_index("frac")
    here = g * members + f
    lane = iota((rows, LANES), 1)
    low = pack_low(q[:, :LANES], inv[:, :LANES], p[:, :LANES], lane, 1)
    high = pack_high(q[:, columns - LANES :], inv[:, columns - LANES :], p[:, columns - LANES :], lane, 1)
    turned = jnp.transpose(jnp.where(lane < LANES // 2, low, high))
    left, right = turned[:SUB], turned[LANES - SUB :]
    if ends is not None:
        sub, lane = iota((SUB, LANES), 0), iota((SUB, LANES), 1)
        left = jnp.where((sub == SUB - 1) & (lane == 1), ends[0], left)
        right = jnp.where((sub == 0) & (lane == LANES - 2), ends[1], right)
    lane = iota((1, LANES), 1)
    spare = jnp.where(g + 2 < groups, here + 2 * members, here - 2 * members)

    for step in (-1, 1):
        layer = (lambda k: k) if step < 0 else (lambda k: rows - 1 - k)

        def span(field, count, at):
            start = 0 if step < 0 else rows - count
            return field[start : start + count, at]

        inside = (g + step >= 0) & (g + step < groups)
        base = here + step * members
        tiles = [slice(h * LANES, (h + 1) * LANES) for h in range(halves)]

        at = jnp.where(inside, base, spare) * size
        for h, tile in enumerate(tiles):
            put_rows(out_ref, at + h * DEPTH, span(q, DEPTH, tile))
            put_rows(out_ref, at + halves * DEPTH + h * (DEPTH - 1), span(inv, DEPTH - 1, tile))
            put_rows(out_ref, at + halves * (2 * DEPTH - 1) + h, span(p, 1, tile))
        if not closed:
            deep, next_p = layer(DEPTH - 1), layer(1)
            extra = jnp.where(
                lane == 0,
                inv[deep : deep + 1, tiles[0]],
                jnp.where(
                    lane == LANES - 1,
                    inv[deep : deep + 1, tiles[-1]],
                    jnp.where(
                        lane == 1,
                        pltpu.roll(p[next_p : next_p + 1, tiles[0]], 1, 1),
                        pltpu.roll(p[next_p : next_p + 1, tiles[-1]], LANES - 1, 1),
                    ),
                ),
            )
            out_ref[at + halves * 2 * DEPTH] = extra

        for side, tile, there in ((-1, tiles[0], f > 0), (1, tiles[-1], f < members - 1)):
            at = jnp.where(inside & there, base + side, spare) * size
            for i, field in enumerate((q, inv, p)):
                put_rows(out_ref, at + i * DEPTH, span(field, DEPTH, tile))

    put_rows(out_ref, jnp.where(f > 0, here - 1, spare) * size, left)
    put_rows(out_ref, jnp.where(f < members - 1, here + 1, spare) * size, right)


def chebyshev(in_ref, q_ref, inv_ref, p_ref, target, scratch, groups, members, size, closed):
    q_ext, inv_ext, p_ext, update_ref, even_ref, odd_ref = scratch
    rows, columns = target.shape
    halves = columns // LANES
    side = halves
    g, f = lax.axis_index("grp"), lax.axis_index("frac")
    here = g * members + f
    last = groups * members - 1

    def taker(dg, df):
        ok = (g + dg >= 0) & (g + dg < groups) & (f + df >= 0) & (f + df < members)
        at = jnp.clip(here + dg * members + df, 0, last) * size
        return lambda start, count: jnp.where(ok, get_rows(in_ref, at + start, count), 0.0)

    def both(low, high, at, count, size):
        return jnp.where(at < count, low, jnp.where(at >= size - count, high, 0.0))

    def filler(count):
        return jnp.zeros((count, LANES), F32)

    for h in range(halves):
        for ext, ref in ((q_ext, q_ref), (inv_ext, inv_ref), (p_ext, p_ref)):
            ext[h, 0:rows, :] = ref[:, h * LANES : (h + 1) * LANES]
    outer = slice(rows, rows + SUB)
    below, above = taker(1, 0), taker(-1, 0)
    lane = iota((1, LANES), 1)
    if not closed:
        low_extra, high_extra = below(halves * 2 * DEPTH, 1), above(halves * 2 * DEPTH, 1)
    for h in range(halves):
        edge = (lane == 0) & (h == 0) | (lane == LANES - 1) & (h == halves - 1)

        def at_edge(high, turn):
            if closed:
                return filler(1)
            row = high_extra if high else low_extra
            return jnp.where(edge, pltpu.roll(row, turn, 1) if turn else row, 0.0)

        turn = LANES - 1 if h == 0 else 1
        at = h * DEPTH
        q_ext[h, outer, :] = jnp.concatenate(
            [below(at, DEPTH), filler(SUB - 2 * DEPTH), above(at, DEPTH)], axis=0
        )
        at = halves * DEPTH + h * (DEPTH - 1)
        inv_ext[h, outer, :] = jnp.concatenate(
            [
                below(at, DEPTH - 1),
                at_edge(False, 0),
                filler(SUB - 2 * DEPTH),
                at_edge(True, 0),
                above(at, DEPTH - 1),
            ],
            axis=0,
        )
        at = halves * (2 * DEPTH - 1) + h
        p_ext[h, outer, :] = jnp.concatenate(
            [
                below(at, 1),
                at_edge(False, turn),
                filler(SUB - 4),
                at_edge(True, turn),
                above(at, 1),
            ],
            axis=0,
        )
    right, left = taker(0, 1)(0, SUB), taker(0, -1)(0, SUB)
    turned = jnp.transpose(
        jnp.concatenate([right, jnp.zeros((LANES - 2 * SUB, rows), F32), left], axis=0)
    )
    lane = iota((rows, LANES), 1)
    q_ext[side, 0:rows, :] = both(turned, turned, lane, DEPTH, LANES)
    inv_ext[side, 0:rows, :] = both(
        pltpu.roll(turned, LANES - DEPTH, 1), pltpu.roll(turned, DEPTH, 1), lane, DEPTH, LANES
    )
    p_ext[side, 0:rows, :] = both(
        pltpu.roll(turned, LANES - 2 * DEPTH, 1), pltpu.roll(turned, 2 * DEPTH, 1), lane, 2, LANES
    )
    lane = iota((DEPTH, LANES), 1)
    low_right, low_left, high_right, high_left = taker(1, 1), taker(1, -1), taker(-1, 1), taker(-1, -1)
    for i, ext in enumerate((q_ext, inv_ext, p_ext)):
        at = i * DEPTH
        ext[side, outer, :] = jnp.concatenate(
            [
                both(low_right(at, DEPTH), low_left(at, DEPTH), lane, DEPTH, LANES),
                filler(SUB - 2 * DEPTH),
                both(high_right(at, DEPTH), high_left(at, DEPTH), lane, DEPTH, LANES),
            ],
            axis=0,
        )

    end = rows + SUB - 1
    for own, other in ((0, end), (end, 0), (rows - 1, rows), (rows, rows - 1)):
        for c in range(halves + 1):
            q_ext[c, own : own + 1, :] += inv_ext[c, own : own + 1, :] * p_ext[c, other : other + 1, :]
    centre = 0.5 * (HIGH_BOUND + LOW_BOUND)
    half_width = 0.5 * (HIGH_BOUND - LOW_BOUND)
    scale_ratio = centre / half_width
    ratio_now = 1.0 / scale_ratio
    lane = iota((SUB, LANES), 1)
    count = rows // SUB + 1

    def keep(ref, c, r, value):
        at = (r + 1) * SUB
        ref[c, at : at + SUB, :] = value
        if r == count - 1:
            ref[c, 0:SUB, :] = value
        if r == 0:
            at = (count + 1) * SUB
            ref[c, at : at + SUB, :] = value

    for r in range(count):
        at = slice(r * SUB, (r + 1) * SUB)
        if closed:
            for c in range(halves + 1):
                start = q_ext[c, at, :]
                keep(even_ref, c, r, start / centre if centre != 1.0 else start)
            continue
        p_side, p_first, p_final = p_ext[side, at, :], p_ext[0, at, :], p_ext[halves - 1, at, :]
        missing = [0.0] * (halves + 1)
        missing[0] += jnp.where(lane == 0, pltpu.roll(p_side, 1, 1), 0.0)
        missing[halves - 1] += jnp.where(lane == LANES - 1, pltpu.roll(p_side, LANES - 1, 1), 0.0)
        missing[side] = jnp.where(
            lane == 0,
            pltpu.roll(p_final, 1, 1),
            jnp.where(lane == LANES - 1, pltpu.roll(p_first, LANES - 1, 1), 0.0),
        )
        for c in range(halves + 1):
            start = q_ext[c, at, :] + inv_ext[c, at, :] * missing[c]
            q_ext[c, at, :] = start
            keep(even_ref, c, r, start / centre if centre != 1.0 else start)
    now_ref, next_ref = even_ref, odd_ref
    for sweep in range(1, SWEEPS):
        ratio_next = 1.0 / (2.0 * scale_ratio - ratio_now)
        final = sweep == SWEEPS - 1
        for r in range(count - 1 if final else count):
            at = slice(r * SUB, (r + 1) * SUB)
            mids = [now_ref[c, (r + 1) * SUB : (r + 2) * SUB, :] for c in range(halves + 1)]
            after = [pltpu.roll(m, 1, 1) for m in mids]
            ahead = [pltpu.roll(m, LANES - 1, 1) for m in mids]
            for c in range(halves if final else halves + 1):
                beside = now_ref[c, (r + 1) * SUB - 1 : (r + 2) * SUB - 1, :]
                beside += now_ref[c, (r + 1) * SUB + 1 : (r + 2) * SUB + 1, :]
                beside += jnp.where(lane == 0, after[(c - 1) % (halves + 1)], after[c])
                beside += jnp.where(lane == LANES - 1, ahead[(c + 1) % (halves + 1)], ahead[c])
                residual = q_ext[c, at, :] - mids[c] + inv_ext[c, at, :] * beside
                old = mids[c] if sweep == 1 else update_ref[c, at, :]
                update = ratio_next * ratio_now * old + (2.0 * ratio_next / half_width) * residual
                if final:
                    tile = slice(c * LANES, (c + 1) * LANES)
                    target[at, tile] = p_ref[at, tile] + mids[c] + update
                else:
                    update_ref[c, at, :] = update
                    keep(next_ref, c, r, mids[c] + update)
        ratio_now = ratio_next
        now_ref, next_ref = next_ref, now_ref


ROW_SEG = 0
ROW_TRANS = 1
ROW_UP = 2
ROW_P = ROW_UP + ITERS
ROW_S = ROW_P + 1
ROW_ENDS = ROW_S + 1


def first_kernel(
    members, cell_any, seg_any, trans_any, count_any, up_any, state_any, frac_any,
    out_ref, hot_ref, row_hot_ref, cell_ref, seg_ref, trans_ref, count_ref, up_ref, state_ref, frac_ref, sem,
):
    _, rows, columns = state_ref.shape
    width = cell_ref.shape[1]
    copies = [
        pltpu.make_async_copy(source, target, sem.at[i])
        for i, (source, target) in enumerate(
            [
                (cell_any, cell_ref),
                (state_any, state_ref),
                (seg_any, seg_ref),
                (trans_any, trans_ref),
                (count_any, count_ref),
                (up_any, up_ref),
                (frac_any, frac_ref),
            ]
        )
    ]
    for copy in copies:
        copy.start()
    copies[0].wait()

    def make_hots(o):
        row, col = cell_parts(cell_ref[o : o + 1, :], columns)
        at = slice(o * width, (o + 1) * width)
        hot_ref[:, at] = one_hot(col, columns)
        row_hot_ref[:, at] = one_hot(row, rows)

    for o in range(members):
        make_hots(o)
    copies[1].wait()
    table = table_of([state_ref[0], state_ref[1]])
    for copy in copies[2:]:
        copy.wait()
    frac = load_segs(frac_ref, 0)
    ends = ends_of(frac)
    left, right = edge_columns(state_ref[0])
    me = lax.axis_index("frac")
    to_left = jnp.concatenate([ends[:, :LANES], left], axis=1)
    to_right = jnp.concatenate([right, ends[:, LANES:]], axis=1)
    whole = jnp.concatenate([frac, load_segs(frac_ref, 1)], axis=0)
    for o in range(members):
        one = slice(o, o + 1)
        row, _ = cell_parts(cell_ref[one, :], columns)
        cell_p, cell_s = pick(table, 2, rows, row, hot_ref[:, o * width : (o + 1) * width])
        live = iota((1, width), 1) < count_ref[0, o]
        out_ref[o, ROW_SEG : ROW_SEG + 1, :] = seg_ref[one, :].astype(F32)
        out_ref[o, ROW_TRANS : ROW_TRANS + 1, :] = jnp.where(live, trans_ref[one, :], 0.0)
        for t in range(ITERS):
            out_ref[o, ROW_UP + t : ROW_UP + t + 1, :] = up_ref[t, one, :].astype(F32)
        out_ref[o, ROW_P : ROW_P + 1, :] = cell_p
        out_ref[o, ROW_S : ROW_S + 1, :] = cell_s
        out_ref[o, ROW_ENDS : ROW_ENDS + 1, :] = jnp.where(me + 1 == o, to_right, to_left)
        out_ref[o, SUB:, :] = whole


def seg_parts(slot_ref, s):
    seg = slot_ref[s, ROW_SEG : ROW_SEG + 1, :].astype(jnp.int32)
    return seg // SEG_COLUMNS, seg % SEG_COLUMNS


def seg_hots(slot_ref, hot_ref, row_hot_ref, members, width):
    for s in range(members):
        row, lane = seg_parts(slot_ref, s)
        at = slice(s * width, (s + 1) * width)
        hot_ref[:, at] = one_hot(lane, SEG_COLUMNS)
        row_hot_ref[:, at] = one_hot(row, row_hot_ref.shape[0])


def seg_gather(slot_ref, hot_ref, fields, s, width, table):
    return pick(table, 2, fields, seg_parts(slot_ref, s)[0], hot_ref[:, s * width : (s + 1) * width])


def cell_spread(t, o, row_hot_ref, sent_ref, cell_row, seg_row, left_ref):
    seg_p, seg_s = seg_row
    cell_p, cell_s = cell_row
    weight, water = flow(
        sent_ref[o, ROW_TRANS : ROW_TRANS + 1, :],
        sent_ref[o, ROW_UP + t : ROW_UP + t + 1, :],
        cell_p,
        cell_s,
        seg_p,
        seg_s,
    )
    spread(left_ref, row_hot_ref, o, [weight, weight * seg_p, water])


def cell_finish(hot_ref, pressure, saturation, perm, left_ref, ring):
    rows = pressure.shape[0]
    couple, source, lost = gathered_sum(left_ref, hot_ref, 3, rows)
    inverse = 1.0 / (4.0 + perm + couple)
    new_saturation = saturation - TAU_STEP * lost / (perm + couple)
    return new_saturation, partial_residual(pressure, couple, source, inverse, ring), inverse


def cell_update(
    members, t, hot_ref, row_hot_ref, sent_ref, cell_rows, seg_rows, pressure, saturation, perm, left_ref, ring
):
    for o in range(members):
        cell_spread(t, o, row_hot_ref, sent_ref, cell_rows(o), seg_rows(o), left_ref)
    return cell_finish(hot_ref, pressure, saturation, perm, left_ref, ring)


def start_kernel(
    groups, members, size, slot_ref, sent_ref, cell_hot_ref, cell_row_hot_ref, frac_ref, aperture_ref,
    state_ref, perm_ref, out_ref, keep_ref, own_ref, new_ref, hot_ref, row_hot_ref,
    left_seg_ref, left_ref,
):
    width = slot_ref.shape[2]
    rows = new_ref.shape[1]
    g = lax.axis_index("grp")
    frac, sat = load_segs(frac_ref, 0), load_segs(frac_ref, 1)
    seg_hots(slot_ref, hot_ref, row_hot_ref, members, width)
    table = table_of([frac, sat])
    for s in range(members):
        seg_p, seg_s = seg_gather(slot_ref, hot_ref, rows, s, width, table)
        cell_p = slot_ref[s, ROW_P : ROW_P + 1, :]
        weight, water = flow(
            slot_ref[s, ROW_TRANS : ROW_TRANS + 1, :],
            slot_ref[s, ROW_UP : ROW_UP + 1, :],
            cell_p,
            slot_ref[s, ROW_S : ROW_S + 1, :],
            seg_p,
            seg_s,
        )
        spread(left_seg_ref, row_hot_ref, s, [weight * cell_p, weight, water])
        o = s
        row, lane = seg_parts(sent_ref, o)
        whole = table_of([slot_ref[o, SUB : SUB + rows, :], slot_ref[o, SUB + rows :, :]])
        seg_p, seg_s = pick(whole, 2, rows, row, one_hot(lane, SEG_COLUMNS))
        cell_spread(
            0,
            o,
            cell_row_hot_ref,
            sent_ref,
            (sent_ref[o, ROW_P : ROW_P + 1, :], sent_ref[o, ROW_S : ROW_S + 1, :]),
            (seg_p, seg_s),
            left_ref,
        )
    inflow, total, gained = gathered_sum(left_seg_ref, hot_ref, 3, rows)
    before, after = chain_ends(slot_ref, ROW_ENDS, members)
    new_frac, new_sat = frac_step(frac, sat, load_segs(aperture_ref), before, after, inflow, total, gained)
    new_ref[0] = new_frac
    new_ref[1] = new_sat
    table = table_of([new_frac, new_sat])
    me = lax.axis_index("frac")
    pressure = state_ref[0]
    new_saturation, q, inv = cell_finish(
        cell_hot_ref,
        pressure,
        state_ref[1],
        perm_ref[...],
        left_ref,
        ring_of(
            slot_ref[jnp.maximum(me - 1, 0), ROW_ENDS : ROW_ENDS + 1, :][:, :LANES],
            slot_ref[jnp.minimum(me + 1, members - 1), ROW_ENDS : ROW_ENDS + 1, :][:, LANES:],
            state_ref.shape[2],
            members,
        ),
    )
    for s in range(members):
        seg_p, seg_s = seg_gather(slot_ref, hot_ref, rows, s, width, table)
        own_ref[s, 0:1, :] = seg_p
        own_ref[s, 1:2, :] = seg_s
        at = (g * members + s) * size
        send_slots(out_ref, at, seg_p, seg_s)
    keep_ref[0] = pressure
    keep_ref[1] = new_saturation
    keep_ref[2] = q
    keep_ref[3] = inv
    ends = (new_frac[0:1, 0:1], new_frac[rows - 1 : rows, SEG_COLUMNS - 1 : SEG_COLUMNS])
    send_halo(out_ref, q, inv, pressure, groups, members, size, True, ends)


def cell_gather(members, cell_ref, hot_ref, fields, put):
    rows, columns = fields[0].shape
    width = cell_ref.shape[1]
    table = table_of(fields)
    for o in range(members):
        row, _ = cell_parts(cell_ref[o : o + 1, :], columns)
        put(o, *pick(table, len(fields), rows, row, hot_ref[:, o * width : (o + 1) * width]))


def middle_kernel(
    groups, members, size, open_size, halo_ref, cell_ref, hot_ref, row_hot_ref, sent_ref, kept_ref, perm_ref,
    out_ref, keep_ref, slots_ref, left_ref, *scratch,
):
    saturation = kept_ref[1]
    g = lax.axis_index("grp")

    def put_s(o, cell_s):
        slots_ref[o, 1:2, :] = cell_s

    cell_gather(members, cell_ref, hot_ref, [saturation], put_s)
    chebyshev(
        halo_ref, kept_ref.at[2], kept_ref.at[3], kept_ref.at[0], keep_ref.at[0], scratch, groups, members, size, True
    )
    pressure = keep_ref[0]

    rows, columns = pressure.shape
    width = cell_ref.shape[1]
    table = table_of([pressure])
    for o in range(members):
        row, _ = cell_parts(cell_ref[o : o + 1, :], columns)
        (cell_p,) = pick(table, 1, rows, row, hot_ref[:, o * width : (o + 1) * width])
        cell_s = slots_ref[o, 1:2, :]
        send_slots(out_ref, (g * members + o) * open_size, cell_p, cell_s)
        cell_spread(
            1,
            o,
            row_hot_ref,
            sent_ref,
            (cell_p, cell_s),
            got_slots(halo_ref, (g * members + o) * size, width),
            left_ref,
        )
    new_saturation, q, inv = cell_finish(hot_ref, pressure, saturation, perm_ref[...], left_ref, None)
    keep_ref[1] = new_saturation
    keep_ref[2] = q
    keep_ref[3] = inv
    send_halo(out_ref, q, inv, pressure, groups, members, open_size, False)


def owner_spread(blocks, t, slot_ref, cell_rows, seg_rows, row_hot_ref, left_ref):
    for s in blocks:
        cell_p, cell_s = cell_rows(s)
        weight, water = flow(
            slot_ref[s, ROW_TRANS : ROW_TRANS + 1, :],
            slot_ref[s, ROW_UP + t : ROW_UP + t + 1, :],
            cell_p,
            cell_s,
            *seg_rows(s),
        )
        spread(left_ref, row_hot_ref, s, [weight * cell_p, weight, water])


def owner_update(
    members, t, slot_ref, cell_rows, seg_rows, frac, sat, aperture, ends, hot_ref, row_hot_ref, left_ref
):
    owner_spread(range(members), t, slot_ref, cell_rows, seg_rows, row_hot_ref, left_ref)
    inflow, total, gained = gathered_sum(left_ref, hot_ref, 3, frac.shape[0])
    return frac_step(frac, sat, aperture, *ends, inflow, total, gained)


def exchange_kernel(
    groups, members, closed_size, size, halo_ref, cell_ref, cell_hot_ref, slot_ref, hot_ref, row_hot_ref, ends_ref, own_ref,
    frac_ref, aperture_ref, kept_ref, out_ref, new_ref, pressure_ref, left_ref, *scratch,
):
    width = slot_ref.shape[2]
    g = lax.axis_index("grp")

    def cell_rows(s):
        return got_slots(halo_ref, (g * members + s) * size, width)

    me = lax.axis_index("frac")
    prior = ends_ref[(g * members + jnp.maximum(me - 1, 0)) * closed_size]
    later = ends_ref[(g * members + jnp.minimum(me + 1, members - 1)) * closed_size + SUB - 1]
    before = jnp.where(me > 0, prior[:, LANES - 2 : LANES - 1], 0.0)
    after = jnp.where(me < members - 1, later[:, 1:2], 0.0)

    rows, columns = pressure_ref.shape
    seg_wide = frac_ref.shape[1]
    owner_spread(
        range(members),
        1,
        slot_ref,
        cell_rows,
        lambda s: (own_ref[s, 0:1, :], own_ref[s, 1:2, :]),
        row_hot_ref,
        left_ref,
    )
    inflow, total, gained = gathered_sum(left_ref, hot_ref, 3, seg_wide)
    new_frac, new_sat = frac_step(
        frac_ref[0], frac_ref[1], load_segs(aperture_ref), before, after, inflow, total, gained
    )
    new_ref[0] = new_frac
    new_ref[1] = new_sat
    seg_table = table_of([new_frac, new_sat])
    ends = ends_of(new_frac)
    s_table = table_of([kept_ref[1]])
    for o in range(members):
        at = slice(o * width, (o + 1) * width)
        row, _ = cell_parts(cell_ref[o : o + 1, :], columns)
        (cell_s,) = pick(s_table, 1, rows, row, cell_hot_ref[:, at])
        out_ref[o, 1:2, :] = cell_s
    chebyshev(
        halo_ref, kept_ref.at[2], kept_ref.at[3], kept_ref.at[0], pressure_ref, scratch, groups, members, size, False
    )
    p_table = table_of([pressure_ref[...]])
    columns_row = jnp.concatenate(edge_columns(pressure_ref[...]), axis=1)
    for o in range(members):
        at = slice(o * width, (o + 1) * width)
        seg_p, seg_s = pick(seg_table, 2, seg_wide, seg_parts(slot_ref, o)[0], hot_ref[:, at])
        out_ref[o, 2:3, :] = seg_p
        out_ref[o, 3:4, :] = seg_s
        out_ref[o, 4:5, :] = ends
        row, _ = cell_parts(cell_ref[o : o + 1, :], columns)
        (cell_p,) = pick(p_table, 1, rows, row, cell_hot_ref[:, at])
        out_ref[o, 0:1, :] = cell_p
        out_ref[o, 5:6, :] = columns_row


def source_last_kernel(
    groups, members, size, hot_ref, row_hot_ref, sent_ref, own_ref, seg_ref, pressure_ref, kept_ref, perm_ref,
    out_ref, keep_ref, left_ref,
):
    me = lax.axis_index("frac")
    pressure = pressure_ref[...]
    new_saturation, q, inv = cell_update(
        members,
        2,
        hot_ref,
        row_hot_ref,
        sent_ref,
        lambda o: (own_ref[o, 0:1, :], own_ref[o, 1:2, :]),
        lambda o: (seg_ref[o, 2:3, :], seg_ref[o, 3:4, :]),
        pressure,
        kept_ref[1],
        perm_ref[...],
        left_ref,
        ring_of(
            seg_ref[jnp.maximum(me - 1, 0), 5:6, :][:, LANES:],
            seg_ref[jnp.minimum(me + 1, members - 1), 5:6, :][:, :LANES],
            pressure_ref.shape[1],
            members,
        ),
    )
    keep_ref[0] = new_saturation
    keep_ref[1] = q
    keep_ref[2] = inv
    send_halo(out_ref, q, inv, pressure, groups, members, size, True)


def final_kernel(
    groups, members, size, halo_ref, pressure_ref, kept_ref, slot_ref, hot_ref, row_hot_ref, own_ref, seg_ref,
    frac_ref, aperture_ref, out_ref, new_ref, left_ref, *scratch,
):
    new_frac, new_sat = owner_update(
        members,
        2,
        slot_ref,
        lambda s: (seg_ref[s, 0:1, :], seg_ref[s, 1:2, :]),
        lambda s: (own_ref[s, 2:3, :], own_ref[s, 3:4, :]),
        frac_ref[0],
        frac_ref[1],
        load_segs(aperture_ref),
        chain_ends(seg_ref, 4, members),
        hot_ref,
        row_hot_ref,
        left_ref,
    )
    store_segs(new_ref, 0, new_frac)
    store_segs(new_ref, 1, new_sat)
    chebyshev(
        halo_ref, kept_ref.at[1], kept_ref.at[2], pressure_ref, out_ref.at[0], scratch, groups, members, size, True
    )
    out_ref[1] = kept_ref[0]


VMEM = pl.BlockSpec(memory_space=pltpu.VMEM)
HBM = pl.BlockSpec(memory_space=pltpu.HBM)


def call(kernel, statics, outs, scratch, *args, spec=VMEM):
    outs = [o if hasattr(o, "dtype") else jax.ShapeDtypeStruct(o, F32) for o in outs]
    return pl.pallas_call(
        functools.partial(kernel, *statics),
        out_shape=outs,
        in_specs=[spec] * len(args),
        out_specs=[VMEM] * len(outs),
        scratch_shapes=scratch,
        compiler_params=pltpu.CompilerParams(vmem_limit_bytes=32 * 1024 * 1024),
        name=kernel.__name__,
    )(*args)


def on_device(
    matrix_state,
    matrix_perm,
    frac_state,
    frac_aperture,
    link_cell,
    link_seg,
    link_trans,
    link_count,
    link_upwind,
):
    groups, members = lax.axis_size("grp"), lax.axis_size("frac")
    devices = groups * members
    cells = link_cell[0, 0]
    width = cells.shape[1]
    _, rows, columns = matrix_state.shape
    seg_dev = frac_state.shape[2]
    seg_rows = seg_dev // LANES
    frac = frac_state.reshape(2, seg_rows, LANES)
    aperture = frac_aperture.reshape(seg_rows, LANES)

    every = members * width
    slots = (members, SUB, width)
    closed_size, open_size = block_rows(columns, width, True), block_rows(columns, width, False)
    both = (groups, members, closed_size)
    halves = (groups, members, closed_size, open_size)
    halo, open_halo = (devices * closed_size, 1, LANES), (devices * open_size, 1, LANES)
    left_cell = pltpu.VMEM((3 * PARTS * rows, every), BF16)
    seg_wide = seg_dev // SEG_COLUMNS
    segs_wide = (2, seg_wide, SEG_COLUMNS)
    left_seg = pltpu.VMEM((3 * PARTS * seg_wide, every), BF16)
    tiles = columns // LANES + 1
    ext = [pltpu.VMEM((tiles, rows + SUB, LANES), F32)] * 4 + [pltpu.VMEM((tiles, rows + 3 * SUB, LANES), F32)] * 2

    def to_group(x):
        return lax.all_to_all(x, "frac", split_axis=0, concat_axis=0, tiled=True)

    def to_all(x):
        return lax.all_to_all(x, ("grp", "frac"), split_axis=0, concat_axis=0, tiled=True)

    def hots(*sizes):
        return [jax.ShapeDtypeStruct((n, every), BF16) for n in sizes]

    sent, cell_hot, cell_row_hot = call(
        first_kernel,
        (members,),
        [(members, SUB + 2 * seg_wide, SEG_COLUMNS)] + hots(columns, rows),
        [
            pltpu.VMEM((members, width), jnp.int32),
            pltpu.VMEM((members, width), jnp.int32),
            pltpu.VMEM((members, width), F32),
            pltpu.SMEM((1, members), jnp.int32),
            pltpu.VMEM((ITERS, members, width), jnp.int32),
            pltpu.VMEM(matrix_state.shape, F32),
            pltpu.VMEM(frac.shape, F32),
            pltpu.SemaphoreType.DMA((7,)),
        ],
        *[
            pltpu.with_memory_space_constraint(x, pltpu.HBM)
            for x in (
                cells, link_seg[0, 0], link_trans[0, 0], link_count[0], link_upwind[:, 0, 0], matrix_state, frac
            )
        ],
        spec=HBM,
    )
    slot = to_group(sent)
    edge, kept, own, frac1, hot, row_hot = call(
        start_kernel,
        both,
        [halo, (4, rows, columns), (members, 2, width), segs_wide] + hots(SEG_COLUMNS, seg_wide),
        [left_seg, left_cell],
        slot, sent, cell_hot, cell_row_hot, frac, aperture, matrix_state, matrix_perm,
    )
    before = to_all(edge)
    edge, kept = call(
        middle_kernel, halves, [open_halo, (4, rows, columns)], [pltpu.VMEM((members, 2, width), F32), left_cell] + ext,
        before, cells, cell_hot, cell_row_hot, sent, kept, matrix_perm,
    )
    around = to_all(edge)
    own, frac2, pressure = call(
        exchange_kernel, halves, [slots, segs_wide, (rows, columns)], [left_seg] + ext,
        around, cells, cell_hot, slot, hot, row_hot, before, own, frac1, aperture, kept,
    )
    segs = to_group(own)
    edge, kept = call(
        source_last_kernel, both, [halo, (3, rows, columns)], [left_cell],
        cell_hot, cell_row_hot, sent, own, segs, pressure, kept, matrix_perm,
    )
    around = to_all(edge)
    matrix_out, frac3 = call(
        final_kernel,
        both,
        [matrix_state.shape, frac.shape],
        [left_seg] + ext,
        around, pressure, kept, slot, hot, row_hot, own, segs, frac2, aperture,
    )
    return matrix_out, frac3.reshape(frac_state.shape)


def solution(mesh):
    return jax.shard_map(
        on_device,
        mesh=mesh,
        in_specs=(
            P(None, "grp", "frac"),
            P("grp", "frac"),
            P(None, "grp", "frac"),
            P("grp", "frac"),
            P("grp", "frac", None, None),
            P("grp", "frac", None, None),
            P("grp", "frac", None, None),
            P("grp", "frac", None),
            P(None, "grp", "frac", None, None),
        ),
        out_specs=(P(None, "grp", "frac"), P(None, "grp", "frac")),
        check_vma=False,
    )
```

```python
import functools

import jax
import jax.numpy as jnp
from jax import lax
from jax.experimental import pallas as pl
from jax.experimental.pallas import tpu as pltpu
from jax.sharding import PartitionSpec as P

ITERS = 3
SWEEPS = 4

LOW_BOUND = 0.02
HIGH_BOUND = 1.98
TAU_STEP = 0.5
MOBILITY_FLOOR = 0.2

F32 = jnp.float32
BF16 = jnp.bfloat16
LANES = 128
SUB = 8
SEG_COLUMNS = 2 * LANES
DEPTH = SWEEPS - 1


def iota(shape, dim):
    return lax.broadcasted_iota(jnp.int32, shape, dim)


def parts_of(x):
    high = x.astype(BF16).astype(F32)
    return high, x - high


PARTS = 2


def table_of(fields):
    split = [parts_of(f) for f in fields]
    return jnp.concatenate([s[p] for p in range(PARTS) for s in split], axis=0).astype(BF16)


def one_hot(index_row, count):
    shape = (count, index_row.shape[1])
    hit = iota(shape, 0).astype(F32).astype(BF16) == index_row.astype(F32).astype(BF16)
    return jnp.where(hit, jnp.ones(shape, BF16), jnp.zeros(shape, BF16))


def pick(table, fields, rows, row_index, hot):
    wide = jnp.dot(table, hot, preferred_element_type=F32)
    hit = iota((rows, row_index.shape[1]), 0) == row_index
    found = []
    for f in range(fields):
        total = sum(wide[(p * fields + f) * rows : (p * fields + f + 1) * rows] for p in range(PARTS))
        found.append(jnp.sum(jnp.where(hit, total, 0.0), axis=0, keepdims=True))
    return found


def spread(left_ref, row_hot_ref, block, values):
    rows = row_hot_ref.shape[0]
    width = values[0].shape[1]
    at = slice(block * width, (block + 1) * width)
    hot = row_hot_ref[:, at]
    for f, value in enumerate(values):
        for p, part in enumerate(parts_of(value)):
            row = (p * len(values) + f) * rows
            left_ref[row : row + rows, at] = hot * part.astype(BF16)


def gathered_sum(left_ref, hot_ref, fields, rows):
    wide = lax.dot_general(
        left_ref[...], hot_ref[...], (((1,), (1,)), ((), ())), preferred_element_type=F32
    )
    return [
        sum(wide[(p * fields + f) * rows : (p * fields + f + 1) * rows] for p in range(PARTS))
        for f in range(fields)
    ]


def flow(trans, upwind, cell_p, cell_s, seg_p, seg_s):
    u = jnp.where(upwind > 0.5, cell_s, seg_s)
    weight = trans * (MOBILITY_FLOOR + u * u)
    water = weight * (cell_p - seg_p) * u
    return weight, water


def cell_parts(cell_row, columns):
    return cell_row // columns, cell_row % columns


def load_segs(ref, *lead):
    rows = ref.shape[-2] // 2
    return jnp.concatenate([ref[(*lead, pl.ds(h, rows, 2), slice(None))] for h in range(2)], axis=1)


def store_segs(ref, lead, value):
    rows = value.shape[0]
    for h in range(2):
        ref[lead, pl.ds(h, rows, 2), :] = value[:, h * LANES : (h + 1) * LANES]


def ends_of(frac):
    rows, columns = frac.shape
    lane = iota((1, columns), 1)
    return jnp.where(lane < columns // 2, frac[0:1], frac[rows - 1 : rows])


def frac_step(frac, sat, aperture, before, after, inflow, total, gained):
    rows, lanes = frac.shape
    row, lane = iota((rows, lanes), 0), iota((rows, lanes), 1)
    back = pltpu.roll(frac, 1, 1)
    left = jnp.where(lane == 0, pltpu.roll(back, 1, 0), back)
    left = jnp.where((lane == 0) & (row == 0), before, left)
    ahead = pltpu.roll(frac, lanes - 1, 1)
    right = jnp.where(lane == lanes - 1, pltpu.roll(ahead, rows - 1, 0), ahead)
    right = jnp.where((lane == lanes - 1) & (row == rows - 1), after, right)
    new_frac = (aperture * frac + inflow + left + right) / (aperture + total + 2.0)
    new_sat = sat + TAU_STEP * gained / (aperture + total)
    return new_frac, new_sat


def chain_ends(ends_ref, row, members):
    me = lax.axis_index("frac")
    lanes = ends_ref.shape[2]
    prior = ends_ref[jnp.maximum(me - 1, 0), row : row + 1, :]
    later = ends_ref[jnp.minimum(me + 1, members - 1), row : row + 1, :]
    before = jnp.where(me > 0, prior[:, lanes - 1 :], 0.0)
    after = jnp.where(me < members - 1, later[:, 0:1], 0.0)
    return before, after


def partial_residual(pressure, couple, source, inverse, ring):
    rows, columns = pressure.shape
    row, col = iota((rows, columns), 0), iota((rows, columns), 1)
    beside = jnp.where(row == 0, 0.0, pltpu.roll(pressure, 1, 0))
    beside += jnp.where(row == rows - 1, 0.0, pltpu.roll(pressure, rows - 1, 0))
    beside += jnp.where(col == 0, 0.0, pltpu.roll(pressure, 1, 1))
    beside += jnp.where(col == columns - 1, 0.0, pltpu.roll(pressure, columns - 1, 1))
    if ring is not None:
        beside += ring
    return inverse * (source - (4.0 + couple) * pressure + beside)


def edge_columns(p):
    rows, columns = p.shape
    lane = iota((rows, LANES), 1)
    turned = jnp.transpose(jnp.where(lane < LANES // 2, p[:, :LANES], p[:, columns - LANES :]))
    return turned[0:1], turned[LANES - 1 : LANES]


def ring_of(left, right, columns, members):
    f = lax.axis_index("frac")
    rows = left.shape[1]
    left = jnp.where(f > 0, left, 0.0)
    right = jnp.where(f < members - 1, right, 0.0)
    turned = jnp.transpose(jnp.concatenate([left, jnp.zeros((LANES - 2, rows), F32), right], axis=0))
    lane = iota((rows, LANES), 1)
    low = jnp.where(lane == 0, turned, 0.0)
    high = jnp.where(lane == LANES - 1, turned, 0.0)
    if columns == LANES:
        return low + high
    return jnp.concatenate([low] + [jnp.zeros((rows, LANES), F32)] * (columns // LANES - 2) + [high], axis=1)


def pack_low(q, inv, p, at, axis):
    return jnp.where(
        at < DEPTH, q, jnp.where(at < 2 * DEPTH, pltpu.roll(inv, DEPTH, axis), pltpu.roll(p, 2 * DEPTH, axis))
    )


def pack_high(q, inv, p, at, axis):
    size = q.shape[axis]
    return jnp.where(
        at >= size - DEPTH,
        q,
        jnp.where(
            at >= size - 2 * DEPTH,
            pltpu.roll(inv, size - DEPTH, axis),
            pltpu.roll(p, size - 2 * DEPTH, axis),
        ),
    )


def block_rows(columns, width, closed):
    vertical = 2 * DEPTH * (columns // LANES)
    lateral = SUB + 2 * (width // LANES)
    return max(vertical, lateral) + (0 if closed else 1)


def put_rows(out_ref, at, values):
    for k in range(values.shape[0]):
        out_ref[at + k] = values[k : k + 1]


def get_rows(in_ref, at, count):
    return jnp.concatenate([in_ref[at + k] for k in range(count)], axis=0)


def send_slots(out_ref, at, first, second):
    halves = first.shape[1] // LANES
    for i, value in enumerate((first, second)):
        for h in range(halves):
            out_ref[at + SUB + i * halves + h] = value[:, h * LANES : (h + 1) * LANES]


def got_slots(in_ref, at, width):
    halves = width // LANES
    return [
        jnp.concatenate([in_ref[at + SUB + i * halves + h] for h in range(halves)], axis=1) for i in range(2)
    ]


def send_halo(out_ref, q, inv, p, groups, members, size, closed, ends=None):
    rows, columns = q.shape
    halves = columns // LANES
    g, f = lax.axis_index("grp"), lax.axis_index("frac")
    here = g * members + f
    lane = iota((rows, LANES), 1)
    low = pack_low(q[:, :LANES], inv[:, :LANES], p[:, :LANES], lane, 1)
    high = pack_high(q[:, columns - LANES :], inv[:, columns - LANES :], p[:, columns - LANES :], lane, 1)
    turned = jnp.transpose(jnp.where(lane < LANES // 2, low, high))
    left, right = turned[:SUB], turned[LANES - SUB :]
    if ends is not None:
        sub, lane = iota((SUB, LANES), 0), iota((SUB, LANES), 1)
        left = jnp.where((sub == SUB - 1) & (lane == 1), ends[0], left)
        right = jnp.where((sub == 0) & (lane == LANES - 2), ends[1], right)
    lane = iota((1, LANES), 1)
    spare = jnp.where(g + 2 < groups, here + 2 * members, here - 2 * members)

    for step in (-1, 1):
        layer = (lambda k: k) if step < 0 else (lambda k: rows - 1 - k)

        def span(field, count, at):
            start = 0 if step < 0 else rows - count
            return field[start : start + count, at]

        inside = (g + step >= 0) & (g + step < groups)
        base = here + step * members
        tiles = [slice(h * LANES, (h + 1) * LANES) for h in range(halves)]

        at = jnp.where(inside, base, spare) * size
        for h, tile in enumerate(tiles):
            put_rows(out_ref, at + h * DEPTH, span(q, DEPTH, tile))
            put_rows(out_ref, at + halves * DEPTH + h * (DEPTH - 1), span(inv, DEPTH - 1, tile))
            put_rows(out_ref, at + halves * (2 * DEPTH - 1) + h, span(p, 1, tile))
        if not closed:
            deep, next_p = layer(DEPTH - 1), layer(1)
            extra = jnp.where(
                lane == 0,
                inv[deep : deep + 1, tiles[0]],
                jnp.where(
                    lane == LANES - 1,
                    inv[deep : deep + 1, tiles[-1]],
                    jnp.where(
                        lane == 1,
                        pltpu.roll(p[next_p : next_p + 1, tiles[0]], 1, 1),
                        pltpu.roll(p[next_p : next_p + 1, tiles[-1]], LANES - 1, 1),
                    ),
                ),
            )
            out_ref[at + halves * 2 * DEPTH] = extra

        for side, tile, there in ((-1, tiles[0], f > 0), (1, tiles[-1], f < members - 1)):
            at = jnp.where(inside & there, base + side, spare) * size
            for i, field in enumerate((q, inv, p)):
                put_rows(out_ref, at + i * DEPTH, span(field, DEPTH, tile))

    put_rows(out_ref, jnp.where(f > 0, here - 1, spare) * size, left)
    put_rows(out_ref, jnp.where(f < members - 1, here + 1, spare) * size, right)


def chebyshev(in_ref, q_ref, inv_ref, p_ref, target, scratch, groups, members, size, closed):
    q_ext, inv_ext, p_ext, update_ref, even_ref, odd_ref = scratch
    rows, columns = target.shape
    halves = columns // LANES
    side = halves
    g, f = lax.axis_index("grp"), lax.axis_index("frac")
    here = g * members + f
    last = groups * members - 1

    def taker(dg, df):
        ok = (g + dg >= 0) & (g + dg < groups) & (f + df >= 0) & (f + df < members)
        at = jnp.clip(here + dg * members + df, 0, last) * size
        return lambda start, count: jnp.where(ok, get_rows(in_ref, at + start, count), 0.0)

    def both(low, high, at, count, size):
        return jnp.where(at < count, low, jnp.where(at >= size - count, high, 0.0))

    def filler(count):
        return jnp.zeros((count, LANES), F32)

    for h in range(halves):
        for ext, ref in ((q_ext, q_ref), (inv_ext, inv_ref), (p_ext, p_ref)):
            ext[h, 0:rows, :] = ref[:, h * LANES : (h + 1) * LANES]
    outer = slice(rows, rows + SUB)
    below, above = taker(1, 0), taker(-1, 0)
    lane = iota((1, LANES), 1)
    if not closed:
        low_extra, high_extra = below(halves * 2 * DEPTH, 1), above(halves * 2 * DEPTH, 1)
    for h in range(halves):
        edge = (lane == 0) & (h == 0) | (lane == LANES - 1) & (h == halves - 1)

        def at_edge(high, turn):
            if closed:
                return filler(1)
            row = high_extra if high else low_extra
            return jnp.where(edge, pltpu.roll(row, turn, 1) if turn else row, 0.0)

        turn = LANES - 1 if h == 0 else 1
        at = h * DEPTH
        q_ext[h, outer, :] = jnp.concatenate(
            [below(at, DEPTH), filler(SUB - 2 * DEPTH), above(at, DEPTH)], axis=0
        )
        at = halves * DEPTH + h * (DEPTH - 1)
        inv_ext[h, outer, :] = jnp.concatenate(
            [
                below(at, DEPTH - 1),
                at_edge(False, 0),
                filler(SUB - 2 * DEPTH),
                at_edge(True, 0),
                above(at, DEPTH - 1),
            ],
            axis=0,
        )
        at = halves * (2 * DEPTH - 1) + h
        p_ext[h, outer, :] = jnp.concatenate(
            [
                below(at, 1),
                at_edge(False, turn),
                filler(SUB - 4),
                at_edge(True, turn),
                above(at, 1),
            ],
            axis=0,
        )
    right, left = taker(0, 1)(0, SUB), taker(0, -1)(0, SUB)
    turned = jnp.transpose(
        jnp.concatenate(
            [
                right[:DEPTH],
                jnp.zeros((LANES - 2 * SUB - DEPTH + 2, rows), F32),
                left[:2],
                right[2 * DEPTH :],
                jnp.zeros((1, rows), F32),
                left[2 : 2 + DEPTH],
                right[DEPTH : 2 * DEPTH],
                left[2 + DEPTH :],
            ],
            axis=0,
        )
    )
    lane = iota((rows, LANES), 1)
    q_ext[side, 0:rows, :] = both(turned, turned, lane, DEPTH, LANES)
    turned_inv, turned_p = pltpu.roll(turned, 2 * DEPTH, 1), pltpu.roll(turned, 4 * DEPTH, 1)
    inv_ext[side, 0:rows, :] = both(turned_inv, turned_inv, lane, DEPTH, LANES)
    p_ext[side, 0:rows, :] = both(turned_p, turned_p, lane, 2, LANES)
    lane = iota((DEPTH, LANES), 1)
    low_right, low_left, high_right, high_left = taker(1, 1), taker(1, -1), taker(-1, 1), taker(-1, -1)
    for i, ext in enumerate((q_ext, inv_ext, p_ext)):
        at = i * DEPTH
        ext[side, outer, :] = jnp.concatenate(
            [
                both(low_right(at, DEPTH), low_left(at, DEPTH), lane, DEPTH, LANES),
                filler(SUB - 2 * DEPTH),
                both(high_right(at, DEPTH), high_left(at, DEPTH), lane, DEPTH, LANES),
            ],
            axis=0,
        )

    end = rows + SUB - 1
    for own, other in ((0, end), (end, 0), (rows - 1, rows), (rows, rows - 1)):
        for c in range(halves + 1):
            q_ext[c, own : own + 1, :] += inv_ext[c, own : own + 1, :] * p_ext[c, other : other + 1, :]
    centre = 0.5 * (HIGH_BOUND + LOW_BOUND)
    half_width = 0.5 * (HIGH_BOUND - LOW_BOUND)
    scale_ratio = centre / half_width
    ratio_now = 1.0 / scale_ratio
    lane = iota((SUB, LANES), 1)
    count = rows // SUB + 1

    def keep(ref, c, r, value):
        at = (r + 1) * SUB
        ref[c, at : at + SUB, :] = value
        if r == count - 1:
            ref[c, 0:SUB, :] = value
        if r == 0:
            at = (count + 1) * SUB
            ref[c, at : at + SUB, :] = value

    for r in range(count):
        at = slice(r * SUB, (r + 1) * SUB)
        if closed:
            for c in range(halves + 1):
                start = q_ext[c, at, :]
                keep(even_ref, c, r, start / centre if centre != 1.0 else start)
            continue
        p_side, p_first, p_final = p_ext[side, at, :], p_ext[0, at, :], p_ext[halves - 1, at, :]
        missing = [0.0] * (halves + 1)
        missing[0] += jnp.where(lane == 0, pltpu.roll(p_side, 1, 1), 0.0)
        missing[halves - 1] += jnp.where(lane == LANES - 1, pltpu.roll(p_side, LANES - 1, 1), 0.0)
        missing[side] = jnp.where(
            lane == 0,
            pltpu.roll(p_final, 1, 1),
            jnp.where(lane == LANES - 1, pltpu.roll(p_first, LANES - 1, 1), 0.0),
        )
        for c in range(halves + 1):
            start = q_ext[c, at, :] + inv_ext[c, at, :] * missing[c]
            q_ext[c, at, :] = start
            keep(even_ref, c, r, start / centre if centre != 1.0 else start)
    now_ref, next_ref = even_ref, odd_ref
    for sweep in range(1, SWEEPS):
        ratio_next = 1.0 / (2.0 * scale_ratio - ratio_now)
        final = sweep == SWEEPS - 1
        for r in range(count - 1 if final else count):
            at = slice(r * SUB, (r + 1) * SUB)
            mids = [now_ref[c, (r + 1) * SUB : (r + 2) * SUB, :] for c in range(halves + 1)]
            after = [pltpu.roll(m, 1, 1) for m in mids]
            ahead = [pltpu.roll(m, LANES - 1, 1) for m in mids]
            for c in range(halves if final else halves + 1):
                beside = now_ref[c, (r + 1) * SUB - 1 : (r + 2) * SUB - 1, :]
                beside += now_ref[c, (r + 1) * SUB + 1 : (r + 2) * SUB + 1, :]
                beside += jnp.where(lane == 0, after[(c - 1) % (halves + 1)], after[c])
                beside += jnp.where(lane == LANES - 1, ahead[(c + 1) % (halves + 1)], ahead[c])
                residual = q_ext[c, at, :] - mids[c] + inv_ext[c, at, :] * beside
                old = mids[c] if sweep == 1 else update_ref[c, at, :]
                update = ratio_next * ratio_now * old + (2.0 * ratio_next / half_width) * residual
                if final:
                    tile = slice(c * LANES, (c + 1) * LANES)
                    target[at, tile] = p_ref[at, tile] + mids[c] + update
                else:
                    update_ref[c, at, :] = update
                    keep(next_ref, c, r, mids[c] + update)
        ratio_now = ratio_next
        now_ref, next_ref = next_ref, now_ref


ROW_SEG = 0
ROW_TRANS = 1
ROW_UP = 2
ROW_P = ROW_UP + ITERS
ROW_S = ROW_P + 1
ROW_ENDS = ROW_S + 1


def first_kernel(
    members, cell_any, seg_any, trans_any, count_any, up_any, state_any, frac_any,
    out_ref, hot_ref, row_hot_ref, cell_ref, seg_ref, trans_ref, count_ref, up_ref, state_ref, frac_ref, sem,
):
    _, rows, columns = state_ref.shape
    width = cell_ref.shape[1]
    copies = [
        pltpu.make_async_copy(source, target, sem.at[i])
        for i, (source, target) in enumerate(
            [
                (cell_any, cell_ref),
                (state_any, state_ref),
                (seg_any, seg_ref),
                (trans_any, trans_ref),
                (count_any, count_ref),
                (up_any, up_ref),
                (frac_any, frac_ref),
            ]
        )
    ]
    for copy in copies:
        copy.start()
    copies[0].wait()

    def make_hots(o):
        row, col = cell_parts(cell_ref[o : o + 1, :], columns)
        at = slice(o * width, (o + 1) * width)
        hot_ref[:, at] = one_hot(col, columns)
        row_hot_ref[:, at] = one_hot(row, rows)

    for o in range(members):
        make_hots(o)
    copies[1].wait()
    table = table_of([state_ref[0], state_ref[1]])
    for copy in copies[2:]:
        copy.wait()
    frac = load_segs(frac_ref, 0)
    ends = ends_of(frac)
    left, right = edge_columns(state_ref[0])
    me = lax.axis_index("frac")
    to_left = jnp.concatenate([ends[:, :LANES], left], axis=1)
    to_right = jnp.concatenate([right, ends[:, LANES:]], axis=1)
    whole = jnp.concatenate([frac, load_segs(frac_ref, 1)], axis=0)
    for o in range(members):
        one = slice(o, o + 1)
        row, _ = cell_parts(cell_ref[one, :], columns)
        cell_p, cell_s = pick(table, 2, rows, row, hot_ref[:, o * width : (o + 1) * width])
        live = iota((1, width), 1) < count_ref[0, o]
        out_ref[o, ROW_SEG : ROW_SEG + 1, :] = seg_ref[one, :].astype(F32)
        out_ref[o, ROW_TRANS : ROW_TRANS + 1, :] = jnp.where(live, trans_ref[one, :], 0.0)
        for t in range(ITERS):
            out_ref[o, ROW_UP + t : ROW_UP + t + 1, :] = up_ref[t, one, :].astype(F32)
        out_ref[o, ROW_P : ROW_P + 1, :] = cell_p
        out_ref[o, ROW_S : ROW_S + 1, :] = cell_s
        out_ref[o, ROW_ENDS : ROW_ENDS + 1, :] = jnp.where(me + 1 == o, to_right, to_left)
        out_ref[o, SUB:, :] = whole


def seg_parts(slot_ref, s):
    seg = slot_ref[s, ROW_SEG : ROW_SEG + 1, :].astype(jnp.int32)
    return seg // SEG_COLUMNS, seg % SEG_COLUMNS


def seg_hots(slot_ref, hot_ref, row_hot_ref, members, width):
    for s in range(members):
        row, lane = seg_parts(slot_ref, s)
        at = slice(s * width, (s + 1) * width)
        hot_ref[:, at] = one_hot(lane, SEG_COLUMNS)
        row_hot_ref[:, at] = one_hot(row, row_hot_ref.shape[0])


def seg_gather(slot_ref, hot_ref, fields, s, width, table):
    return pick(table, 2, fields, seg_parts(slot_ref, s)[0], hot_ref[:, s * width : (s + 1) * width])


def cell_spread(t, o, row_hot_ref, sent_ref, cell_row, seg_row, left_ref):
    seg_p, seg_s = seg_row
    cell_p, cell_s = cell_row
    weight, water = flow(
        sent_ref[o, ROW_TRANS : ROW_TRANS + 1, :],
        sent_ref[o, ROW_UP + t : ROW_UP + t + 1, :],
        cell_p,
        cell_s,
        seg_p,
        seg_s,
    )
    spread(left_ref, row_hot_ref, o, [weight, weight * seg_p, water])


def cell_finish(hot_ref, pressure, saturation, perm, left_ref, ring):
    rows = pressure.shape[0]
    couple, source, lost = gathered_sum(left_ref, hot_ref, 3, rows)
    inverse = 1.0 / (4.0 + perm + couple)
    new_saturation = saturation - TAU_STEP * lost / (perm + couple)
    return new_saturation, partial_residual(pressure, couple, source, inverse, ring), inverse


def cell_update(
    members, t, hot_ref, row_hot_ref, sent_ref, cell_rows, seg_rows, pressure, saturation, perm, left_ref, ring
):
    for o in range(members):
        cell_spread(t, o, row_hot_ref, sent_ref, cell_rows(o), seg_rows(o), left_ref)
    return cell_finish(hot_ref, pressure, saturation, perm, left_ref, ring)


def start_kernel(
    groups, members, size, slot_ref, sent_ref, cell_hot_ref, cell_row_hot_ref, frac_ref, aperture_ref,
    state_ref, perm_ref, out_ref, keep_ref, own_ref, new_ref, hot_ref, row_hot_ref,
    left_seg_ref, left_ref,
):
    width = slot_ref.shape[2]
    rows = new_ref.shape[1]
    g = lax.axis_index("grp")
    frac, sat = load_segs(frac_ref, 0), load_segs(frac_ref, 1)
    seg_hots(slot_ref, hot_ref, row_hot_ref, members, width)
    table = table_of([frac, sat])
    for s in range(members):
        o = s
        row, lane = seg_parts(sent_ref, o)
        whole = table_of([slot_ref[o, SUB : SUB + rows, :], slot_ref[o, SUB + rows :, :]])
        seg_p, seg_s = pick(whole, 2, rows, row, one_hot(lane, SEG_COLUMNS))
        cell_spread(
            0,
            o,
            cell_row_hot_ref,
            sent_ref,
            (sent_ref[o, ROW_P : ROW_P + 1, :], sent_ref[o, ROW_S : ROW_S + 1, :]),
            (seg_p, seg_s),
            left_ref,
        )
        seg_p, seg_s = seg_gather(slot_ref, hot_ref, rows, s, width, table)
        cell_p = slot_ref[s, ROW_P : ROW_P + 1, :]
        weight, water = flow(
            slot_ref[s, ROW_TRANS : ROW_TRANS + 1, :],
            slot_ref[s, ROW_UP : ROW_UP + 1, :],
            cell_p,
            slot_ref[s, ROW_S : ROW_S + 1, :],
            seg_p,
            seg_s,
        )
        spread(left_seg_ref, row_hot_ref, s, [weight * cell_p, weight, water])
    inflow, total, gained = gathered_sum(left_seg_ref, hot_ref, 3, rows)
    before, after = chain_ends(slot_ref, ROW_ENDS, members)
    new_frac, new_sat = frac_step(frac, sat, load_segs(aperture_ref), before, after, inflow, total, gained)
    new_ref[0] = new_frac
    new_ref[1] = new_sat
    table = table_of([new_frac, new_sat])
    me = lax.axis_index("frac")
    pressure = state_ref[0]
    new_saturation, q, inv = cell_finish(
        cell_hot_ref,
        pressure,
        state_ref[1],
        perm_ref[...],
        left_ref,
        ring_of(
            slot_ref[jnp.maximum(me - 1, 0), ROW_ENDS : ROW_ENDS + 1, :][:, :LANES],
            slot_ref[jnp.minimum(me + 1, members - 1), ROW_ENDS : ROW_ENDS + 1, :][:, LANES:],
            state_ref.shape[2],
            members,
        ),
    )
    for s in range(members):
        seg_p, seg_s = seg_gather(slot_ref, hot_ref, rows, s, width, table)
        own_ref[s, 0:1, :] = seg_p
        own_ref[s, 1:2, :] = seg_s
        at = (g * members + s) * size
        send_slots(out_ref, at, seg_p, seg_s)
    keep_ref[0] = pressure
    keep_ref[1] = new_saturation
    keep_ref[2] = q
    keep_ref[3] = inv
    ends = (new_frac[0:1, 0:1], new_frac[rows - 1 : rows, SEG_COLUMNS - 1 : SEG_COLUMNS])
    send_halo(out_ref, q, inv, pressure, groups, members, size, True, ends)


def cell_gather(members, cell_ref, hot_ref, fields, put):
    rows, columns = fields[0].shape
    width = cell_ref.shape[1]
    table = table_of(fields)
    for o in range(members):
        row, _ = cell_parts(cell_ref[o : o + 1, :], columns)
        put(o, *pick(table, len(fields), rows, row, hot_ref[:, o * width : (o + 1) * width]))


def middle_kernel(
    groups, members, size, open_size, halo_ref, cell_ref, hot_ref, row_hot_ref, sent_ref, kept_ref, perm_ref,
    out_ref, keep_ref, slots_ref, left_ref, *scratch,
):
    saturation = kept_ref[1]
    g = lax.axis_index("grp")

    def put_s(o, cell_s):
        slots_ref[o, 1:2, :] = cell_s

    cell_gather(members, cell_ref, hot_ref, [saturation], put_s)
    chebyshev(
        halo_ref, kept_ref.at[2], kept_ref.at[3], kept_ref.at[0], keep_ref.at[0], scratch, groups, members, size, True
    )
    pressure = keep_ref[0]

    rows, columns = pressure.shape
    width = cell_ref.shape[1]
    table = table_of([pressure])
    for o in range(members):
        row, _ = cell_parts(cell_ref[o : o + 1, :], columns)
        (cell_p,) = pick(table, 1, rows, row, hot_ref[:, o * width : (o + 1) * width])
        cell_s = slots_ref[o, 1:2, :]
        send_slots(out_ref, (g * members + o) * open_size, cell_p, cell_s)
        cell_spread(
            1,
            o,
            row_hot_ref,
            sent_ref,
            (cell_p, cell_s),
            got_slots(halo_ref, (g * members + o) * size, width),
            left_ref,
        )
    new_saturation, q, inv = cell_finish(hot_ref, pressure, saturation, perm_ref[...], left_ref, None)
    keep_ref[1] = new_saturation
    keep_ref[2] = q
    keep_ref[3] = inv
    send_halo(out_ref, q, inv, pressure, groups, members, open_size, False)


def owner_spread(blocks, t, slot_ref, cell_rows, seg_rows, row_hot_ref, left_ref):
    for s in blocks:
        cell_p, cell_s = cell_rows(s)
        weight, water = flow(
            slot_ref[s, ROW_TRANS : ROW_TRANS + 1, :],
            slot_ref[s, ROW_UP + t : ROW_UP + t + 1, :],
            cell_p,
            cell_s,
            *seg_rows(s),
        )
        spread(left_ref, row_hot_ref, s, [weight * cell_p, weight, water])


def owner_update(
    members, t, slot_ref, cell_rows, seg_rows, frac, sat, aperture, ends, hot_ref, row_hot_ref, left_ref
):
    owner_spread(range(members), t, slot_ref, cell_rows, seg_rows, row_hot_ref, left_ref)
    inflow, total, gained = gathered_sum(left_ref, hot_ref, 3, frac.shape[0])
    return frac_step(frac, sat, aperture, *ends, inflow, total, gained)


def exchange_kernel(
    groups, members, closed_size, size, halo_ref, cell_ref, cell_hot_ref, slot_ref, hot_ref, row_hot_ref, ends_ref, own_ref,
    frac_ref, aperture_ref, kept_ref, out_ref, new_ref, pressure_ref, left_ref, *scratch,
):
    width = slot_ref.shape[2]
    g = lax.axis_index("grp")

    def cell_rows(s):
        return got_slots(halo_ref, (g * members + s) * size, width)

    me = lax.axis_index("frac")
    prior = ends_ref[(g * members + jnp.maximum(me - 1, 0)) * closed_size]
    later = ends_ref[(g * members + jnp.minimum(me + 1, members - 1)) * closed_size + SUB - 1]
    before = jnp.where(me > 0, prior[:, LANES - 2 : LANES - 1], 0.0)
    after = jnp.where(me < members - 1, later[:, 1:2], 0.0)

    rows, columns = pressure_ref.shape
    seg_wide = frac_ref.shape[1]
    owner_spread(
        range(members),
        1,
        slot_ref,
        cell_rows,
        lambda s: (own_ref[s, 0:1, :], own_ref[s, 1:2, :]),
        row_hot_ref,
        left_ref,
    )
    inflow, total, gained = gathered_sum(left_ref, hot_ref, 3, seg_wide)
    new_frac, new_sat = frac_step(
        frac_ref[0], frac_ref[1], load_segs(aperture_ref), before, after, inflow, total, gained
    )
    new_ref[0] = new_frac
    new_ref[1] = new_sat
    seg_table = table_of([new_frac, new_sat])
    ends = ends_of(new_frac)
    s_table = table_of([kept_ref[1]])
    for o in range(members):
        at = slice(o * width, (o + 1) * width)
        row, _ = cell_parts(cell_ref[o : o + 1, :], columns)
        (cell_s,) = pick(s_table, 1, rows, row, cell_hot_ref[:, at])
        out_ref[o, 1:2, :] = cell_s
    chebyshev(
        halo_ref, kept_ref.at[2], kept_ref.at[3], kept_ref.at[0], pressure_ref, scratch, groups, members, size, False
    )
    p_table = table_of([pressure_ref[...]])
    columns_row = jnp.concatenate(edge_columns(pressure_ref[...]), axis=1)
    for o in range(members):
        at = slice(o * width, (o + 1) * width)
        seg_p, seg_s = pick(seg_table, 2, seg_wide, seg_parts(slot_ref, o)[0], hot_ref[:, at])
        out_ref[o, 2:3, :] = seg_p
        out_ref[o, 3:4, :] = seg_s
        out_ref[o, 4:5, :] = ends
        row, _ = cell_parts(cell_ref[o : o + 1, :], columns)
        (cell_p,) = pick(p_table, 1, rows, row, cell_hot_ref[:, at])
        out_ref[o, 0:1, :] = cell_p
        out_ref[o, 5:6, :] = columns_row


def source_last_kernel(
    groups, members, size, hot_ref, row_hot_ref, sent_ref, own_ref, seg_ref, pressure_ref, kept_ref, perm_ref,
    out_ref, keep_ref, left_ref,
):
    me = lax.axis_index("frac")
    pressure = pressure_ref[...]
    new_saturation, q, inv = cell_update(
        members,
        2,
        hot_ref,
        row_hot_ref,
        sent_ref,
        lambda o: (own_ref[o, 0:1, :], own_ref[o, 1:2, :]),
        lambda o: (seg_ref[o, 2:3, :], seg_ref[o, 3:4, :]),
        pressure,
        kept_ref[1],
        perm_ref[...],
        left_ref,
        ring_of(
            seg_ref[jnp.maximum(me - 1, 0), 5:6, :][:, LANES:],
            seg_ref[jnp.minimum(me + 1, members - 1), 5:6, :][:, :LANES],
            pressure_ref.shape[1],
            members,
        ),
    )
    keep_ref[0] = new_saturation
    keep_ref[1] = q
    keep_ref[2] = inv
    send_halo(out_ref, q, inv, pressure, groups, members, size, True)


def final_kernel(
    groups, members, size, halo_ref, pressure_ref, kept_ref, slot_ref, hot_ref, row_hot_ref, own_ref, seg_ref,
    frac_ref, aperture_ref, out_ref, new_ref, left_ref, *scratch,
):
    new_frac, new_sat = owner_update(
        members,
        2,
        slot_ref,
        lambda s: (seg_ref[s, 0:1, :], seg_ref[s, 1:2, :]),
        lambda s: (own_ref[s, 2:3, :], own_ref[s, 3:4, :]),
        frac_ref[0],
        frac_ref[1],
        load_segs(aperture_ref),
        chain_ends(seg_ref, 4, members),
        hot_ref,
        row_hot_ref,
        left_ref,
    )
    store_segs(new_ref, 0, new_frac)
    store_segs(new_ref, 1, new_sat)
    chebyshev(
        halo_ref, kept_ref.at[1], kept_ref.at[2], pressure_ref, out_ref.at[0], scratch, groups, members, size, True
    )
    out_ref[1] = kept_ref[0]


VMEM = pl.BlockSpec(memory_space=pltpu.VMEM)
HBM = pl.BlockSpec(memory_space=pltpu.HBM)


def call(kernel, statics, outs, scratch, *args, spec=VMEM):
    outs = [o if hasattr(o, "dtype") else jax.ShapeDtypeStruct(o, F32) for o in outs]
    return pl.pallas_call(
        functools.partial(kernel, *statics),
        out_shape=outs,
        in_specs=[spec] * len(args),
        out_specs=[VMEM] * len(outs),
        scratch_shapes=scratch,
        compiler_params=pltpu.CompilerParams(vmem_limit_bytes=32 * 1024 * 1024),
        name=kernel.__name__,
    )(*args)


def on_device(
    matrix_state,
    matrix_perm,
    frac_state,
    frac_aperture,
    link_cell,
    link_seg,
    link_trans,
    link_count,
    link_upwind,
):
    groups, members = lax.axis_size("grp"), lax.axis_size("frac")
    devices = groups * members
    cells = link_cell[0, 0]
    width = cells.shape[1]
    _, rows, columns = matrix_state.shape
    seg_dev = frac_state.shape[2]
    seg_rows = seg_dev // LANES
    frac = frac_state.reshape(2, seg_rows, LANES)
    aperture = frac_aperture.reshape(seg_rows, LANES)

    every = members * width
    slots = (members, SUB, width)
    closed_size, open_size = block_rows(columns, width, True), block_rows(columns, width, False)
    both = (groups, members, closed_size)
    halves = (groups, members, closed_size, open_size)
    halo, open_halo = (devices * closed_size, 1, LANES), (devices * open_size, 1, LANES)
    left_cell = pltpu.VMEM((3 * PARTS * rows, every), BF16)
    seg_wide = seg_dev // SEG_COLUMNS
    segs_wide = (2, seg_wide, SEG_COLUMNS)
    left_seg = pltpu.VMEM((3 * PARTS * seg_wide, every), BF16)
    tiles = columns // LANES + 1
    ext = [pltpu.VMEM((tiles, rows + SUB, LANES), F32)] * 4 + [pltpu.VMEM((tiles, rows + 3 * SUB, LANES), F32)] * 2

    def to_group(x):
        return lax.all_to_all(x, "frac", split_axis=0, concat_axis=0, tiled=True)

    def to_all(x):
        return lax.all_to_all(x, ("grp", "frac"), split_axis=0, concat_axis=0, tiled=True)

    def hots(*sizes):
        return [jax.ShapeDtypeStruct((n, every), BF16) for n in sizes]

    sent, cell_hot, cell_row_hot = call(
        first_kernel,
        (members,),
        [(members, SUB + 2 * seg_wide, SEG_COLUMNS)] + hots(columns, rows),
        [
            pltpu.VMEM((members, width), jnp.int32),
            pltpu.VMEM((members, width), jnp.int32),
            pltpu.VMEM((members, width), F32),
            pltpu.SMEM((1, members), jnp.int32),
            pltpu.VMEM((ITERS, members, width), jnp.int32),
            pltpu.VMEM(matrix_state.shape, F32),
            pltpu.VMEM(frac.shape, F32),
            pltpu.SemaphoreType.DMA((7,)),
        ],
        *[
            pltpu.with_memory_space_constraint(x, pltpu.HBM)
            for x in (
                cells, link_seg[0, 0], link_trans[0, 0], link_count[0], link_upwind[:, 0, 0], matrix_state, frac
            )
        ],
        spec=HBM,
    )
    slot = to_group(sent)
    edge, kept, own, frac1, hot, row_hot = call(
        start_kernel,
        both,
        [halo, (4, rows, columns), (members, 2, width), segs_wide] + hots(SEG_COLUMNS, seg_wide),
        [left_seg, left_cell],
        slot, sent, cell_hot, cell_row_hot, frac, aperture, matrix_state, matrix_perm,
    )
    before = to_all(edge)
    edge, kept = call(
        middle_kernel, halves, [open_halo, (4, rows, columns)], [pltpu.VMEM((members, 2, width), F32), left_cell] + ext,
        before, cells, cell_hot, cell_row_hot, sent, kept, matrix_perm,
    )
    around = to_all(edge)
    own, frac2, pressure = call(
        exchange_kernel, halves, [slots, segs_wide, (rows, columns)], [left_seg] + ext,
        around, cells, cell_hot, slot, hot, row_hot, before, own, frac1, aperture, kept,
    )
    segs = to_group(own)
    edge, kept = call(
        source_last_kernel, both, [halo, (3, rows, columns)], [left_cell],
        cell_hot, cell_row_hot, sent, own, segs, pressure, kept, matrix_perm,
    )
    around = to_all(edge)
    matrix_out, frac3 = call(
        final_kernel,
        both,
        [matrix_state.shape, frac.shape],
        [left_seg] + ext,
        around, pressure, kept, slot, hot, row_hot, own, segs, frac2, aperture,
    )
    return matrix_out, frac3.reshape(frac_state.shape)


def solution(mesh):
    return jax.shard_map(
        on_device,
        mesh=mesh,
        in_specs=(
            P(None, "grp", "frac"),
            P("grp", "frac"),
            P(None, "grp", "frac"),
            P("grp", "frac"),
            P("grp", "frac", None, None),
            P("grp", "frac", None, None),
            P("grp", "frac", None, None),
            P("grp", "frac", None),
            P(None, "grp", "frac", None, None),
        ),
        out_specs=(P(None, "grp", "frac"), P(None, "grp", "frac")),
        check_vma=False,
    )
```

```python
import functools

import jax
import jax.numpy as jnp
from jax import lax
from jax.experimental import pallas as pl
from jax.experimental.pallas import tpu as pltpu
from jax.sharding import PartitionSpec as P

ITERS = 3
SWEEPS = 4

LOW_BOUND = 0.02
HIGH_BOUND = 1.98
TAU_STEP = 0.5
MOBILITY_FLOOR = 0.2

F32 = jnp.float32
BF16 = jnp.bfloat16
LANES = 128
SUB = 8
SEG_COLUMNS = 2 * LANES
DEPTH = SWEEPS - 1


def iota(shape, dim):
    return lax.broadcasted_iota(jnp.int32, shape, dim)


def parts_of(x):
    high = x.astype(BF16).astype(F32)
    return high, x - high


PARTS = 2


def table_of(fields):
    split = [parts_of(f) for f in fields]
    return jnp.concatenate([s[p] for p in range(PARTS) for s in split], axis=0).astype(BF16)


def one_hot(index_row, count):
    shape = (count, index_row.shape[1])
    hit = iota(shape, 0).astype(F32).astype(BF16) == index_row.astype(F32).astype(BF16)
    return jnp.where(hit, jnp.ones(shape, BF16), jnp.zeros(shape, BF16))


def pick(table, fields, rows, row_index, hot):
    wide = jnp.dot(table, hot, preferred_element_type=F32)
    hit = iota((rows, row_index.shape[1]), 0) == row_index
    found = []
    for f in range(fields):
        total = sum(wide[(p * fields + f) * rows : (p * fields + f + 1) * rows] for p in range(PARTS))
        found.append(jnp.sum(jnp.where(hit, total, 0.0), axis=0, keepdims=True))
    return found


def spread(left_ref, row_hot_ref, block, values):
    rows = row_hot_ref.shape[0]
    width = values[0].shape[1]
    at = slice(block * width, (block + 1) * width)
    hot = row_hot_ref[:, at]
    for f, value in enumerate(values):
        for p, part in enumerate(parts_of(value)):
            row = (p * len(values) + f) * rows
            left_ref[row : row + rows, at] = hot * part.astype(BF16)


def gathered_sum(left_ref, hot_ref, fields, rows):
    wide = lax.dot_general(
        left_ref[...], hot_ref[...], (((1,), (1,)), ((), ())), preferred_element_type=F32
    )
    return [
        sum(wide[(p * fields + f) * rows : (p * fields + f + 1) * rows] for p in range(PARTS))
        for f in range(fields)
    ]


def flow(trans, upwind, cell_p, cell_s, seg_p, seg_s):
    u = jnp.where(upwind > 0.5, cell_s, seg_s)
    weight = trans * (MOBILITY_FLOOR + u * u)
    water = weight * (cell_p - seg_p) * u
    return weight, water


def cell_parts(cell_row, columns):
    return cell_row // columns, cell_row % columns


def load_segs(ref, *lead):
    rows = ref.shape[-2] // 2
    return jnp.concatenate([ref[(*lead, pl.ds(h, rows, 2), slice(None))] for h in range(2)], axis=1)


def store_segs(ref, lead, value):
    rows = value.shape[0]
    for h in range(2):
        ref[lead, pl.ds(h, rows, 2), :] = value[:, h * LANES : (h + 1) * LANES]


def ends_of(frac):
    rows, columns = frac.shape
    lane = iota((1, columns), 1)
    return jnp.where(lane < columns // 2, frac[0:1], frac[rows - 1 : rows])


def frac_step(frac, sat, aperture, before, after, inflow, total, gained):
    rows, lanes = frac.shape
    row, lane = iota((rows, lanes), 0), iota((rows, lanes), 1)
    back = pltpu.roll(frac, 1, 1)
    left = jnp.where(lane == 0, pltpu.roll(back, 1, 0), back)
    left = jnp.where((lane == 0) & (row == 0), before, left)
    ahead = pltpu.roll(frac, lanes - 1, 1)
    right = jnp.where(lane == lanes - 1, pltpu.roll(ahead, rows - 1, 0), ahead)
    right = jnp.where((lane == lanes - 1) & (row == rows - 1), after, right)
    new_frac = (aperture * frac + inflow + left + right) / (aperture + total + 2.0)
    new_sat = sat + TAU_STEP * gained / (aperture + total)
    return new_frac, new_sat


def chain_ends(ends_ref, row, members):
    me = lax.axis_index("frac")
    lanes = ends_ref.shape[2]
    prior = ends_ref[jnp.maximum(me - 1, 0), row : row + 1, :]
    later = ends_ref[jnp.minimum(me + 1, members - 1), row : row + 1, :]
    before = jnp.where(me > 0, prior[:, lanes - 1 :], 0.0)
    after = jnp.where(me < members - 1, later[:, 0:1], 0.0)
    return before, after


def partial_residual(pressure, couple, source, inverse, ring):
    rows, columns = pressure.shape
    row, col = iota((rows, columns), 0), iota((rows, columns), 1)
    beside = jnp.where(row == 0, 0.0, pltpu.roll(pressure, 1, 0))
    beside += jnp.where(row == rows - 1, 0.0, pltpu.roll(pressure, rows - 1, 0))
    beside += jnp.where(col == 0, 0.0, pltpu.roll(pressure, 1, 1))
    beside += jnp.where(col == columns - 1, 0.0, pltpu.roll(pressure, columns - 1, 1))
    if ring is not None:
        beside += ring
    return inverse * (source - (4.0 + couple) * pressure + beside)


def edge_columns(p):
    rows, columns = p.shape
    lane = iota((rows, LANES), 1)
    turned = jnp.transpose(jnp.where(lane < LANES // 2, p[:, :LANES], p[:, columns - LANES :]))
    return turned[0:1], turned[LANES - 1 : LANES]


def ring_of(left, right, columns, members):
    f = lax.axis_index("frac")
    rows = left.shape[1]
    left = jnp.where(f > 0, left, 0.0)
    right = jnp.where(f < members - 1, right, 0.0)
    turned = jnp.transpose(jnp.concatenate([left, jnp.zeros((LANES - 2, rows), F32), right], axis=0))
    lane = iota((rows, LANES), 1)
    low = jnp.where(lane == 0, turned, 0.0)
    high = jnp.where(lane == LANES - 1, turned, 0.0)
    if columns == LANES:
        return low + high
    return jnp.concatenate([low] + [jnp.zeros((rows, LANES), F32)] * (columns // LANES - 2) + [high], axis=1)


def pack_low(q, inv, p, at, axis):
    return jnp.where(
        at < DEPTH, q, jnp.where(at < 2 * DEPTH, pltpu.roll(inv, DEPTH, axis), pltpu.roll(p, 2 * DEPTH, axis))
    )


def pack_high(q, inv, p, at, axis):
    size = q.shape[axis]
    return jnp.where(
        at >= size - DEPTH,
        q,
        jnp.where(
            at >= size - 2 * DEPTH,
            pltpu.roll(inv, size - DEPTH, axis),
            pltpu.roll(p, size - 2 * DEPTH, axis),
        ),
    )


def block_rows(columns, width, closed):
    vertical = 2 * DEPTH * (columns // LANES)
    lateral = SUB + 2 * (width // LANES)
    return max(vertical, lateral) + (0 if closed else 1)


def put_rows(out_ref, at, values):
    for k in range(values.shape[0]):
        out_ref[at + k] = values[k : k + 1]


def get_rows(in_ref, at, count):
    return jnp.concatenate([in_ref[at + k] for k in range(count)], axis=0)


def send_slots(out_ref, at, first, second):
    halves = first.shape[1] // LANES
    for i, value in enumerate((first, second)):
        for h in range(halves):
            out_ref[at + SUB + i * halves + h] = value[:, h * LANES : (h + 1) * LANES]


def got_slots(in_ref, at, width):
    halves = width // LANES
    return [
        jnp.concatenate([in_ref[at + SUB + i * halves + h] for h in range(halves)], axis=1) for i in range(2)
    ]


def send_halo(out_ref, q, inv, p, groups, members, size, closed, ends=None):
    rows, columns = q.shape
    halves = columns // LANES
    g, f = lax.axis_index("grp"), lax.axis_index("frac")
    here = g * members + f
    lane = iota((rows, LANES), 1)
    low = pack_low(q[:, :LANES], inv[:, :LANES], p[:, :LANES], lane, 1)
    high = pack_high(q[:, columns - LANES :], inv[:, columns - LANES :], p[:, columns - LANES :], lane, 1)
    turned = jnp.transpose(jnp.where(lane < LANES // 2, low, high))
    left, right = turned[:SUB], turned[LANES - SUB :]
    if ends is not None:
        sub, lane = iota((SUB, LANES), 0), iota((SUB, LANES), 1)
        left = jnp.where((sub == SUB - 1) & (lane == 1), ends[0], left)
        right = jnp.where((sub == 0) & (lane == LANES - 2), ends[1], right)
    lane = iota((1, LANES), 1)
    spare = jnp.where(g + 2 < groups, here + 2 * members, here - 2 * members)

    for step in (-1, 1):
        layer = (lambda k: k) if step < 0 else (lambda k: rows - 1 - k)

        def span(field, count, at):
            start = 0 if step < 0 else rows - count
            return field[start : start + count, at]

        inside = (g + step >= 0) & (g + step < groups)
        base = here + step * members
        tiles = [slice(h * LANES, (h + 1) * LANES) for h in range(halves)]

        at = jnp.where(inside, base, spare) * size
        for h, tile in enumerate(tiles):
            put_rows(out_ref, at + h * DEPTH, span(q, DEPTH, tile))
            put_rows(out_ref, at + halves * DEPTH + h * (DEPTH - 1), span(inv, DEPTH - 1, tile))
            put_rows(out_ref, at + halves * (2 * DEPTH - 1) + h, span(p, 1, tile))
        if not closed:
            deep, next_p = layer(DEPTH - 1), layer(1)
            extra = jnp.where(
                lane == 0,
                inv[deep : deep + 1, tiles[0]],
                jnp.where(
                    lane == LANES - 1,
                    inv[deep : deep + 1, tiles[-1]],
                    jnp.where(
                        lane == 1,
                        pltpu.roll(p[next_p : next_p + 1, tiles[0]], 1, 1),
                        pltpu.roll(p[next_p : next_p + 1, tiles[-1]], LANES - 1, 1),
                    ),
                ),
            )
            out_ref[at + halves * 2 * DEPTH] = extra

        for side, tile, there in ((-1, tiles[0], f > 0), (1, tiles[-1], f < members - 1)):
            at = jnp.where(inside & there, base + side, spare) * size
            for i, field in enumerate((q, inv, p)):
                put_rows(out_ref, at + i * DEPTH, span(field, DEPTH, tile))

    put_rows(out_ref, jnp.where(f > 0, here - 1, spare) * size, left)
    put_rows(out_ref, jnp.where(f < members - 1, here + 1, spare) * size, right)


def chebyshev(in_ref, q_ref, inv_ref, p_ref, target, scratch, groups, members, size, closed):
    q_ext, inv_ext, p_ext, update_ref, even_ref, odd_ref = scratch
    rows, columns = target.shape
    halves = columns // LANES
    side = halves
    g, f = lax.axis_index("grp"), lax.axis_index("frac")
    here = g * members + f
    last = groups * members - 1

    def taker(dg, df):
        ok = (g + dg >= 0) & (g + dg < groups) & (f + df >= 0) & (f + df < members)
        at = jnp.clip(here + dg * members + df, 0, last) * size
        return lambda start, count: jnp.where(ok, get_rows(in_ref, at + start, count), 0.0)

    def both(low, high, at, count, size):
        return jnp.where(at < count, low, jnp.where(at >= size - count, high, 0.0))

    def filler(count):
        return jnp.zeros((count, LANES), F32)

    for h in range(halves):
        for ext, ref in ((q_ext, q_ref), (inv_ext, inv_ref), (p_ext, p_ref)):
            ext[h, 0:rows, :] = ref[:, h * LANES : (h + 1) * LANES]
    outer = slice(rows, rows + SUB)
    below, above = taker(1, 0), taker(-1, 0)
    lane = iota((1, LANES), 1)
    if not closed:
        low_extra, high_extra = below(halves * 2 * DEPTH, 1), above(halves * 2 * DEPTH, 1)
    for h in range(halves):
        edge = (lane == 0) & (h == 0) | (lane == LANES - 1) & (h == halves - 1)

        def at_edge(high, turn):
            if closed:
                return filler(1)
            row = high_extra if high else low_extra
            return jnp.where(edge, pltpu.roll(row, turn, 1) if turn else row, 0.0)

        turn = LANES - 1 if h == 0 else 1
        at = h * DEPTH
        q_ext[h, outer, :] = jnp.concatenate(
            [below(at, DEPTH), filler(SUB - 2 * DEPTH), above(at, DEPTH)], axis=0
        )
        at = halves * DEPTH + h * (DEPTH - 1)
        inv_ext[h, outer, :] = jnp.concatenate(
            [
                below(at, DEPTH - 1),
                at_edge(False, 0),
                filler(SUB - 2 * DEPTH),
                at_edge(True, 0),
                above(at, DEPTH - 1),
            ],
            axis=0,
        )
        at = halves * (2 * DEPTH - 1) + h
        p_ext[h, outer, :] = jnp.concatenate(
            [
                below(at, 1),
                at_edge(False, turn),
                filler(SUB - 4),
                at_edge(True, turn),
                above(at, 1),
            ],
            axis=0,
        )
    right, left = taker(0, 1)(0, SUB), taker(0, -1)(0, SUB)
    turned = jnp.transpose(
        jnp.concatenate(
            [
                right[:DEPTH],
                jnp.zeros((LANES - 2 * SUB - DEPTH + 2, rows), F32),
                left[:2],
                right[2 * DEPTH :],
                jnp.zeros((1, rows), F32),
                left[2 : 2 + DEPTH],
                right[DEPTH : 2 * DEPTH],
                left[2 + DEPTH :],
            ],
            axis=0,
        )
    )
    lane = iota((rows, LANES), 1)
    q_ext[side, 0:rows, :] = both(turned, turned, lane, DEPTH, LANES)
    turned_inv, turned_p = pltpu.roll(turned, 2 * DEPTH, 1), pltpu.roll(turned, 4 * DEPTH, 1)
    inv_ext[side, 0:rows, :] = both(turned_inv, turned_inv, lane, DEPTH, LANES)
    p_ext[side, 0:rows, :] = both(turned_p, turned_p, lane, 2, LANES)
    lane = iota((DEPTH, LANES), 1)
    low_right, low_left, high_right, high_left = taker(1, 1), taker(1, -1), taker(-1, 1), taker(-1, -1)
    for i, ext in enumerate((q_ext, inv_ext, p_ext)):
        at = i * DEPTH
        ext[side, outer, :] = jnp.concatenate(
            [
                both(low_right(at, DEPTH), low_left(at, DEPTH), lane, DEPTH, LANES),
                filler(SUB - 2 * DEPTH),
                both(high_right(at, DEPTH), high_left(at, DEPTH), lane, DEPTH, LANES),
            ],
            axis=0,
        )

    end = rows + SUB - 1
    for own, other in ((0, end), (end, 0), (rows - 1, rows), (rows, rows - 1)):
        for c in range(halves + 1):
            q_ext[c, own : own + 1, :] += inv_ext[c, own : own + 1, :] * p_ext[c, other : other + 1, :]
    centre = 0.5 * (HIGH_BOUND + LOW_BOUND)
    half_width = 0.5 * (HIGH_BOUND - LOW_BOUND)
    scale_ratio = centre / half_width
    ratio_now = 1.0 / scale_ratio
    lane = iota((SUB, LANES), 1)
    count = rows // SUB + 1

    def keep(ref, c, r, value):
        at = (r + 1) * SUB
        ref[c, at : at + SUB, :] = value
        if r == count - 1:
            ref[c, 0:SUB, :] = value
        if r == 0:
            at = (count + 1) * SUB
            ref[c, at : at + SUB, :] = value

    for r in range(count):
        at = slice(r * SUB, (r + 1) * SUB)
        if closed:
            for c in range(halves + 1):
                start = q_ext[c, at, :]
                keep(even_ref, c, r, start / centre if centre != 1.0 else start)
            continue
        p_side, p_first, p_final = p_ext[side, at, :], p_ext[0, at, :], p_ext[halves - 1, at, :]
        missing = [0.0] * (halves + 1)
        missing[0] += jnp.where(lane == 0, pltpu.roll(p_side, 1, 1), 0.0)
        missing[halves - 1] += jnp.where(lane == LANES - 1, pltpu.roll(p_side, LANES - 1, 1), 0.0)
        missing[side] = jnp.where(
            lane == 0,
            pltpu.roll(p_final, 1, 1),
            jnp.where(lane == LANES - 1, pltpu.roll(p_first, LANES - 1, 1), 0.0),
        )
        for c in range(halves + 1):
            start = q_ext[c, at, :] + inv_ext[c, at, :] * missing[c]
            q_ext[c, at, :] = start
            keep(even_ref, c, r, start / centre if centre != 1.0 else start)
    now_ref, next_ref = even_ref, odd_ref
    for sweep in range(1, SWEEPS):
        ratio_next = 1.0 / (2.0 * scale_ratio - ratio_now)
        final = sweep == SWEEPS - 1
        for r in range(count - 1 if final else count):
            at = slice(r * SUB, (r + 1) * SUB)
            mids = [now_ref[c, (r + 1) * SUB : (r + 2) * SUB, :] for c in range(halves + 1)]
            after = [pltpu.roll(m, 1, 1) for m in mids]
            ahead = [pltpu.roll(m, LANES - 1, 1) for m in mids]
            for c in range(halves if final else halves + 1):
                beside = now_ref[c, (r + 1) * SUB - 1 : (r + 2) * SUB - 1, :]
                beside += now_ref[c, (r + 1) * SUB + 1 : (r + 2) * SUB + 1, :]
                beside += jnp.where(lane == 0, after[(c - 1) % (halves + 1)], after[c])
                beside += jnp.where(lane == LANES - 1, ahead[(c + 1) % (halves + 1)], ahead[c])
                residual = q_ext[c, at, :] - mids[c] + inv_ext[c, at, :] * beside
                old = mids[c] if sweep == 1 else update_ref[c, at, :]
                update = ratio_next * ratio_now * old + (2.0 * ratio_next / half_width) * residual
                if final:
                    tile = slice(c * LANES, (c + 1) * LANES)
                    target[at, tile] = p_ref[at, tile] + mids[c] + update
                else:
                    update_ref[c, at, :] = update
                    keep(next_ref, c, r, mids[c] + update)
        ratio_now = ratio_next
        now_ref, next_ref = next_ref, now_ref


ROW_SEG = 0
ROW_TRANS = 1
ROW_UP = 2
ROW_P = ROW_UP + ITERS
ROW_S = ROW_P + 1
ROW_ENDS = ROW_S + 1


def first_kernel(
    members, cell_any, seg_any, trans_any, count_any, up_any, state_any, frac_any,
    out_ref, hot_ref, row_hot_ref, cell_ref, seg_ref, trans_ref, count_ref, up_ref, state_ref, frac_ref, sem,
):
    _, rows, columns = state_ref.shape
    width = cell_ref.shape[1]
    copies = [
        pltpu.make_async_copy(source, target, sem.at[i])
        for i, (source, target) in enumerate(
            [
                (cell_any, cell_ref),
                (state_any, state_ref),
                (seg_any, seg_ref),
                (trans_any, trans_ref),
                (count_any, count_ref),
                (up_any, up_ref),
                (frac_any, frac_ref),
            ]
        )
    ]
    for i in (0, 1, 6, 2, 3, 4, 5):
        copies[i].start()
    copies[0].wait()

    def make_hots(o):
        row, col = cell_parts(cell_ref[o : o + 1, :], columns)
        at = slice(o * width, (o + 1) * width)
        hot_ref[:, at] = one_hot(col, columns)
        row_hot_ref[:, at] = one_hot(row, rows)

    for o in range(members):
        make_hots(o)
    copies[1].wait()
    table = table_of([state_ref[0], state_ref[1]])
    copies[6].wait()
    frac = load_segs(frac_ref, 0)
    ends = ends_of(frac)
    left, right = edge_columns(state_ref[0])
    me = lax.axis_index("frac")
    to_left = jnp.concatenate([ends[:, :LANES], left], axis=1)
    to_right = jnp.concatenate([right, ends[:, LANES:]], axis=1)
    whole = jnp.concatenate([frac, load_segs(frac_ref, 1)], axis=0)
    for o in range(members):
        one = slice(o, o + 1)
        row, _ = cell_parts(cell_ref[one, :], columns)
        cell_p, cell_s = pick(table, 2, rows, row, hot_ref[:, o * width : (o + 1) * width])
        out_ref[o, ROW_P : ROW_P + 1, :] = cell_p
        out_ref[o, ROW_S : ROW_S + 1, :] = cell_s
        out_ref[o, ROW_ENDS : ROW_ENDS + 1, :] = jnp.where(me + 1 == o, to_right, to_left)
        out_ref[o, SUB:, :] = whole
    for copy in copies[2:6]:
        copy.wait()
    for o in range(members):
        one = slice(o, o + 1)
        live = iota((1, width), 1) < count_ref[0, o]
        out_ref[o, ROW_SEG : ROW_SEG + 1, :] = seg_ref[one, :].astype(F32)
        out_ref[o, ROW_TRANS : ROW_TRANS + 1, :] = jnp.where(live, trans_ref[one, :], 0.0)
        for t in range(ITERS):
            out_ref[o, ROW_UP + t : ROW_UP + t + 1, :] = up_ref[t, one, :].astype(F32)


def seg_parts(slot_ref, s):
    seg = slot_ref[s, ROW_SEG : ROW_SEG + 1, :].astype(jnp.int32)
    return seg // SEG_COLUMNS, seg % SEG_COLUMNS


def seg_hots(slot_ref, hot_ref, row_hot_ref, members, width):
    for s in range(members):
        row, lane = seg_parts(slot_ref, s)
        at = slice(s * width, (s + 1) * width)
        hot_ref[:, at] = one_hot(lane, SEG_COLUMNS)
        row_hot_ref[:, at] = one_hot(row, row_hot_ref.shape[0])


def seg_gather(slot_ref, hot_ref, fields, s, width, table):
    return pick(table, 2, fields, seg_parts(slot_ref, s)[0], hot_ref[:, s * width : (s + 1) * width])


def cell_spread(t, o, row_hot_ref, sent_ref, cell_row, seg_row, left_ref):
    seg_p, seg_s = seg_row
    cell_p, cell_s = cell_row
    weight, water = flow(
        sent_ref[o, ROW_TRANS : ROW_TRANS + 1, :],
        sent_ref[o, ROW_UP + t : ROW_UP + t + 1, :],
        cell_p,
        cell_s,
        seg_p,
        seg_s,
    )
    spread(left_ref, row_hot_ref, o, [weight, weight * seg_p, water])


def cell_finish(hot_ref, pressure, saturation, perm, left_ref, ring):
    rows = pressure.shape[0]
    couple, source, lost = gathered_sum(left_ref, hot_ref, 3, rows)
    inverse = 1.0 / (4.0 + perm + couple)
    new_saturation = saturation - TAU_STEP * lost / (perm + couple)
    return new_saturation, partial_residual(pressure, couple, source, inverse, ring), inverse


def cell_update(
    members, t, hot_ref, row_hot_ref, sent_ref, cell_rows, seg_rows, pressure, saturation, perm, left_ref, ring
):
    for o in range(members):
        cell_spread(t, o, row_hot_ref, sent_ref, cell_rows(o), seg_rows(o), left_ref)
    return cell_finish(hot_ref, pressure, saturation, perm, left_ref, ring)


def start_kernel(
    groups, members, size, slot_ref, sent_ref, cell_hot_ref, cell_row_hot_ref, frac_ref, aperture_ref,
    state_ref, perm_ref, out_ref, keep_ref, own_ref, new_ref, hot_ref, row_hot_ref,
    left_seg_ref, left_ref,
):
    width = slot_ref.shape[2]
    rows = new_ref.shape[1]
    g = lax.axis_index("grp")
    frac, sat = load_segs(frac_ref, 0), load_segs(frac_ref, 1)
    seg_hots(slot_ref, hot_ref, row_hot_ref, members, width)
    table = table_of([frac, sat])
    for s in range(members):
        o = s
        row, lane = seg_parts(sent_ref, o)
        whole = table_of([slot_ref[o, SUB : SUB + rows, :], slot_ref[o, SUB + rows :, :]])
        seg_p, seg_s = pick(whole, 2, rows, row, one_hot(lane, SEG_COLUMNS))
        cell_spread(
            0,
            o,
            cell_row_hot_ref,
            sent_ref,
            (sent_ref[o, ROW_P : ROW_P + 1, :], sent_ref[o, ROW_S : ROW_S + 1, :]),
            (seg_p, seg_s),
            left_ref,
        )
        seg_p, seg_s = seg_gather(slot_ref, hot_ref, rows, s, width, table)
        cell_p = slot_ref[s, ROW_P : ROW_P + 1, :]
        weight, water = flow(
            slot_ref[s, ROW_TRANS : ROW_TRANS + 1, :],
            slot_ref[s, ROW_UP : ROW_UP + 1, :],
            cell_p,
            slot_ref[s, ROW_S : ROW_S + 1, :],
            seg_p,
            seg_s,
        )
        spread(left_seg_ref, row_hot_ref, s, [weight * cell_p, weight, water])
    inflow, total, gained = gathered_sum(left_seg_ref, hot_ref, 3, rows)
    before, after = chain_ends(slot_ref, ROW_ENDS, members)
    new_frac, new_sat = frac_step(frac, sat, load_segs(aperture_ref), before, after, inflow, total, gained)
    new_ref[0] = new_frac
    new_ref[1] = new_sat
    table = table_of([new_frac, new_sat])
    me = lax.axis_index("frac")
    pressure = state_ref[0]
    new_saturation, q, inv = cell_finish(
        cell_hot_ref,
        pressure,
        state_ref[1],
        perm_ref[...],
        left_ref,
        ring_of(
            slot_ref[jnp.maximum(me - 1, 0), ROW_ENDS : ROW_ENDS + 1, :][:, :LANES],
            slot_ref[jnp.minimum(me + 1, members - 1), ROW_ENDS : ROW_ENDS + 1, :][:, LANES:],
            state_ref.shape[2],
            members,
        ),
    )
    for s in range(members):
        seg_p, seg_s = seg_gather(slot_ref, hot_ref, rows, s, width, table)
        own_ref[s, 0:1, :] = seg_p
        own_ref[s, 1:2, :] = seg_s
        at = (g * members + s) * size
        send_slots(out_ref, at, seg_p, seg_s)
    keep_ref[0] = pressure
    keep_ref[1] = new_saturation
    keep_ref[2] = q
    keep_ref[3] = inv
    ends = (new_frac[0:1, 0:1], new_frac[rows - 1 : rows, SEG_COLUMNS - 1 : SEG_COLUMNS])
    send_halo(out_ref, q, inv, pressure, groups, members, size, True, ends)


def cell_gather(members, cell_ref, hot_ref, fields, put):
    rows, columns = fields[0].shape
    width = cell_ref.shape[1]
    table = table_of(fields)
    for o in range(members):
        row, _ = cell_parts(cell_ref[o : o + 1, :], columns)
        put(o, *pick(table, len(fields), rows, row, hot_ref[:, o * width : (o + 1) * width]))


def middle_kernel(
    groups, members, size, open_size, halo_ref, cell_ref, hot_ref, row_hot_ref, sent_ref, kept_ref, perm_ref,
    out_ref, keep_ref, slots_ref, left_ref, *scratch,
):
    saturation = kept_ref[1]
    g = lax.axis_index("grp")

    def put_s(o, cell_s):
        slots_ref[o, 1:2, :] = cell_s

    cell_gather(members, cell_ref, hot_ref, [saturation], put_s)
    chebyshev(
        halo_ref, kept_ref.at[2], kept_ref.at[3], kept_ref.at[0], keep_ref.at[0], scratch, groups, members, size, True
    )
    pressure = keep_ref[0]

    rows, columns = pressure.shape
    width = cell_ref.shape[1]
    table = table_of([pressure])
    for o in range(members):
        row, _ = cell_parts(cell_ref[o : o + 1, :], columns)
        (cell_p,) = pick(table, 1, rows, row, hot_ref[:, o * width : (o + 1) * width])
        cell_s = slots_ref[o, 1:2, :]
        send_slots(out_ref, (g * members + o) * open_size, cell_p, cell_s)
        cell_spread(
            1,
            o,
            row_hot_ref,
            sent_ref,
            (cell_p, cell_s),
            got_slots(halo_ref, (g * members + o) * size, width),
            left_ref,
        )
    new_saturation, q, inv = cell_finish(hot_ref, pressure, saturation, perm_ref[...], left_ref, None)
    keep_ref[1] = new_saturation
    keep_ref[2] = q
    keep_ref[3] = inv
    send_halo(out_ref, q, inv, pressure, groups, members, open_size, False)


def owner_spread(blocks, t, slot_ref, cell_rows, seg_rows, row_hot_ref, left_ref):
    for s in blocks:
        cell_p, cell_s = cell_rows(s)
        weight, water = flow(
            slot_ref[s, ROW_TRANS : ROW_TRANS + 1, :],
            slot_ref[s, ROW_UP + t : ROW_UP + t + 1, :],
            cell_p,
            cell_s,
            *seg_rows(s),
        )
        spread(left_ref, row_hot_ref, s, [weight * cell_p, weight, water])


def owner_update(
    members, t, slot_ref, cell_rows, seg_rows, frac, sat, aperture, ends, hot_ref, row_hot_ref, left_ref
):
    owner_spread(range(members), t, slot_ref, cell_rows, seg_rows, row_hot_ref, left_ref)
    inflow, total, gained = gathered_sum(left_ref, hot_ref, 3, frac.shape[0])
    return frac_step(frac, sat, aperture, *ends, inflow, total, gained)


def exchange_kernel(
    groups, members, closed_size, size, halo_ref, cell_ref, cell_hot_ref, slot_ref, hot_ref, row_hot_ref, ends_ref, own_ref,
    frac_ref, aperture_ref, kept_ref, out_ref, new_ref, pressure_ref, left_ref, *scratch,
):
    width = slot_ref.shape[2]
    g = lax.axis_index("grp")

    def cell_rows(s):
        return got_slots(halo_ref, (g * members + s) * size, width)

    me = lax.axis_index("frac")
    prior = ends_ref[(g * members + jnp.maximum(me - 1, 0)) * closed_size]
    later = ends_ref[(g * members + jnp.minimum(me + 1, members - 1)) * closed_size + SUB - 1]
    before = jnp.where(me > 0, prior[:, LANES - 2 : LANES - 1], 0.0)
    after = jnp.where(me < members - 1, later[:, 1:2], 0.0)

    rows, columns = pressure_ref.shape
    seg_wide = frac_ref.shape[1]
    owner_spread(
        range(members),
        1,
        slot_ref,
        cell_rows,
        lambda s: (own_ref[s, 0:1, :], own_ref[s, 1:2, :]),
        row_hot_ref,
        left_ref,
    )
    inflow, total, gained = gathered_sum(left_ref, hot_ref, 3, seg_wide)
    new_frac, new_sat = frac_step(
        frac_ref[0], frac_ref[1], load_segs(aperture_ref), before, after, inflow, total, gained
    )
    new_ref[0] = new_frac
    new_ref[1] = new_sat
    seg_table = table_of([new_frac, new_sat])
    ends = ends_of(new_frac)
    s_table = table_of([kept_ref[1]])
    for o in range(members):
        at = slice(o * width, (o + 1) * width)
        row, _ = cell_parts(cell_ref[o : o + 1, :], columns)
        (cell_s,) = pick(s_table, 1, rows, row, cell_hot_ref[:, at])
        out_ref[o, 1:2, :] = cell_s
    chebyshev(
        halo_ref, kept_ref.at[2], kept_ref.at[3], kept_ref.at[0], pressure_ref, scratch, groups, members, size, False
    )
    p_table = table_of([pressure_ref[...]])
    columns_row = jnp.concatenate(edge_columns(pressure_ref[...]), axis=1)
    for o in range(members):
        at = slice(o * width, (o + 1) * width)
        seg_p, seg_s = pick(seg_table, 2, seg_wide, seg_parts(slot_ref, o)[0], hot_ref[:, at])
        out_ref[o, 2:3, :] = seg_p
        out_ref[o, 3:4, :] = seg_s
        out_ref[o, 4:5, :] = ends
        row, _ = cell_parts(cell_ref[o : o + 1, :], columns)
        (cell_p,) = pick(p_table, 1, rows, row, cell_hot_ref[:, at])
        out_ref[o, 0:1, :] = cell_p
        out_ref[o, 5:6, :] = columns_row


def source_last_kernel(
    groups, members, size, hot_ref, row_hot_ref, sent_ref, own_ref, seg_ref, pressure_ref, kept_ref, perm_ref,
    out_ref, keep_ref, left_ref,
):
    me = lax.axis_index("frac")
    pressure = pressure_ref[...]
    new_saturation, q, inv = cell_update(
        members,
        2,
        hot_ref,
        row_hot_ref,
        sent_ref,
        lambda o: (own_ref[o, 0:1, :], own_ref[o, 1:2, :]),
        lambda o: (seg_ref[o, 2:3, :], seg_ref[o, 3:4, :]),
        pressure,
        kept_ref[1],
        perm_ref[...],
        left_ref,
        ring_of(
            seg_ref[jnp.maximum(me - 1, 0), 5:6, :][:, LANES:],
            seg_ref[jnp.minimum(me + 1, members - 1), 5:6, :][:, :LANES],
            pressure_ref.shape[1],
            members,
        ),
    )
    keep_ref[0] = new_saturation
    keep_ref[1] = q
    keep_ref[2] = inv
    send_halo(out_ref, q, inv, pressure, groups, members, size, True)


def final_kernel(
    groups, members, size, halo_ref, pressure_ref, kept_ref, slot_ref, hot_ref, row_hot_ref, own_ref, seg_ref,
    frac_ref, aperture_ref, out_ref, new_ref, left_ref, *scratch,
):
    new_frac, new_sat = owner_update(
        members,
        2,
        slot_ref,
        lambda s: (seg_ref[s, 0:1, :], seg_ref[s, 1:2, :]),
        lambda s: (own_ref[s, 2:3, :], own_ref[s, 3:4, :]),
        frac_ref[0],
        frac_ref[1],
        load_segs(aperture_ref),
        chain_ends(seg_ref, 4, members),
        hot_ref,
        row_hot_ref,
        left_ref,
    )
    store_segs(new_ref, 0, new_frac)
    store_segs(new_ref, 1, new_sat)
    chebyshev(
        halo_ref, kept_ref.at[1], kept_ref.at[2], pressure_ref, out_ref.at[0], scratch, groups, members, size, True
    )
    out_ref[1] = kept_ref[0]


VMEM = pl.BlockSpec(memory_space=pltpu.VMEM)
HBM = pl.BlockSpec(memory_space=pltpu.HBM)


def call(kernel, statics, outs, scratch, *args, spec=VMEM):
    outs = [o if hasattr(o, "dtype") else jax.ShapeDtypeStruct(o, F32) for o in outs]
    return pl.pallas_call(
        functools.partial(kernel, *statics),
        out_shape=outs,
        in_specs=[spec] * len(args),
        out_specs=[VMEM] * len(outs),
        scratch_shapes=scratch,
        compiler_params=pltpu.CompilerParams(vmem_limit_bytes=32 * 1024 * 1024),
        name=kernel.__name__,
    )(*args)


def on_device(
    matrix_state,
    matrix_perm,
    frac_state,
    frac_aperture,
    link_cell,
    link_seg,
    link_trans,
    link_count,
    link_upwind,
):
    groups, members = lax.axis_size("grp"), lax.axis_size("frac")
    devices = groups * members
    cells = link_cell[0, 0]
    width = cells.shape[1]
    _, rows, columns = matrix_state.shape
    seg_dev = frac_state.shape[2]
    seg_rows = seg_dev // LANES
    frac = frac_state.reshape(2, seg_rows, LANES)
    aperture = frac_aperture.reshape(seg_rows, LANES)

    every = members * width
    slots = (members, SUB, width)
    closed_size, open_size = block_rows(columns, width, True), block_rows(columns, width, False)
    both = (groups, members, closed_size)
    halves = (groups, members, closed_size, open_size)
    halo, open_halo = (devices * closed_size, 1, LANES), (devices * open_size, 1, LANES)
    left_cell = pltpu.VMEM((3 * PARTS * rows, every), BF16)
    seg_wide = seg_dev // SEG_COLUMNS
    segs_wide = (2, seg_wide, SEG_COLUMNS)
    left_seg = pltpu.VMEM((3 * PARTS * seg_wide, every), BF16)
    tiles = columns // LANES + 1
    ext = [pltpu.VMEM((tiles, rows + SUB, LANES), F32)] * 4 + [pltpu.VMEM((tiles, rows + 3 * SUB, LANES), F32)] * 2

    def to_group(x):
        return lax.all_to_all(x, "frac", split_axis=0, concat_axis=0, tiled=True)

    def to_all(x):
        return lax.all_to_all(x, ("grp", "frac"), split_axis=0, concat_axis=0, tiled=True)

    def hots(*sizes):
        return [jax.ShapeDtypeStruct((n, every), BF16) for n in sizes]

    sent, cell_hot, cell_row_hot = call(
        first_kernel,
        (members,),
        [(members, SUB + 2 * seg_wide, SEG_COLUMNS)] + hots(columns, rows),
        [
            pltpu.VMEM((members, width), jnp.int32),
            pltpu.VMEM((members, width), jnp.int32),
            pltpu.VMEM((members, width), F32),
            pltpu.SMEM((1, members), jnp.int32),
            pltpu.VMEM((ITERS, members, width), jnp.int32),
            pltpu.VMEM(matrix_state.shape, F32),
            pltpu.VMEM(frac.shape, F32),
            pltpu.SemaphoreType.DMA((7,)),
        ],
        *[
            pltpu.with_memory_space_constraint(x, pltpu.HBM)
            for x in (
                cells, link_seg[0, 0], link_trans[0, 0], link_count[0], link_upwind[:, 0, 0], matrix_state, frac
            )
        ],
        spec=HBM,
    )
    slot = to_group(sent)
    edge, kept, own, frac1, hot, row_hot = call(
        start_kernel,
        both,
        [halo, (4, rows, columns), (members, 2, width), segs_wide] + hots(SEG_COLUMNS, seg_wide),
        [left_seg, left_cell],
        slot, sent, cell_hot, cell_row_hot, frac, aperture, matrix_state, matrix_perm,
    )
    before = to_all(edge)
    edge, kept = call(
        middle_kernel, halves, [open_halo, (4, rows, columns)], [pltpu.VMEM((members, 2, width), F32), left_cell] + ext,
        before, cells, cell_hot, cell_row_hot, sent, kept, matrix_perm,
    )
    around = to_all(edge)
    own, frac2, pressure = call(
        exchange_kernel, halves, [slots, segs_wide, (rows, columns)], [left_seg] + ext,
        around, cells, cell_hot, slot, hot, row_hot, before, own, frac1, aperture, kept,
    )
    segs = to_group(own)
    edge, kept = call(
        source_last_kernel, both, [halo, (3, rows, columns)], [left_cell],
        cell_hot, cell_row_hot, sent, own, segs, pressure, kept, matrix_perm,
    )
    around = to_all(edge)
    matrix_out, frac3 = call(
        final_kernel,
        both,
        [matrix_state.shape, frac.shape],
        [left_seg] + ext,
        around, pressure, kept, slot, hot, row_hot, own, segs, frac2, aperture,
    )
    return matrix_out, frac3.reshape(frac_state.shape)


def solution(mesh):
    return jax.shard_map(
        on_device,
        mesh=mesh,
        in_specs=(
            P(None, "grp", "frac"),
            P("grp", "frac"),
            P(None, "grp", "frac"),
            P("grp", "frac"),
            P("grp", "frac", None, None),
            P("grp", "frac", None, None),
            P("grp", "frac", None, None),
            P("grp", "frac", None),
            P(None, "grp", "frac", None, None),
        ),
        out_specs=(P(None, "grp", "frac"), P(None, "grp", "frac")),
        check_vma=False,
    )
```

```python
import functools

import jax
import jax.numpy as jnp
from jax import lax
from jax.experimental import pallas as pl
from jax.experimental.pallas import tpu as pltpu
from jax.sharding import PartitionSpec as P

ITERS = 3
SWEEPS = 4

LOW_BOUND = 0.02
HIGH_BOUND = 1.98
TAU_STEP = 0.5
MOBILITY_FLOOR = 0.2

F32 = jnp.float32
BF16 = jnp.bfloat16
LANES = 128
SUB = 8
SEG_COLUMNS = 2 * LANES
DEPTH = SWEEPS - 1


def iota(shape, dim):
    return lax.broadcasted_iota(jnp.int32, shape, dim)


def parts_of(x):
    high = x.astype(BF16).astype(F32)
    return high, x - high


PARTS = 2


def table_of(fields):
    split = [parts_of(f) for f in fields]
    return jnp.concatenate([s[p] for p in range(PARTS) for s in split], axis=0).astype(BF16)


def one_hot(index_row, count):
    shape = (count, index_row.shape[1])
    hit = iota(shape, 0).astype(F32).astype(BF16) == index_row.astype(F32).astype(BF16)
    return jnp.where(hit, jnp.ones(shape, BF16), jnp.zeros(shape, BF16))


def pick(table, fields, rows, row_index, hot):
    wide = jnp.dot(table, hot, preferred_element_type=F32)
    hit = iota((rows, row_index.shape[1]), 0) == row_index
    found = []
    for f in range(fields):
        total = sum(wide[(p * fields + f) * rows : (p * fields + f + 1) * rows] for p in range(PARTS))
        found.append(jnp.sum(jnp.where(hit, total, 0.0), axis=0, keepdims=True))
    return found


def spread(left_ref, row_hot_ref, block, values):
    rows = row_hot_ref.shape[0]
    width = values[0].shape[1]
    at = slice(block * width, (block + 1) * width)
    hot = row_hot_ref[:, at]
    for f, value in enumerate(values):
        for p, part in enumerate(parts_of(value)):
            row = (p * len(values) + f) * rows
            left_ref[row : row + rows, at] = hot * part.astype(BF16)


def gathered_sum(left_ref, hot_ref, fields, rows):
    wide = lax.dot_general(
        left_ref[...], hot_ref[...], (((1,), (1,)), ((), ())), preferred_element_type=F32
    )
    return [
        sum(wide[(p * fields + f) * rows : (p * fields + f + 1) * rows] for p in range(PARTS))
        for f in range(fields)
    ]


def flow(trans, upwind, cell_p, cell_s, seg_p, seg_s):
    u = jnp.where(upwind > 0.5, cell_s, seg_s)
    weight = trans * (MOBILITY_FLOOR + u * u)
    water = weight * (cell_p - seg_p) * u
    return weight, water


def cell_parts(cell_row, columns):
    return cell_row // columns, cell_row % columns


def load_segs(ref, *lead):
    rows = ref.shape[-2] // 2
    return jnp.concatenate([ref[(*lead, pl.ds(h, rows, 2), slice(None))] for h in range(2)], axis=1)


def store_segs(ref, lead, value):
    rows = value.shape[0]
    for h in range(2):
        ref[lead, pl.ds(h, rows, 2), :] = value[:, h * LANES : (h + 1) * LANES]


def ends_of(frac):
    rows, columns = frac.shape
    lane = iota((1, columns), 1)
    return jnp.where(lane < columns // 2, frac[0:1], frac[rows - 1 : rows])


def frac_step(frac, sat, aperture, before, after, inflow, total, gained):
    rows, lanes = frac.shape
    row, lane = iota((rows, lanes), 0), iota((rows, lanes), 1)
    back = pltpu.roll(frac, 1, 1)
    left = jnp.where(lane == 0, pltpu.roll(back, 1, 0), back)
    left = jnp.where((lane == 0) & (row == 0), before, left)
    ahead = pltpu.roll(frac, lanes - 1, 1)
    right = jnp.where(lane == lanes - 1, pltpu.roll(ahead, rows - 1, 0), ahead)
    right = jnp.where((lane == lanes - 1) & (row == rows - 1), after, right)
    new_frac = (aperture * frac + inflow + left + right) / (aperture + total + 2.0)
    new_sat = sat + TAU_STEP * gained / (aperture + total)
    return new_frac, new_sat


def chain_ends(ends_ref, row, members):
    me = lax.axis_index("frac")
    lanes = ends_ref.shape[2]
    prior = ends_ref[jnp.maximum(me - 1, 0), row : row + 1, :]
    later = ends_ref[jnp.minimum(me + 1, members - 1), row : row + 1, :]
    before = jnp.where(me > 0, prior[:, lanes - 1 :], 0.0)
    after = jnp.where(me < members - 1, later[:, 0:1], 0.0)
    return before, after


def partial_residual(pressure, couple, source, inverse, ring):
    rows, columns = pressure.shape
    row, col = iota((rows, columns), 0), iota((rows, columns), 1)
    beside = jnp.where(row == 0, 0.0, pltpu.roll(pressure, 1, 0))
    beside += jnp.where(row == rows - 1, 0.0, pltpu.roll(pressure, rows - 1, 0))
    beside += jnp.where(col == 0, 0.0, pltpu.roll(pressure, 1, 1))
    beside += jnp.where(col == columns - 1, 0.0, pltpu.roll(pressure, columns - 1, 1))
    if ring is not None:
        beside += ring
    return inverse * (source - (4.0 + couple) * pressure + beside)


def edge_columns(p):
    rows, columns = p.shape
    lane = iota((rows, LANES), 1)
    turned = jnp.transpose(jnp.where(lane < LANES // 2, p[:, :LANES], p[:, columns - LANES :]))
    return turned[0:1], turned[LANES - 1 : LANES]


def ring_of(left, right, columns, members):
    f = lax.axis_index("frac")
    rows = left.shape[1]
    left = jnp.where(f > 0, left, 0.0)
    right = jnp.where(f < members - 1, right, 0.0)
    turned = jnp.transpose(jnp.concatenate([left, jnp.zeros((LANES - 2, rows), F32), right], axis=0))
    lane = iota((rows, LANES), 1)
    low = jnp.where(lane == 0, turned, 0.0)
    high = jnp.where(lane == LANES - 1, turned, 0.0)
    if columns == LANES:
        return low + high
    return jnp.concatenate([low] + [jnp.zeros((rows, LANES), F32)] * (columns // LANES - 2) + [high], axis=1)


def pack_low(q, inv, p, at, axis):
    return jnp.where(
        at < DEPTH, q, jnp.where(at < 2 * DEPTH, pltpu.roll(inv, DEPTH, axis), pltpu.roll(p, 2 * DEPTH, axis))
    )


def pack_high(q, inv, p, at, axis):
    size = q.shape[axis]
    return jnp.where(
        at >= size - DEPTH,
        q,
        jnp.where(
            at >= size - 2 * DEPTH,
            pltpu.roll(inv, size - DEPTH, axis),
            pltpu.roll(p, size - 2 * DEPTH, axis),
        ),
    )


def block_rows(columns, width, closed):
    vertical = 2 * DEPTH * (columns // LANES)
    lateral = SUB + 2 * (width // LANES)
    return max(vertical, lateral) + (0 if closed else 1)


def put_rows(out_ref, at, values):
    for k in range(values.shape[0]):
        out_ref[at + k] = values[k : k + 1]


def get_rows(in_ref, at, count):
    return jnp.concatenate([in_ref[at + k] for k in range(count)], axis=0)


def send_slots(out_ref, at, first, second):
    halves = first.shape[1] // LANES
    for i, value in enumerate((first, second)):
        for h in range(halves):
            out_ref[at + SUB + i * halves + h] = value[:, h * LANES : (h + 1) * LANES]


def got_slots(in_ref, at, width):
    halves = width // LANES
    return [
        jnp.concatenate([in_ref[at + SUB + i * halves + h] for h in range(halves)], axis=1) for i in range(2)
    ]


def send_halo(out_ref, q, inv, p, groups, members, size, closed, ends=None):
    rows, columns = q.shape
    halves = columns // LANES
    g, f = lax.axis_index("grp"), lax.axis_index("frac")
    here = g * members + f
    lane = iota((rows, LANES), 1)
    low = pack_low(q[:, :LANES], inv[:, :LANES], p[:, :LANES], lane, 1)
    high = pack_high(q[:, columns - LANES :], inv[:, columns - LANES :], p[:, columns - LANES :], lane, 1)
    turned = jnp.transpose(jnp.where(lane < LANES // 2, low, high))
    left, right = turned[:SUB], turned[LANES - SUB :]
    if ends is not None:
        sub, lane = iota((SUB, LANES), 0), iota((SUB, LANES), 1)
        left = jnp.where((sub == SUB - 1) & (lane == 1), ends[0], left)
        right = jnp.where((sub == 0) & (lane == LANES - 2), ends[1], right)
    lane = iota((1, LANES), 1)
    spare = jnp.where(g + 2 < groups, here + 2 * members, here - 2 * members)

    for step in (-1, 1):
        layer = (lambda k: k) if step < 0 else (lambda k: rows - 1 - k)

        def span(field, count, at):
            start = 0 if step < 0 else rows - count
            return field[start : start + count, at]

        inside = (g + step >= 0) & (g + step < groups)
        base = here + step * members
        tiles = [slice(h * LANES, (h + 1) * LANES) for h in range(halves)]

        at = jnp.where(inside, base, spare) * size
        for h, tile in enumerate(tiles):
            put_rows(out_ref, at + h * DEPTH, span(q, DEPTH, tile))
            put_rows(out_ref, at + halves * DEPTH + h * (DEPTH - 1), span(inv, DEPTH - 1, tile))
            put_rows(out_ref, at + halves * (2 * DEPTH - 1) + h, span(p, 1, tile))
        if not closed:
            deep, next_p = layer(DEPTH - 1), layer(1)
            extra = jnp.where(
                lane == 0,
                inv[deep : deep + 1, tiles[0]],
                jnp.where(
                    lane == LANES - 1,
                    inv[deep : deep + 1, tiles[-1]],
                    jnp.where(
                        lane == 1,
                        pltpu.roll(p[next_p : next_p + 1, tiles[0]], 1, 1),
                        pltpu.roll(p[next_p : next_p + 1, tiles[-1]], LANES - 1, 1),
                    ),
                ),
            )
            out_ref[at + halves * 2 * DEPTH] = extra

        for side, tile, there in ((-1, tiles[0], f > 0), (1, tiles[-1], f < members - 1)):
            at = jnp.where(inside & there, base + side, spare) * size
            for i, field in enumerate((q, inv, p)):
                put_rows(out_ref, at + i * DEPTH, span(field, DEPTH, tile))

    put_rows(out_ref, jnp.where(f > 0, here - 1, spare) * size, left)
    put_rows(out_ref, jnp.where(f < members - 1, here + 1, spare) * size, right)


def chebyshev(in_ref, q_ref, inv_ref, p_ref, target, scratch, groups, members, size, closed):
    q_ext, inv_ext, p_ext, update_ref, even_ref, odd_ref = scratch
    rows, columns = target.shape
    halves = columns // LANES
    side = halves
    g, f = lax.axis_index("grp"), lax.axis_index("frac")
    here = g * members + f
    last = groups * members - 1

    def taker(dg, df):
        ok = (g + dg >= 0) & (g + dg < groups) & (f + df >= 0) & (f + df < members)
        at = jnp.clip(here + dg * members + df, 0, last) * size
        return lambda start, count: jnp.where(ok, get_rows(in_ref, at + start, count), 0.0)

    def both(low, high, at, count, size):
        return jnp.where(at < count, low, jnp.where(at >= size - count, high, 0.0))

    def filler(count):
        return jnp.zeros((count, LANES), F32)

    for h in range(halves):
        for ext, ref in ((q_ext, q_ref), (inv_ext, inv_ref), (p_ext, p_ref)):
            ext[h, 0:rows, :] = ref[:, h * LANES : (h + 1) * LANES]
    outer = slice(rows, rows + SUB)
    below, above = taker(1, 0), taker(-1, 0)
    lane = iota((1, LANES), 1)
    if not closed:
        low_extra, high_extra = below(halves * 2 * DEPTH, 1), above(halves * 2 * DEPTH, 1)
    for h in range(halves):
        edge = (lane == 0) & (h == 0) | (lane == LANES - 1) & (h == halves - 1)

        def at_edge(high, turn):
            if closed:
                return filler(1)
            row = high_extra if high else low_extra
            return jnp.where(edge, pltpu.roll(row, turn, 1) if turn else row, 0.0)

        turn = LANES - 1 if h == 0 else 1
        at = h * DEPTH
        q_ext[h, outer, :] = jnp.concatenate(
            [below(at, DEPTH), filler(SUB - 2 * DEPTH), above(at, DEPTH)], axis=0
        )
        at = halves * DEPTH + h * (DEPTH - 1)
        inv_ext[h, outer, :] = jnp.concatenate(
            [
                below(at, DEPTH - 1),
                at_edge(False, 0),
                filler(SUB - 2 * DEPTH),
                at_edge(True, 0),
                above(at, DEPTH - 1),
            ],
            axis=0,
        )
        at = halves * (2 * DEPTH - 1) + h
        p_ext[h, outer, :] = jnp.concatenate(
            [
                below(at, 1),
                at_edge(False, turn),
                filler(SUB - 4),
                at_edge(True, turn),
                above(at, 1),
            ],
            axis=0,
        )
    right, left = taker(0, 1)(0, SUB), taker(0, -1)(0, SUB)
    turned = jnp.transpose(
        jnp.concatenate(
            [
                right[:DEPTH],
                jnp.zeros((LANES - 2 * SUB - DEPTH + 2, rows), F32),
                left[:2],
                right[2 * DEPTH :],
                jnp.zeros((1, rows), F32),
                left[2 : 2 + DEPTH],
                right[DEPTH : 2 * DEPTH],
                left[2 + DEPTH :],
            ],
            axis=0,
        )
    )
    lane = iota((rows, LANES), 1)
    q_ext[side, 0:rows, :] = both(turned, turned, lane, DEPTH, LANES)
    turned_inv, turned_p = pltpu.roll(turned, 2 * DEPTH, 1), pltpu.roll(turned, 4 * DEPTH, 1)
    inv_ext[side, 0:rows, :] = both(turned_inv, turned_inv, lane, DEPTH, LANES)
    p_ext[side, 0:rows, :] = both(turned_p, turned_p, lane, 2, LANES)
    lane = iota((DEPTH, LANES), 1)
    low_right, low_left, high_right, high_left = taker(1, 1), taker(1, -1), taker(-1, 1), taker(-1, -1)
    for i, ext in enumerate((q_ext, inv_ext, p_ext)):
        at = i * DEPTH
        ext[side, outer, :] = jnp.concatenate(
            [
                both(low_right(at, DEPTH), low_left(at, DEPTH), lane, DEPTH, LANES),
                filler(SUB - 2 * DEPTH),
                both(high_right(at, DEPTH), high_left(at, DEPTH), lane, DEPTH, LANES),
            ],
            axis=0,
        )

    end = rows + SUB - 1
    for own, other in ((0, end), (end, 0), (rows - 1, rows), (rows, rows - 1)):
        for c in range(halves + 1):
            q_ext[c, own : own + 1, :] += inv_ext[c, own : own + 1, :] * p_ext[c, other : other + 1, :]
    centre = 0.5 * (HIGH_BOUND + LOW_BOUND)
    half_width = 0.5 * (HIGH_BOUND - LOW_BOUND)
    scale_ratio = centre / half_width
    ratio_now = 1.0 / scale_ratio
    lane = iota((SUB, LANES), 1)
    count = rows // SUB + 1

    def keep(ref, c, r, value):
        at = (r + 1) * SUB
        ref[c, at : at + SUB, :] = value
        if r == count - 1:
            ref[c, 0:SUB, :] = value
        if r == 0:
            at = (count + 1) * SUB
            ref[c, at : at + SUB, :] = value

    for r in range(count):
        at = slice(r * SUB, (r + 1) * SUB)
        if closed:
            for c in range(halves + 1):
                start = q_ext[c, at, :]
                keep(even_ref, c, r, start / centre if centre != 1.0 else start)
            continue
        p_side, p_first, p_final = p_ext[side, at, :], p_ext[0, at, :], p_ext[halves - 1, at, :]
        missing = [0.0] * (halves + 1)
        missing[0] += jnp.where(lane == 0, pltpu.roll(p_side, 1, 1), 0.0)
        missing[halves - 1] += jnp.where(lane == LANES - 1, pltpu.roll(p_side, LANES - 1, 1), 0.0)
        missing[side] = jnp.where(
            lane == 0,
            pltpu.roll(p_final, 1, 1),
            jnp.where(lane == LANES - 1, pltpu.roll(p_first, LANES - 1, 1), 0.0),
        )
        for c in range(halves + 1):
            start = q_ext[c, at, :] + inv_ext[c, at, :] * missing[c]
            q_ext[c, at, :] = start
            keep(even_ref, c, r, start / centre if centre != 1.0 else start)
    now_ref, next_ref = even_ref, odd_ref
    for sweep in range(1, SWEEPS):
        ratio_next = 1.0 / (2.0 * scale_ratio - ratio_now)
        final = sweep == SWEEPS - 1
        for r in range(count - 1 if final else count):
            at = slice(r * SUB, (r + 1) * SUB)
            mids = [now_ref[c, (r + 1) * SUB : (r + 2) * SUB, :] for c in range(halves + 1)]
            after = [pltpu.roll(m, 1, 1) for m in mids]
            ahead = [pltpu.roll(m, LANES - 1, 1) for m in mids]
            for c in range(halves if final else halves + 1):
                beside = now_ref[c, (r + 1) * SUB - 1 : (r + 2) * SUB - 1, :]
                beside += now_ref[c, (r + 1) * SUB + 1 : (r + 2) * SUB + 1, :]
                beside += jnp.where(lane == 0, after[(c - 1) % (halves + 1)], after[c])
                beside += jnp.where(lane == LANES - 1, ahead[(c + 1) % (halves + 1)], ahead[c])
                residual = q_ext[c, at, :] - mids[c] + inv_ext[c, at, :] * beside
                old = mids[c] if sweep == 1 else update_ref[c, at, :]
                update = ratio_next * ratio_now * old + (2.0 * ratio_next / half_width) * residual
                if final:
                    tile = slice(c * LANES, (c + 1) * LANES)
                    target[at, tile] = p_ref[at, tile] + mids[c] + update
                else:
                    update_ref[c, at, :] = update
                    keep(next_ref, c, r, mids[c] + update)
        ratio_now = ratio_next
        now_ref, next_ref = next_ref, now_ref


ROW_SEG = 0
ROW_TRANS = 1
ROW_UP = 2
ROW_P = ROW_UP + ITERS
ROW_S = ROW_P + 1
ROW_ENDS = ROW_S + 1


def first_kernel(
    members, cell_any, seg_any, trans_any, count_any, up_any, state_any, frac_any,
    out_ref, hot_ref, row_hot_ref, cell_ref, seg_ref, trans_ref, count_ref, up_ref, state_ref, frac_ref, sem,
):
    _, rows, columns = state_ref.shape
    width = cell_ref.shape[1]
    copies = [
        pltpu.make_async_copy(source, target, sem.at[i])
        for i, (source, target) in enumerate(
            [
                (cell_any, cell_ref),
                (state_any, state_ref),
                (seg_any, seg_ref),
                (trans_any, trans_ref),
                (count_any, count_ref),
                (up_any, up_ref),
                (frac_any, frac_ref),
            ]
        )
    ]
    for i in (0, 1, 6, 2, 3, 4, 5):
        copies[i].start()
    copies[0].wait()

    def make_hots(o):
        row, col = cell_parts(cell_ref[o : o + 1, :], columns)
        at = slice(o * width, (o + 1) * width)
        hot_ref[:, at] = one_hot(col, columns)
        row_hot_ref[:, at] = one_hot(row, rows)

    for o in range(members):
        make_hots(o)
    copies[1].wait()
    table = table_of([state_ref[0], state_ref[1]])
    copies[6].wait()
    frac = load_segs(frac_ref, 0)
    ends = ends_of(frac)
    left, right = edge_columns(state_ref[0])
    me = lax.axis_index("frac")
    to_left = jnp.concatenate([ends[:, :LANES], left], axis=1)
    to_right = jnp.concatenate([right, ends[:, LANES:]], axis=1)
    whole = jnp.concatenate([frac, load_segs(frac_ref, 1)], axis=0)
    for o in range(members):
        one = slice(o, o + 1)
        row, _ = cell_parts(cell_ref[one, :], columns)
        cell_p, cell_s = pick(table, 2, rows, row, hot_ref[:, o * width : (o + 1) * width])
        out_ref[o, ROW_P : ROW_P + 1, :] = cell_p
        out_ref[o, ROW_S : ROW_S + 1, :] = cell_s
        out_ref[o, ROW_ENDS : ROW_ENDS + 1, :] = jnp.where(me + 1 == o, to_right, to_left)
        out_ref[o, SUB:, :] = whole
    for copy in copies[2:6]:
        copy.wait()
    for o in range(members):
        one = slice(o, o + 1)
        live = iota((1, width), 1) < count_ref[0, o]
        out_ref[o, ROW_SEG : ROW_SEG + 1, :] = seg_ref[one, :].astype(F32)
        out_ref[o, ROW_TRANS : ROW_TRANS + 1, :] = jnp.where(live, trans_ref[one, :], 0.0)
        for t in range(ITERS):
            out_ref[o, ROW_UP + t : ROW_UP + t + 1, :] = up_ref[t, one, :].astype(F32)


def seg_parts(slot_ref, s):
    seg = slot_ref[s, ROW_SEG : ROW_SEG + 1, :].astype(jnp.int32)
    return seg // SEG_COLUMNS, seg % SEG_COLUMNS


def seg_hots(slot_ref, hot_ref, row_hot_ref, members, width):
    for s in range(members):
        row, lane = seg_parts(slot_ref, s)
        at = slice(s * width, (s + 1) * width)
        hot_ref[:, at] = one_hot(lane, SEG_COLUMNS)
        row_hot_ref[:, at] = one_hot(row, row_hot_ref.shape[0])


def seg_gather(slot_ref, hot_ref, fields, s, width, table):
    return pick(table, 2, fields, seg_parts(slot_ref, s)[0], hot_ref[:, s * width : (s + 1) * width])


def cell_spread(t, o, row_hot_ref, sent_ref, cell_row, seg_row, left_ref):
    seg_p, seg_s = seg_row
    cell_p, cell_s = cell_row
    weight, water = flow(
        sent_ref[o, ROW_TRANS : ROW_TRANS + 1, :],
        sent_ref[o, ROW_UP + t : ROW_UP + t + 1, :],
        cell_p,
        cell_s,
        seg_p,
        seg_s,
    )
    spread(left_ref, row_hot_ref, o, [weight, weight * seg_p, water])


def cell_finish(hot_ref, pressure, saturation, perm, left_ref, ring):
    rows = pressure.shape[0]
    couple, source, lost = gathered_sum(left_ref, hot_ref, 3, rows)
    inverse = 1.0 / (4.0 + perm + couple)
    new_saturation = saturation - TAU_STEP * lost / (perm + couple)
    return new_saturation, partial_residual(pressure, couple, source, inverse, ring), inverse


def cell_update(
    members, t, hot_ref, row_hot_ref, sent_ref, cell_rows, seg_rows, pressure, saturation, perm, left_ref, ring
):
    for o in range(members):
        cell_spread(t, o, row_hot_ref, sent_ref, cell_rows(o), seg_rows(o), left_ref)
    return cell_finish(hot_ref, pressure, saturation, perm, left_ref, ring)


def start_kernel(
    groups, members, size, slot_ref, sent_ref, cell_hot_ref, cell_row_hot_ref, frac_ref, aperture_ref,
    state_ref, perm_ref, out_ref, keep_ref, own_ref, new_ref, hot_ref, row_hot_ref,
    left_seg_ref, left_ref,
):
    width = slot_ref.shape[2]
    rows = new_ref.shape[1]
    g = lax.axis_index("grp")
    frac, sat = load_segs(frac_ref, 0), load_segs(frac_ref, 1)
    seg_hots(slot_ref, hot_ref, row_hot_ref, members, width)
    table = table_of([frac, sat])
    for s in range(members):
        o = s
        row, lane = seg_parts(sent_ref, o)
        whole = table_of([slot_ref[o, SUB : SUB + rows, :], slot_ref[o, SUB + rows :, :]])
        seg_p, seg_s = pick(whole, 2, rows, row, one_hot(lane, SEG_COLUMNS))
        cell_spread(
            0,
            o,
            cell_row_hot_ref,
            sent_ref,
            (sent_ref[o, ROW_P : ROW_P + 1, :], sent_ref[o, ROW_S : ROW_S + 1, :]),
            (seg_p, seg_s),
            left_ref,
        )
        seg_p, seg_s = seg_gather(slot_ref, hot_ref, rows, s, width, table)
        cell_p = slot_ref[s, ROW_P : ROW_P + 1, :]
        weight, water = flow(
            slot_ref[s, ROW_TRANS : ROW_TRANS + 1, :],
            slot_ref[s, ROW_UP : ROW_UP + 1, :],
            cell_p,
            slot_ref[s, ROW_S : ROW_S + 1, :],
            seg_p,
            seg_s,
        )
        spread(left_seg_ref, row_hot_ref, s, [weight * cell_p, weight, water])
    inflow, total, gained = gathered_sum(left_seg_ref, hot_ref, 3, rows)
    before, after = chain_ends(slot_ref, ROW_ENDS, members)
    new_frac, new_sat = frac_step(frac, sat, load_segs(aperture_ref), before, after, inflow, total, gained)
    new_ref[0] = new_frac
    new_ref[1] = new_sat
    table = table_of([new_frac, new_sat])
    me = lax.axis_index("frac")
    pressure = state_ref[0]
    new_saturation, q, inv = cell_finish(
        cell_hot_ref,
        pressure,
        state_ref[1],
        perm_ref[...],
        left_ref,
        ring_of(
            slot_ref[jnp.maximum(me - 1, 0), ROW_ENDS : ROW_ENDS + 1, :][:, :LANES],
            slot_ref[jnp.minimum(me + 1, members - 1), ROW_ENDS : ROW_ENDS + 1, :][:, LANES:],
            state_ref.shape[2],
            members,
        ),
    )
    for s in range(members):
        seg_p, seg_s = seg_gather(slot_ref, hot_ref, rows, s, width, table)
        own_ref[s, 0:1, :] = seg_p
        own_ref[s, 1:2, :] = seg_s
        at = (g * members + s) * size
        send_slots(out_ref, at, seg_p, seg_s)
    keep_ref[0] = pressure
    keep_ref[1] = new_saturation
    keep_ref[2] = q
    keep_ref[3] = inv
    ends = (new_frac[0:1, 0:1], new_frac[rows - 1 : rows, SEG_COLUMNS - 1 : SEG_COLUMNS])
    send_halo(out_ref, q, inv, pressure, groups, members, size, True, ends)


def cell_gather(members, cell_ref, hot_ref, fields, put):
    rows, columns = fields[0].shape
    width = cell_ref.shape[1]
    table = table_of(fields)
    for o in range(members):
        row, _ = cell_parts(cell_ref[o : o + 1, :], columns)
        put(o, *pick(table, len(fields), rows, row, hot_ref[:, o * width : (o + 1) * width]))


def middle_kernel(
    groups, members, size, open_size, halo_ref, cell_ref, hot_ref, row_hot_ref, sent_ref, kept_ref, perm_ref,
    out_ref, keep_ref, slots_ref, left_ref, *scratch,
):
    saturation = kept_ref[1]
    g = lax.axis_index("grp")

    def put_s(o, cell_s):
        slots_ref[o, 1:2, :] = cell_s

    cell_gather(members, cell_ref, hot_ref, [saturation], put_s)
    chebyshev(
        halo_ref, kept_ref.at[2], kept_ref.at[3], kept_ref.at[0], keep_ref.at[0], scratch, groups, members, size, True
    )
    pressure = keep_ref[0]

    rows, columns = pressure.shape
    width = cell_ref.shape[1]
    table = table_of([pressure])
    for o in range(members):
        row, _ = cell_parts(cell_ref[o : o + 1, :], columns)
        (cell_p,) = pick(table, 1, rows, row, hot_ref[:, o * width : (o + 1) * width])
        cell_s = slots_ref[o, 1:2, :]
        send_slots(out_ref, (g * members + o) * open_size, cell_p, cell_s)
        cell_spread(
            1,
            o,
            row_hot_ref,
            sent_ref,
            (cell_p, cell_s),
            got_slots(halo_ref, (g * members + o) * size, width),
            left_ref,
        )
    new_saturation, q, inv = cell_finish(hot_ref, pressure, saturation, perm_ref[...], left_ref, None)
    keep_ref[1] = new_saturation
    keep_ref[2] = q
    keep_ref[3] = inv
    send_halo(out_ref, q, inv, pressure, groups, members, open_size, False)


def owner_spread(blocks, t, slot_ref, cell_rows, seg_rows, row_hot_ref, left_ref):
    for s in blocks:
        cell_p, cell_s = cell_rows(s)
        weight, water = flow(
            slot_ref[s, ROW_TRANS : ROW_TRANS + 1, :],
            slot_ref[s, ROW_UP + t : ROW_UP + t + 1, :],
            cell_p,
            cell_s,
            *seg_rows(s),
        )
        spread(left_ref, row_hot_ref, s, [weight * cell_p, weight, water])


def owner_update(
    members, t, slot_ref, cell_rows, seg_rows, frac, sat, aperture, ends, hot_ref, row_hot_ref, left_ref
):
    owner_spread(range(members), t, slot_ref, cell_rows, seg_rows, row_hot_ref, left_ref)
    inflow, total, gained = gathered_sum(left_ref, hot_ref, 3, frac.shape[0])
    return frac_step(frac, sat, aperture, *ends, inflow, total, gained)


def exchange_kernel(
    groups, members, closed_size, size, halo_ref, cell_ref, cell_hot_ref, slot_ref, hot_ref, row_hot_ref, ends_ref, own_ref,
    frac_ref, aperture_ref, kept_ref, out_ref, new_ref, pressure_ref, left_ref, *scratch,
):
    width = slot_ref.shape[2]
    g = lax.axis_index("grp")

    def cell_rows(s):
        return got_slots(halo_ref, (g * members + s) * size, width)

    me = lax.axis_index("frac")
    prior = ends_ref[(g * members + jnp.maximum(me - 1, 0)) * closed_size]
    later = ends_ref[(g * members + jnp.minimum(me + 1, members - 1)) * closed_size + SUB - 1]
    before = jnp.where(me > 0, prior[:, LANES - 2 : LANES - 1], 0.0)
    after = jnp.where(me < members - 1, later[:, 1:2], 0.0)

    rows, columns = pressure_ref.shape
    seg_wide = frac_ref.shape[1]
    owner_spread(
        range(members),
        1,
        slot_ref,
        cell_rows,
        lambda s: (own_ref[s, 0:1, :], own_ref[s, 1:2, :]),
        row_hot_ref,
        left_ref,
    )
    inflow, total, gained = gathered_sum(left_ref, hot_ref, 3, seg_wide)
    new_frac, new_sat = frac_step(
        frac_ref[0], frac_ref[1], load_segs(aperture_ref), before, after, inflow, total, gained
    )
    new_ref[0] = new_frac
    new_ref[1] = new_sat
    seg_table = table_of([new_frac, new_sat])
    ends = ends_of(new_frac)
    s_table = table_of([kept_ref[1]])
    for o in range(members):
        at = slice(o * width, (o + 1) * width)
        row, _ = cell_parts(cell_ref[o : o + 1, :], columns)
        (cell_s,) = pick(s_table, 1, rows, row, cell_hot_ref[:, at])
        out_ref[o, 1:2, :] = cell_s
    chebyshev(
        halo_ref, kept_ref.at[2], kept_ref.at[3], kept_ref.at[0], pressure_ref, scratch, groups, members, size, False
    )
    p_table = table_of([pressure_ref[...]])
    columns_row = jnp.concatenate(edge_columns(pressure_ref[...]), axis=1)
    for o in range(members):
        at = slice(o * width, (o + 1) * width)
        seg_p, seg_s = pick(seg_table, 2, seg_wide, seg_parts(slot_ref, o)[0], hot_ref[:, at])
        out_ref[o, 2:3, :] = seg_p
        out_ref[o, 3:4, :] = seg_s
        out_ref[o, 4:5, :] = ends
        row, _ = cell_parts(cell_ref[o : o + 1, :], columns)
        (cell_p,) = pick(p_table, 1, rows, row, cell_hot_ref[:, at])
        out_ref[o, 0:1, :] = cell_p
        out_ref[o, 5:6, :] = columns_row


def source_last_kernel(
    groups, members, size, hot_ref, row_hot_ref, sent_ref, own_ref, seg_ref, pressure_ref, kept_ref, perm_ref,
    out_ref, keep_ref, left_ref,
):
    me = lax.axis_index("frac")
    pressure = pressure_ref[...]
    new_saturation, q, inv = cell_update(
        members,
        2,
        hot_ref,
        row_hot_ref,
        sent_ref,
        lambda o: (own_ref[o, 0:1, :], own_ref[o, 1:2, :]),
        lambda o: (seg_ref[o, 2:3, :], seg_ref[o, 3:4, :]),
        pressure,
        kept_ref[1],
        perm_ref[...],
        left_ref,
        ring_of(
            seg_ref[jnp.maximum(me - 1, 0), 5:6, :][:, LANES:],
            seg_ref[jnp.minimum(me + 1, members - 1), 5:6, :][:, :LANES],
            pressure_ref.shape[1],
            members,
        ),
    )
    keep_ref[0] = new_saturation
    keep_ref[1] = q
    keep_ref[2] = inv
    send_halo(out_ref, q, inv, pressure, groups, members, size, True)


def final_kernel(
    groups, members, size, halo_ref, pressure_ref, kept_ref, slot_ref, hot_ref, row_hot_ref, own_ref, seg_ref,
    frac_ref, aperture_ref, out_any, new_any, left_ref, field_ref, new_ref, sem, *scratch,
):
    copies = [
        pltpu.make_async_copy(source, target, sem.at[i])
        for i, (source, target) in enumerate(
            [(kept_ref.at[0], out_any.at[1]), (new_ref, new_any), (field_ref, out_any.at[0])]
        )
    ]
    copies[0].start()
    new_frac, new_sat = owner_update(
        members,
        2,
        slot_ref,
        lambda s: (seg_ref[s, 0:1, :], seg_ref[s, 1:2, :]),
        lambda s: (own_ref[s, 2:3, :], own_ref[s, 3:4, :]),
        frac_ref[0],
        frac_ref[1],
        load_segs(aperture_ref),
        chain_ends(seg_ref, 4, members),
        hot_ref,
        row_hot_ref,
        left_ref,
    )
    store_segs(new_ref, 0, new_frac)
    store_segs(new_ref, 1, new_sat)
    copies[1].start()
    chebyshev(
        halo_ref, kept_ref.at[1], kept_ref.at[2], pressure_ref, field_ref, scratch, groups, members, size, True
    )
    copies[2].start()
    for copy in copies:
        copy.wait()


VMEM = pl.BlockSpec(memory_space=pltpu.VMEM)
HBM = pl.BlockSpec(memory_space=pltpu.HBM)


def call(kernel, statics, outs, scratch, *args, spec=VMEM, out_spec=VMEM):
    outs = [o if hasattr(o, "dtype") else jax.ShapeDtypeStruct(o, F32) for o in outs]
    return pl.pallas_call(
        functools.partial(kernel, *statics),
        out_shape=outs,
        in_specs=[spec] * len(args),
        out_specs=[out_spec] * len(outs),
        scratch_shapes=scratch,
        compiler_params=pltpu.CompilerParams(vmem_limit_bytes=32 * 1024 * 1024),
        name=kernel.__name__,
    )(*args)


def on_device(
    matrix_state,
    matrix_perm,
    frac_state,
    frac_aperture,
    link_cell,
    link_seg,
    link_trans,
    link_count,
    link_upwind,
):
    groups, members = lax.axis_size("grp"), lax.axis_size("frac")
    devices = groups * members
    cells = link_cell[0, 0]
    width = cells.shape[1]
    _, rows, columns = matrix_state.shape
    seg_dev = frac_state.shape[2]
    seg_rows = seg_dev // LANES
    frac = frac_state.reshape(2, seg_rows, LANES)
    aperture = frac_aperture.reshape(seg_rows, LANES)

    every = members * width
    slots = (members, SUB, width)
    closed_size, open_size = block_rows(columns, width, True), block_rows(columns, width, False)
    both = (groups, members, closed_size)
    halves = (groups, members, closed_size, open_size)
    halo, open_halo = (devices * closed_size, 1, LANES), (devices * open_size, 1, LANES)
    left_cell = pltpu.VMEM((3 * PARTS * rows, every), BF16)
    seg_wide = seg_dev // SEG_COLUMNS
    segs_wide = (2, seg_wide, SEG_COLUMNS)
    left_seg = pltpu.VMEM((3 * PARTS * seg_wide, every), BF16)
    tiles = columns // LANES + 1
    ext = [pltpu.VMEM((tiles, rows + SUB, LANES), F32)] * 4 + [pltpu.VMEM((tiles, rows + 3 * SUB, LANES), F32)] * 2

    def to_group(x):
        return lax.all_to_all(x, "frac", split_axis=0, concat_axis=0, tiled=True)

    def to_all(x):
        return lax.all_to_all(x, ("grp", "frac"), split_axis=0, concat_axis=0, tiled=True)

    def hots(*sizes):
        return [jax.ShapeDtypeStruct((n, every), BF16) for n in sizes]

    sent, cell_hot, cell_row_hot = call(
        first_kernel,
        (members,),
        [(members, SUB + 2 * seg_wide, SEG_COLUMNS)] + hots(columns, rows),
        [
            pltpu.VMEM((members, width), jnp.int32),
            pltpu.VMEM((members, width), jnp.int32),
            pltpu.VMEM((members, width), F32),
            pltpu.SMEM((1, members), jnp.int32),
            pltpu.VMEM((ITERS, members, width), jnp.int32),
            pltpu.VMEM(matrix_state.shape, F32),
            pltpu.VMEM(frac.shape, F32),
            pltpu.SemaphoreType.DMA((7,)),
        ],
        *[
            pltpu.with_memory_space_constraint(x, pltpu.HBM)
            for x in (
                cells, link_seg[0, 0], link_trans[0, 0], link_count[0], link_upwind[:, 0, 0], matrix_state, frac
            )
        ],
        spec=HBM,
    )
    slot = to_group(sent)
    edge, kept, own, frac1, hot, row_hot = call(
        start_kernel,
        both,
        [halo, (4, rows, columns), (members, 2, width), segs_wide] + hots(SEG_COLUMNS, seg_wide),
        [left_seg, left_cell],
        slot, sent, cell_hot, cell_row_hot, frac, aperture, matrix_state, matrix_perm,
    )
    before = to_all(edge)
    edge, kept = call(
        middle_kernel, halves, [open_halo, (4, rows, columns)], [pltpu.VMEM((members, 2, width), F32), left_cell] + ext,
        before, cells, cell_hot, cell_row_hot, sent, kept, matrix_perm,
    )
    around = to_all(edge)
    own, frac2, pressure = call(
        exchange_kernel, halves, [slots, segs_wide, (rows, columns)], [left_seg] + ext,
        around, cells, cell_hot, slot, hot, row_hot, before, own, frac1, aperture, kept,
    )
    segs = to_group(own)
    edge, kept = call(
        source_last_kernel, both, [halo, (3, rows, columns)], [left_cell],
        cell_hot, cell_row_hot, sent, own, segs, pressure, kept, matrix_perm,
    )
    around = to_all(edge)
    matrix_out, frac3 = call(
        final_kernel,
        both,
        [matrix_state.shape, frac.shape],
        [left_seg, pltpu.VMEM((rows, columns), F32), pltpu.VMEM(frac.shape, F32), pltpu.SemaphoreType.DMA((3,))] + ext,
        around, pressure, kept, slot, hot, row_hot, own, segs, frac2, aperture,
        out_spec=HBM,
    )
    return matrix_out, frac3.reshape(frac_state.shape)


def solution(mesh):
    return jax.shard_map(
        on_device,
        mesh=mesh,
        in_specs=(
            P(None, "grp", "frac"),
            P("grp", "frac"),
            P(None, "grp", "frac"),
            P("grp", "frac"),
            P("grp", "frac", None, None),
            P("grp", "frac", None, None),
            P("grp", "frac", None, None),
            P("grp", "frac", None),
            P(None, "grp", "frac", None, None),
        ),
        out_specs=(P(None, "grp", "frac"), P(None, "grp", "frac")),
        check_vma=False,
    )
```
